32 devices in a mesh: ctx: 8 (over y, x, core), wsh: 4 (over z).
Axes of the slice: x: 2, y: 2, z: 4, core: 2. Of those that a mesh axis runs over, the one named last changes fastest.
Arguments:
- tokens: bfloat16 [4, 2048, 1024], P('wsh', 'ctx'), may hold values from -6 to 6
- cotangent: bfloat16 [4, 2048, 1024], P('wsh', 'ctx'), may hold values from -6 to 6
- doc_starts: int32 [4, 2], P('wsh'), may hold values from 0 to 1848, as said below
- doc_lengths: int32 [4, 2], P('wsh'), may hold values from 200 to 1848, as said below
- query_weight: float32 [2, 1024, 1024], P(None, 'wsh'), may hold values from -0.1875 to 0.1875
- key_weight: float32 [2, 1024, 1024], P(None, 'wsh'), may hold values from -0.1875 to 0.1875
- value_weight: float32 [2, 1024, 1024], P(None, 'wsh'), may hold values from -0.1875 to 0.1875
- out_weight: float32 [2, 1024, 1024], P(None, 'wsh'), may hold values from -0.75 to 0.75
- inner_weight: float32 [2, 1024, 4096], P(None, 'wsh'), may hold values from -0.1875 to 0.1875
- outer_weight: float32 [2, 4096, 1024], P(None, None, 'wsh'), may hold values from -0.09375 to 0.09375
- query_bias: float32 [2, 1024], P(None, 'wsh'), may hold values from -1.8 to 1.8
- value_bias: float32 [2, 1024], P(None, 'wsh'), may hold values from -1.8 to 1.8
- out_bias: float32 [2, 1024], P(None, 'wsh'), may hold values from -1.8 to 1.8
- inner_bias: float32 [2, 4096], P(None, 'wsh'), may hold values from -1.8 to 1.8
- outer_bias: float32 [2, 1024], P(None, 'wsh'), may hold values from -1.8 to 1.8
- first_gain: float32 [2, 1024], P(None, 'wsh'), may hold values from 0.5 to 1.5
- first_shift: float32 [2, 1024], P(None, 'wsh'), may hold values from -1.8 to 1.8
- second_gain: float32 [2, 1024], P(None, 'wsh'), may hold values from 0.5 to 1.5
- second_shift: float32 [2, 1024], P(None, 'wsh'), may hold values from -1.8 to 1.8
Outputs:
- out_first: bfloat16 [4, 2048, 1024], P('wsh', 'ctx')
- out_second: bfloat16 [4, 2048, 1024], P('wsh', 'ctx')
- grad_tokens: bfloat16 [4, 2048, 1024], P('wsh', 'ctx')
- grad_query_weight: float32 [2, 1024, 1024], P(None, 'wsh')
- grad_key_weight: float32 [2, 1024, 1024], P(None, 'wsh')
- grad_value_weight: float32 [2, 1024, 1024], P(None, 'wsh')
- grad_out_weight: float32 [2, 1024, 1024], P(None, 'wsh')
- grad_inner_weight: float32 [2, 1024, 4096], P(None, 'wsh')
- grad_outer_weight: float32 [2, 4096, 1024], P(None, None, 'wsh')
- grad_query_bias: float32 [2, 1024], P(None, 'wsh')
- grad_value_bias: float32 [2, 1024], P(None, 'wsh')
- grad_out_bias: float32 [2, 1024], P(None, 'wsh')
- grad_inner_bias: float32 [2, 4096], P(None, 'wsh')
- grad_outer_bias: float32 [2, 1024], P(None, 'wsh')
- grad_first_gain: float32 [2, 1024], P(None, 'wsh')
- grad_first_shift: float32 [2, 1024], P(None, 'wsh')
- grad_second_gain: float32 [2, 1024], P(None, 'wsh')
- grad_second_shift: float32 [2, 1024], P(None, 'wsh')
The draws below stay inside these ranges and needn't reach their ends.
Inputs may be any that keep to these rules, and one draw needn't show every extreme that they name: The documents of a sequence lie one after another in order from position 0 and cover all 2048 positions; doc_starts is 0 for the first and each start is the previous start plus the previous length. `doc_lengths`: each document has 200 to 1848 tokens, never more than 2000; in every sequence one has exactly 1848.
All inputs are finite; a program needn't handle non-finite values.
Results may differ from the reference program's by a relative error of at most 0.023.
Values may be sent and summed in bfloat16 or wider, within the bound.
No kernel may reach another device: no remote copies, remote signals or barrier semaphores. Data moves between devices by JAX's collectives and lax.ppermute only.
A program may use at most 384 MiB of HBM per device.

```python
import jax
import jax.numpy as jnp
from jax import lax

D = 1024
HEADS = 16
HDIM = 64
FF = 4096
LAYERS = 2
DOC_MIN = 200
LEN = 2048
NSEQ = 4
NDOC = 2
DOC_MAX = 1848


def doc_table(key):
    base_key = jax.random.fold_in(key, 7)
    first_key, second_key = jax.random.split(base_key)
    rest_docs = NDOC - 1
    extra_rows = LEN - DOC_MAX - rest_docs * DOC_MIN
    shares_raw = jax.random.randint(first_key, (NSEQ, rest_docs), 50, 101)
    weight_total = jnp.sum(shares_raw, axis=1, keepdims=True)
    shares = extra_rows * shares_raw // weight_total
    leftover = extra_rows - jnp.sum(shares, axis=1, keepdims=True)
    last_slot = (jnp.arange(rest_docs) == rest_docs - 1).astype(jnp.int32)
    others = DOC_MIN + shares + leftover * last_slot[None, :]
    placed = jax.random.randint(second_key, (NSEQ, 1), 0, NDOC)
    column = jnp.arange(NDOC, dtype=jnp.int32)[None, :]
    source = jnp.clip(column - (column > placed).astype(jnp.int32), 0, rest_docs - 1)
    source = jnp.broadcast_to(source, (NSEQ, NDOC))
    picked = jnp.take_along_axis(others, source, axis=1)
    lengths_all = jnp.where(column == placed, DOC_MAX, picked).astype(jnp.int32)
    starts_all = (jnp.cumsum(lengths_all, axis=1) - lengths_all).astype(jnp.int32)
    return (starts_all, lengths_all)


def draw_doc_starts(key, part):
    return doc_table(key)[0]


def draw_doc_lengths(key, part):
    return doc_table(key)[1]


def steps_of(own_key, dims, cuts, least, largest):
    def one(axis_at, parts):
        draws = jax.random.uniform(jax.random.fold_in(jax.random.fold_in(own_key, 6), axis_at), (parts,), jnp.float32, least / len(cuts), largest / len(cuts))
        return jnp.repeat(jnp.exp(draws), dims[axis_at] // parts).reshape((-1,) + (1,) * (len(dims) - axis_at - 1))

    level = one(*cuts[0])
    for cut in cuts[1:]:
        level = level * one(*cut)
    return level


def scatter_about(key, extent, width, bound, pieces=(), kind=jnp.bfloat16):
    result = width * jax.random.normal(key, extent, jnp.float32)
    if pieces:
        result = result * steps_of(key, extent, pieces, -0.22, 0.18)
    return jnp.clip(result, -bound, bound).astype(kind)


def setup_inputs(seed: int = 0) -> dict:
    arg_keys = jax.random.split(jax.random.key(seed), 20)
    return {
        "tokens": scatter_about(arg_keys[0], (NSEQ, LEN, D), 1.0, 6.0, ((0, 4), (1, 8))),
        "cotangent": scatter_about(arg_keys[1], (NSEQ, LEN, D), 1.0, 6.0, ((0, 4), (1, 8))),
        "doc_starts": draw_doc_starts(jax.random.fold_in(arg_keys[19], 71), 0),
        "doc_lengths": draw_doc_lengths(jax.random.fold_in(arg_keys[19], 71), 0),
        "query_weight": scatter_about(arg_keys[4], (LAYERS, D, D), D ** -0.5, 0.1875, ((1, 4),), jnp.float32),
        "key_weight": scatter_about(arg_keys[5], (LAYERS, D, D), D ** -0.5, 0.1875, ((1, 4),), jnp.float32),
        "value_weight": scatter_about(arg_keys[6], (LAYERS, D, D), D ** -0.5, 0.1875, ((1, 4),), jnp.float32),
        "out_weight": scatter_about(arg_keys[7], (LAYERS, D, D), (D // 16) ** -0.5, 0.75, ((1, 4),), jnp.float32),
        "inner_weight": scatter_about(arg_keys[8], (LAYERS, D, FF), D ** -0.5, 0.1875, ((1, 4),), jnp.float32),
        "outer_weight": scatter_about(arg_keys[9], (LAYERS, FF, D), FF ** -0.5, 0.09375, ((2, 4),), jnp.float32),
        "query_bias": scatter_about(arg_keys[10], (LAYERS, D), 0.3, 1.8, ((1, 4),), jnp.float32),
        "value_bias": scatter_about(arg_keys[11], (LAYERS, D), 0.3, 1.8, ((1, 4),), jnp.float32),
        "out_bias": scatter_about(arg_keys[12], (LAYERS, D), 0.3, 1.8, ((1, 4),), jnp.float32),
        "inner_bias": scatter_about(arg_keys[13], (LAYERS, FF), 0.3, 1.8, ((1, 4),), jnp.float32),
        "outer_bias": scatter_about(arg_keys[14], (LAYERS, D), 0.3, 1.8, ((1, 4),), jnp.float32),
        "first_gain": jnp.clip(1.0 + 0.1 * jax.random.normal(arg_keys[15], (LAYERS, D), jnp.float32), 0.5, 1.5),
        "first_shift": scatter_about(arg_keys[16], (LAYERS, D), 0.3, 1.8, ((1, 4),), jnp.float32),
        "second_gain": jnp.clip(1.0 + 0.1 * jax.random.normal(arg_keys[17], (LAYERS, D), jnp.float32), 0.5, 1.5),
        "second_shift": scatter_about(arg_keys[18], (LAYERS, D), 0.3, 1.8, ((1, 4),), jnp.float32),
    }


@jax.custom_vjp
def low(v):
    return lax.optimization_barrier(v.astype(jnp.bfloat16)).astype(jnp.float32)

@jax.custom_vjp
def low_back(v):
    return v

def low_keep(v):
    return (low(v), None)

def low_pass(kept, grad):
    return (grad,)

def back_keep(v):
    return (v, None)

def back_low(kept, grad):
    return (low(grad),)
low.defvjp(low_keep, low_pass)
low_back.defvjp(back_keep, back_low)
epsilon = 1e-05
neg_fill = -1e+30
highest = lax.Precision.HIGHEST

def normalize(values_in, gain_row, shift_row):
    centre = values_in - lax.optimization_barrier(jnp.mean(values_in, axis=-1, keepdims=True))
    spread = lax.optimization_barrier(jnp.mean(centre * centre, axis=-1, keepdims=True))
    return centre * lax.rsqrt(spread + epsilon) * gain_row + shift_row

def matmul(left, right):
    return jnp.einsum('...d,de->...e', left, right, precision=highest)

def doc_labels(starts, lengths):
    positions = jnp.arange(LEN, dtype=jnp.int32)
    inside = (positions[None, :, None] >= starts[:, None, :]) & (positions[None, :, None] < (starts + lengths)[:, None, :])
    labels = jnp.arange(1, starts.shape[1] + 1, dtype=jnp.int32)
    return lax.optimization_barrier(jnp.sum(jnp.where(inside, labels[None, None, :], 0), axis=2)).astype(jnp.int32)

def attend_sequence(queries, key_rows, value_rows, labels, score_scale):
    block = min(512, LEN)
    query_blocks = queries.reshape(LEN // block, block, HEADS, HDIM)
    label_blocks = labels.reshape(LEN // block, block)
    key_heads = key_rows.reshape(LEN, HEADS, HDIM)
    value_heads = value_rows.reshape(LEN, HEADS, HDIM)

    def one_block(packed):
        query_part, label_part = packed
        raw_scores = jnp.einsum('qhd,khd->hqk', query_part, key_heads, precision=highest)
        raw_scores = low_back(raw_scores)
        allowed = (label_part[:, None] == labels[None, :]) & (label_part[:, None] > 0)
        scores = jnp.where(allowed[None], raw_scores * score_scale, neg_fill)
        row_peak = lax.optimization_barrier(jnp.max(scores, axis=2, keepdims=True))
        exponent = jnp.exp(scores - row_peak)
        probability = low(exponent / lax.optimization_barrier(jnp.sum(exponent, axis=2, keepdims=True)))
        mixed_part = jnp.einsum('hqk,khd->qhd', probability, value_heads, precision=highest)
        return mixed_part.reshape(block, HEADS * HDIM)
    mixed_all = lax.map(jax.checkpoint(one_block), (query_blocks, label_blocks))
    return mixed_all.reshape(LEN, HEADS * HDIM)

def encoder_layer(activation, weights, labels, score_scale):
    query_weight, key_weight, value_weight, out_weight, inner_weight, outer_weight, query_bias, value_bias, out_bias, inner_bias, outer_bias, first_gain, first_shift, second_gain, second_shift = tuple((low(piece) for piece in weights))
    activation = low(activation)
    queries = low(low_back(matmul(activation, query_weight) + query_bias))
    key_rows = low(low_back(matmul(activation, key_weight)))
    value_rows = low(low_back(matmul(activation, value_weight) + value_bias))
    mixed_heads = lax.map(lambda packed: attend_sequence(packed[0], packed[1], packed[2], packed[3], score_scale), (queries, key_rows, value_rows, labels))
    mixed_heads = low(low_back(mixed_heads))
    branch = low_back(matmul(mixed_heads, out_weight) + out_bias)
    hidden = normalize(activation + branch, first_gain, first_shift)
    inner_pre = low_back(matmul(low(hidden), inner_weight) + inner_bias)
    active = low(jax.nn.gelu(inner_pre, approximate=False))
    outer_out = low_back(matmul(active, outer_weight) + outer_bias)
    return normalize(hidden + outer_out, second_gain, second_shift)

def reference(tokens, cotangent, doc_starts, doc_lengths, query_weight, key_weight, value_weight, out_weight, inner_weight, outer_weight, query_bias, value_bias, out_bias, inner_bias, outer_bias, first_gain, first_shift, second_gain, second_shift):
    labels = doc_labels(doc_starts, doc_lengths)
    params = (query_weight, key_weight, value_weight, out_weight, inner_weight, outer_weight, query_bias, value_bias, out_bias, inner_bias, outer_bias, first_gain, first_shift, second_gain, second_shift)
    score_scale = HDIM ** (-0.5)

    def forward(inputs, weights):
        results = []
        current = inputs
        for layer_index in range(LAYERS):
            current = encoder_layer(current, tuple((piece[layer_index] for piece in weights)), labels, score_scale)
            results.append(current)
        return (results[0], results[LAYERS - 1])
    (first, second), pull = jax.vjp(forward, tokens.astype(jnp.float32), params)
    grad_input, grads = pull((jnp.zeros_like(first), cotangent.astype(jnp.float32)))
    return (first.astype(jnp.bfloat16), second.astype(jnp.bfloat16), grad_input.astype(jnp.bfloat16), grads[0], grads[1], grads[2], grads[3], grads[4], grads[5], grads[6], grads[7], grads[8], grads[9], grads[10], grads[11], grads[12], grads[13], grads[14])
```

```python
import functools

import jax
import jax.numpy as jnp
from jax import lax
from jax.experimental import pallas as pl
from jax.experimental.pallas import tpu as pltpu
from jax.sharding import PartitionSpec as P

HEADS = 16
HDIM = 64
LAYERS = 2
DOC_CAP = 2000


epsilon = 1e-05
neg_fill = -1e30
head_pair = 2


def from_behind(block, axis, distance):
    devices = range(lax.axis_size(axis))
    route = [(i - distance, i) for i in devices if i - distance in devices]
    return lax.ppermute(block, axis, route)


def normalize(values_in, gain_row, shift_row):
    centre = values_in - jnp.mean(values_in, axis=-1, keepdims=True)
    spread = jnp.mean(centre * centre, axis=-1, keepdims=True)
    return centre * lax.rsqrt(spread + epsilon) * gain_row + shift_row


def exact_gelu(values_in):
    return jax.nn.gelu(values_in, approximate=False)


def product(form, left, right):
    return jnp.einsum(form, left, right, preferred_element_type=jnp.float32)


def doc_labels(positions, starts, lengths):
    inside = (positions[:, None] >= starts[None, :]) & (
        positions[:, None] < (starts + lengths)[None, :]
    )
    labels = jnp.arange(1, starts.shape[0] + 1, dtype=jnp.int32)
    return jnp.sum(jnp.where(inside, labels[None, :], 0), axis=1)


def extend_rows(rows_in, dim, reach, mover):
    pieces = []
    for offset in range(-reach, reach + 1):
        if offset == 0:
            pieces.append(rows_in)
        else:
            pieces.append(mover(rows_in, -offset))
    return jnp.concatenate(pieces, axis=dim)


def move_keys_fwd(rows_in, steps):
    return from_behind(rows_in, "ctx", steps)


def move_keys_back(rows_in, steps):
    return from_behind(rows_in, "ctx", steps)


def fetch_forward(params, layer_index):
    shards = [piece[layer_index].astype(jnp.bfloat16) for piece in params]
    return (
        lax.all_gather(shards[0], "wsh", axis=0, tiled=True),
        lax.all_gather(shards[1], "wsh", axis=0, tiled=True),
        lax.all_gather(shards[2], "wsh", axis=0, tiled=True),
        lax.all_gather(shards[3], "wsh", axis=0, tiled=True),
        lax.all_gather(shards[4], "wsh", axis=0, tiled=True),
        lax.all_gather(shards[5], "wsh", axis=1, tiled=True),
        lax.all_gather(shards[6], "wsh", axis=0, tiled=True),
        lax.all_gather(shards[7], "wsh", axis=0, tiled=True),
        lax.all_gather(shards[8], "wsh", axis=0, tiled=True),
        lax.all_gather(shards[9], "wsh", axis=0, tiled=True),
        lax.all_gather(shards[10], "wsh", axis=0, tiled=True),
        lax.all_gather(shards[11], "wsh", axis=0, tiled=True),
        lax.all_gather(shards[12], "wsh", axis=0, tiled=True),
        lax.all_gather(shards[13], "wsh", axis=0, tiled=True),
        lax.all_gather(shards[14], "wsh", axis=0, tiled=True),
    )


def fetch_backward(params, layer_index):
    shards = [piece[layer_index].astype(jnp.bfloat16) for piece in params]
    return (
        lax.all_gather(shards[0], "wsh", axis=0, tiled=True),
        lax.all_gather(shards[1], "wsh", axis=0, tiled=True),
        lax.all_gather(shards[2], "wsh", axis=0, tiled=True),
        lax.all_gather(shards[3], "wsh", axis=0, tiled=True),
        lax.all_gather(shards[4], "wsh", axis=0, tiled=True),
        lax.all_gather(shards[5], "wsh", axis=1, tiled=True),
        lax.all_gather(shards[6], "wsh", axis=0, tiled=True),
        lax.all_gather(shards[7], "wsh", axis=0, tiled=True),
        lax.all_gather(shards[8], "wsh", axis=0, tiled=True),
        lax.all_gather(shards[9], "wsh", axis=0, tiled=True),
        lax.all_gather(shards[10], "wsh", axis=0, tiled=True),
        lax.all_gather(shards[11], "wsh", axis=0, tiled=True),
        lax.all_gather(shards[12], "wsh", axis=0, tiled=True),
        lax.all_gather(shards[13], "wsh", axis=0, tiled=True),
        lax.all_gather(shards[14], "wsh", axis=0, tiled=True),
    )


def reduce_grads(local_grads):
    shares = (
        lax.psum_scatter(
            local_grads[0].astype(jnp.bfloat16), "wsh", scatter_dimension=0, tiled=True
        ).astype(jnp.float32),
        lax.psum_scatter(
            local_grads[1].astype(jnp.bfloat16), "wsh", scatter_dimension=0, tiled=True
        ).astype(jnp.float32),
        lax.psum_scatter(
            local_grads[2].astype(jnp.bfloat16), "wsh", scatter_dimension=0, tiled=True
        ).astype(jnp.float32),
        lax.psum_scatter(
            local_grads[3].astype(jnp.bfloat16), "wsh", scatter_dimension=0, tiled=True
        ).astype(jnp.float32),
        lax.psum_scatter(
            local_grads[4].astype(jnp.bfloat16), "wsh", scatter_dimension=0, tiled=True
        ).astype(jnp.float32),
        lax.psum_scatter(
            local_grads[5].astype(jnp.bfloat16), "wsh", scatter_dimension=1, tiled=True
        ).astype(jnp.float32),
        lax.psum_scatter(
            local_grads[6].astype(jnp.bfloat16), "wsh", scatter_dimension=0, tiled=True
        ).astype(jnp.float32),
        lax.psum_scatter(
            local_grads[7].astype(jnp.bfloat16), "wsh", scatter_dimension=0, tiled=True
        ).astype(jnp.float32),
        lax.psum_scatter(
            local_grads[8].astype(jnp.bfloat16), "wsh", scatter_dimension=0, tiled=True
        ).astype(jnp.float32),
        lax.psum_scatter(
            local_grads[9].astype(jnp.bfloat16), "wsh", scatter_dimension=0, tiled=True
        ).astype(jnp.float32),
        lax.psum_scatter(
            local_grads[10].astype(jnp.bfloat16), "wsh", scatter_dimension=0, tiled=True
        ).astype(jnp.float32),
        lax.psum_scatter(
            local_grads[11].astype(jnp.bfloat16), "wsh", scatter_dimension=0, tiled=True
        ).astype(jnp.float32),
        lax.psum_scatter(
            local_grads[12].astype(jnp.bfloat16), "wsh", scatter_dimension=0, tiled=True
        ).astype(jnp.float32),
        lax.psum_scatter(
            local_grads[13].astype(jnp.bfloat16), "wsh", scatter_dimension=0, tiled=True
        ).astype(jnp.float32),
        lax.psum_scatter(
            local_grads[14].astype(jnp.bfloat16), "wsh", scatter_dimension=0, tiled=True
        ).astype(jnp.float32),
    )
    return (
        lax.psum(shares[0].astype(jnp.bfloat16), "ctx").astype(jnp.float32),
        lax.psum(shares[1].astype(jnp.bfloat16), "ctx").astype(jnp.float32),
        lax.psum(shares[2].astype(jnp.bfloat16), "ctx").astype(jnp.float32),
        lax.psum(shares[3].astype(jnp.bfloat16), "ctx").astype(jnp.float32),
        lax.psum(shares[4].astype(jnp.bfloat16), "ctx").astype(jnp.float32),
        lax.psum(shares[5].astype(jnp.bfloat16), "ctx").astype(jnp.float32),
        lax.psum(shares[6].astype(jnp.bfloat16), "ctx").astype(jnp.float32),
        lax.psum(shares[7].astype(jnp.bfloat16), "ctx").astype(jnp.float32),
        lax.psum(shares[8].astype(jnp.bfloat16), "ctx").astype(jnp.float32),
        lax.psum(shares[9].astype(jnp.bfloat16), "ctx").astype(jnp.float32),
        lax.psum(shares[10].astype(jnp.bfloat16), "ctx").astype(jnp.float32),
        lax.psum(shares[11].astype(jnp.bfloat16), "ctx").astype(jnp.float32),
        lax.psum(shares[12].astype(jnp.bfloat16), "ctx").astype(jnp.float32),
        lax.psum(shares[13].astype(jnp.bfloat16), "ctx").astype(jnp.float32),
        lax.psum(shares[14].astype(jnp.bfloat16), "ctx").astype(jnp.float32),
    )


def attend(queries, key_ext, value_ext, allowed, score_scale):
    rows_local = queries.shape[0]
    rows_keys = key_ext.shape[0]
    groups = HEADS // head_pair
    span = head_pair * HDIM
    query_groups = queries.reshape(rows_local, groups, span)
    key_groups = key_ext.reshape(rows_keys, groups, span)
    value_groups = value_ext.reshape(rows_keys, groups, span)

    def one_group(group_index, carry):
        mixed_all, log_all = carry
        query_part = lax.dynamic_index_in_dim(query_groups, group_index, 1, keepdims=False).reshape(
            rows_local, head_pair, HDIM
        )
        key_part = lax.dynamic_index_in_dim(key_groups, group_index, 1, keepdims=False).reshape(
            rows_keys, head_pair, HDIM
        )
        value_part = lax.dynamic_index_in_dim(value_groups, group_index, 1, keepdims=False).reshape(
            rows_keys, head_pair, HDIM
        )
        raw_scores = product("qhd,khd->hqk", query_part, key_part)
        scores = jnp.where(allowed[None], raw_scores * score_scale, neg_fill)
        row_peak = jnp.max(scores, axis=2, keepdims=True)
        exponent = jnp.exp(scores - row_peak)
        row_total = jnp.sum(exponent, axis=2, keepdims=True)
        probability = (exponent / row_total).astype(jnp.bfloat16)
        mixed_part = product("hqk,khd->qhd", probability, value_part)
        mixed_all = lax.dynamic_update_index_in_dim(
            mixed_all, mixed_part.reshape(rows_local, span), group_index, 1
        )
        log_all = lax.dynamic_update_index_in_dim(
            log_all, (row_peak + jnp.log(row_total))[:, :, 0], group_index, 0
        )
        return (mixed_all, log_all)

    start_carry = (
        jnp.zeros((rows_local, groups, span), jnp.float32),
        jnp.zeros((groups, head_pair, rows_local), jnp.float32),
    )
    mixed_all, log_all = lax.fori_loop(0, groups, one_group, start_carry)
    return (mixed_all.reshape(rows_local, groups * span), log_all)


def attend_back(queries, key_ext, value_ext, grad_mixed, log_all, allowed, score_scale):
    rows_local = queries.shape[0]
    rows_keys = key_ext.shape[0]
    groups = HEADS // head_pair
    span = head_pair * HDIM
    query_groups = queries.reshape(rows_local, groups, span)
    key_groups = key_ext.reshape(rows_keys, groups, span)
    value_groups = value_ext.reshape(rows_keys, groups, span)
    grad_groups = grad_mixed.reshape(rows_local, groups, span)

    def one_group(group_index, carry):
        query_part = lax.dynamic_index_in_dim(query_groups, group_index, 1, keepdims=False).reshape(
            rows_local, head_pair, HDIM
        )
        key_part = lax.dynamic_index_in_dim(key_groups, group_index, 1, keepdims=False).reshape(
            rows_keys, head_pair, HDIM
        )
        value_part = lax.dynamic_index_in_dim(value_groups, group_index, 1, keepdims=False).reshape(
            rows_keys, head_pair, HDIM
        )
        grad_part = lax.dynamic_index_in_dim(grad_groups, group_index, 1, keepdims=False).reshape(
            rows_local, head_pair, HDIM
        )
        log_part = lax.dynamic_index_in_dim(log_all, group_index, 0, keepdims=False)
        raw_scores = product("qhd,khd->hqk", query_part, key_part)
        scores = jnp.where(allowed[None], raw_scores * score_scale, neg_fill)
        probability = jnp.exp(scores - log_part[:, :, None])
        grad_prob = product("qhd,khd->hqk", grad_part, value_part)
        row_delta = jnp.sum(probability * grad_prob, axis=2, keepdims=True)
        grad_scores = (probability * (grad_prob - row_delta) * score_scale).astype(jnp.bfloat16)
        query_term = product("hqk,khd->qhd", grad_scores, key_part)
        grad_query = lax.dynamic_update_index_in_dim(
            carry[0], query_term.reshape(rows_local, span), group_index, 1
        )
        delta_all = lax.dynamic_update_index_in_dim(carry[1], row_delta[:, :, 0], group_index, 0)
        key_term = product("hqk,qhd->khd", grad_scores, query_part)
        value_term = product("hqk,qhd->khd", probability.astype(jnp.bfloat16), grad_part)
        grad_key = lax.dynamic_update_index_in_dim(
            carry[2], key_term.reshape(rows_keys, span), group_index, 1
        )
        grad_value = lax.dynamic_update_index_in_dim(
            carry[3], value_term.reshape(rows_keys, span), group_index, 1
        )
        return (grad_query, delta_all, grad_key, grad_value)

    start_carry = (
        jnp.zeros((rows_local, groups, span), jnp.float32),
        jnp.zeros((groups, head_pair, rows_local), jnp.float32),
    )
    start_carry = start_carry + (
        jnp.zeros((rows_keys, groups, span), jnp.float32),
        jnp.zeros((rows_keys, groups, span), jnp.float32),
    )
    finals = lax.fori_loop(0, groups, one_group, start_carry)
    grad_query = finals[0].reshape(rows_local, groups * span)
    return (
        grad_query,
        finals[2].reshape(rows_keys, groups * span),
        finals[3].reshape(rows_keys, groups * span),
    )


def layer_forward(activation, gathered, allowed, halo_rows, score_scale):
    (
        query_weight,
        key_weight,
        value_weight,
        out_weight,
        inner_weight,
        outer_weight,
        query_bias,
        value_bias,
        out_bias,
        inner_bias,
        outer_bias,
        first_gain,
        first_shift,
        second_gain,
        second_shift,
    ) = gathered
    rows_local = activation.shape[0]
    queries = (product("td,de->te", activation, query_weight) + query_bias).astype(jnp.bfloat16)
    key_rows = product("td,de->te", activation, key_weight).astype(jnp.bfloat16)
    value_rows = (product("td,de->te", activation, value_weight) + value_bias).astype(jnp.bfloat16)
    stacked = jnp.stack([key_rows, value_rows])
    extended = extend_rows(stacked, 1, halo_rows // rows_local, move_keys_fwd)
    mixed_heads, log_all = attend(queries, extended[0], extended[1], allowed, score_scale)
    mixed_low = mixed_heads.astype(jnp.bfloat16)
    first_pre = activation.astype(jnp.float32) + (
        product("td,de->te", mixed_low, out_weight) + out_bias
    )
    hidden = normalize(first_pre, first_gain.astype(jnp.float32), first_shift.astype(jnp.float32))
    hidden_low = hidden.astype(jnp.bfloat16)
    inner_pre = product("td,df->tf", hidden_low, inner_weight) + inner_bias
    active_low = exact_gelu(inner_pre).astype(jnp.bfloat16)
    second_pre = hidden + (product("tf,fd->td", active_low, outer_weight) + outer_bias)
    result_rows = normalize(
        second_pre, second_gain.astype(jnp.float32), second_shift.astype(jnp.float32)
    )
    saved = (
        activation,
        queries,
        extended,
        log_all,
        mixed_low,
        first_pre,
        hidden_low,
        inner_pre,
        active_low,
        second_pre,
    )
    return (saved, result_rows)


def return_rows(grad_ext, halo_rows, rows_local):
    reach = halo_rows // rows_local
    total = grad_ext[:, halo_rows : halo_rows + rows_local]
    for offset in range(-reach, reach + 1):
        if offset != 0:
            begin = halo_rows + offset * rows_local
            block_rows = grad_ext[:, begin : begin + rows_local]
            total = total + from_behind(block_rows.astype(jnp.bfloat16), "ctx", offset).astype(
                block_rows.dtype
            )
    return total


def layer_backward(gradient, saved, weights, allowed, halo_rows, score_scale):
    (
        query_weight,
        key_weight,
        value_weight,
        out_weight,
        inner_weight,
        outer_weight,
        query_bias,
        value_bias,
        out_bias,
        inner_bias,
        outer_bias,
        first_gain,
        first_shift,
        second_gain,
        second_shift,
    ) = weights
    (
        activation,
        queries,
        extended,
        log_all,
        mixed_low,
        first_pre,
        hidden_low,
        inner_pre,
        active_low,
        second_pre,
    ) = saved
    rows_local = activation.shape[0]
    reach = halo_rows // rows_local
    _, second_pull = jax.vjp(
        normalize, second_pre, second_gain.astype(jnp.float32), second_shift.astype(jnp.float32)
    )
    grad_second, grad_second_gain, grad_second_shift = second_pull(gradient)
    grad_outer = grad_second.astype(jnp.bfloat16)
    grad_outer_weight = product("tf,td->fd", active_low, grad_outer)
    grad_outer_bias = jnp.sum(grad_outer.astype(jnp.float32), axis=0)
    grad_active = product("td,fd->tf", grad_outer, outer_weight)
    _, gelu_pull = jax.vjp(exact_gelu, inner_pre)
    (grad_inner,) = gelu_pull(grad_active)
    grad_inner_low = grad_inner.astype(jnp.bfloat16)
    grad_inner_weight = product("td,tf->df", hidden_low, grad_inner_low)
    grad_inner_bias = jnp.sum(grad_inner_low.astype(jnp.float32), axis=0)
    grad_hidden = grad_second + product("tf,df->td", grad_inner_low, inner_weight)
    _, first_pull = jax.vjp(
        normalize, first_pre, first_gain.astype(jnp.float32), first_shift.astype(jnp.float32)
    )
    grad_first, grad_first_gain, grad_first_shift = first_pull(grad_hidden)
    grad_branch = grad_first.astype(jnp.bfloat16)
    grad_out_weight = product("te,td->ed", mixed_low, grad_branch)
    grad_out_bias = jnp.sum(grad_branch.astype(jnp.float32), axis=0)
    grad_mixed = product("td,ed->te", grad_branch, out_weight).astype(jnp.bfloat16)
    own_rows = extended[:, halo_rows : halo_rows + rows_local]
    key_ext = extend_rows(own_rows, 1, reach, move_keys_back)
    query_sum, key_win, value_win = attend_back(
        queries, key_ext[0], key_ext[1], grad_mixed, log_all, allowed, score_scale
    )
    owned = return_rows(jnp.stack([key_win, value_win]), halo_rows, rows_local)
    key_sum = owned[0]
    value_sum = owned[1]
    grad_query = query_sum.astype(jnp.bfloat16)
    grad_key = key_sum.astype(jnp.bfloat16)
    grad_value = value_sum.astype(jnp.bfloat16)
    grad_query_weight = product("te,td->ed", activation, grad_query)
    grad_key_weight = product("te,td->ed", activation, grad_key)
    grad_value_weight = product("te,td->ed", activation, grad_value)
    grad_query_bias = jnp.sum(grad_query.astype(jnp.float32), axis=0)
    grad_value_bias = jnp.sum(grad_value.astype(jnp.float32), axis=0)
    grad_activation = (
        grad_first
        + product("td,ed->te", grad_query, query_weight)
        + product("td,ed->te", grad_key, key_weight)
        + product("td,ed->te", grad_value, value_weight)
    )
    local_grads = (
        grad_query_weight,
        grad_key_weight,
        grad_value_weight,
        grad_out_weight,
        grad_inner_weight,
        grad_outer_weight,
        grad_query_bias,
        grad_value_bias,
        grad_out_bias,
        grad_inner_bias,
        grad_outer_bias,
        grad_first_gain,
        grad_first_shift,
        grad_second_gain,
        grad_second_shift,
    )
    return (grad_activation, local_grads)


def window_body(
    tokens,
    cotangent,
    doc_starts,
    doc_lengths,
    query_weight,
    key_weight,
    value_weight,
    out_weight,
    inner_weight,
    outer_weight,
    query_bias,
    value_bias,
    out_bias,
    inner_bias,
    outer_bias,
    first_gain,
    first_shift,
    second_gain,
    second_shift,
):
    params = (
        query_weight,
        key_weight,
        value_weight,
        out_weight,
        inner_weight,
        outer_weight,
        query_bias,
        value_bias,
        out_bias,
        inner_bias,
        outer_bias,
        first_gain,
        first_shift,
        second_gain,
        second_shift,
    )
    rows_local = tokens.shape[1]
    ctx_count = lax.axis_size("ctx")
    reach = min(-(-(DOC_CAP - 1) // rows_local), ctx_count - 1)
    halo_rows = reach * rows_local
    window = rows_local + 2 * halo_rows
    row_start = lax.axis_index("ctx") * rows_local
    local_positions = row_start + jnp.arange(rows_local, dtype=jnp.int32)
    window_positions = row_start - halo_rows + jnp.arange(window, dtype=jnp.int32)
    local_labels = doc_labels(local_positions, doc_starts[0], doc_lengths[0])
    window_labels = doc_labels(window_positions, doc_starts[0], doc_lengths[0])
    allowed = (local_labels[:, None] == window_labels[None, :]) & (local_labels[:, None] > 0)
    score_scale = HDIM ** (-0.5)
    activation = tokens[0]
    stashed = []
    outputs = []
    for layer_index in range(LAYERS):
        gathered = fetch_forward(params, layer_index)
        saved, result_rows = layer_forward(activation, gathered, allowed, halo_rows, score_scale)
        stashed.append((saved, gathered))
        outputs.append(result_rows)
        activation = result_rows.astype(jnp.bfloat16)
    gradient = cotangent[0].astype(jnp.float32)
    reduced = [None] * LAYERS
    for layer_index in reversed(range(LAYERS)):
        saved, gathered = stashed[layer_index]
        weights_now = fetch_backward(params, layer_index)
        gradient, local_grads = layer_backward(
            gradient, saved, weights_now, allowed, halo_rows, score_scale
        )
        reduced[layer_index] = reduce_grads(local_grads)
    stacked_grads = [
        jnp.stack([reduced[layer_index][member] for layer_index in range(LAYERS)])
        for member in range(15)
    ]
    heads_out = [
        outputs[0].astype(jnp.bfloat16)[None],
        outputs[LAYERS - 1].astype(jnp.bfloat16)[None],
        gradient.astype(jnp.bfloat16)[None],
    ]
    return tuple(heads_out + stacked_grads)


NN = (((1,), (0,)), ((), ()))
NT = (((1,), (1,)), ((), ()))
TN = (((0,), (0,)), ((), ()))
LANES = 128
QUERY_BLOCK = 256
CORE, ALONG_X, ALONG_Y = 1, 2, 4


def mm(left, right, dims=NN):
    return lax.dot_general(left, right, dims, preferred_element_type=jnp.float32)


def swap(block, mask):
    devices = range(lax.axis_size("ctx"))
    return lax.ppermute(block, "ctx", [(i, i ^ mask) for i in devices])


def turn(block, distance):
    count = lax.axis_size("wsh")
    return lax.ppermute(block, "wsh", [(i, (i + distance) % count) for i in range(count)])


def low(values_in):
    return values_in.astype(jnp.bfloat16)


def wide(values_in):
    return values_in.astype(jnp.float32)


def mask_features(label_col):
    rows = label_col.shape[0]
    lane = lax.broadcasted_iota(jnp.int32, (rows, LANES), 1)
    hit = lax.rem(lane, HDIM) == jnp.broadcast_to(label_col, (rows, LANES))
    return (
        jnp.where(hit, neg_fill, 0.0).astype(jnp.bfloat16),
        jnp.where(hit, 0.0, 1.0).astype(jnp.bfloat16),
    )


def fill_key_scratch(key_rows, label_col, key_mask):
    lane = lax.broadcasted_iota(jnp.int32, key_rows.shape, 1)
    _, key_features = mask_features(label_col)
    key_mask[0] = jnp.where(lane < HDIM, key_rows, key_features)
    key_mask[1] = jnp.where(lane < HDIM, key_features, key_rows)


def attention_forward_kernel(
    query_ref, key_ref, value_ref, label_ref, query_label_ref, mixed_ref, log_ref, key_mask, value_t
):
    @pl.when(pl.program_id(0) == 0)
    def _():
        fill_key_scratch(key_ref[...], label_ref[...], key_mask)
        value_t[...] = value_ref[...].T

    scaled = low(wide(query_ref[...]) * HDIM ** (-0.5))
    lane = lax.broadcasted_iota(jnp.int32, scaled.shape, 1)
    features, _ = mask_features(query_label_ref[...])
    parts = []
    for head in range(2):
        mine = (lane < HDIM) if head == 0 else (lane >= HDIM)
        scores = mm(key_mask[head], jnp.where(mine, scaled, features), NT)
        peak = jnp.max(scores, axis=0, keepdims=True)
        exponent = jnp.exp(scores - peak)
        total = jnp.sum(exponent, axis=0, keepdims=True)
        mixed = mm(value_t[pl.ds(HDIM * head, HDIM), :], low(exponent))
        parts.append(mixed / total)
        log_ref[pl.ds(head, 1), :] = peak + jnp.log(total)
    mixed_ref[...] = low(jnp.concatenate(parts, axis=0).T)


def attention_forward(packed, labels):
    rows = packed.shape[0]
    mine = pl.BlockSpec((QUERY_BLOCK, LANES), lambda i: (i, 0))
    return pl.pallas_call(
        attention_forward_kernel,
        grid=(rows // QUERY_BLOCK,),
        in_specs=[
            mine,
            pl.BlockSpec((rows, LANES), lambda i: (0, 1)),
            pl.BlockSpec((rows, LANES), lambda i: (0, 2)),
            pl.BlockSpec((rows, 1), lambda i: (0, 0)),
            pl.BlockSpec((QUERY_BLOCK, 1), lambda i: (i, 0)),
        ],
        out_specs=[mine, pl.BlockSpec((2, QUERY_BLOCK), lambda i: (0, i))],
        out_shape=[
            jax.ShapeDtypeStruct((rows, LANES), jnp.bfloat16),
            jax.ShapeDtypeStruct((2, rows), jnp.float32),
        ],
        scratch_shapes=[
            pltpu.VMEM((2, rows, LANES), jnp.bfloat16),
            pltpu.VMEM((LANES, rows), jnp.bfloat16),
        ],
        cost_estimate=pl.CostEstimate(
            flops=16 * rows * rows * LANES, bytes_accessed=rows * 1024, transcendentals=2 * rows * rows
        ),
        name="attention_forward",
    )(packed, packed, packed, labels, labels)


def attention_backward_kernel(
    query_ref,
    key_ref,
    value_ref,
    label_ref,
    query_label_ref,
    grad_ref,
    log_ref,
    out_query_ref,
    out_key_ref,
    out_value_ref,
    key_mask,
    key_t,
    key_sum,
    value_sum,
):
    step = pl.program_id(0)

    @pl.when(step == 0)
    def _():
        fill_key_scratch(key_ref[...], label_ref[...], key_mask)
        key_t[...] = key_ref[...].T
        key_sum[...] = jnp.zeros_like(key_sum)
        value_sum[...] = jnp.zeros_like(value_sum)

    scaled = low(wide(query_ref[...]) * HDIM ** (-0.5))
    grad = grad_ref[...]
    value_rows = value_ref[...]
    lane = lax.broadcasted_iota(jnp.int32, scaled.shape, 1)
    features, _ = mask_features(query_label_ref[...])
    zero = jnp.zeros(scaled.shape, jnp.bfloat16)
    parts = []
    for head in range(2):
        mine = (lane < HDIM) if head == 0 else (lane >= HDIM)
        query_own = jnp.where(mine, scaled, zero)
        grad_own = jnp.where(mine, grad, zero)
        scores = mm(key_mask[head], jnp.where(mine, scaled, features), NT)
        probability = jnp.exp(scores - log_ref[pl.ds(head, 1), :])
        grad_prob = mm(value_rows, grad_own, NT)
        delta = jnp.sum(probability * grad_prob, axis=0, keepdims=True)
        grad_scores = low(probability * (grad_prob - delta))
        key_sum[...] += mm(grad_scores, query_own)
        value_sum[...] += mm(low(probability), grad_own)
        parts.append(mm(key_t[pl.ds(HDIM * head, HDIM), :], grad_scores) * HDIM ** (-0.5))
    out_query_ref[...] = low(jnp.concatenate(parts, axis=0).T)

    @pl.when(step == pl.num_programs(0) - 1)
    def _():
        out_key_ref[...] = low(key_sum[...])
        out_value_ref[...] = low(value_sum[...])


def attention_backward(packed, labels, grad, log_all):
    rows = packed.shape[0]
    mine = pl.BlockSpec((QUERY_BLOCK, LANES), lambda i: (i, 0))
    whole = pl.BlockSpec((rows, LANES), lambda i: (0, 0))
    return pl.pallas_call(
        attention_backward_kernel,
        grid=(rows // QUERY_BLOCK,),
        in_specs=[
            mine,
            pl.BlockSpec((rows, LANES), lambda i: (0, 1)),
            pl.BlockSpec((rows, LANES), lambda i: (0, 2)),
            pl.BlockSpec((rows, 1), lambda i: (0, 0)),
            pl.BlockSpec((QUERY_BLOCK, 1), lambda i: (i, 0)),
            mine,
            pl.BlockSpec((2, QUERY_BLOCK), lambda i: (0, i)),
        ],
        out_specs=[mine, whole, whole],
        out_shape=[jax.ShapeDtypeStruct((rows, LANES), jnp.bfloat16)] * 3,
        scratch_shapes=[
            pltpu.VMEM((2, rows, LANES), jnp.bfloat16),
            pltpu.VMEM((LANES, rows), jnp.bfloat16),
            pltpu.VMEM((rows, LANES), jnp.float32),
            pltpu.VMEM((rows, LANES), jnp.float32),
        ],
        cost_estimate=pl.CostEstimate(
            flops=16 * rows * rows * LANES, bytes_accessed=rows * 2048, transcendentals=2 * rows * rows
        ),
        name="attention_backward",
    )(packed, packed, packed, labels, labels, grad, log_all)


def cast_blocks(weight, order, block, dim):
    layers = weight.shape[0]
    count = order.shape[0]
    shape = [weight.shape[1], weight.shape[2]]
    shape[dim] = block

    def read(layer, index, order_ref):
        place = [0, 0]
        place[dim] = order_ref[index]
        return (layer, *place)

    def kernel(order_ref, in_ref, out_ref):
        out_ref[0] = low(in_ref[...])

    return pl.pallas_call(
        kernel,
        grid_spec=pltpu.PrefetchScalarGridSpec(
            num_scalar_prefetch=1,
            grid=(layers, count),
            in_specs=[pl.BlockSpec((1, *shape), read)],
            out_specs=pl.BlockSpec((1, 1, *shape), lambda layer, index, order_ref: (layer, index, 0, 0)),
        ),
        out_shape=jax.ShapeDtypeStruct((layers, count, *shape), jnp.bfloat16),
        cost_estimate=pl.CostEstimate(
            flops=0, bytes_accessed=layers * count * shape[0] * shape[1] * 6, transcendentals=0
        ),
        name="cast_blocks",
    )(order, weight)


def place_blocks(near, far, order, layer, dim, widths, previous):
    count = near.shape[0]
    rows, columns = near.shape[1:]
    parts = len(widths)
    outs, specs = [], []
    for width in widths:
        shape = [rows, width]
        full = list(shape)
        full[dim] *= 2 * count

        def where(index, order_ref, dim=dim):
            place = [0, 0]
            place[dim] = order_ref[index]
            return (layer, *place)

        outs.append(jax.ShapeDtypeStruct((LAYERS, *full), jnp.float32))
        specs.append(pl.BlockSpec((1, *shape), where))

    def kernel(order_ref, near_ref, far_ref, *refs):
        out_refs = refs[-parts:]

        def write(source):
            begin = 0
            for out_ref, width in zip(out_refs, widths):
                out_ref[0] = wide(source[0, :, begin : begin + width])
                begin += width

        @pl.when(pl.program_id(0) < count)
        def _():
            write(near_ref)

        @pl.when(pl.program_id(0) >= count)
        def _():
            write(far_ref)

    held = [] if previous is None else list(previous)
    return pl.pallas_call(
        kernel,
        grid_spec=pltpu.PrefetchScalarGridSpec(
            num_scalar_prefetch=1,
            grid=(2 * count,),
            in_specs=[
                pl.BlockSpec((1, rows, columns), lambda i, order_ref: (jnp.minimum(i, count - 1), 0, 0)),
                pl.BlockSpec((1, rows, columns), lambda i, order_ref: (jnp.maximum(i - count, 0), 0, 0)),
            ]
            + [pl.BlockSpec(memory_space=pl.ANY)] * len(held),
            out_specs=specs,
        ),
        out_shape=outs,
        input_output_aliases={3 + i: i for i in range(len(held))},
        cost_estimate=pl.CostEstimate(
            flops=0, bytes_accessed=12 * count * rows * columns, transcendentals=0
        ),
        name="place_blocks",
    )(order, near, far, *held)


def block_columns(values_in, order, width):
    return jnp.concatenate(
        [lax.dynamic_slice_in_dim(values_in, block * width, width, 1) for block in order], axis=1
    )


def norm_forward(values_in, gain_row, shift_row):
    centre = values_in - jnp.mean(values_in, axis=-1, keepdims=True)
    spread = jnp.mean(centre * centre, axis=-1, keepdims=True)
    inverse = lax.rsqrt(spread + epsilon)
    unit = centre * inverse
    return (unit * gain_row + shift_row, unit, inverse)


def norm_backward(grad, unit, inverse, gain_row):
    grad_unit = grad * gain_row
    back = inverse * (
        grad_unit
        - jnp.mean(grad_unit, axis=-1, keepdims=True)
        - unit * jnp.mean(grad_unit * unit, axis=-1, keepdims=True)
    )
    return (back, jnp.sum(grad * unit, axis=0), jnp.sum(grad, axis=0))


def spread_tokens(rows_in):
    half = rows_in.shape[1] // 2
    left, right = rows_in[:, :half], rows_in[:, half:]
    left_pair = jnp.stack([left, swap(left, ALONG_X)])
    right_pair = jnp.stack([right, swap(right, ALONG_Y)])
    left_far = swap(left_pair, ALONG_Y)
    right_far = swap(right_pair, ALONG_X)
    left_all = jnp.concatenate([left_pair, left_far])
    right_all = jnp.stack([right_pair[0], right_far[0], right_pair[1], right_far[1]])
    near = jnp.concatenate([left_all, right_all], axis=2)
    far = swap(near, CORE)
    both = jnp.stack([near, far], axis=1)
    return both.reshape(8 * rows_in.shape[0], rows_in.shape[1])


def collect_tokens(partial):
    rows = partial.shape[0] // 8
    width = partial.shape[1]
    blocks = partial.reshape(4, 2, rows, width)
    near = blocks[:, 0] + wide(swap(low(blocks[:, 1]), CORE))
    half = width // 2
    left, right = near[:, :, :half], near[:, :, half:]
    left_sent = swap(low(jnp.stack([left[1], left[3]])), ALONG_X)
    right_sent = swap(low(right[2:]), ALONG_Y)
    left = jnp.stack([left[0], left[2]]) + wide(left_sent)
    right = right[:2] + wide(right_sent)
    left = left[0] + wide(swap(low(left[1]), ALONG_Y))
    right = right[0] + wide(swap(low(right[1]), ALONG_X))
    return jnp.concatenate([left, right], axis=1)


def plane_pieces(piece, first, second):
    pair = jnp.stack([piece, swap(piece, first)])
    near = jnp.concatenate([pair, swap(pair, second)])
    return (near, swap(near, CORE))


def exchange_heads(blocks, rows):
    parts = [blocks[k * rows : (k + 1) * rows] for k in range(8)]
    return [parts[0]] + [swap(parts[k], k) for k in range(1, 8)]


def head_split_body(
    tokens,
    cotangent,
    doc_starts,
    doc_lengths,
    query_weight,
    key_weight,
    value_weight,
    out_weight,
    inner_weight,
    outer_weight,
    query_bias,
    value_bias,
    out_bias,
    inner_bias,
    outer_bias,
    first_gain,
    first_shift,
    second_gain,
    second_shift,
):
    rows = tokens.shape[1]
    width = tokens.shape[2]
    here = lax.axis_index("ctx")
    plane = lax.axis_index("wsh")
    planes = lax.axis_size("wsh")
    shard = width // planes
    hidden = inner_weight.shape[2]
    piece = hidden // 8
    core = here % 2
    chip = here // 2
    relative = jnp.arange(8, dtype=jnp.int32)
    turned = [(plane - r) % planes for r in range(planes)]
    unturned = turned
    positions = ((here ^ relative)[:, None] * rows + jnp.arange(rows, dtype=jnp.int32)).reshape(-1)
    labels = doc_labels(positions, doc_starts[0], doc_lengths[0])[:, None]

    inner_order = core * 4 + (chip ^ jnp.arange(4, dtype=jnp.int32))
    inner_own = cast_blocks(inner_weight, inner_order, piece, 1)
    outer_own = cast_blocks(outer_weight, inner_order, piece, 0)
    joint_own = jnp.concatenate(
        [
            low(lax.dynamic_slice_in_dim(weight, here * LANES, LANES, 2))
            for weight in (query_weight, key_weight, value_weight)
        ],
        axis=2,
    )
    small_own = low(
        jnp.concatenate(
            [
                query_bias,
                value_bias,
                out_bias,
                outer_bias,
                first_gain,
                first_shift,
                second_gain,
                second_shift,
                inner_bias,
            ],
            axis=1,
        )
    )
    small_turned = jnp.stack([small_own] + [turn(small_own, r) for r in range(1, planes)])
    small_all = jnp.stack(
        [lax.dynamic_index_in_dim(small_turned, unturned[i], 0, keepdims=False) for i in range(planes)], axis=1
    )

    def small(layer, index):
        return small_all[layer, :, index * shard : (index + 1) * shard].reshape(width)

    inner_bias_all = small_all[:, :, 8 * shard :].reshape(LAYERS, hidden)

    def gather_joint(layer):
        own = joint_own[layer]
        stack = jnp.stack([own] + [turn(own, r) for r in range(1, planes)])
        return jnp.concatenate(
            [lax.dynamic_index_in_dim(stack, unturned[i], 0, keepdims=False) for i in range(planes)], axis=0
        )

    def gather_inner(layer):
        own = inner_own[layer]
        others = jnp.concatenate([turn(own[0], r) for r in range(1, planes)], axis=0)
        by_x = swap(others, ALONG_X)
        near_y = swap(others, ALONG_Y)
        far_y = swap(by_x, ALONG_Y)
        return jnp.concatenate(
            [jnp.concatenate([own[j], part], axis=0) for j, part in enumerate((others, by_x, near_y, far_y))],
            axis=1,
        )

    def gather_outer(layer):
        own = outer_own[layer]
        others = jnp.concatenate([turn(own[0], r) for r in range(1, planes)], axis=1)
        by_y = swap(others, ALONG_Y)
        near_x = swap(others, ALONG_X)
        far_x = swap(by_y, ALONG_X)
        return jnp.concatenate(
            [jnp.concatenate([own[j], part], axis=1) for j, part in enumerate((others, near_x, by_y, far_x))],
            axis=0,
        )

    activation = tokens[0]
    stashed = []
    outputs = []
    for layer in range(LAYERS):
        joint = gather_joint(layer)
        out_full = lax.all_gather(low(out_weight[layer]), "wsh", axis=0, tiled=True)
        inner_full = gather_inner(layer)
        outer_full = gather_outer(layer)
        first_gain_row, first_shift_row = wide(small(layer, 4)), wide(small(layer, 5))
        second_gain_row, second_shift_row = wide(small(layer, 6)), wide(small(layer, 7))

        everyone = spread_tokens(activation)
        query_bias_own = lax.dynamic_slice_in_dim(small(layer, 0), here * LANES, LANES, 0)
        value_bias_own = lax.dynamic_slice_in_dim(small(layer, 1), here * LANES, LANES, 0)
        joint_bias = jnp.concatenate([query_bias_own, jnp.zeros_like(query_bias_own), value_bias_own])
        packed = low(mm(everyone, joint) + wide(joint_bias))
        mixed, log_all = attention_forward(packed, labels)
        mixed_heads = jnp.concatenate(exchange_heads(mixed, rows), axis=1)
        mixed_tokens = block_columns(mixed_heads, [here ^ k for k in range(8)], LANES)
        first_pre = wide(activation) + (mm(mixed_tokens, out_full) + wide(small(layer, 2)))
        hidden_rows, first_unit, first_inverse = norm_forward(first_pre, first_gain_row, first_shift_row)
        hidden_turned = block_columns(low(hidden_rows), turned, shard)
        hidden_pair = jnp.concatenate([hidden_turned, swap(hidden_turned, CORE)], axis=0)
        inner_bias_own = jnp.concatenate(
            [lax.dynamic_slice_in_dim(inner_bias_all[layer], inner_order[j] * piece, piece, 0) for j in range(4)]
        )
        inner_pre = mm(hidden_pair, inner_full) + wide(inner_bias_own)
        below = 0.5 * (1.0 + lax.erf(inner_pre * (2.0**-0.5)))
        active = low(inner_pre * below)
        slope = low(below + inner_pre * jnp.exp(-0.5 * inner_pre * inner_pre) * ((2.0 * jnp.pi) ** -0.5))
        outer_pair = mm(active, outer_full)
        outer_turned = outer_pair[:rows] + wide(swap(low(outer_pair[rows:]), CORE))
        outer_out = block_columns(outer_turned, unturned, shard)
        second_pre = hidden_rows + (outer_out + wide(small(layer, 3)))
        result, second_unit, second_inverse = norm_forward(second_pre, second_gain_row, second_shift_row)
        stashed.append(
            (
                everyone,
                packed,
                log_all,
                mixed_tokens,
                first_unit,
                first_inverse,
                hidden_pair,
                active,
                slope,
                second_unit,
                second_inverse,
                joint,
                out_full,
                inner_full,
                outer_full,
                first_gain_row,
                second_gain_row,
            )
        )
        activation = low(result)
        outputs.append(activation)

    joint_order = here ^ jnp.array([0, 2, 4, 6, 1, 3, 5, 7], jnp.int32)
    swapped_order = here ^ jnp.array([0, 4, 2, 6, 1, 5, 3, 7], jnp.int32)
    inner_place = (joint_order % 2) * 4 + joint_order // 2
    outer_place = (swapped_order % 2) * 4 + swapped_order // 2
    gradient = wide(cotangent[0])
    small_grads = [None] * LAYERS
    out_grads = [None] * LAYERS
    joint_out = inner_out = outer_out = None
    for layer in reversed(range(LAYERS)):
        (
            everyone,
            packed,
            log_all,
            mixed_tokens,
            first_unit,
            first_inverse,
            hidden_pair,
            active,
            slope,
            second_unit,
            second_inverse,
            joint,
            out_full,
            inner_full,
            outer_full,
            first_gain_row,
            second_gain_row,
        ) = stashed[layer]
        grad_second, grad_second_gain, grad_second_shift = norm_backward(
            gradient, second_unit, second_inverse, second_gain_row
        )
        grad_outer = low(grad_second)
        grad_outer_bias = jnp.sum(wide(grad_outer), axis=0)
        grad_turned = block_columns(grad_outer, turned, shard)
        grad_pair = jnp.concatenate([grad_turned, swap(grad_turned, CORE)], axis=0)
        grad_inner = low(mm(grad_pair, outer_full, NT) * wide(slope))
        hidden_back = mm(grad_inner, inner_full, NT)
        hidden_back = hidden_back[:rows] + wide(swap(low(hidden_back[rows:]), CORE))
        grad_hidden = grad_second + block_columns(hidden_back, unturned, shard)
        grad_outer_weight = low(mm(active, grad_pair, TN))
        grad_inner_weight = low(mm(hidden_pair, grad_inner, TN))
        grad_inner_bias = jnp.sum(wide(grad_inner), axis=0)
        grad_first, grad_first_gain, grad_first_shift = norm_backward(
            grad_hidden, first_unit, first_inverse, first_gain_row
        )
        grad_branch = low(grad_first)
        grad_out_bias = jnp.sum(wide(grad_branch), axis=0)
        grad_mixed_tokens = low(mm(grad_branch, out_full, NT))
        grad_mixed = jnp.concatenate(
            [
                part if k == 0 else swap(part, k)
                for k, part in enumerate(
                    lax.dynamic_slice_in_dim(grad_mixed_tokens, (here ^ k) * LANES, LANES, 1) for k in range(8)
                )
            ],
            axis=0,
        )
        grad_out_weight = low(mm(mixed_tokens, grad_branch, TN))
        grad_query, grad_key, grad_value = attention_backward(packed, labels, grad_mixed, log_all)
        grad_packed = jnp.concatenate([grad_query, grad_key, grad_value], axis=1)
        gradient = grad_first + collect_tokens(mm(grad_packed, joint, NT))
        grad_joint = mm(everyone, grad_packed, TN)
        joint_bias_grad = jnp.sum(wide(grad_packed), axis=0)

        joint_parts = [
            lax.dynamic_slice_in_dim(grad_joint, ((plane + s) % planes) * shard, shard, 0) for s in range(planes)
        ]
        joint_sum = joint_parts[0]
        for s in range(1, planes):
            joint_sum = joint_sum + wide(turn(low(joint_parts[s]), s))
        blocks = [grad_inner_weight[:, j * piece : (j + 1) * piece] for j in range(4)]
        came = swap(jnp.stack([blocks[1], blocks[3]]), ALONG_X)
        kept = (wide(blocks[0]) + wide(came[0]), low(wide(blocks[2]) + wide(came[1])))
        inner_sum = low(kept[0] + wide(swap(kept[1], ALONG_Y)))
        inner_total = wide(inner_sum[:shard])
        for r in range(1, planes):
            inner_total = inner_total + wide(turn(inner_sum[r * shard : (r + 1) * shard], planes - r))
        blocks = [grad_outer_weight[j * piece : (j + 1) * piece] for j in range(4)]
        came = swap(jnp.stack([blocks[2], blocks[3]]), ALONG_Y)
        kept = (wide(blocks[0]) + wide(came[0]), low(wide(blocks[1]) + wide(came[1])))
        outer_sum = low(kept[0] + wide(swap(kept[1], ALONG_X)))
        outer_total = wide(outer_sum[:, :shard])
        for r in range(1, planes):
            outer_total = outer_total + wide(turn(outer_sum[:, r * shard : (r + 1) * shard], planes - r))
        joint_near, joint_far = plane_pieces(low(joint_sum), ALONG_X, ALONG_Y)
        inner_near, inner_far = plane_pieces(low(inner_total), ALONG_X, ALONG_Y)
        outer_near, outer_far = plane_pieces(low(outer_total), ALONG_Y, ALONG_X)
        joint_out = place_blocks(joint_near, joint_far, joint_order, layer, 1, (LANES,) * 3, joint_out)
        inner_out = place_blocks(inner_near, inner_far, inner_place, layer, 1, (piece,), inner_out)
        outer_out = place_blocks(outer_near, outer_far, outer_place, layer, 0, (shard,), outer_out)
        out_share = lax.psum_scatter(grad_out_weight, "wsh", scatter_dimension=0, tiled=True)
        out_grads[layer] = wide(lax.psum(out_share, "ctx"))

        placed_query = lax.dynamic_update_slice(
            jnp.zeros((width,), jnp.float32), joint_bias_grad[:LANES], (here * LANES,)
        )
        placed_value = lax.dynamic_update_slice(
            jnp.zeros((width,), jnp.float32), joint_bias_grad[2 * LANES :], (here * LANES,)
        )
        placed_inner = jnp.zeros((hidden,), jnp.float32)
        for j in range(4):
            placed_inner = lax.dynamic_update_slice(
                placed_inner, grad_inner_bias[j * piece : (j + 1) * piece], (inner_order[j] * piece,)
            )
        small_grads[layer] = jnp.concatenate(
            [
                row.reshape(planes, -1)
                for row in (
                    placed_query,
                    placed_value,
                    grad_out_bias,
                    grad_outer_bias,
                    grad_first_gain,
                    grad_first_shift,
                    grad_second_gain,
                    grad_second_shift,
                    placed_inner,
                )
            ],
            axis=1,
        )
    small_sum = lax.psum(jnp.stack(small_grads), ("ctx", "wsh"))
    small_mine = lax.dynamic_index_in_dim(small_sum, plane, 1, keepdims=False)
    small_outs = [small_mine[:, i * shard : (i + 1) * shard] for i in range(8)]
    inner_bias_out = small_mine[:, 8 * shard :]
    return (
        outputs[0][None],
        outputs[1][None],
        low(gradient)[None],
        *joint_out,
        jnp.stack(out_grads),
        inner_out[0],
        outer_out[0],
        small_outs[0],
        small_outs[1],
        small_outs[2],
        inner_bias_out,
        small_outs[3],
        small_outs[4],
        small_outs[5],
        small_outs[6],
        small_outs[7],
    )


def choose_body(mesh):
    if mesh.shape["ctx"] == 8 and HEADS // 8 == 2:
        return head_split_body
    return window_body


def solution(mesh):
    in_specs = (
        P("wsh", "ctx", None),
        P("wsh", "ctx", None),
        P("wsh", None),
        P("wsh", None),
        P(None, "wsh", None),
        P(None, "wsh", None),
        P(None, "wsh", None),
        P(None, "wsh", None),
        P(None, "wsh", None),
        P(None, None, "wsh"),
        P(None, "wsh"),
        P(None, "wsh"),
        P(None, "wsh"),
        P(None, "wsh"),
        P(None, "wsh"),
        P(None, "wsh"),
        P(None, "wsh"),
        P(None, "wsh"),
        P(None, "wsh"),
    )
    out_specs = (
        P("wsh", "ctx", None),
        P("wsh", "ctx", None),
        P("wsh", "ctx", None),
        P(None, "wsh", None),
        P(None, "wsh", None),
        P(None, "wsh", None),
        P(None, "wsh", None),
        P(None, "wsh", None),
        P(None, None, "wsh"),
        P(None, "wsh"),
        P(None, "wsh"),
        P(None, "wsh"),
        P(None, "wsh"),
        P(None, "wsh"),
        P(None, "wsh"),
        P(None, "wsh"),
        P(None, "wsh"),
        P(None, "wsh"),
    )
    return jax.shard_map(choose_body(mesh), mesh=mesh, in_specs=in_specs, out_specs=out_specs, check_vma=False)
```

```python
import functools

import jax
import jax.numpy as jnp
from jax import lax
from jax.experimental import pallas as pl
from jax.experimental.pallas import tpu as pltpu
from jax.sharding import PartitionSpec as P

HEADS = 16
HDIM = 64
LAYERS = 2
DOC_CAP = 2000


epsilon = 1e-05
neg_fill = -1e30
head_pair = 2


def from_behind(block, axis, distance):
    devices = range(lax.axis_size(axis))
    route = [(i - distance, i) for i in devices if i - distance in devices]
    return lax.ppermute(block, axis, route)


def normalize(values_in, gain_row, shift_row):
    centre = values_in - jnp.mean(values_in, axis=-1, keepdims=True)
    spread = jnp.mean(centre * centre, axis=-1, keepdims=True)
    return centre * lax.rsqrt(spread + epsilon) * gain_row + shift_row


def exact_gelu(values_in):
    return jax.nn.gelu(values_in, approximate=False)


def product(form, left, right):
    return jnp.einsum(form, left, right, preferred_element_type=jnp.float32)


def doc_labels(positions, starts, lengths):
    inside = (positions[:, None] >= starts[None, :]) & (
        positions[:, None] < (starts + lengths)[None, :]
    )
    labels = jnp.arange(1, starts.shape[0] + 1, dtype=jnp.int32)
    return jnp.sum(jnp.where(inside, labels[None, :], 0), axis=1)


def extend_rows(rows_in, dim, reach, mover):
    pieces = []
    for offset in range(-reach, reach + 1):
        if offset == 0:
            pieces.append(rows_in)
        else:
            pieces.append(mover(rows_in, -offset))
    return jnp.concatenate(pieces, axis=dim)


def move_keys_fwd(rows_in, steps):
    return from_behind(rows_in, "ctx", steps)


def move_keys_back(rows_in, steps):
    return from_behind(rows_in, "ctx", steps)


def fetch_forward(params, layer_index):
    shards = [piece[layer_index].astype(jnp.bfloat16) for piece in params]
    return (
        lax.all_gather(shards[0], "wsh", axis=0, tiled=True),
        lax.all_gather(shards[1], "wsh", axis=0, tiled=True),
        lax.all_gather(shards[2], "wsh", axis=0, tiled=True),
        lax.all_gather(shards[3], "wsh", axis=0, tiled=True),
        lax.all_gather(shards[4], "wsh", axis=0, tiled=True),
        lax.all_gather(shards[5], "wsh", axis=1, tiled=True),
        lax.all_gather(shards[6], "wsh", axis=0, tiled=True),
        lax.all_gather(shards[7], "wsh", axis=0, tiled=True),
        lax.all_gather(shards[8], "wsh", axis=0, tiled=True),
        lax.all_gather(shards[9], "wsh", axis=0, tiled=True),
        lax.all_gather(shards[10], "wsh", axis=0, tiled=True),
        lax.all_gather(shards[11], "wsh", axis=0, tiled=True),
        lax.all_gather(shards[12], "wsh", axis=0, tiled=True),
        lax.all_gather(shards[13], "wsh", axis=0, tiled=True),
        lax.all_gather(shards[14], "wsh", axis=0, tiled=True),
    )


def fetch_backward(params, layer_index):
    shards = [piece[layer_index].astype(jnp.bfloat16) for piece in params]
    return (
        lax.all_gather(shards[0], "wsh", axis=0, tiled=True),
        lax.all_gather(shards[1], "wsh", axis=0, tiled=True),
        lax.all_gather(shards[2], "wsh", axis=0, tiled=True),
        lax.all_gather(shards[3], "wsh", axis=0, tiled=True),
        lax.all_gather(shards[4], "wsh", axis=0, tiled=True),
        lax.all_gather(shards[5], "wsh", axis=1, tiled=True),
        lax.all_gather(shards[6], "wsh", axis=0, tiled=True),
        lax.all_gather(shards[7], "wsh", axis=0, tiled=True),
        lax.all_gather(shards[8], "wsh", axis=0, tiled=True),
        lax.all_gather(shards[9], "wsh", axis=0, tiled=True),
        lax.all_gather(shards[10], "wsh", axis=0, tiled=True),
        lax.all_gather(shards[11], "wsh", axis=0, tiled=True),
        lax.all_gather(shards[12], "wsh", axis=0, tiled=True),
        lax.all_gather(shards[13], "wsh", axis=0, tiled=True),
        lax.all_gather(shards[14], "wsh", axis=0, tiled=True),
    )


def reduce_grads(local_grads):
    shares = (
        lax.psum_scatter(
            local_grads[0].astype(jnp.bfloat16), "wsh", scatter_dimension=0, tiled=True
        ).astype(jnp.float32),
        lax.psum_scatter(
            local_grads[1].astype(jnp.bfloat16), "wsh", scatter_dimension=0, tiled=True
        ).astype(jnp.float32),
        lax.psum_scatter(
            local_grads[2].astype(jnp.bfloat16), "wsh", scatter_dimension=0, tiled=True
        ).astype(jnp.float32),
        lax.psum_scatter(
            local_grads[3].astype(jnp.bfloat16), "wsh", scatter_dimension=0, tiled=True
        ).astype(jnp.float32),
        lax.psum_scatter(
            local_grads[4].astype(jnp.bfloat16), "wsh", scatter_dimension=0, tiled=True
        ).astype(jnp.float32),
        lax.psum_scatter(
            local_grads[5].astype(jnp.bfloat16), "wsh", scatter_dimension=1, tiled=True
        ).astype(jnp.float32),
        lax.psum_scatter(
            local_grads[6].astype(jnp.bfloat16), "wsh", scatter_dimension=0, tiled=True
        ).astype(jnp.float32),
        lax.psum_scatter(
            local_grads[7].astype(jnp.bfloat16), "wsh", scatter_dimension=0, tiled=True
        ).astype(jnp.float32),
        lax.psum_scatter(
            local_grads[8].astype(jnp.bfloat16), "wsh", scatter_dimension=0, tiled=True
        ).astype(jnp.float32),
        lax.psum_scatter(
            local_grads[9].astype(jnp.bfloat16), "wsh", scatter_dimension=0, tiled=True
        ).astype(jnp.float32),
        lax.psum_scatter(
            local_grads[10].astype(jnp.bfloat16), "wsh", scatter_dimension=0, tiled=True
        ).astype(jnp.float32),
        lax.psum_scatter(
            local_grads[11].astype(jnp.bfloat16), "wsh", scatter_dimension=0, tiled=True
        ).astype(jnp.float32),
        lax.psum_scatter(
            local_grads[12].astype(jnp.bfloat16), "wsh", scatter_dimension=0, tiled=True
        ).astype(jnp.float32),
        lax.psum_scatter(
            local_grads[13].astype(jnp.bfloat16), "wsh", scatter_dimension=0, tiled=True
        ).astype(jnp.float32),
        lax.psum_scatter(
            local_grads[14].astype(jnp.bfloat16), "wsh", scatter_dimension=0, tiled=True
        ).astype(jnp.float32),
    )
    return (
        lax.psum(shares[0].astype(jnp.bfloat16), "ctx").astype(jnp.float32),
        lax.psum(shares[1].astype(jnp.bfloat16), "ctx").astype(jnp.float32),
        lax.psum(shares[2].astype(jnp.bfloat16), "ctx").astype(jnp.float32),
        lax.psum(shares[3].astype(jnp.bfloat16), "ctx").astype(jnp.float32),
        lax.psum(shares[4].astype(jnp.bfloat16), "ctx").astype(jnp.float32),
        lax.psum(shares[5].astype(jnp.bfloat16), "ctx").astype(jnp.float32),
        lax.psum(shares[6].astype(jnp.bfloat16), "ctx").astype(jnp.float32),
        lax.psum(shares[7].astype(jnp.bfloat16), "ctx").astype(jnp.float32),
        lax.psum(shares[8].astype(jnp.bfloat16), "ctx").astype(jnp.float32),
        lax.psum(shares[9].astype(jnp.bfloat16), "ctx").astype(jnp.float32),
        lax.psum(shares[10].astype(jnp.bfloat16), "ctx").astype(jnp.float32),
        lax.psum(shares[11].astype(jnp.bfloat16), "ctx").astype(jnp.float32),
        lax.psum(shares[12].astype(jnp.bfloat16), "ctx").astype(jnp.float32),
        lax.psum(shares[13].astype(jnp.bfloat16), "ctx").astype(jnp.float32),
        lax.psum(shares[14].astype(jnp.bfloat16), "ctx").astype(jnp.float32),
    )


def attend(queries, key_ext, value_ext, allowed, score_scale):
    rows_local = queries.shape[0]
    rows_keys = key_ext.shape[0]
    groups = HEADS // head_pair
    span = head_pair * HDIM
    query_groups = queries.reshape(rows_local, groups, span)
    key_groups = key_ext.reshape(rows_keys, groups, span)
    value_groups = value_ext.reshape(rows_keys, groups, span)

    def one_group(group_index, carry):
        mixed_all, log_all = carry
        query_part = lax.dynamic_index_in_dim(query_groups, group_index, 1, keepdims=False).reshape(
            rows_local, head_pair, HDIM
        )
        key_part = lax.dynamic_index_in_dim(key_groups, group_index, 1, keepdims=False).reshape(
            rows_keys, head_pair, HDIM
        )
        value_part = lax.dynamic_index_in_dim(value_groups, group_index, 1, keepdims=False).reshape(
            rows_keys, head_pair, HDIM
        )
        raw_scores = product("qhd,khd->hqk", query_part, key_part)
        scores = jnp.where(allowed[None], raw_scores * score_scale, neg_fill)
        row_peak = jnp.max(scores, axis=2, keepdims=True)
        exponent = jnp.exp(scores - row_peak)
        row_total = jnp.sum(exponent, axis=2, keepdims=True)
        probability = (exponent / row_total).astype(jnp.bfloat16)
        mixed_part = product("hqk,khd->qhd", probability, value_part)
        mixed_all = lax.dynamic_update_index_in_dim(
            mixed_all, mixed_part.reshape(rows_local, span), group_index, 1
        )
        log_all = lax.dynamic_update_index_in_dim(
            log_all, (row_peak + jnp.log(row_total))[:, :, 0], group_index, 0
        )
        return (mixed_all, log_all)

    start_carry = (
        jnp.zeros((rows_local, groups, span), jnp.float32),
        jnp.zeros((groups, head_pair, rows_local), jnp.float32),
    )
    mixed_all, log_all = lax.fori_loop(0, groups, one_group, start_carry)
    return (mixed_all.reshape(rows_local, groups * span), log_all)


def attend_back(queries, key_ext, value_ext, grad_mixed, log_all, allowed, score_scale):
    rows_local = queries.shape[0]
    rows_keys = key_ext.shape[0]
    groups = HEADS // head_pair
    span = head_pair * HDIM
    query_groups = queries.reshape(rows_local, groups, span)
    key_groups = key_ext.reshape(rows_keys, groups, span)
    value_groups = value_ext.reshape(rows_keys, groups, span)
    grad_groups = grad_mixed.reshape(rows_local, groups, span)

    def one_group(group_index, carry):
        query_part = lax.dynamic_index_in_dim(query_groups, group_index, 1, keepdims=False).reshape(
            rows_local, head_pair, HDIM
        )
        key_part = lax.dynamic_index_in_dim(key_groups, group_index, 1, keepdims=False).reshape(
            rows_keys, head_pair, HDIM
        )
        value_part = lax.dynamic_index_in_dim(value_groups, group_index, 1, keepdims=False).reshape(
            rows_keys, head_pair, HDIM
        )
        grad_part = lax.dynamic_index_in_dim(grad_groups, group_index, 1, keepdims=False).reshape(
            rows_local, head_pair, HDIM
        )
        log_part = lax.dynamic_index_in_dim(log_all, group_index, 0, keepdims=False)
        raw_scores = product("qhd,khd->hqk", query_part, key_part)
        scores = jnp.where(allowed[None], raw_scores * score_scale, neg_fill)
        probability = jnp.exp(scores - log_part[:, :, None])
        grad_prob = product("qhd,khd->hqk", grad_part, value_part)
        row_delta = jnp.sum(probability * grad_prob, axis=2, keepdims=True)
        grad_scores = (probability * (grad_prob - row_delta) * score_scale).astype(jnp.bfloat16)
        query_term = product("hqk,khd->qhd", grad_scores, key_part)
        grad_query = lax.dynamic_update_index_in_dim(
            carry[0], query_term.reshape(rows_local, span), group_index, 1
        )
        delta_all = lax.dynamic_update_index_in_dim(carry[1], row_delta[:, :, 0], group_index, 0)
        key_term = product("hqk,qhd->khd", grad_scores, query_part)
        value_term = product("hqk,qhd->khd", probability.astype(jnp.bfloat16), grad_part)
        grad_key = lax.dynamic_update_index_in_dim(
            carry[2], key_term.reshape(rows_keys, span), group_index, 1
        )
        grad_value = lax.dynamic_update_index_in_dim(
            carry[3], value_term.reshape(rows_keys, span), group_index, 1
        )
        return (grad_query, delta_all, grad_key, grad_value)

    start_carry = (
        jnp.zeros((rows_local, groups, span), jnp.float32),
        jnp.zeros((groups, head_pair, rows_local), jnp.float32),
    )
    start_carry = start_carry + (
        jnp.zeros((rows_keys, groups, span), jnp.float32),
        jnp.zeros((rows_keys, groups, span), jnp.float32),
    )
    finals = lax.fori_loop(0, groups, one_group, start_carry)
    grad_query = finals[0].reshape(rows_local, groups * span)
    return (
        grad_query,
        finals[2].reshape(rows_keys, groups * span),
        finals[3].reshape(rows_keys, groups * span),
    )


def layer_forward(activation, gathered, allowed, halo_rows, score_scale):
    (
        query_weight,
        key_weight,
        value_weight,
        out_weight,
        inner_weight,
        outer_weight,
        query_bias,
        value_bias,
        out_bias,
        inner_bias,
        outer_bias,
        first_gain,
        first_shift,
        second_gain,
        second_shift,
    ) = gathered
    rows_local = activation.shape[0]
    queries = (product("td,de->te", activation, query_weight) + query_bias).astype(jnp.bfloat16)
    key_rows = product("td,de->te", activation, key_weight).astype(jnp.bfloat16)
    value_rows = (product("td,de->te", activation, value_weight) + value_bias).astype(jnp.bfloat16)
    stacked = jnp.stack([key_rows, value_rows])
    extended = extend_rows(stacked, 1, halo_rows // rows_local, move_keys_fwd)
    mixed_heads, log_all = attend(queries, extended[0], extended[1], allowed, score_scale)
    mixed_low = mixed_heads.astype(jnp.bfloat16)
    first_pre = activation.astype(jnp.float32) + (
        product("td,de->te", mixed_low, out_weight) + out_bias
    )
    hidden = normalize(first_pre, first_gain.astype(jnp.float32), first_shift.astype(jnp.float32))
    hidden_low = hidden.astype(jnp.bfloat16)
    inner_pre = product("td,df->tf", hidden_low, inner_weight) + inner_bias
    active_low = exact_gelu(inner_pre).astype(jnp.bfloat16)
    second_pre = hidden + (product("tf,fd->td", active_low, outer_weight) + outer_bias)
    result_rows = normalize(
        second_pre, second_gain.astype(jnp.float32), second_shift.astype(jnp.float32)
    )
    saved = (
        activation,
        queries,
        extended,
        log_all,
        mixed_low,
        first_pre,
        hidden_low,
        inner_pre,
        active_low,
        second_pre,
    )
    return (saved, result_rows)


def return_rows(grad_ext, halo_rows, rows_local):
    reach = halo_rows // rows_local
    total = grad_ext[:, halo_rows : halo_rows + rows_local]
    for offset in range(-reach, reach + 1):
        if offset != 0:
            begin = halo_rows + offset * rows_local
            block_rows = grad_ext[:, begin : begin + rows_local]
            total = total + from_behind(block_rows.astype(jnp.bfloat16), "ctx", offset).astype(
                block_rows.dtype
            )
    return total


def layer_backward(gradient, saved, weights, allowed, halo_rows, score_scale):
    (
        query_weight,
        key_weight,
        value_weight,
        out_weight,
        inner_weight,
        outer_weight,
        query_bias,
        value_bias,
        out_bias,
        inner_bias,
        outer_bias,
        first_gain,
        first_shift,
        second_gain,
        second_shift,
    ) = weights
    (
        activation,
        queries,
        extended,
        log_all,
        mixed_low,
        first_pre,
        hidden_low,
        inner_pre,
        active_low,
        second_pre,
    ) = saved
    rows_local = activation.shape[0]
    reach = halo_rows // rows_local
    _, second_pull = jax.vjp(
        normalize, second_pre, second_gain.astype(jnp.float32), second_shift.astype(jnp.float32)
    )
    grad_second, grad_second_gain, grad_second_shift = second_pull(gradient)
    grad_outer = grad_second.astype(jnp.bfloat16)
    grad_outer_weight = product("tf,td->fd", active_low, grad_outer)
    grad_outer_bias = jnp.sum(grad_outer.astype(jnp.float32), axis=0)
    grad_active = product("td,fd->tf", grad_outer, outer_weight)
    _, gelu_pull = jax.vjp(exact_gelu, inner_pre)
    (grad_inner,) = gelu_pull(grad_active)
    grad_inner_low = grad_inner.astype(jnp.bfloat16)
    grad_inner_weight = product("td,tf->df", hidden_low, grad_inner_low)
    grad_inner_bias = jnp.sum(grad_inner_low.astype(jnp.float32), axis=0)
    grad_hidden = grad_second + product("tf,df->td", grad_inner_low, inner_weight)
    _, first_pull = jax.vjp(
        normalize, first_pre, first_gain.astype(jnp.float32), first_shift.astype(jnp.float32)
    )
    grad_first, grad_first_gain, grad_first_shift = first_pull(grad_hidden)
    grad_branch = grad_first.astype(jnp.bfloat16)
    grad_out_weight = product("te,td->ed", mixed_low, grad_branch)
    grad_out_bias = jnp.sum(grad_branch.astype(jnp.float32), axis=0)
    grad_mixed = product("td,ed->te", grad_branch, out_weight).astype(jnp.bfloat16)
    own_rows = extended[:, halo_rows : halo_rows + rows_local]
    key_ext = extend_rows(own_rows, 1, reach, move_keys_back)
    query_sum, key_win, value_win = attend_back(
        queries, key_ext[0], key_ext[1], grad_mixed, log_all, allowed, score_scale
    )
    owned = return_rows(jnp.stack([key_win, value_win]), halo_rows, rows_local)
    key_sum = owned[0]
    value_sum = owned[1]
    grad_query = query_sum.astype(jnp.bfloat16)
    grad_key = key_sum.astype(jnp.bfloat16)
    grad_value = value_sum.astype(jnp.bfloat16)
    grad_query_weight = product("te,td->ed", activation, grad_query)
    grad_key_weight = product("te,td->ed", activation, grad_key)
    grad_value_weight = product("te,td->ed", activation, grad_value)
    grad_query_bias = jnp.sum(grad_query.astype(jnp.float32), axis=0)
    grad_value_bias = jnp.sum(grad_value.astype(jnp.float32), axis=0)
    grad_activation = (
        grad_first
        + product("td,ed->te", grad_query, query_weight)
        + product("td,ed->te", grad_key, key_weight)
        + product("td,ed->te", grad_value, value_weight)
    )
    local_grads = (
        grad_query_weight,
        grad_key_weight,
        grad_value_weight,
        grad_out_weight,
        grad_inner_weight,
        grad_outer_weight,
        grad_query_bias,
        grad_value_bias,
        grad_out_bias,
        grad_inner_bias,
        grad_outer_bias,
        grad_first_gain,
        grad_first_shift,
        grad_second_gain,
        grad_second_shift,
    )
    return (grad_activation, local_grads)


def window_body(
    tokens,
    cotangent,
    doc_starts,
    doc_lengths,
    query_weight,
    key_weight,
    value_weight,
    out_weight,
    inner_weight,
    outer_weight,
    query_bias,
    value_bias,
    out_bias,
    inner_bias,
    outer_bias,
    first_gain,
    first_shift,
    second_gain,
    second_shift,
):
    params = (
        query_weight,
        key_weight,
        value_weight,
        out_weight,
        inner_weight,
        outer_weight,
        query_bias,
        value_bias,
        out_bias,
        inner_bias,
        outer_bias,
        first_gain,
        first_shift,
        second_gain,
        second_shift,
    )
    rows_local = tokens.shape[1]
    ctx_count = lax.axis_size("ctx")
    reach = min(-(-(DOC_CAP - 1) // rows_local), ctx_count - 1)
    halo_rows = reach * rows_local
    window = rows_local + 2 * halo_rows
    row_start = lax.axis_index("ctx") * rows_local
    local_positions = row_start + jnp.arange(rows_local, dtype=jnp.int32)
    window_positions = row_start - halo_rows + jnp.arange(window, dtype=jnp.int32)
    local_labels = doc_labels(local_positions, doc_starts[0], doc_lengths[0])
    window_labels = doc_labels(window_positions, doc_starts[0], doc_lengths[0])
    allowed = (local_labels[:, None] == window_labels[None, :]) & (local_labels[:, None] > 0)
    score_scale = HDIM ** (-0.5)
    activation = tokens[0]
    stashed = []
    outputs = []
    for layer_index in range(LAYERS):
        gathered = fetch_forward(params, layer_index)
        saved, result_rows = layer_forward(activation, gathered, allowed, halo_rows, score_scale)
        stashed.append((saved, gathered))
        outputs.append(result_rows)
        activation = result_rows.astype(jnp.bfloat16)
    gradient = cotangent[0].astype(jnp.float32)
    reduced = [None] * LAYERS
    for layer_index in reversed(range(LAYERS)):
        saved, gathered = stashed[layer_index]
        weights_now = fetch_backward(params, layer_index)
        gradient, local_grads = layer_backward(
            gradient, saved, weights_now, allowed, halo_rows, score_scale
        )
        reduced[layer_index] = reduce_grads(local_grads)
    stacked_grads = [
        jnp.stack([reduced[layer_index][member] for layer_index in range(LAYERS)])
        for member in range(15)
    ]
    heads_out = [
        outputs[0].astype(jnp.bfloat16)[None],
        outputs[LAYERS - 1].astype(jnp.bfloat16)[None],
        gradient.astype(jnp.bfloat16)[None],
    ]
    return tuple(heads_out + stacked_grads)


NN = (((1,), (0,)), ((), ()))
NT = (((1,), (1,)), ((), ()))
TN = (((0,), (0,)), ((), ()))
LANES = 128
QUERY_BLOCK = 256
CORE, ALONG_X, ALONG_Y = 1, 2, 4


def mm(left, right, dims=NN):
    return lax.dot_general(left, right, dims, preferred_element_type=jnp.float32)


def swap(block, mask):
    devices = range(lax.axis_size("ctx"))
    return lax.ppermute(block, "ctx", [(i, i ^ mask) for i in devices])


def turn(block, distance):
    count = lax.axis_size("wsh")
    return lax.ppermute(block, "wsh", [(i, (i + distance) % count) for i in range(count)])


def low(values_in):
    return values_in.astype(jnp.bfloat16)


def wide(values_in):
    return values_in.astype(jnp.float32)


def mask_features(label_col):
    rows = label_col.shape[0]
    lane = lax.broadcasted_iota(jnp.int32, (rows, LANES), 1)
    hit = lax.rem(lane, HDIM) == jnp.broadcast_to(label_col, (rows, LANES))
    return (
        jnp.where(hit, neg_fill, 0.0).astype(jnp.bfloat16),
        jnp.where(hit, 0.0, 1.0).astype(jnp.bfloat16),
    )


def fill_key_scratch(key_rows, label_col, key_mask):
    lane = lax.broadcasted_iota(jnp.int32, key_rows.shape, 1)
    _, key_features = mask_features(label_col)
    key_mask[0] = jnp.where(lane < HDIM, key_rows, key_features)
    key_mask[1] = jnp.where(lane < HDIM, key_features, key_rows)


def attention_forward_kernel(
    order_ref, query_ref, key_ref, value_ref, label_ref, query_label_ref, mixed_ref, log_ref, key_mask, value_t
):
    @pl.when(pl.program_id(0) == 0)
    def _():
        fill_key_scratch(key_ref[...], label_ref[...], key_mask)
        value_t[...] = value_ref[...].T

    scaled = low(wide(query_ref[...]) * HDIM ** (-0.5))
    lane = lax.broadcasted_iota(jnp.int32, scaled.shape, 1)
    features, _ = mask_features(query_label_ref[...])
    parts = []
    for head in range(2):
        mine = (lane < HDIM) if head == 0 else (lane >= HDIM)
        scores = mm(key_mask[head], jnp.where(mine, scaled, features), NT)
        peak = jnp.max(scores, axis=0, keepdims=True)
        exponent = jnp.exp(scores - peak)
        total = jnp.sum(exponent, axis=0, keepdims=True)
        mixed = mm(value_t[pl.ds(HDIM * head, HDIM), :], low(exponent))
        parts.append(mixed / total)
        log_ref[pl.ds(head, 1), :] = peak + jnp.log(total)
    mixed_ref[...] = low(jnp.concatenate(parts, axis=0).T)


def attention_forward(packed, labels, order):
    rows = packed.shape[0]
    mine = pl.BlockSpec((QUERY_BLOCK, LANES), lambda i, order_ref: (i, 0))
    return pl.pallas_call(
        attention_forward_kernel,
        grid_spec=pltpu.PrefetchScalarGridSpec(
            num_scalar_prefetch=1,
            grid=(rows // QUERY_BLOCK,),
            in_specs=[
                mine,
                pl.BlockSpec((rows, LANES), lambda i, order_ref: (0, 1)),
                pl.BlockSpec((rows, LANES), lambda i, order_ref: (0, 2)),
                pl.BlockSpec((rows, 1), lambda i, order_ref: (0, 0)),
                pl.BlockSpec((QUERY_BLOCK, 1), lambda i, order_ref: (i, 0)),
            ],
            out_specs=[
                pl.BlockSpec((QUERY_BLOCK, LANES), lambda i, order_ref: (order_ref[i], 0)),
                pl.BlockSpec((2, QUERY_BLOCK), lambda i, order_ref: (0, i)),
            ],
            scratch_shapes=[
                pltpu.VMEM((2, rows, LANES), jnp.bfloat16),
                pltpu.VMEM((LANES, rows), jnp.bfloat16),
            ],
        ),
        out_shape=[
            jax.ShapeDtypeStruct((rows, LANES), jnp.bfloat16),
            jax.ShapeDtypeStruct((2, rows), jnp.float32),
        ],
        cost_estimate=pl.CostEstimate(
            flops=16 * rows * rows * LANES, bytes_accessed=rows * 1024, transcendentals=2 * rows * rows
        ),
        name="attention_forward",
    )(order, packed, packed, packed, labels, labels)


def attention_backward_kernel(
    order_ref,
    query_ref,
    key_ref,
    value_ref,
    label_ref,
    query_label_ref,
    grad_ref,
    log_ref,
    out_query_ref,
    out_key_ref,
    out_value_ref,
    key_mask,
    key_t,
    key_sum,
    value_sum,
):
    step = pl.program_id(0)

    @pl.when(step == 0)
    def _():
        fill_key_scratch(key_ref[...], label_ref[...], key_mask)
        key_t[...] = key_ref[...].T
        key_sum[...] = jnp.zeros_like(key_sum)
        value_sum[...] = jnp.zeros_like(value_sum)

    scaled = low(wide(query_ref[...]) * HDIM ** (-0.5))
    grad = grad_ref[...]
    value_rows = value_ref[...]
    lane = lax.broadcasted_iota(jnp.int32, scaled.shape, 1)
    features, _ = mask_features(query_label_ref[...])
    zero = jnp.zeros(scaled.shape, jnp.bfloat16)
    parts = []
    for head in range(2):
        mine = (lane < HDIM) if head == 0 else (lane >= HDIM)
        query_own = jnp.where(mine, scaled, zero)
        grad_own = jnp.where(mine, grad, zero)
        scores = mm(key_mask[head], jnp.where(mine, scaled, features), NT)
        probability = jnp.exp(scores - log_ref[pl.ds(head, 1), :])
        grad_prob = mm(value_rows, grad_own, NT)
        delta = jnp.sum(probability * grad_prob, axis=0, keepdims=True)
        grad_scores = low(probability * (grad_prob - delta))
        key_sum[...] += mm(grad_scores, query_own)
        value_sum[...] += mm(low(probability), grad_own)
        parts.append(mm(key_t[pl.ds(HDIM * head, HDIM), :], grad_scores) * HDIM ** (-0.5))
    out_query_ref[...] = low(jnp.concatenate(parts, axis=0).T)

    @pl.when(step == pl.num_programs(0) - 1)
    def _():
        out_key_ref[...] = low(key_sum[...])
        out_value_ref[...] = low(value_sum[...])


def attention_backward(packed, labels, grad, log_all, order):
    rows = packed.shape[0]
    mine = pl.BlockSpec((QUERY_BLOCK, LANES), lambda i, order_ref: (i, 0))
    whole = pl.BlockSpec((rows, LANES), lambda i, order_ref: (0, 0))
    return pl.pallas_call(
        attention_backward_kernel,
        grid_spec=pltpu.PrefetchScalarGridSpec(
            num_scalar_prefetch=1,
            grid=(rows // QUERY_BLOCK,),
            in_specs=[
                mine,
                pl.BlockSpec((rows, LANES), lambda i, order_ref: (0, 1)),
                pl.BlockSpec((rows, LANES), lambda i, order_ref: (0, 2)),
                pl.BlockSpec((rows, 1), lambda i, order_ref: (0, 0)),
                pl.BlockSpec((QUERY_BLOCK, 1), lambda i, order_ref: (i, 0)),
                pl.BlockSpec((QUERY_BLOCK, LANES), lambda i, order_ref: (order_ref[i], 0)),
                pl.BlockSpec((2, QUERY_BLOCK), lambda i, order_ref: (0, i)),
            ],
            out_specs=[mine, whole, whole],
            scratch_shapes=[
                pltpu.VMEM((2, rows, LANES), jnp.bfloat16),
                pltpu.VMEM((LANES, rows), jnp.bfloat16),
                pltpu.VMEM((rows, LANES), jnp.float32),
                pltpu.VMEM((rows, LANES), jnp.float32),
            ],
        ),
        out_shape=[jax.ShapeDtypeStruct((rows, LANES), jnp.bfloat16)] * 3,
        cost_estimate=pl.CostEstimate(
            flops=16 * rows * rows * LANES, bytes_accessed=rows * 2048, transcendentals=2 * rows * rows
        ),
        name="attention_backward",
    )(order, packed, packed, packed, labels, labels, grad, log_all)


def own_pieces(inner_weight, outer_weight, out_weight, joint_weights, here, first_block):
    layers, shard, hidden = inner_weight.shape
    piece = hidden // 8
    total = 2 * piece + LANES

    def kernel(place_ref, inner_ref, outer_ref, out_ref, query_ref, key_ref, value_ref, wide_ref, joint_ref):
        wide_ref[0, :, :piece] = low(inner_ref[0])
        wide_ref[0, :, piece : 2 * piece] = low(outer_ref[0]).T
        wide_ref[0, :, 2 * piece :] = low(out_ref[0])
        for at, ref in enumerate((query_ref, key_ref, value_ref)):
            joint_ref[0, :, at * LANES : (at + 1) * LANES] = low(ref[0])

    column = pl.BlockSpec((1, shard, LANES), lambda layer, place_ref: (layer, 0, place_ref[0]))
    return pl.pallas_call(
        kernel,
        grid_spec=pltpu.PrefetchScalarGridSpec(
            num_scalar_prefetch=1,
            grid=(layers,),
            in_specs=[
                pl.BlockSpec((1, shard, piece), lambda layer, place_ref: (layer, 0, place_ref[1])),
                pl.BlockSpec((1, piece, shard), lambda layer, place_ref: (layer, place_ref[1], 0)),
                column,
                column,
                column,
                column,
            ],
            out_specs=[
                pl.BlockSpec((1, shard, total), lambda layer, place_ref: (layer, 0, 0)),
                pl.BlockSpec((1, shard, 3 * LANES), lambda layer, place_ref: (layer, 0, 0)),
            ],
        ),
        out_shape=[
            jax.ShapeDtypeStruct((layers, shard, total), jnp.bfloat16),
            jax.ShapeDtypeStruct((layers, shard, 3 * LANES), jnp.bfloat16),
        ],
        cost_estimate=pl.CostEstimate(
            flops=0, bytes_accessed=layers * shard * (total + 3 * LANES) * 6, transcendentals=0
        ),
        name="own_pieces",
    )(jnp.stack([here, first_block]).astype(jnp.int32), inner_weight, outer_weight, out_weight, *joint_weights)


def own_blocks(inner_weight, outer_weight, out_weight, inner_order, out_order):
    layers, shard, hidden = inner_weight.shape
    piece = hidden // 8

    def kernel(inner_order_ref, out_order_ref, *refs):
        ins, (inner_out, outer_out, out_out) = refs[:-3], refs[-3:]
        for j in range(4):
            inner_out[0, j] = low(ins[j][0])
            outer_out[0, j] = low(ins[4 + j][0]).T
        for j in range(8):
            out_out[0, :, j * LANES : (j + 1) * LANES] = low(ins[8 + j][0])

    def inner_at(j):
        return pl.BlockSpec((1, shard, piece), lambda layer, inner_ref, out_ref: (layer, 0, inner_ref[layer * 4 + j]))

    def outer_at(j):
        return pl.BlockSpec((1, piece, shard), lambda layer, inner_ref, out_ref: (layer, inner_ref[layer * 4 + j], 0))

    def out_at(j):
        return pl.BlockSpec((1, shard, LANES), lambda layer, inner_ref, out_ref: (layer, 0, out_ref[layer * 8 + j]))

    block = pl.BlockSpec((1, 4, shard, piece), lambda layer, *_: (layer, 0, 0, 0))
    return pl.pallas_call(
        kernel,
        grid_spec=pltpu.PrefetchScalarGridSpec(
            num_scalar_prefetch=2,
            grid=(layers,),
            in_specs=[inner_at(j) for j in range(4)]
            + [outer_at(j) for j in range(4)]
            + [out_at(j) for j in range(8)],
            out_specs=[block, block, pl.BlockSpec((1, shard, 8 * LANES), lambda layer, *_: (layer, 0, 0))],
        ),
        out_shape=[
            jax.ShapeDtypeStruct((layers, 4, shard, piece), jnp.bfloat16),
            jax.ShapeDtypeStruct((layers, 4, shard, piece), jnp.bfloat16),
            jax.ShapeDtypeStruct((layers, shard, 8 * LANES), jnp.bfloat16),
        ],
        cost_estimate=pl.CostEstimate(
            flops=0, bytes_accessed=layers * 8 * shard * (piece + LANES) * 6, transcendentals=0
        ),
        name="own_blocks",
    )(inner_order, out_order, *[inner_weight] * 4, *[outer_weight] * 4, *[out_weight] * 8)


def place_pieces(near, far, order, layer, previous):
    count = 4
    shard, columns = near.shape[1:]
    piece = (columns - 4 * LANES) // 2
    width = 8 * LANES
    offset = far.shape[0] - count

    def column(index, order_ref):
        return (layer, 0, order_ref[index])

    def inner_place(index, order_ref):
        return (order_ref[index] % 2) * 4 + order_ref[index] // 2

    square = jax.ShapeDtypeStruct((LAYERS, shard, width), jnp.float32)
    outs = [square] * 4 + [
        jax.ShapeDtypeStruct((LAYERS, shard, 8 * piece), jnp.float32),
        jax.ShapeDtypeStruct((LAYERS, 8 * piece, shard), jnp.float32),
    ]
    specs = [pl.BlockSpec((1, shard, LANES), column)] * 4 + [
        pl.BlockSpec((1, shard, piece), lambda i, order_ref: (layer, 0, inner_place(i, order_ref))),
        pl.BlockSpec((1, piece, shard), lambda i, order_ref: (layer, inner_place(i, order_ref), 0)),
    ]

    def kernel(order_ref, near_ref, far_ref, *refs):
        query_out, key_out, value_out, out_out, inner_out, outer_out = refs[-6:]

        def write(source):
            inner_out[0] = wide(source[0, :, :piece])
            outer_out[0] = wide(source[0, :, piece : 2 * piece].T)
            for at, ref in enumerate((out_out, query_out, key_out, value_out)):
                begin = 2 * piece + at * LANES
                ref[0] = wide(source[0, :, begin : begin + LANES])

        @pl.when(pl.program_id(0) < count)
        def _():
            write(near_ref)

        @pl.when(pl.program_id(0) >= count)
        def _():
            write(far_ref)

    held = [] if previous is None else list(previous)
    return pl.pallas_call(
        kernel,
        grid_spec=pltpu.PrefetchScalarGridSpec(
            num_scalar_prefetch=1,
            grid=(2 * count,),
            in_specs=[
                pl.BlockSpec((1, shard, columns), lambda i, order_ref: (jnp.minimum(i, count - 1), 0, 0)),
                pl.BlockSpec(
                    (1, shard, columns), lambda i, order_ref: (jnp.maximum(i - count, 0) + offset, 0, 0)
                ),
            ]
            + [pl.BlockSpec(memory_space=pl.ANY)] * len(held),
            out_specs=specs,
        ),
        out_shape=outs,
        input_output_aliases={3 + i: i for i in range(len(held))},
        cost_estimate=pl.CostEstimate(
            flops=0, bytes_accessed=12 * count * shard * columns, transcendentals=0
        ),
        name="place_pieces",
    )(order, near, far, *held)


def half_erfc(values_in):
    scaled = values_in * (2.0**-0.5)
    part = 1.0 / (1.0 + 0.5 * scaled)
    series = 0.17087277
    for coefficient in (
        -0.82215223,
        1.48851587,
        -1.13520398,
        0.27886807,
        -0.18628806,
        0.09678418,
        0.37409196,
        1.00002368,
        -1.26551223,
    ):
        series = coefficient + part * series
    return 0.5 * part * jnp.exp(series - scaled * scaled)


def load_weights(step, own_inner, own_outer, inner_refs, outer_refs, inner_now, outer_now):
    shard = own_inner.shape[2]
    inner_now[:shard] = own_inner[0, 0]
    outer_now[:shard] = own_outer[0, 0]
    if len(inner_refs) == 1:
        inner_now[shard:] = inner_refs[0][0]
        outer_now[shard:] = outer_refs[0][0]
        return
    for j in range(len(inner_refs)):

        @pl.when(step == j)
        def _(j=j):
            inner_now[shard:] = inner_refs[j][...]
            outer_now[shard:] = outer_refs[j][...]


def weight_operands(weights, layer):
    own_inner, own_outer, inner_parts, outer_parts = weights
    shard, piece = own_inner.shape[2:]
    own = pl.BlockSpec((1, 1, shard, piece), lambda i: (layer, i, 0, 0))
    rest = 3 * shard
    if inner_parts is outer_parts:
        specs = [
            pl.BlockSpec((1, rest, piece), lambda i: (i, 0, 0)),
            pl.BlockSpec((1, rest, piece), lambda i: (i, 0, 1)),
        ]
        return ([own_inner, own_outer, inner_parts, outer_parts], [own, own] + specs, 1)
    fixed = pl.BlockSpec((rest, piece), lambda i: (0, 0), pipeline_mode=pl.Buffered(1))
    return (
        [own_inner, own_outer, *inner_parts, *outer_parts],
        [own, own] + [fixed] * (2 * len(inner_parts)),
        len(inner_parts),
    )


def accumulate(step, total, part):
    @pl.when(step == 0)
    def _():
        total[...] = part

    @pl.when(step > 0)
    def _():
        total[...] += part


def finish_pair(step, total, near_ref, far_ref):
    rows = near_ref.shape[0]

    @pl.when(step == pl.num_programs(0) - 1)
    def _():
        near_ref[...] = total[:rows]
        far_ref[...] = low(total[rows:])


def feed_forward_kernel(count, hidden_ref, bias_ref, own_inner, own_outer, *refs):
    inner_refs, outer_refs = refs[:count], refs[count : 2 * count]
    near_ref, far_ref, active_ref, slope_ref, total, inner_now, outer_now = refs[2 * count :]
    step = pl.program_id(0)
    load_weights(step, own_inner, own_outer, inner_refs, outer_refs, inner_now, outer_now)
    pre = mm(hidden_ref[...], inner_now[...]) + bias_ref[...]
    tail = half_erfc(jnp.abs(pre))
    below = jnp.where(pre < 0.0, tail, 1.0 - tail)
    active = low(pre * below)
    active_ref[...] = active
    slope_ref[...] = low(below + pre * (jnp.exp(-0.5 * pre * pre) * 0.3989422804014327))
    accumulate(step, total, mm(active, outer_now[...], NT))
    finish_pair(step, total, near_ref, far_ref)


def feed_forward(hidden_pair, bias_row, weights, layer):
    rows, width = hidden_pair.shape
    hidden = bias_row.shape[1]
    block = hidden // 4
    arrays, specs, count = weight_operands(weights, layer)
    column = pl.BlockSpec((rows, block), lambda i: (0, i))
    half = pl.BlockSpec((rows // 2, width), lambda i: (0, 0))
    return pl.pallas_call(
        functools.partial(feed_forward_kernel, count),
        grid=(4,),
        in_specs=[
            pl.BlockSpec((rows, width), lambda i: (0, 0)),
            pl.BlockSpec((1, block), lambda i: (0, i)),
            *specs,
        ],
        out_specs=[half, half, column, column],
        out_shape=[
            jax.ShapeDtypeStruct((rows // 2, width), jnp.float32),
            jax.ShapeDtypeStruct((rows // 2, width), jnp.bfloat16),
            jax.ShapeDtypeStruct((rows, hidden), jnp.bfloat16),
            jax.ShapeDtypeStruct((rows, hidden), jnp.bfloat16),
        ],
        scratch_shapes=[
            pltpu.VMEM((rows, width), jnp.float32),
            pltpu.VMEM((width, block), jnp.bfloat16),
            pltpu.VMEM((width, block), jnp.bfloat16),
        ],
        cost_estimate=pl.CostEstimate(
            flops=4 * rows * width * hidden, bytes_accessed=4 * width * hidden, transcendentals=2 * rows * hidden
        ),
        name="feed_forward",
    )(hidden_pair, bias_row, *arrays)


def feed_backward_kernel(count, grad_ref, slope_ref, own_inner, own_outer, *refs):
    inner_refs, outer_refs = refs[:count], refs[count : 2 * count]
    near_ref, far_ref, inner_grad_ref, bias_ref, total, inner_now, outer_now = refs[2 * count :]
    step = pl.program_id(0)
    load_weights(step, own_inner, own_outer, inner_refs, outer_refs, inner_now, outer_now)
    inner_grad = low(mm(grad_ref[...], outer_now[...]) * wide(slope_ref[...]))
    inner_grad_ref[...] = inner_grad
    bias_ref[...] = jnp.sum(wide(inner_grad), axis=0, keepdims=True)
    accumulate(step, total, mm(inner_grad, inner_now[...], NT))
    finish_pair(step, total, near_ref, far_ref)


def feed_backward(grad_pair, slope, weights, layer):
    rows, width = grad_pair.shape
    hidden = slope.shape[1]
    block = hidden // 4
    arrays, specs, count = weight_operands(weights, layer)
    column = pl.BlockSpec((rows, block), lambda i: (0, i))
    half = pl.BlockSpec((rows // 2, width), lambda i: (0, 0))
    return pl.pallas_call(
        functools.partial(feed_backward_kernel, count),
        grid=(4,),
        in_specs=[pl.BlockSpec((rows, width), lambda i: (0, 0)), column, *specs],
        out_specs=[half, half, column, pl.BlockSpec((1, block), lambda i: (0, i))],
        out_shape=[
            jax.ShapeDtypeStruct((rows // 2, width), jnp.float32),
            jax.ShapeDtypeStruct((rows // 2, width), jnp.bfloat16),
            jax.ShapeDtypeStruct((rows, hidden), jnp.bfloat16),
            jax.ShapeDtypeStruct((1, hidden), jnp.float32),
        ],
        scratch_shapes=[
            pltpu.VMEM((rows, width), jnp.float32),
            pltpu.VMEM((width, block), jnp.bfloat16),
            pltpu.VMEM((width, block), jnp.bfloat16),
        ],
        cost_estimate=pl.CostEstimate(
            flops=4 * rows * width * hidden, bytes_accessed=4 * width * hidden, transcendentals=0
        ),
        name="feed_backward",
    )(grad_pair, slope, *arrays)


def weight_gradient_kernel(
    split,
    rows_ref,
    hidden_ref,
    grad_ref,
    mixed_ref,
    inner_grad_ref,
    active_ref,
    branch_ref,
    *refs,
):
    outs, (hidden_t, grad_t, mixed_t) = refs[:-3], refs[-3:]
    step = pl.program_id(0)
    piece = active_ref.shape[1]

    @pl.when(step == 0)
    def _():
        hidden_t[...] = hidden_ref[...].T
        grad_t[...] = grad_ref[...].T
        mixed_t[...] = mixed_ref[...].T

    def write(store):
        store(0, piece, low(mm(hidden_t[...], inner_grad_ref[...])))
        store(piece, 2 * piece, low(mm(grad_t[...], active_ref[...])))
        store(2 * piece, 2 * piece + LANES, low(mm(mixed_t[...], branch_ref[...])))

    if not split:
        (out_ref,) = outs

        def store(begin, end, value):
            shard = value.shape[0] // 4
            for r in range(4):
                place = pl.multiple_of(rows_ref[r] * shard, shard)
                out_ref[0, pl.ds(place, shard), begin:end] = value[r * shard : (r + 1) * shard]

        write(store)
        return
    first_keep, first_send, second_keep, second_send = outs
    for j in range(4):

        @pl.when(step == j)
        def _(j=j):
            first = (first_send if j % 2 else first_keep, j // 2)
            second = (second_send if j // 2 else second_keep, j % 2)

            def store(begin, end, value):
                half = value.shape[0] // 2
                first[0][first[1], :, begin:end] = value[:half]
                second[0][second[1], :, begin:end] = value[half:]

            write(store)


def weight_gradients(hidden_pair, grad_pair, mixed_pair, inner_grad, active, branch_pair, plane_rows, split):
    rows, width = hidden_pair.shape
    hidden = active.shape[1]
    piece = hidden // 4
    total = 2 * piece + LANES
    whole = pl.BlockSpec((rows, width), lambda i, rows_ref: (0, 0))
    column = pl.BlockSpec((rows, piece), lambda i, rows_ref: (0, i))
    if split:
        shape = (2, width // 2, total)
        out_specs = [pl.BlockSpec(shape, lambda i, rows_ref: (0, 0, 0), pipeline_mode=pl.Buffered(1))] * 4
        out_shape = [jax.ShapeDtypeStruct(shape, jnp.bfloat16)] * 4
    else:
        out_specs = [pl.BlockSpec((1, width, total), lambda i, rows_ref: (i, 0, 0))]
        out_shape = [jax.ShapeDtypeStruct((4, width, total), jnp.bfloat16)]
    return pl.pallas_call(
        functools.partial(weight_gradient_kernel, split),
        grid_spec=pltpu.PrefetchScalarGridSpec(
            num_scalar_prefetch=1,
            grid=(4,),
            in_specs=[
                whole,
                whole,
                whole,
                column,
                column,
                pl.BlockSpec((rows, LANES), lambda i, rows_ref: (0, i)),
            ],
            out_specs=out_specs,
            scratch_shapes=[pltpu.VMEM((width, rows), jnp.bfloat16)] * 3,
        ),
        out_shape=out_shape,
        cost_estimate=pl.CostEstimate(
            flops=4 * rows * width * hidden, bytes_accessed=8 * width * hidden, transcendentals=0
        ),
        name="weight_gradients",
    )(plane_rows, hidden_pair, grad_pair, mixed_pair, inner_grad, active, branch_pair)


def block_columns(values_in, order, width):
    return jnp.concatenate(
        [lax.dynamic_slice_in_dim(values_in, block * width, width, 1) for block in order], axis=1
    )


def norm_forward(values_in, gain_row, shift_row):
    centre = values_in - jnp.mean(values_in, axis=-1, keepdims=True)
    spread = jnp.mean(centre * centre, axis=-1, keepdims=True)
    inverse = lax.rsqrt(spread + epsilon)
    unit = centre * inverse
    return (unit * gain_row + shift_row, unit, inverse)


def norm_backward(grad, unit, inverse, gain_row):
    grad_unit = grad * gain_row
    back = inverse * (
        grad_unit
        - jnp.mean(grad_unit, axis=-1, keepdims=True)
        - unit * jnp.mean(grad_unit * unit, axis=-1, keepdims=True)
    )
    return (back, jnp.sum(grad * unit, axis=0), jnp.sum(grad, axis=0))


def spread_tokens(rows_in):
    half = rows_in.shape[1] // 2
    left, right = rows_in[:, :half], rows_in[:, half:]
    left_pair = jnp.stack([left, swap(left, ALONG_X)])
    right_pair = jnp.stack([right, swap(right, ALONG_Y)])
    left_far = swap(left_pair, ALONG_Y)
    right_far = swap(right_pair, ALONG_X)
    left_all = jnp.concatenate([left_pair, left_far])
    right_all = jnp.stack([right_pair[0], right_far[0], right_pair[1], right_far[1]])
    near = jnp.concatenate([left_all, right_all], axis=2)
    far = swap(near, CORE)
    both = jnp.stack([near, far], axis=1)
    return both.reshape(8 * rows_in.shape[0], rows_in.shape[1])


def plane_groups():
    count = lax.axis_size("ctx")
    return [list(range(0, count, 2)), list(range(1, count, 2))]


def collect_tokens(partial, chip):
    rows = partial.shape[0] // 8
    width = partial.shape[1]
    blocks = partial.reshape(4, 2, rows, width)
    near = low(blocks[:, 0] + wide(swap(low(blocks[:, 1]), CORE)))
    sent = jnp.stack([lax.dynamic_index_in_dim(near, chip ^ j, 0, keepdims=False) for j in range(4)])
    came = lax.all_to_all(sent, "ctx", 0, 0, axis_index_groups=plane_groups(), tiled=True)
    return jnp.sum(wide(came), axis=0)


def plane_pieces(piece):
    half = piece.shape[1] // 2
    left, right = piece[:, :half], piece[:, half:]
    left_pair = jnp.stack([left, swap(left, ALONG_X)])
    right_pair = jnp.stack([right, swap(right, ALONG_Y)])
    left_far = swap(left_pair, ALONG_Y)
    right_far = swap(right_pair, ALONG_X)
    left_all = jnp.concatenate([left_pair, left_far])
    right_all = jnp.stack([right_pair[0], right_far[0], right_pair[1], right_far[1]])
    near = jnp.concatenate([left_all, right_all], axis=2)
    return (near, swap(near, CORE))


def exchange(blocks):
    return lax.all_to_all(blocks, "ctx", 0, 0, tiled=True)


def head_split_body(
    tokens,
    cotangent,
    doc_starts,
    doc_lengths,
    query_weight,
    key_weight,
    value_weight,
    out_weight,
    inner_weight,
    outer_weight,
    query_bias,
    value_bias,
    out_bias,
    inner_bias,
    outer_bias,
    first_gain,
    first_shift,
    second_gain,
    second_shift,
):
    rows = tokens.shape[1]
    width = tokens.shape[2]
    here = lax.axis_index("ctx")
    plane = lax.axis_index("wsh")
    planes = lax.axis_size("wsh")
    shard = width // planes
    hidden = inner_weight.shape[2]
    piece = hidden // 8
    core = here % 2
    chip = here // 2
    relative = jnp.arange(8, dtype=jnp.int32)
    turned = [(plane - r) % planes for r in range(planes)]
    unturned = turned
    positions = ((here ^ relative)[:, None] * rows + jnp.arange(rows, dtype=jnp.int32)).reshape(-1)
    labels = doc_labels(positions, doc_starts[0], doc_lengths[0])[:, None]

    four = jnp.arange(4, dtype=jnp.int32)
    chip_order = [chip ^ four, four]
    inner_order = [core * 4 + order for order in chip_order]
    out_order = [jnp.concatenate([2 * order + core, 2 * order + 1 - core]) for order in chip_order]
    block_order = here ^ relative
    plane_rows = jnp.stack(turned).astype(jnp.int32)
    wide_own, joint_own = own_pieces(
        inner_weight,
        outer_weight,
        out_weight,
        (query_weight, key_weight, value_weight),
        here,
        core * 4 + chip,
    )
    inner_own, outer_own, out_own = own_blocks(
        inner_weight, outer_weight, out_weight, jnp.concatenate(inner_order), jnp.concatenate(out_order)
    )
    small_own = low(
        jnp.concatenate(
            [
                query_bias,
                value_bias,
                out_bias,
                outer_bias,
                first_gain,
                first_shift,
                second_gain,
                second_shift,
                inner_bias,
            ],
            axis=1,
        )
    )
    wide_piece = 2 * piece + LANES
    joint_width = 3 * LANES
    small_rows = small_own.size // joint_width
    first_joint = jnp.concatenate([joint_own[0], small_own.reshape(small_rows, joint_width)], axis=0)
    joint_turned = jnp.stack([first_joint] + [turn(first_joint, r) for r in range(1, planes)])
    joint_plain = jnp.stack([lax.dynamic_index_in_dim(joint_turned, i, 0, keepdims=False) for i in unturned])
    small_all = joint_plain[:, shard:].reshape(planes, LAYERS, -1)

    def small(layer, index):
        return small_all[:, layer, index * shard : (index + 1) * shard].reshape(width)

    inner_bias_all = small_all[:, :, 8 * shard :].swapaxes(0, 1).reshape(LAYERS, hidden)

    def ordered(stack, order):
        return jnp.concatenate([lax.dynamic_index_in_dim(stack, i, 0, keepdims=False) for i in order], axis=0)

    joint_first = joint_plain[:, :shard].reshape(width, joint_width)
    wide_first, _ = lax.optimization_barrier((wide_own[0], joint_first))
    others_first = jnp.concatenate([turn(wide_first, r) for r in range(1, planes)], axis=0)
    second_own, _ = lax.optimization_barrier(
        (jnp.concatenate([wide_own[1], joint_own[1]], axis=1), others_first)
    )
    second_stack = lax.all_gather(second_own, "wsh", axis=0)
    joint_second = second_stack[:, :, wide_piece:].reshape(width, joint_width)
    others_second = ordered(second_stack[:, :, :wide_piece], turned[1:])
    second_parts = lax.all_gather(others_second, "ctx", axis=0, axis_index_groups=plane_groups())

    def layer_weights(layer):
        if layer == 0:
            first = jnp.concatenate([others_first[:, :piece], others_first[:, 2 * piece :]], axis=1)
            second = others_first[:, piece : 2 * piece]
            first_x = swap(first, ALONG_X)
            second_y = swap(second, ALONG_Y)
            firsts = (first, first_x, swap(first, ALONG_Y), swap(first_x, ALONG_Y))
            seconds = (second, swap(second, ALONG_X), second_y, swap(second_y, ALONG_X))
            near = jnp.concatenate([part[:, piece:] for part in firsts], axis=1)
            weights = (inner_own, outer_own, firsts, seconds)
        else:
            near = jnp.concatenate([second_parts[j, :, 2 * piece :] for j in range(4)], axis=1)
            weights = (inner_own, outer_own, second_parts, second_parts)
        out_full = jnp.concatenate(
            [out_own[layer], jnp.concatenate([near, swap(near, CORE)], axis=1)], axis=0
        )
        return (joint_first if layer == 0 else joint_second, weights, out_full)

    def out_place(layer, block):
        at = (block // 2) ^ chip if layer == 0 else block // 2
        return at + 4 * ((block % 2) ^ core)

    activation = tokens[0]
    stashed = []
    outputs = []
    for layer in range(LAYERS):
        joint, weights, out_full = layer_weights(layer)
        first_gain_row, first_shift_row = wide(small(layer, 4)), wide(small(layer, 5))
        second_gain_row, second_shift_row = wide(small(layer, 6)), wide(small(layer, 7))

        everyone = spread_tokens(activation)
        query_bias_own = lax.dynamic_slice_in_dim(small(layer, 0), here * LANES, LANES, 0)
        value_bias_own = lax.dynamic_slice_in_dim(small(layer, 1), here * LANES, LANES, 0)
        joint_bias = jnp.concatenate([query_bias_own, jnp.zeros_like(query_bias_own), value_bias_own])
        packed = low(mm(everyone, joint) + wide(joint_bias))
        mixed, log_all = attention_forward(packed, labels, block_order)
        mixed_heads = exchange(mixed.reshape(8, rows, LANES))
        mixed_turned = jnp.concatenate(
            [
                lax.dynamic_index_in_dim(mixed_heads, 2 * turned[r] + i, 0, keepdims=False)
                for r in range(planes)
                for i in range(2)
            ],
            axis=1,
        )
        mixed_pair = jnp.concatenate([mixed_turned, swap(mixed_turned, CORE)], axis=0)
        attended = block_columns(mm(mixed_turned, out_full), [out_place(layer, b) for b in range(8)], LANES)
        first_pre = wide(activation) + (attended + wide(small(layer, 2)))
        hidden_rows, first_unit, first_inverse = norm_forward(first_pre, first_gain_row, first_shift_row)
        hidden_turned = block_columns(low(hidden_rows), turned, shard)
        hidden_pair = jnp.concatenate([hidden_turned, swap(hidden_turned, CORE)], axis=0)
        inner_bias_own = jnp.concatenate(
            [lax.dynamic_slice_in_dim(inner_bias_all[layer], inner_order[layer][j] * piece, piece, 0) for j in range(4)]
        )
        outer_near, outer_far, active, slope = feed_forward(
            hidden_pair, wide(inner_bias_own)[None], weights, layer
        )
        outer_turned = outer_near + wide(swap(outer_far, CORE))
        outer_out = block_columns(outer_turned, unturned, shard)
        second_pre = hidden_rows + (outer_out + wide(small(layer, 3)))
        result, second_unit, second_inverse = norm_forward(second_pre, second_gain_row, second_shift_row)
        stashed.append(
            (
                everyone,
                packed,
                log_all,
                mixed_pair,
                first_unit,
                first_inverse,
                hidden_pair,
                active,
                slope,
                second_unit,
                second_inverse,
                joint,
                out_full,
                weights,
                first_gain_row,
                second_gain_row,
            )
        )
        activation = low(result)
        outputs.append(activation)

    gradient = wide(cotangent[0])
    small_grads = [None] * LAYERS
    placed = None
    for layer in reversed(range(LAYERS)):
        (
            everyone,
            packed,
            log_all,
            mixed_pair,
            first_unit,
            first_inverse,
            hidden_pair,
            active,
            slope,
            second_unit,
            second_inverse,
            joint,
            out_full,
            weights,
            first_gain_row,
            second_gain_row,
        ) = stashed[layer]
        grad_second, grad_second_gain, grad_second_shift = norm_backward(
            gradient, second_unit, second_inverse, second_gain_row
        )
        grad_outer = low(grad_second)
        grad_outer_bias = jnp.sum(wide(grad_outer), axis=0)
        grad_turned = block_columns(grad_outer, turned, shard)
        grad_pair = jnp.concatenate([grad_turned, swap(grad_turned, CORE)], axis=0)
        hidden_near, hidden_far, grad_inner, grad_inner_bias = feed_backward(grad_pair, slope, weights, layer)
        hidden_back = hidden_near + wide(swap(hidden_far, CORE))
        grad_hidden = grad_second + block_columns(hidden_back, unturned, shard)
        grad_first, grad_first_gain, grad_first_shift = norm_backward(
            grad_hidden, first_unit, first_inverse, first_gain_row
        )
        grad_branch = low(grad_first)
        grad_out_bias = jnp.sum(wide(grad_branch), axis=0)
        branch_spread = block_columns(grad_branch, [out_order[layer][p] for p in range(8)], LANES)
        grad_mixed_turned = low(mm(branch_spread, out_full, NT))
        grad_mixed = exchange(
            jnp.stack(
                [
                    lax.dynamic_slice_in_dim(grad_mixed_turned, unturned[i // 2] * shard + (i % 2) * LANES, LANES, 1)
                    for i in range(8)
                ]
            )
        ).reshape(8 * rows, LANES)
        branch_half = 4 * LANES
        branch_pair = jnp.concatenate(
            [branch_spread[:, :branch_half], swap(branch_spread[:, branch_half:], CORE)], axis=0
        )
        summed = weight_gradients(
            hidden_pair, grad_pair, mixed_pair, grad_inner, active, branch_pair, plane_rows, layer == 0
        )
        grad_query, grad_key, grad_value = attention_backward(packed, labels, grad_mixed, log_all, block_order)
        grad_packed = jnp.concatenate([grad_query, grad_key, grad_value], axis=1)
        gradient = grad_first + collect_tokens(mm(grad_packed, joint, NT), chip)
        grad_joint = low(mm(everyone, grad_packed, TN))
        joint_bias_grad = jnp.sum(wide(grad_packed), axis=0)

        if layer == 0:
            first_keep, first_send, second_keep, second_send = summed
            came = swap(first_send, ALONG_X)
            first_sum = (
                wide(first_keep[0])
                + wide(came[0])
                + wide(swap(low(wide(first_keep[1]) + wide(came[1])), ALONG_Y))
            )
            came = swap(second_send, ALONG_Y)
            second_sum = (
                wide(second_keep[0])
                + wide(came[0])
                + wide(swap(low(wide(second_keep[1]) + wide(came[1])), ALONG_X))
            )
            total = first_sum[:shard]
            for r, rows_sent in enumerate((first_sum[shard:], second_sum[:shard], second_sum[shard:]), 1):
                total = total + wide(turn(low(rows_sent), planes - r))
            joint_total = wide(lax.dynamic_slice_in_dim(grad_joint, plane * shard, shard, 0))
            for r in range(1, planes):
                part = lax.dynamic_slice_in_dim(grad_joint, turned[r] * shard, shard, 0)
                joint_total = joint_total + wide(turn(part, planes - r))
            near, far = plane_pieces(low(jnp.concatenate([total, joint_total], axis=1)))
            near_first = here ^ (2 * four)
            placed = place_pieces(near, far, jnp.concatenate([near_first, near_first ^ 1]), layer, placed)
        else:
            plane_sum = lax.psum_scatter(
                summed[0].reshape(4 * width, wide_piece),
                "ctx",
                scatter_dimension=0,
                axis_index_groups=plane_groups(),
                tiled=True,
            )
            total = lax.psum_scatter(plane_sum, "wsh", scatter_dimension=0, tiled=True)
            joint_total = lax.psum_scatter(grad_joint, "wsh", scatter_dimension=0, tiled=True)
            everything = lax.all_gather(jnp.concatenate([total, joint_total], axis=1), "ctx", axis=0)
            placed = place_pieces(everything, everything, relative, layer, placed)

        placed_query, placed_value = [
            lax.dynamic_update_slice(jnp.zeros((width,), jnp.float32), part, (here * LANES,))
            for part in (joint_bias_grad[:LANES], joint_bias_grad[2 * LANES :])
        ]
        placed_inner = jnp.zeros((hidden,), jnp.float32)
        for j in range(4):
            placed_inner = lax.dynamic_update_slice(
                placed_inner, grad_inner_bias[0, j * piece : (j + 1) * piece], (inner_order[layer][j] * piece,)
            )
        small_grads[layer] = jnp.concatenate(
            [
                row.reshape(planes, -1)
                for row in (
                    placed_query,
                    placed_value,
                    grad_out_bias,
                    grad_outer_bias,
                    grad_first_gain,
                    grad_first_shift,
                    grad_second_gain,
                    grad_second_shift,
                    placed_inner,
                )
            ],
            axis=1,
        )
    small_sent = jnp.concatenate(small_grads, axis=1)
    small_plane = jnp.sum(lax.all_to_all(small_sent, "wsh", 0, 0, tiled=True), axis=0)
    small_mine = jnp.sum(lax.all_gather(small_plane, "ctx", axis=0), axis=0).reshape(LAYERS, -1)
    small_outs = [small_mine[:, i * shard : (i + 1) * shard] for i in range(8)]
    return (
        outputs[0][None],
        outputs[1][None],
        low(gradient)[None],
        *placed,
        small_outs[0],
        small_outs[1],
        small_outs[2],
        small_mine[:, 8 * shard :],
        small_outs[3],
        small_outs[4],
        small_outs[5],
        small_outs[6],
        small_outs[7],
    )


def choose_body(mesh):
    if mesh.shape["ctx"] == 8 and HEADS // 8 == 2:
        return head_split_body
    return window_body


def solution(mesh):
    in_specs = (
        P("wsh", "ctx", None),
        P("wsh", "ctx", None),
        P("wsh", None),
        P("wsh", None),
        P(None, "wsh", None),
        P(None, "wsh", None),
        P(None, "wsh", None),
        P(None, "wsh", None),
        P(None, "wsh", None),
        P(None, None, "wsh"),
        P(None, "wsh"),
        P(None, "wsh"),
        P(None, "wsh"),
        P(None, "wsh"),
        P(None, "wsh"),
        P(None, "wsh"),
        P(None, "wsh"),
        P(None, "wsh"),
        P(None, "wsh"),
    )
    out_specs = (
        P("wsh", "ctx", None),
        P("wsh", "ctx", None),
        P("wsh", "ctx", None),
        P(None, "wsh", None),
        P(None, "wsh", None),
        P(None, "wsh", None),
        P(None, "wsh", None),
        P(None, "wsh", None),
        P(None, None, "wsh"),
        P(None, "wsh"),
        P(None, "wsh"),
        P(None, "wsh"),
        P(None, "wsh"),
        P(None, "wsh"),
        P(None, "wsh"),
        P(None, "wsh"),
        P(None, "wsh"),
        P(None, "wsh"),
    )
    return jax.shard_map(choose_body(mesh), mesh=mesh, in_specs=in_specs, out_specs=out_specs, check_vma=False)
```

```python
import functools

import jax
import jax.numpy as jnp
from jax import lax
from jax.experimental import pallas as pl
from jax.experimental.pallas import tpu as pltpu
from jax.sharding import PartitionSpec as P

HEADS = 16
HDIM = 64
LAYERS = 2
DOC_CAP = 2000


epsilon = 1e-05
neg_fill = -1e30
head_pair = 2


def from_behind(block, axis, distance):
    devices = range(lax.axis_size(axis))
    route = [(i - distance, i) for i in devices if i - distance in devices]
    return lax.ppermute(block, axis, route)


def normalize(values_in, gain_row, shift_row):
    centre = values_in - jnp.mean(values_in, axis=-1, keepdims=True)
    spread = jnp.mean(centre * centre, axis=-1, keepdims=True)
    return centre * lax.rsqrt(spread + epsilon) * gain_row + shift_row


def exact_gelu(values_in):
    return jax.nn.gelu(values_in, approximate=False)


def product(form, left, right):
    return jnp.einsum(form, left, right, preferred_element_type=jnp.float32)


def doc_labels(positions, starts, lengths):
    inside = (positions[:, None] >= starts[None, :]) & (
        positions[:, None] < (starts + lengths)[None, :]
    )
    labels = jnp.arange(1, starts.shape[0] + 1, dtype=jnp.int32)
    return jnp.sum(jnp.where(inside, labels[None, :], 0), axis=1)


def extend_rows(rows_in, dim, reach, mover):
    pieces = []
    for offset in range(-reach, reach + 1):
        if offset == 0:
            pieces.append(rows_in)
        else:
            pieces.append(mover(rows_in, -offset))
    return jnp.concatenate(pieces, axis=dim)


def move_keys_fwd(rows_in, steps):
    return from_behind(rows_in, "ctx", steps)


def move_keys_back(rows_in, steps):
    return from_behind(rows_in, "ctx", steps)


def fetch_forward(params, layer_index):
    shards = [piece[layer_index].astype(jnp.bfloat16) for piece in params]
    return (
        lax.all_gather(shards[0], "wsh", axis=0, tiled=True),
        lax.all_gather(shards[1], "wsh", axis=0, tiled=True),
        lax.all_gather(shards[2], "wsh", axis=0, tiled=True),
        lax.all_gather(shards[3], "wsh", axis=0, tiled=True),
        lax.all_gather(shards[4], "wsh", axis=0, tiled=True),
        lax.all_gather(shards[5], "wsh", axis=1, tiled=True),
        lax.all_gather(shards[6], "wsh", axis=0, tiled=True),
        lax.all_gather(shards[7], "wsh", axis=0, tiled=True),
        lax.all_gather(shards[8], "wsh", axis=0, tiled=True),
        lax.all_gather(shards[9], "wsh", axis=0, tiled=True),
        lax.all_gather(shards[10], "wsh", axis=0, tiled=True),
        lax.all_gather(shards[11], "wsh", axis=0, tiled=True),
        lax.all_gather(shards[12], "wsh", axis=0, tiled=True),
        lax.all_gather(shards[13], "wsh", axis=0, tiled=True),
        lax.all_gather(shards[14], "wsh", axis=0, tiled=True),
    )


def fetch_backward(params, layer_index):
    shards = [piece[layer_index].astype(jnp.bfloat16) for piece in params]
    return (
        lax.all_gather(shards[0], "wsh", axis=0, tiled=True),
        lax.all_gather(shards[1], "wsh", axis=0, tiled=True),
        lax.all_gather(shards[2], "wsh", axis=0, tiled=True),
        lax.all_gather(shards[3], "wsh", axis=0, tiled=True),
        lax.all_gather(shards[4], "wsh", axis=0, tiled=True),
        lax.all_gather(shards[5], "wsh", axis=1, tiled=True),
        lax.all_gather(shards[6], "wsh", axis=0, tiled=True),
        lax.all_gather(shards[7], "wsh", axis=0, tiled=True),
        lax.all_gather(shards[8], "wsh", axis=0, tiled=True),
        lax.all_gather(shards[9], "wsh", axis=0, tiled=True),
        lax.all_gather(shards[10], "wsh", axis=0, tiled=True),
        lax.all_gather(shards[11], "wsh", axis=0, tiled=True),
        lax.all_gather(shards[12], "wsh", axis=0, tiled=True),
        lax.all_gather(shards[13], "wsh", axis=0, tiled=True),
        lax.all_gather(shards[14], "wsh", axis=0, tiled=True),
    )


def reduce_grads(local_grads):
    shares = (
        lax.psum_scatter(
            local_grads[0].astype(jnp.bfloat16), "wsh", scatter_dimension=0, tiled=True
        ).astype(jnp.float32),
        lax.psum_scatter(
            local_grads[1].astype(jnp.bfloat16), "wsh", scatter_dimension=0, tiled=True
        ).astype(jnp.float32),
        lax.psum_scatter(
            local_grads[2].astype(jnp.bfloat16), "wsh", scatter_dimension=0, tiled=True
        ).astype(jnp.float32),
        lax.psum_scatter(
            local_grads[3].astype(jnp.bfloat16), "wsh", scatter_dimension=0, tiled=True
        ).astype(jnp.float32),
        lax.psum_scatter(
            local_grads[4].astype(jnp.bfloat16), "wsh", scatter_dimension=0, tiled=True
        ).astype(jnp.float32),
        lax.psum_scatter(
            local_grads[5].astype(jnp.bfloat16), "wsh", scatter_dimension=1, tiled=True
        ).astype(jnp.float32),
        lax.psum_scatter(
            local_grads[6].astype(jnp.bfloat16), "wsh", scatter_dimension=0, tiled=True
        ).astype(jnp.float32),
        lax.psum_scatter(
            local_grads[7].astype(jnp.bfloat16), "wsh", scatter_dimension=0, tiled=True
        ).astype(jnp.float32),
        lax.psum_scatter(
            local_grads[8].astype(jnp.bfloat16), "wsh", scatter_dimension=0, tiled=True
        ).astype(jnp.float32),
        lax.psum_scatter(
            local_grads[9].astype(jnp.bfloat16), "wsh", scatter_dimension=0, tiled=True
        ).astype(jnp.float32),
        lax.psum_scatter(
            local_grads[10].astype(jnp.bfloat16), "wsh", scatter_dimension=0, tiled=True
        ).astype(jnp.float32),
        lax.psum_scatter(
            local_grads[11].astype(jnp.bfloat16), "wsh", scatter_dimension=0, tiled=True
        ).astype(jnp.float32),
        lax.psum_scatter(
            local_grads[12].astype(jnp.bfloat16), "wsh", scatter_dimension=0, tiled=True
        ).astype(jnp.float32),
        lax.psum_scatter(
            local_grads[13].astype(jnp.bfloat16), "wsh", scatter_dimension=0, tiled=True
        ).astype(jnp.float32),
        lax.psum_scatter(
            local_grads[14].astype(jnp.bfloat16), "wsh", scatter_dimension=0, tiled=True
        ).astype(jnp.float32),
    )
    return (
        lax.psum(shares[0].astype(jnp.bfloat16), "ctx").astype(jnp.float32),
        lax.psum(shares[1].astype(jnp.bfloat16), "ctx").astype(jnp.float32),
        lax.psum(shares[2].astype(jnp.bfloat16), "ctx").astype(jnp.float32),
        lax.psum(shares[3].astype(jnp.bfloat16), "ctx").astype(jnp.float32),
        lax.psum(shares[4].astype(jnp.bfloat16), "ctx").astype(jnp.float32),
        lax.psum(shares[5].astype(jnp.bfloat16), "ctx").astype(jnp.float32),
        lax.psum(shares[6].astype(jnp.bfloat16), "ctx").astype(jnp.float32),
        lax.psum(shares[7].astype(jnp.bfloat16), "ctx").astype(jnp.float32),
        lax.psum(shares[8].astype(jnp.bfloat16), "ctx").astype(jnp.float32),
        lax.psum(shares[9].astype(jnp.bfloat16), "ctx").astype(jnp.float32),
        lax.psum(shares[10].astype(jnp.bfloat16), "ctx").astype(jnp.float32),
        lax.psum(shares[11].astype(jnp.bfloat16), "ctx").astype(jnp.float32),
        lax.psum(shares[12].astype(jnp.bfloat16), "ctx").astype(jnp.float32),
        lax.psum(shares[13].astype(jnp.bfloat16), "ctx").astype(jnp.float32),
        lax.psum(shares[14].astype(jnp.bfloat16), "ctx").astype(jnp.float32),
    )


def attend(queries, key_ext, value_ext, allowed, score_scale):
    rows_local = queries.shape[0]
    rows_keys = key_ext.shape[0]
    groups = HEADS // head_pair
    span = head_pair * HDIM
    query_groups = queries.reshape(rows_local, groups, span)
    key_groups = key_ext.reshape(rows_keys, groups, span)
    value_groups = value_ext.reshape(rows_keys, groups, span)

    def one_group(group_index, carry):
        mixed_all, log_all = carry
        query_part = lax.dynamic_index_in_dim(query_groups, group_index, 1, keepdims=False).reshape(
            rows_local, head_pair, HDIM
        )
        key_part = lax.dynamic_index_in_dim(key_groups, group_index, 1, keepdims=False).reshape(
            rows_keys, head_pair, HDIM
        )
        value_part = lax.dynamic_index_in_dim(value_groups, group_index, 1, keepdims=False).reshape(
            rows_keys, head_pair, HDIM
        )
        raw_scores = product("qhd,khd->hqk", query_part, key_part)
        scores = jnp.where(allowed[None], raw_scores * score_scale, neg_fill)
        row_peak = jnp.max(scores, axis=2, keepdims=True)
        exponent = jnp.exp(scores - row_peak)
        row_total = jnp.sum(exponent, axis=2, keepdims=True)
        probability = (exponent / row_total).astype(jnp.bfloat16)
        mixed_part = product("hqk,khd->qhd", probability, value_part)
        mixed_all = lax.dynamic_update_index_in_dim(
            mixed_all, mixed_part.reshape(rows_local, span), group_index, 1
        )
        log_all = lax.dynamic_update_index_in_dim(
            log_all, (row_peak + jnp.log(row_total))[:, :, 0], group_index, 0
        )
        return (mixed_all, log_all)

    start_carry = (
        jnp.zeros((rows_local, groups, span), jnp.float32),
        jnp.zeros((groups, head_pair, rows_local), jnp.float32),
    )
    mixed_all, log_all = lax.fori_loop(0, groups, one_group, start_carry)
    return (mixed_all.reshape(rows_local, groups * span), log_all)


def attend_back(queries, key_ext, value_ext, grad_mixed, log_all, allowed, score_scale):
    rows_local = queries.shape[0]
    rows_keys = key_ext.shape[0]
    groups = HEADS // head_pair
    span = head_pair * HDIM
    query_groups = queries.reshape(rows_local, groups, span)
    key_groups = key_ext.reshape(rows_keys, groups, span)
    value_groups = value_ext.reshape(rows_keys, groups, span)
    grad_groups = grad_mixed.reshape(rows_local, groups, span)

    def one_group(group_index, carry):
        query_part = lax.dynamic_index_in_dim(query_groups, group_index, 1, keepdims=False).reshape(
            rows_local, head_pair, HDIM
        )
        key_part = lax.dynamic_index_in_dim(key_groups, group_index, 1, keepdims=False).reshape(
            rows_keys, head_pair, HDIM
        )
        value_part = lax.dynamic_index_in_dim(value_groups, group_index, 1, keepdims=False).reshape(
            rows_keys, head_pair, HDIM
        )
        grad_part = lax.dynamic_index_in_dim(grad_groups, group_index, 1, keepdims=False).reshape(
            rows_local, head_pair, HDIM
        )
        log_part = lax.dynamic_index_in_dim(log_all, group_index, 0, keepdims=False)
        raw_scores = product("qhd,khd->hqk", query_part, key_part)
        scores = jnp.where(allowed[None], raw_scores * score_scale, neg_fill)
        probability = jnp.exp(scores - log_part[:, :, None])
        grad_prob = product("qhd,khd->hqk", grad_part, value_part)
        row_delta = jnp.sum(probability * grad_prob, axis=2, keepdims=True)
        grad_scores = (probability * (grad_prob - row_delta) * score_scale).astype(jnp.bfloat16)
        query_term = product("hqk,khd->qhd", grad_scores, key_part)
        grad_query = lax.dynamic_update_index_in_dim(
            carry[0], query_term.reshape(rows_local, span), group_index, 1
        )
        delta_all = lax.dynamic_update_index_in_dim(carry[1], row_delta[:, :, 0], group_index, 0)
        key_term = product("hqk,qhd->khd", grad_scores, query_part)
        value_term = product("hqk,qhd->khd", probability.astype(jnp.bfloat16), grad_part)
        grad_key = lax.dynamic_update_index_in_dim(
            carry[2], key_term.reshape(rows_keys, span), group_index, 1
        )
        grad_value = lax.dynamic_update_index_in_dim(
            carry[3], value_term.reshape(rows_keys, span), group_index, 1
        )
        return (grad_query, delta_all, grad_key, grad_value)

    start_carry = (
        jnp.zeros((rows_local, groups, span), jnp.float32),
        jnp.zeros((groups, head_pair, rows_local), jnp.float32),
    )
    start_carry = start_carry + (
        jnp.zeros((rows_keys, groups, span), jnp.float32),
        jnp.zeros((rows_keys, groups, span), jnp.float32),
    )
    finals = lax.fori_loop(0, groups, one_group, start_carry)
    grad_query = finals[0].reshape(rows_local, groups * span)
    return (
        grad_query,
        finals[2].reshape(rows_keys, groups * span),
        finals[3].reshape(rows_keys, groups * span),
    )


def layer_forward(activation, gathered, allowed, halo_rows, score_scale):
    (
        query_weight,
        key_weight,
        value_weight,
        out_weight,
        inner_weight,
        outer_weight,
        query_bias,
        value_bias,
        out_bias,
        inner_bias,
        outer_bias,
        first_gain,
        first_shift,
        second_gain,
        second_shift,
    ) = gathered
    rows_local = activation.shape[0]
    queries = (product("td,de->te", activation, query_weight) + query_bias).astype(jnp.bfloat16)
    key_rows = product("td,de->te", activation, key_weight).astype(jnp.bfloat16)
    value_rows = (product("td,de->te", activation, value_weight) + value_bias).astype(jnp.bfloat16)
    stacked = jnp.stack([key_rows, value_rows])
    extended = extend_rows(stacked, 1, halo_rows // rows_local, move_keys_fwd)
    mixed_heads, log_all = attend(queries, extended[0], extended[1], allowed, score_scale)
    mixed_low = mixed_heads.astype(jnp.bfloat16)
    first_pre = activation.astype(jnp.float32) + (
        product("td,de->te", mixed_low, out_weight) + out_bias
    )
    hidden = normalize(first_pre, first_gain.astype(jnp.float32), first_shift.astype(jnp.float32))
    hidden_low = hidden.astype(jnp.bfloat16)
    inner_pre = product("td,df->tf", hidden_low, inner_weight) + inner_bias
    active_low = exact_gelu(inner_pre).astype(jnp.bfloat16)
    second_pre = hidden + (product("tf,fd->td", active_low, outer_weight) + outer_bias)
    result_rows = normalize(
        second_pre, second_gain.astype(jnp.float32), second_shift.astype(jnp.float32)
    )
    saved = (
        activation,
        queries,
        extended,
        log_all,
        mixed_low,
        first_pre,
        hidden_low,
        inner_pre,
        active_low,
        second_pre,
    )
    return (saved, result_rows)


def return_rows(grad_ext, halo_rows, rows_local):
    reach = halo_rows // rows_local
    total = grad_ext[:, halo_rows : halo_rows + rows_local]
    for offset in range(-reach, reach + 1):
        if offset != 0:
            begin = halo_rows + offset * rows_local
            block_rows = grad_ext[:, begin : begin + rows_local]
            total = total + from_behind(block_rows.astype(jnp.bfloat16), "ctx", offset).astype(
                block_rows.dtype
            )
    return total


def layer_backward(gradient, saved, weights, allowed, halo_rows, score_scale):
    (
        query_weight,
        key_weight,
        value_weight,
        out_weight,
        inner_weight,
        outer_weight,
        query_bias,
        value_bias,
        out_bias,
        inner_bias,
        outer_bias,
        first_gain,
        first_shift,
        second_gain,
        second_shift,
    ) = weights
    (
        activation,
        queries,
        extended,
        log_all,
        mixed_low,
        first_pre,
        hidden_low,
        inner_pre,
        active_low,
        second_pre,
    ) = saved
    rows_local = activation.shape[0]
    reach = halo_rows // rows_local
    _, second_pull = jax.vjp(
        normalize, second_pre, second_gain.astype(jnp.float32), second_shift.astype(jnp.float32)
    )
    grad_second, grad_second_gain, grad_second_shift = second_pull(gradient)
    grad_outer = grad_second.astype(jnp.bfloat16)
    grad_outer_weight = product("tf,td->fd", active_low, grad_outer)
    grad_outer_bias = jnp.sum(grad_outer.astype(jnp.float32), axis=0)
    grad_active = product("td,fd->tf", grad_outer, outer_weight)
    _, gelu_pull = jax.vjp(exact_gelu, inner_pre)
    (grad_inner,) = gelu_pull(grad_active)
    grad_inner_low = grad_inner.astype(jnp.bfloat16)
    grad_inner_weight = product("td,tf->df", hidden_low, grad_inner_low)
    grad_inner_bias = jnp.sum(grad_inner_low.astype(jnp.float32), axis=0)
    grad_hidden = grad_second + product("tf,df->td", grad_inner_low, inner_weight)
    _, first_pull = jax.vjp(
        normalize, first_pre, first_gain.astype(jnp.float32), first_shift.astype(jnp.float32)
    )
    grad_first, grad_first_gain, grad_first_shift = first_pull(grad_hidden)
    grad_branch = grad_first.astype(jnp.bfloat16)
    grad_out_weight = product("te,td->ed", mixed_low, grad_branch)
    grad_out_bias = jnp.sum(grad_branch.astype(jnp.float32), axis=0)
    grad_mixed = product("td,ed->te", grad_branch, out_weight).astype(jnp.bfloat16)
    own_rows = extended[:, halo_rows : halo_rows + rows_local]
    key_ext = extend_rows(own_rows, 1, reach, move_keys_back)
    query_sum, key_win, value_win = attend_back(
        queries, key_ext[0], key_ext[1], grad_mixed, log_all, allowed, score_scale
    )
    owned = return_rows(jnp.stack([key_win, value_win]), halo_rows, rows_local)
    key_sum = owned[0]
    value_sum = owned[1]
    grad_query = query_sum.astype(jnp.bfloat16)
    grad_key = key_sum.astype(jnp.bfloat16)
    grad_value = value_sum.astype(jnp.bfloat16)
    grad_query_weight = product("te,td->ed", activation, grad_query)
    grad_key_weight = product("te,td->ed", activation, grad_key)
    grad_value_weight = product("te,td->ed", activation, grad_value)
    grad_query_bias = jnp.sum(grad_query.astype(jnp.float32), axis=0)
    grad_value_bias = jnp.sum(grad_value.astype(jnp.float32), axis=0)
    grad_activation = (
        grad_first
        + product("td,ed->te", grad_query, query_weight)
        + product("td,ed->te", grad_key, key_weight)
        + product("td,ed->te", grad_value, value_weight)
    )
    local_grads = (
        grad_query_weight,
        grad_key_weight,
        grad_value_weight,
        grad_out_weight,
        grad_inner_weight,
        grad_outer_weight,
        grad_query_bias,
        grad_value_bias,
        grad_out_bias,
        grad_inner_bias,
        grad_outer_bias,
        grad_first_gain,
        grad_first_shift,
        grad_second_gain,
        grad_second_shift,
    )
    return (grad_activation, local_grads)


def window_body(
    tokens,
    cotangent,
    doc_starts,
    doc_lengths,
    query_weight,
    key_weight,
    value_weight,
    out_weight,
    inner_weight,
    outer_weight,
    query_bias,
    value_bias,
    out_bias,
    inner_bias,
    outer_bias,
    first_gain,
    first_shift,
    second_gain,
    second_shift,
):
    params = (
        query_weight,
        key_weight,
        value_weight,
        out_weight,
        inner_weight,
        outer_weight,
        query_bias,
        value_bias,
        out_bias,
        inner_bias,
        outer_bias,
        first_gain,
        first_shift,
        second_gain,
        second_shift,
    )
    rows_local = tokens.shape[1]
    ctx_count = lax.axis_size("ctx")
    reach = min(-(-(DOC_CAP - 1) // rows_local), ctx_count - 1)
    halo_rows = reach * rows_local
    window = rows_local + 2 * halo_rows
    row_start = lax.axis_index("ctx") * rows_local
    local_positions = row_start + jnp.arange(rows_local, dtype=jnp.int32)
    window_positions = row_start - halo_rows + jnp.arange(window, dtype=jnp.int32)
    local_labels = doc_labels(local_positions, doc_starts[0], doc_lengths[0])
    window_labels = doc_labels(window_positions, doc_starts[0], doc_lengths[0])
    allowed = (local_labels[:, None] == window_labels[None, :]) & (local_labels[:, None] > 0)
    score_scale = HDIM ** (-0.5)
    activation = tokens[0]
    stashed = []
    outputs = []
    for layer_index in range(LAYERS):
        gathered = fetch_forward(params, layer_index)
        saved, result_rows = layer_forward(activation, gathered, allowed, halo_rows, score_scale)
        stashed.append((saved, gathered))
        outputs.append(result_rows)
        activation = result_rows.astype(jnp.bfloat16)
    gradient = cotangent[0].astype(jnp.float32)
    reduced = [None] * LAYERS
    for layer_index in reversed(range(LAYERS)):
        saved, gathered = stashed[layer_index]
        weights_now = fetch_backward(params, layer_index)
        gradient, local_grads = layer_backward(
            gradient, saved, weights_now, allowed, halo_rows, score_scale
        )
        reduced[layer_index] = reduce_grads(local_grads)
    stacked_grads = [
        jnp.stack([reduced[layer_index][member] for layer_index in range(LAYERS)])
        for member in range(15)
    ]
    heads_out = [
        outputs[0].astype(jnp.bfloat16)[None],
        outputs[LAYERS - 1].astype(jnp.bfloat16)[None],
        gradient.astype(jnp.bfloat16)[None],
    ]
    return tuple(heads_out + stacked_grads)


NN = (((1,), (0,)), ((), ()))
NT = (((1,), (1,)), ((), ()))
TN = (((0,), (0,)), ((), ()))
LANES = 128
QUERY_BLOCK = 256
CORE, ALONG_X, ALONG_Y = 1, 2, 4
SMALL_COST = pl.CostEstimate(flops=1000, bytes_accessed=1000, transcendentals=0)


def lasting(microseconds):
    return pl.CostEstimate(
        flops=int(microseconds * 1.15e9), bytes_accessed=int(microseconds * 3.6e6), transcendentals=0
    )


def mm(left, right, dims=NN):
    return lax.dot_general(left, right, dims, preferred_element_type=jnp.float32)


def swap(block, mask):
    devices = range(lax.axis_size("ctx"))
    return lax.ppermute(block, "ctx", [(i, i ^ mask) for i in devices])


def turn(block, distance):
    count = lax.axis_size("wsh")
    return lax.ppermute(block, "wsh", [(i, (i + distance) % count) for i in range(count)])


def low(values_in):
    return values_in.astype(jnp.bfloat16)


def wide(values_in):
    return values_in.astype(jnp.float32)


def mask_features(label_col):
    rows = label_col.shape[0]
    lane = lax.broadcasted_iota(jnp.int32, (rows, LANES), 1)
    hit = lax.rem(lane, HDIM) == jnp.broadcast_to(label_col, (rows, LANES))
    return (
        jnp.where(hit, neg_fill, 0.0).astype(jnp.bfloat16),
        jnp.where(hit, 0.0, 1.0).astype(jnp.bfloat16),
    )


def fill_key_scratch(key_rows, label_col, key_mask):
    lane = lax.broadcasted_iota(jnp.int32, key_rows.shape, 1)
    _, key_features = mask_features(label_col)
    key_mask[0] = jnp.where(lane < HDIM, key_rows, key_features)
    key_mask[1] = jnp.where(lane < HDIM, key_features, key_rows)


def attention_forward_kernel(
    order_ref, query_ref, key_ref, value_ref, label_ref, query_label_ref, mixed_ref, log_ref, key_mask, value_t
):
    @pl.when(pl.program_id(0) == 0)
    def _():
        fill_key_scratch(key_ref[...], label_ref[...], key_mask)
        value_t[...] = value_ref[...].T

    scaled = low(wide(query_ref[...]) * HDIM ** (-0.5))
    lane = lax.broadcasted_iota(jnp.int32, scaled.shape, 1)
    features, _ = mask_features(query_label_ref[...])
    parts = []
    for head in range(2):
        mine = (lane < HDIM) if head == 0 else (lane >= HDIM)
        scores = mm(key_mask[head], jnp.where(mine, scaled, features), NT)
        peak = jnp.max(scores, axis=0, keepdims=True)
        exponent = jnp.exp(scores - peak)
        total = jnp.sum(exponent, axis=0, keepdims=True)
        mixed = mm(value_t[pl.ds(HDIM * head, HDIM), :], low(exponent))
        parts.append(mixed / total)
        log_ref[pl.ds(head, 1), :] = peak + jnp.log(total)
    mixed_ref[...] = low(jnp.concatenate(parts, axis=0).T)


def attention_forward(packed, labels, order):
    rows = packed.shape[0]
    mine = pl.BlockSpec((QUERY_BLOCK, LANES), lambda i, order_ref: (i, 0))
    return pl.pallas_call(
        attention_forward_kernel,
        grid_spec=pltpu.PrefetchScalarGridSpec(
            num_scalar_prefetch=1,
            grid=(rows // QUERY_BLOCK,),
            in_specs=[
                mine,
                pl.BlockSpec((rows, LANES), lambda i, order_ref: (0, 1)),
                pl.BlockSpec((rows, LANES), lambda i, order_ref: (0, 2)),
                pl.BlockSpec((rows, 1), lambda i, order_ref: (0, 0)),
                pl.BlockSpec((QUERY_BLOCK, 1), lambda i, order_ref: (i, 0)),
            ],
            out_specs=[
                pl.BlockSpec((QUERY_BLOCK, LANES), lambda i, order_ref: (order_ref[i], 0)),
                pl.BlockSpec((2, QUERY_BLOCK), lambda i, order_ref: (0, i)),
            ],
            scratch_shapes=[
                pltpu.VMEM((2, rows, LANES), jnp.bfloat16),
                pltpu.VMEM((LANES, rows), jnp.bfloat16),
            ],
        ),
        out_shape=[
            jax.ShapeDtypeStruct((rows, LANES), jnp.bfloat16),
            jax.ShapeDtypeStruct((2, rows), jnp.float32),
        ],
        cost_estimate=lasting(25),
        name="attention_forward",
    )(order, packed, packed, packed, labels, labels)


def attention_backward_kernel(
    order_ref,
    query_ref,
    key_ref,
    value_ref,
    label_ref,
    query_label_ref,
    grad_ref,
    log_ref,
    out_query_ref,
    out_key_ref,
    out_value_ref,
    key_mask,
    key_t,
    key_sum,
    value_sum,
):
    step = pl.program_id(0)

    @pl.when(step == 0)
    def _():
        fill_key_scratch(key_ref[...], label_ref[...], key_mask)
        key_t[...] = key_ref[...].T
        key_sum[...] = jnp.zeros_like(key_sum)
        value_sum[...] = jnp.zeros_like(value_sum)

    scaled = low(wide(query_ref[...]) * HDIM ** (-0.5))
    grad = grad_ref[...]
    value_rows = value_ref[...]
    lane = lax.broadcasted_iota(jnp.int32, scaled.shape, 1)
    features, _ = mask_features(query_label_ref[...])
    zero = jnp.zeros(scaled.shape, jnp.bfloat16)
    parts = []
    for head in range(2):
        mine = (lane < HDIM) if head == 0 else (lane >= HDIM)
        query_own = jnp.where(mine, scaled, zero)
        grad_own = jnp.where(mine, grad, zero)
        scores = mm(key_mask[head], jnp.where(mine, scaled, features), NT)
        probability = jnp.exp(scores - log_ref[pl.ds(head, 1), :])
        grad_prob = mm(value_rows, grad_own, NT)
        delta = jnp.sum(probability * grad_prob, axis=0, keepdims=True)
        grad_scores = low(probability * (grad_prob - delta))
        key_sum[...] += mm(grad_scores, query_own)
        value_sum[...] += mm(low(probability), grad_own)
        parts.append(mm(key_t[pl.ds(HDIM * head, HDIM), :], grad_scores) * HDIM ** (-0.5))
    out_query_ref[...] = low(jnp.concatenate(parts, axis=0).T)

    @pl.when(step == pl.num_programs(0) - 1)
    def _():
        out_key_ref[...] = low(key_sum[...])
        out_value_ref[...] = low(value_sum[...])


def attention_backward(packed, labels, grad, log_all, order):
    rows = packed.shape[0]
    mine = pl.BlockSpec((QUERY_BLOCK, LANES), lambda i, order_ref: (i, 0))
    whole = pl.BlockSpec((rows, LANES), lambda i, order_ref: (0, 0))
    return pl.pallas_call(
        attention_backward_kernel,
        grid_spec=pltpu.PrefetchScalarGridSpec(
            num_scalar_prefetch=1,
            grid=(rows // QUERY_BLOCK,),
            in_specs=[
                mine,
                pl.BlockSpec((rows, LANES), lambda i, order_ref: (0, 1)),
                pl.BlockSpec((rows, LANES), lambda i, order_ref: (0, 2)),
                pl.BlockSpec((rows, 1), lambda i, order_ref: (0, 0)),
                pl.BlockSpec((QUERY_BLOCK, 1), lambda i, order_ref: (i, 0)),
                pl.BlockSpec((QUERY_BLOCK, LANES), lambda i, order_ref: (order_ref[i], 0)),
                pl.BlockSpec((2, QUERY_BLOCK), lambda i, order_ref: (0, i)),
            ],
            out_specs=[mine, whole, whole],
            scratch_shapes=[
                pltpu.VMEM((2, rows, LANES), jnp.bfloat16),
                pltpu.VMEM((LANES, rows), jnp.bfloat16),
                pltpu.VMEM((rows, LANES), jnp.float32),
                pltpu.VMEM((rows, LANES), jnp.float32),
            ],
        ),
        out_shape=[jax.ShapeDtypeStruct((rows, LANES), jnp.bfloat16)] * 3,
        cost_estimate=lasting(33),
        name="attention_backward",
    )(order, packed, packed, packed, labels, labels, grad, log_all)


def own_pieces(inner_weight, outer_weight, out_weight, joint_weights, small_params, here, first_block):
    layers, shard, hidden = inner_weight.shape
    piece = hidden // 8
    width = 3 * LANES

    def kernel(place_ref, inner_ref, outer_ref, out_ref, query_ref, key_ref, value_ref, *refs):
        small_refs, (first_ref, second_ref, joint_ref) = refs[:-3], refs[-3:]
        first_ref[0, :, :piece] = low(inner_ref[0])
        first_ref[0, :, piece:] = low(out_ref[0])
        second_ref[0] = low(outer_ref[0]).T
        for at, ref in enumerate((query_ref, key_ref, value_ref)):
            joint_ref[0, :shard, at * LANES : (at + 1) * LANES] = low(ref[0])
        rows = [jnp.concatenate([ref[...] for ref in small_refs[:8]], axis=0)]
        rows += [small_refs[8][:, q * shard : (q + 1) * shard] for q in range(4)]
        rows += [jnp.zeros((8, shard), jnp.float32)]
        packed = low(jnp.concatenate(rows, axis=0))
        joint_ref[0, shard:] = jnp.concatenate([packed, jnp.zeros((32, width - shard), jnp.bfloat16)], axis=1)

    column = pl.BlockSpec((1, shard, LANES), lambda layer, place_ref: (layer, 0, place_ref[0]))
    return pl.pallas_call(
        kernel,
        grid_spec=pltpu.PrefetchScalarGridSpec(
            num_scalar_prefetch=1,
            grid=(layers,),
            in_specs=[
                pl.BlockSpec((1, shard, piece), lambda layer, place_ref: (layer, 0, place_ref[1])),
                pl.BlockSpec((1, piece, shard), lambda layer, place_ref: (layer, place_ref[1], 0)),
                column,
                column,
                column,
                column,
            ]
            + [pl.BlockSpec(param.shape, lambda layer, place_ref: (0, 0)) for param in small_params],
            out_specs=[
                pl.BlockSpec((1, shard, piece + LANES), lambda layer, place_ref: (layer, 0, 0)),
                pl.BlockSpec((1, shard, piece), lambda layer, place_ref: (layer, 0, 0)),
                pl.BlockSpec((1, shard + 32, width), lambda layer, place_ref: (layer, 0, 0)),
            ],
        ),
        out_shape=[
            jax.ShapeDtypeStruct((layers, shard, piece + LANES), jnp.bfloat16),
            jax.ShapeDtypeStruct((layers, shard, piece), jnp.bfloat16),
            jax.ShapeDtypeStruct((layers, shard + 32, width), jnp.bfloat16),
        ],
        cost_estimate=lasting(4),
        name="own_pieces",
    )(
        jnp.stack([here, first_block]).astype(jnp.int32),
        inner_weight,
        outer_weight,
        out_weight,
        *joint_weights,
        *small_params,
    )


def own_blocks(inner_weight, outer_weight, out_weight, inner_order, out_order, after):
    layers, shard, hidden = inner_weight.shape
    piece = hidden // 8

    def kernel(inner_order_ref, out_order_ref, *refs):
        ins, (inner_out, outer_out, out_out) = refs[:16], refs[-3:]
        for j in range(4):
            inner_out[0, j] = low(ins[j][0])
            outer_out[0, j] = low(ins[4 + j][0]).T
        for j in range(8):
            out_out[0, :, j * LANES : (j + 1) * LANES] = low(ins[8 + j][0])

    def inner_at(j):
        return pl.BlockSpec((1, shard, piece), lambda layer, inner_ref, out_ref: (layer, 0, inner_ref[layer * 4 + j]))

    def outer_at(j):
        return pl.BlockSpec((1, piece, shard), lambda layer, inner_ref, out_ref: (layer, inner_ref[layer * 4 + j], 0))

    def out_at(j):
        return pl.BlockSpec((1, shard, LANES), lambda layer, inner_ref, out_ref: (layer, 0, out_ref[layer * 8 + j]))

    block = pl.BlockSpec((1, 4, shard, piece), lambda layer, *_: (layer, 0, 0, 0))
    return pl.pallas_call(
        kernel,
        grid_spec=pltpu.PrefetchScalarGridSpec(
            num_scalar_prefetch=2,
            grid=(layers,),
            in_specs=[inner_at(j) for j in range(4)]
            + [outer_at(j) for j in range(4)]
            + [out_at(j) for j in range(8)]
            + [pl.BlockSpec(memory_space=pl.ANY)],
            out_specs=[block, block, pl.BlockSpec((1, shard, 8 * LANES), lambda layer, *_: (layer, 0, 0))],
        ),
        out_shape=[
            jax.ShapeDtypeStruct((layers, 4, shard, piece), jnp.bfloat16),
            jax.ShapeDtypeStruct((layers, 4, shard, piece), jnp.bfloat16),
            jax.ShapeDtypeStruct((layers, shard, 8 * LANES), jnp.bfloat16),
        ],
        cost_estimate=lasting(7),
        name="own_blocks",
    )(inner_order, out_order, *[inner_weight] * 4, *[outer_weight] * 4, *[out_weight] * 8, after)


def place_pieces(near, far, order, layer, previous):
    count = 4
    shard, columns = near.shape[1:]
    piece = (columns - 4 * LANES) // 2
    width = 8 * LANES
    offset = far.shape[0] - count

    def column(index, order_ref):
        return (layer, 0, order_ref[index])

    def inner_place(index, order_ref):
        return (order_ref[index] % 2) * 4 + order_ref[index] // 2

    square = jax.ShapeDtypeStruct((LAYERS, shard, width), jnp.float32)
    outs = [square] * 4 + [
        jax.ShapeDtypeStruct((LAYERS, shard, 8 * piece), jnp.float32),
        jax.ShapeDtypeStruct((LAYERS, 8 * piece, shard), jnp.float32),
        jax.ShapeDtypeStruct((8, LANES), jnp.float32),
    ]
    specs = [pl.BlockSpec((1, shard, LANES), column)] * 4 + [
        pl.BlockSpec((1, shard, piece), lambda i, order_ref: (layer, 0, inner_place(i, order_ref))),
        pl.BlockSpec((1, piece, shard), lambda i, order_ref: (layer, inner_place(i, order_ref), 0)),
        pl.BlockSpec((8, LANES), lambda i, order_ref: (0, 0)),
    ]

    def kernel(order_ref, near_ref, far_ref, *refs):
        query_out, key_out, value_out, out_out, inner_out, outer_out, token_out = refs[-7:]
        token_out[...] = jnp.zeros_like(token_out)

        def write(source):
            inner_out[0] = wide(source[0, :, :piece])
            outer_out[0] = wide(source[0, :, piece : 2 * piece].T)
            for at, ref in enumerate((out_out, query_out, key_out, value_out)):
                begin = 2 * piece + at * LANES
                ref[0] = wide(source[0, :, begin : begin + LANES])

        @pl.when(pl.program_id(0) < count)
        def _():
            write(near_ref)

        @pl.when(pl.program_id(0) >= count)
        def _():
            write(far_ref)

    held = [] if previous is None else list(previous)
    return pl.pallas_call(
        kernel,
        grid_spec=pltpu.PrefetchScalarGridSpec(
            num_scalar_prefetch=1,
            grid=(2 * count,),
            in_specs=[
                pl.BlockSpec((1, shard, columns), lambda i, order_ref: (jnp.minimum(i, count - 1), 0, 0)),
                pl.BlockSpec(
                    (1, shard, columns), lambda i, order_ref: (jnp.maximum(i - count, 0) + offset, 0, 0)
                ),
            ]
            + [pl.BlockSpec(memory_space=pl.ANY)] * len(held),
            out_specs=specs,
        ),
        out_shape=outs,
        input_output_aliases={3 + i: i for i in range(len(held))},
        cost_estimate=lasting(10),
        name="place_pieces",
    )(order, near, far, *held)


def half_erfc(values_in):
    scaled = values_in * (2.0**-0.5)
    part = 1.0 / (1.0 + 0.5 * scaled)
    series = 0.17087277
    for coefficient in (
        -0.82215223,
        1.48851587,
        -1.13520398,
        0.27886807,
        -0.18628806,
        0.09678418,
        0.37409196,
        1.00002368,
        -1.26551223,
    ):
        series = coefficient + part * series
    return 0.5 * part * jnp.exp(series - scaled * scaled)


def load_weights(step, own_inner, own_outer, inner_refs, outer_refs, inner_now, outer_now):
    shard = own_inner.shape[2]
    inner_now[:shard] = own_inner[0, 0]
    outer_now[:shard] = own_outer[0, 0]
    if len(inner_refs) == 1:
        inner_now[shard:] = inner_refs[0][0]
        outer_now[shard:] = outer_refs[0][0]
        return
    chunks = len(inner_refs) // 4
    rows = inner_refs[0].shape[0]
    for j in range(4):

        @pl.when(step == j)
        def _(j=j):
            for chunk in range(chunks):
                begin = shard + chunk * rows
                inner_now[begin : begin + rows] = inner_refs[j * chunks + chunk][...]
                outer_now[begin : begin + rows] = outer_refs[j * chunks + chunk][...]


def weight_operands(weights, layer):
    own_inner, own_outer, inner_parts, outer_parts = weights
    shard, piece = own_inner.shape[2:]
    own = pl.BlockSpec((1, 1, shard, piece), lambda i: (layer, i, 0, 0))
    if len(inner_parts) == 1:
        rest = inner_parts[0].shape[1]
        part = pl.BlockSpec((1, rest, piece), lambda i: (i, 0, 0))
        return ([own_inner, own_outer, *inner_parts, *outer_parts], [own, own, part, part], 1)
    rows = inner_parts[0].shape[0]
    fixed = pl.BlockSpec((rows, piece), lambda i: (0, 0), pipeline_mode=pl.Buffered(1))
    return (
        [own_inner, own_outer, *inner_parts, *outer_parts],
        [own, own] + [fixed] * (2 * len(inner_parts)),
        len(inner_parts),
    )


def accumulate(step, total, part):
    @pl.when(step == 0)
    def _():
        total[...] = part

    @pl.when(step > 0)
    def _():
        total[...] += part


def finish_pair(step, total, near_ref, far_ref):
    rows = near_ref.shape[0]

    @pl.when(step == pl.num_programs(0) - 1)
    def _():
        near_ref[...] = total[:rows]
        far_ref[...] = low(total[rows:])


def feed_forward_kernel(count, hidden_ref, bias_ref, own_inner, own_outer, *refs):
    inner_refs, outer_refs = refs[:count], refs[count : 2 * count]
    near_ref, far_ref, active_ref, slope_ref, total, inner_now, outer_now = refs[2 * count :]
    step = pl.program_id(0)
    load_weights(step, own_inner, own_outer, inner_refs, outer_refs, inner_now, outer_now)
    pre = mm(hidden_ref[...], inner_now[...]) + bias_ref[...]
    tail = half_erfc(jnp.abs(pre))
    below = jnp.where(pre < 0.0, tail, 1.0 - tail)
    active = low(pre * below)
    active_ref[...] = active
    slope_ref[...] = low(below + pre * (jnp.exp(-0.5 * pre * pre) * 0.3989422804014327))
    accumulate(step, total, mm(active, outer_now[...], NT))
    finish_pair(step, total, near_ref, far_ref)


def feed_forward(hidden_pair, bias_row, weights, layer):
    rows, width = hidden_pair.shape
    hidden = bias_row.shape[1]
    block = hidden // 4
    arrays, specs, count = weight_operands(weights, layer)
    column = pl.BlockSpec((rows, block), lambda i: (0, i))
    half = pl.BlockSpec((rows // 2, width), lambda i: (0, 0))
    return pl.pallas_call(
        functools.partial(feed_forward_kernel, count),
        grid=(4,),
        in_specs=[
            pl.BlockSpec((rows, width), lambda i: (0, 0)),
            pl.BlockSpec((1, block), lambda i: (0, i)),
            *specs,
        ],
        out_specs=[half, half, column, column],
        out_shape=[
            jax.ShapeDtypeStruct((rows // 2, width), jnp.float32),
            jax.ShapeDtypeStruct((rows // 2, width), jnp.bfloat16),
            jax.ShapeDtypeStruct((rows, hidden), jnp.bfloat16),
            jax.ShapeDtypeStruct((rows, hidden), jnp.bfloat16),
        ],
        scratch_shapes=[
            pltpu.VMEM((rows, width), jnp.float32),
            pltpu.VMEM((width, block), jnp.bfloat16),
            pltpu.VMEM((width, block), jnp.bfloat16),
        ],
        cost_estimate=lasting(16),
        name="feed_forward",
    )(hidden_pair, bias_row, *arrays)


def feed_backward_kernel(count, grad_ref, slope_ref, own_inner, own_outer, *refs):
    inner_refs, outer_refs = refs[:count], refs[count : 2 * count]
    near_ref, far_ref, inner_grad_ref, bias_ref, total, inner_now, outer_now = refs[2 * count :]
    step = pl.program_id(0)
    load_weights(step, own_inner, own_outer, inner_refs, outer_refs, inner_now, outer_now)
    inner_grad = low(mm(grad_ref[...], outer_now[...]) * wide(slope_ref[...]))
    inner_grad_ref[...] = inner_grad
    bias_ref[...] = jnp.sum(wide(inner_grad), axis=0, keepdims=True)
    accumulate(step, total, mm(inner_grad, inner_now[...], NT))
    finish_pair(step, total, near_ref, far_ref)


def feed_backward(grad_pair, slope, weights, layer):
    rows, width = grad_pair.shape
    hidden = slope.shape[1]
    block = hidden // 4
    arrays, specs, count = weight_operands(weights, layer)
    column = pl.BlockSpec((rows, block), lambda i: (0, i))
    half = pl.BlockSpec((rows // 2, width), lambda i: (0, 0))
    return pl.pallas_call(
        functools.partial(feed_backward_kernel, count),
        grid=(4,),
        in_specs=[pl.BlockSpec((rows, width), lambda i: (0, 0)), column, *specs],
        out_specs=[half, half, column, pl.BlockSpec((1, block), lambda i: (0, i))],
        out_shape=[
            jax.ShapeDtypeStruct((rows // 2, width), jnp.float32),
            jax.ShapeDtypeStruct((rows // 2, width), jnp.bfloat16),
            jax.ShapeDtypeStruct((rows, hidden), jnp.bfloat16),
            jax.ShapeDtypeStruct((1, hidden), jnp.float32),
        ],
        scratch_shapes=[
            pltpu.VMEM((rows, width), jnp.float32),
            pltpu.VMEM((width, block), jnp.bfloat16),
            pltpu.VMEM((width, block), jnp.bfloat16),
        ],
        cost_estimate=lasting(11),
        name="feed_backward",
    )(grad_pair, slope, *arrays)


def weight_gradient_kernel(
    split,
    rows_ref,
    hidden_ref,
    grad_ref,
    mixed_ref,
    inner_grad_ref,
    active_ref,
    branch_ref,
    after_ref,
    *refs,
):
    outs, (hidden_t, grad_t, mixed_t) = refs[:-3], refs[-3:]
    step = pl.program_id(0)
    piece = active_ref.shape[1]

    @pl.when(step == 0)
    def _():
        hidden_t[...] = hidden_ref[...].T
        grad_t[...] = grad_ref[...].T
        mixed_t[...] = mixed_ref[...].T

    def write(store):
        store(0, piece, low(mm(hidden_t[...], inner_grad_ref[...])))
        store(piece, 2 * piece, low(mm(grad_t[...], active_ref[...])))
        store(2 * piece, 2 * piece + LANES, low(mm(mixed_t[...], branch_ref[...])))

    if not split:
        first_out, second_out = outs

        def store(begin, end, value):
            shard = value.shape[0] // 4
            ref = second_out if begin == piece else first_out
            column = {0: 0, piece: 0, 2 * piece: piece}[begin]
            for r in range(4):
                place = pl.multiple_of(rows_ref[r] * shard, shard)
                ref[0, pl.ds(place, shard), column : column + end - begin] = value[r * shard : (r + 1) * shard]

        write(store)
        return
    first_keep, first_send, second_keep, second_send = outs
    for j in range(4):

        @pl.when(step == j)
        def _(j=j):
            first = (first_send if j % 2 else first_keep, j // 2)
            second = (second_send if j // 2 else second_keep, j % 2)

            def store(begin, end, value):
                half = value.shape[0] // 2
                first[0][first[1], :, begin:end] = value[:half]
                second[0][second[1], :, begin:end] = value[half:]

            write(store)


def weight_gradients(hidden_pair, grad_pair, mixed_pair, inner_grad, active, branch_pair, plane_rows, split, after):
    rows, width = hidden_pair.shape
    hidden = active.shape[1]
    piece = hidden // 4
    total = 2 * piece + LANES
    whole = pl.BlockSpec((rows, width), lambda i, rows_ref: (0, 0))
    column = pl.BlockSpec((rows, piece), lambda i, rows_ref: (0, i))
    if split:
        shape = (2, width // 2, total)
        out_specs = [pl.BlockSpec(shape, lambda i, rows_ref: (0, 0, 0), pipeline_mode=pl.Buffered(1))] * 4
        out_shape = [jax.ShapeDtypeStruct(shape, jnp.bfloat16)] * 4
    else:
        out_specs = [
            pl.BlockSpec((1, width, columns), lambda i, rows_ref: (i, 0, 0)) for columns in (piece + LANES, piece)
        ]
        out_shape = [jax.ShapeDtypeStruct((4, width, columns), jnp.bfloat16) for columns in (piece + LANES, piece)]
    return pl.pallas_call(
        functools.partial(weight_gradient_kernel, split),
        grid_spec=pltpu.PrefetchScalarGridSpec(
            num_scalar_prefetch=1,
            grid=(4,),
            in_specs=[
                whole,
                whole,
                whole,
                column,
                column,
                pl.BlockSpec((rows, LANES), lambda i, rows_ref: (0, i)),
                pl.BlockSpec(memory_space=pl.ANY),
            ],
            out_specs=out_specs,
            scratch_shapes=[pltpu.VMEM((width, rows), jnp.bfloat16)] * 3,
        ),
        out_shape=out_shape,
        cost_estimate=lasting(13),
        name="weight_gradients",
    )(plane_rows, hidden_pair, grad_pair, mixed_pair, inner_grad, active, branch_pair, after)


def block_columns(values_in, order, width):
    return jnp.concatenate(
        [lax.dynamic_slice_in_dim(values_in, block * width, width, 1) for block in order], axis=1
    )


def norm_forward(values_in, gain_row, shift_row):
    centre = values_in - jnp.mean(values_in, axis=-1, keepdims=True)
    spread = jnp.mean(centre * centre, axis=-1, keepdims=True)
    inverse = lax.rsqrt(spread + epsilon)
    unit = centre * inverse
    return (unit * gain_row + shift_row, unit, inverse)


def norm_backward(grad, unit, inverse, gain_row):
    grad_unit = grad * gain_row
    back = inverse * (
        grad_unit
        - jnp.mean(grad_unit, axis=-1, keepdims=True)
        - unit * jnp.mean(grad_unit * unit, axis=-1, keepdims=True)
    )
    return (back, jnp.sum(grad * unit, axis=0), jnp.sum(grad, axis=0))


def attention_output_kernel(
    place_ref,
    heads_ref,
    own_ref,
    near_ref,
    far_ref,
    activation_ref,
    bias_ref,
    gain_ref,
    shift_ref,
    mixed_ref,
    unit_ref,
    inverse_ref,
    hidden_ref,
    turned_ref,
    held,
    held_low,
):
    shard = own_ref.shape[0]
    half = near_ref.shape[1]
    for p in range(8):
        mixed_ref[:, p * LANES : (p + 1) * LANES] = heads_ref[place_ref[p]]
    own, rest = mixed_ref[:, :shard], mixed_ref[:, shard:]
    held[:, :half] = mm(own, own_ref[:, :half]) + mm(rest, near_ref[...])
    held[:, half:] = mm(own, own_ref[:, half:]) + mm(rest, far_ref[...])
    attended = jnp.concatenate(
        [held[:, pl.ds(pl.multiple_of(place_ref[8 + b] * LANES, LANES), LANES)] for b in range(8)], axis=1
    )
    first_pre = wide(activation_ref[...]) + (attended + bias_ref[...])
    hidden, unit, inverse = norm_forward(first_pre, gain_ref[...], shift_ref[...])
    unit_ref[...] = unit
    inverse_ref[...] = inverse
    hidden_ref[...] = hidden
    held_low[...] = low(hidden)
    for r in range(4):
        turned_ref[:, r * shard : (r + 1) * shard] = held_low[
            :, pl.ds(pl.multiple_of(place_ref[16 + r] * shard, shard), shard)
        ]


def attention_output(heads, out_weights, activation, bias_row, gain_row, shift_row, places):
    rows, width = activation.shape
    wide_rows = jax.ShapeDtypeStruct((rows, width), jnp.float32)
    low_rows = jax.ShapeDtypeStruct((rows, width), jnp.bfloat16)
    return pl.pallas_call(
        attention_output_kernel,
        grid_spec=pltpu.PrefetchScalarGridSpec(
            num_scalar_prefetch=1,
            grid=(1,),
            in_specs=[
                pl.BlockSpec(array.shape, lambda i, place_ref, rank=array.ndim: (0,) * rank)
                for array in (heads, *out_weights, activation, bias_row, gain_row, shift_row)
            ],
            out_specs=[
                pl.BlockSpec((rows, width), lambda i, place_ref: (0, 0)),
                pl.BlockSpec((rows, width), lambda i, place_ref: (0, 0)),
                pl.BlockSpec((rows, 1), lambda i, place_ref: (0, 0)),
                pl.BlockSpec((rows, width), lambda i, place_ref: (0, 0)),
                pl.BlockSpec((rows, width), lambda i, place_ref: (0, 0)),
            ],
            scratch_shapes=[pltpu.VMEM((rows, width), jnp.float32), pltpu.VMEM((rows, width), jnp.bfloat16)],
        ),
        out_shape=[low_rows, wide_rows, jax.ShapeDtypeStruct((rows, 1), jnp.float32), wide_rows, low_rows],
        cost_estimate=lasting(5),
        name="attention_output",
    )(places, heads, *out_weights, activation, bias_row, gain_row, shift_row)


def attention_output_back_kernel(
    place_ref,
    near_back_ref,
    came_ref,
    grad_ref,
    unit_ref,
    inverse_ref,
    gain_ref,
    own_ref,
    near_ref,
    far_ref,
    first_ref,
    rows_ref,
    spread_ref,
    sent_ref,
    held,
    held_low,
):
    shard = own_ref.shape[0]
    half = near_ref.shape[1]
    held[...] = near_back_ref[...] + wide(came_ref[...])
    back = jnp.concatenate(
        [held[:, pl.ds(pl.multiple_of(place_ref[16 + r] * shard, shard), shard)] for r in range(4)], axis=1
    )
    grad_first, gain_row, shift_row = norm_backward(
        grad_ref[...] + back, unit_ref[...], inverse_ref[...], gain_ref[...]
    )
    first_ref[...] = grad_first
    branch = low(grad_first)
    rows_ref[0:1] = gain_row[None]
    rows_ref[1:2] = shift_row[None]
    rows_ref[2:3] = jnp.sum(wide(branch), axis=0, keepdims=True)
    held_low[...] = branch
    for p in range(8):
        spread_ref[:, p * LANES : (p + 1) * LANES] = held_low[
            :, pl.ds(pl.multiple_of(place_ref[24 + p] * LANES, LANES), LANES)
        ]
    spread = spread_ref[...]
    held_low[:, :shard] = low(mm(spread, own_ref[...], NT))
    held_low[:, shard:] = low(mm(spread[:, :half], near_ref[...], NT) + mm(spread[:, half:], far_ref[...], NT))
    for head in range(8):
        begin = place_ref[16 + head // 2] * shard + (head % 2) * LANES
        sent_ref[head] = held_low[:, pl.ds(pl.multiple_of(begin, LANES), LANES)]


def attention_output_back(near_back, came, grad_second, unit, inverse, gain_row, out_weights, places):
    rows, width = grad_second.shape
    operands = (near_back, came, grad_second, unit, inverse, gain_row, *out_weights)
    whole = pl.BlockSpec((rows, width), lambda i, place_ref: (0, 0))
    return pl.pallas_call(
        attention_output_back_kernel,
        grid_spec=pltpu.PrefetchScalarGridSpec(
            num_scalar_prefetch=1,
            grid=(1,),
            in_specs=[pl.BlockSpec(array.shape, lambda i, place_ref: (0, 0)) for array in operands],
            out_specs=[
                whole,
                pl.BlockSpec((3, width), lambda i, place_ref: (0, 0)),
                whole,
                pl.BlockSpec((8, rows, LANES), lambda i, place_ref: (0, 0, 0)),
            ],
            scratch_shapes=[pltpu.VMEM((rows, width), jnp.float32), pltpu.VMEM((rows, width), jnp.bfloat16)],
        ),
        out_shape=[
            jax.ShapeDtypeStruct((rows, width), jnp.float32),
            jax.ShapeDtypeStruct((3, width), jnp.float32),
            jax.ShapeDtypeStruct((rows, width), jnp.bfloat16),
            jax.ShapeDtypeStruct((8, rows, LANES), jnp.bfloat16),
        ],
        cost_estimate=lasting(6),
        name="attention_output_back",
    )(places, *operands)


def token_gradient_kernel(
    place_ref, query_ref, key_ref, value_ref, joint_ref, *refs
):
    near_ref, far_ref, packed_ref, bias_ref = refs[-4:]
    step = pl.program_id(0)
    packed = jnp.concatenate([query_ref[...], key_ref[...], value_ref[...]], axis=1)
    packed_ref[...] = packed
    accumulate(step, bias_ref, jnp.sum(wide(packed), axis=0, keepdims=True))
    part = mm(packed, joint_ref[...], NT)

    @pl.when(step < 4)
    def _():
        near_ref[0] = part

    @pl.when(step >= 4)
    def _():
        far_ref[0] = low(part)


def token_gradients(grads, joint, chips, after):
    tokens = grads[0].shape[0]
    rows = tokens // 8
    width, columns = joint.shape
    block = pl.BlockSpec((rows, LANES), lambda i, place_ref: (i, 0))
    return pl.pallas_call(
        token_gradient_kernel,
        grid_spec=pltpu.PrefetchScalarGridSpec(
            num_scalar_prefetch=1,
            grid=(8,),
            in_specs=[block, block, block, pl.BlockSpec((width, columns), lambda i, place_ref: (0, 0))]
            + [pl.BlockSpec(memory_space=pl.ANY)] * len(after),
            out_specs=[
                pl.BlockSpec((1, rows, width), lambda i, place_ref: (place_ref[jnp.minimum(i, 3)], 0, 0)),
                pl.BlockSpec((1, rows, width), lambda i, place_ref: (place_ref[jnp.maximum(i - 4, 0)], 0, 0)),
                pl.BlockSpec((rows, columns), lambda i, place_ref: (i, 0)),
                pl.BlockSpec((1, columns), lambda i, place_ref: (0, 0)),
            ],
        ),
        out_shape=[
            jax.ShapeDtypeStruct((4, rows, width), jnp.float32),
            jax.ShapeDtypeStruct((4, rows, width), jnp.bfloat16),
            jax.ShapeDtypeStruct((tokens, columns), jnp.bfloat16),
            jax.ShapeDtypeStruct((1, columns), jnp.float32),
        ],
        cost_estimate=lasting(60 if after else 10),
        name="token_gradients",
    )(chips, *grads, joint, *after)


def gate(values_in, *points):
    anywhere = pl.BlockSpec(memory_space=pl.ANY)
    return pl.pallas_call(
        lambda *refs: None,
        in_specs=[anywhere] * (len(values_in) + len(points)),
        out_specs=[anywhere] * len(values_in),
        out_shape=[jax.ShapeDtypeStruct(value.shape, value.dtype) for value in values_in],
        input_output_aliases={i: i for i in range(len(values_in))},
        cost_estimate=SMALL_COST,
        name="gate",
    )(*values_in, *points)


def spread_tokens(rows_in):
    half = rows_in.shape[1] // 2
    left, right = rows_in[:, :half], rows_in[:, half:]
    left_pair = jnp.stack([left, swap(left, ALONG_X)])
    right_pair = jnp.stack([right, swap(right, ALONG_Y)])
    left_far = swap(left_pair, ALONG_Y)
    right_far = swap(right_pair, ALONG_X)
    left_all = jnp.concatenate([left_pair, left_far])
    right_all = jnp.stack([right_pair[0], right_far[0], right_pair[1], right_far[1]])
    near = jnp.concatenate([left_all, right_all], axis=2).reshape(4 * rows_in.shape[0], rows_in.shape[1])
    return (near, swap(near, CORE))


def plane_groups():
    count = lax.axis_size("ctx")
    return [list(range(0, count, 2)), list(range(1, count, 2))]


def collect_tokens(near, far_came, *points):
    sent = low(near + wide(far_came))
    if points:
        (sent,) = gate([sent], *points)
    came = lax.all_to_all(sent, "ctx", 0, 0, axis_index_groups=plane_groups(), tiled=True)
    return jnp.sum(wide(came), axis=0)


def plane_pieces(piece, *points):
    half = piece.shape[1] // 2
    left, right = piece[:, :half], piece[:, half:]
    left_pair = jnp.stack([left, swap(left, ALONG_X)])
    right_pair = jnp.stack([right, swap(right, ALONG_Y)])
    left_far, right_far = gate([swap(left_pair, ALONG_Y), swap(right_pair, ALONG_X)], *points)
    left_all = jnp.concatenate([left_pair, left_far])
    right_all = jnp.stack([right_pair[0], right_far[0], right_pair[1], right_far[1]])
    near = jnp.concatenate([left_all, right_all], axis=2)
    return (near, swap(near, CORE))


def exchange(blocks):
    return lax.all_to_all(blocks, "ctx", 0, 0, tiled=True)


def head_split_body(
    tokens,
    cotangent,
    doc_starts,
    doc_lengths,
    query_weight,
    key_weight,
    value_weight,
    out_weight,
    inner_weight,
    outer_weight,
    query_bias,
    value_bias,
    out_bias,
    inner_bias,
    outer_bias,
    first_gain,
    first_shift,
    second_gain,
    second_shift,
):
    rows = tokens.shape[1]
    width = tokens.shape[2]
    here = lax.axis_index("ctx")
    plane = lax.axis_index("wsh")
    planes = lax.axis_size("wsh")
    shard = width // planes
    hidden = inner_weight.shape[2]
    piece = hidden // 8
    core = here % 2
    chip = here // 2
    relative = jnp.arange(8, dtype=jnp.int32)
    spread = jnp.array((0, 2, 4, 6, 1, 3, 5, 7), jnp.int32)
    turned = [(plane - r) % planes for r in range(planes)]
    unturned = turned
    positions = ((here ^ spread)[:, None] * rows + jnp.arange(rows, dtype=jnp.int32)).reshape(-1)
    labels = doc_labels(positions, doc_starts[0], doc_lengths[0])[:, None]

    four = jnp.arange(4, dtype=jnp.int32)
    chip_order = [chip ^ four, four]
    inner_order = [core * 4 + order for order in chip_order]
    out_order = [jnp.concatenate([2 * order + core, 2 * order + 1 - core]) for order in chip_order]
    block_order = here ^ spread
    plane_rows = jnp.stack(turned).astype(jnp.int32)
    first_own, second_own, joint_own = own_pieces(
        inner_weight,
        outer_weight,
        out_weight,
        (query_weight, key_weight, value_weight),
        (
            query_bias,
            value_bias,
            out_bias,
            outer_bias,
            first_gain,
            first_shift,
            second_gain,
            second_shift,
            inner_bias,
        ),
        here,
        core * 4 + chip,
    )
    joint_width = 3 * LANES

    def ordered(stack, order):
        return jnp.concatenate([lax.dynamic_index_in_dim(stack, i, 0, keepdims=False) for i in order], axis=0)

    first_joint = joint_own[0]
    joint_turned = jnp.stack([first_joint] + [turn(first_joint, r) for r in range(1, planes)])
    joint_first = ordered(joint_turned[:, :shard], unturned)
    small_all = ordered(joint_turned[:, None, shard:, :shard], unturned)

    def small(layer, index):
        return small_all[:, 2 * index + layer].reshape(width)

    inner_bias_all = small_all[:, 16:24].reshape(planes, 4, LAYERS, shard).transpose(2, 0, 1, 3).reshape(LAYERS, hidden)

    inner_near = ordered(lax.all_gather(first_own[0], "wsh", axis=0), turned[1:])
    first_tokens = spread_tokens(tokens[0])
    (outer_sent,) = gate([second_own[0]], first_tokens[0])
    outer_stack = lax.all_gather(outer_sent, "wsh", axis=0)
    middle = 3 * shard // 2

    def spread_first(near):
        left, right = near[:middle], near[middle:]
        return (left, right, swap(left, ALONG_X), swap(right, ALONG_Y))

    def spread_second(left, right, left_x, right_y):
        lefts = (left, left_x, swap(left, ALONG_Y), swap(left_x, ALONG_Y))
        rights = (right, swap(right, ALONG_X), right_y, swap(right_y, ALONG_X))
        return [part for pair in zip(lefts, rights) for part in pair]

    inner_half = spread_first(inner_near)
    layer_own = jnp.concatenate([first_own[1], second_own[1], joint_own[1, :shard]], axis=1)
    wide_piece = 2 * piece + LANES

    def layer_weights(layer):
        if layer == 0:
            near = jnp.concatenate(
                [
                    jnp.concatenate([inner_first[2 * j][:, piece:], inner_first[2 * j + 1][:, piece:]], axis=0)
                    for j in range(4)
                ],
                axis=1,
            )
            weights = (inner_own, outer_own, inner_first, outer_first)
        else:
            near = jnp.concatenate([inner_second[j, :, piece:] for j in range(4)], axis=1)
            weights = (inner_own, outer_own, [inner_second])
        return (weights, (out_own[layer], near, swap(near, CORE)))

    def out_place(layer, block):
        at = (block // 2) ^ chip if layer == 0 else block // 2
        return at + 4 * ((block % 2) ^ core)

    activation = tokens[0]
    stashed = []
    outputs = []
    for layer in range(LAYERS):
        joint = joint_first if layer == 0 else joint_second
        first_gain_row, first_shift_row = wide(small(layer, 4)), wide(small(layer, 5))
        second_gain_row, second_shift_row = wide(small(layer, 6)), wide(small(layer, 7))

        near_tokens, far_tokens = first_tokens if layer == 0 else spread_tokens(activation)
        everyone = jnp.concatenate([near_tokens, far_tokens], axis=0)
        query_bias_own = lax.dynamic_slice_in_dim(small(layer, 0), here * LANES, LANES, 0)
        value_bias_own = lax.dynamic_slice_in_dim(small(layer, 1), here * LANES, LANES, 0)
        joint_bias = wide(jnp.concatenate([query_bias_own, jnp.zeros_like(query_bias_own), value_bias_own]))
        packed = low(mm(everyone, joint) + joint_bias)
        if layer == 0:
            (packed,) = gate([packed], inner_near)
            (layer_own,) = gate([layer_own], packed)
            second_stack = lax.all_gather(layer_own, "wsh", axis=0)
        mixed, log_all = attention_forward(packed, labels, block_order)
        if layer == 0:
            inner_own, outer_own, out_own = own_blocks(
                inner_weight,
                outer_weight,
                out_weight,
                jnp.concatenate(inner_order),
                jnp.concatenate(out_order),
                mixed,
            )
            left_x, right_y, outer_stack = gate([*inner_half[2:], outer_stack], mixed)
            inner_first = spread_second(*inner_half[:2], left_x, right_y)
            outer_first = spread_second(*spread_first(ordered(outer_stack, turned[1:])))
        else:
            (inner_second,) = gate([inner_second], mixed)
        weights, out_weights = layer_weights(layer)
        mixed_heads = exchange(mixed.reshape(8, rows, LANES))
        places = jnp.stack(
            [2 * turned[p // 2] + p % 2 for p in range(8)]
            + [out_place(layer, b) for b in range(8)]
            + turned
            + [jnp.int32(0)] * 4
            + [out_order[layer][p] for p in range(8)]
        ).astype(jnp.int32)
        mixed_turned, first_unit, first_inverse, hidden_rows, hidden_turned = attention_output(
            mixed_heads,
            out_weights,
            activation,
            wide(small(layer, 2))[None],
            first_gain_row[None],
            first_shift_row[None],
            places,
        )
        if layer == 1:
            weights = (*weights, gate([outer_second], hidden_turned))
        mixed_pair = jnp.concatenate([mixed_turned, swap(mixed_turned, CORE)], axis=0)
        hidden_pair = jnp.concatenate([hidden_turned, swap(hidden_turned, CORE)], axis=0)
        inner_bias_own = jnp.concatenate(
            [lax.dynamic_slice_in_dim(inner_bias_all[layer], inner_order[layer][j] * piece, piece, 0) for j in range(4)]
        )
        outer_near, outer_far, active, slope = feed_forward(
            hidden_pair, wide(inner_bias_own)[None], weights, layer
        )
        outer_turned = outer_near + wide(swap(outer_far, CORE))
        if layer == 0:
            (second_stack,) = gate([second_stack], active)
            joint_second = second_stack[:, :, wide_piece:].reshape(width, joint_width)
            others_second = ordered(second_stack[:, :, :wide_piece], turned[1:])
            inner_second, outer_second = [
                lax.all_gather(part, "ctx", axis=0, axis_index_groups=plane_groups())
                for part in (others_second[:, : piece + LANES], others_second[:, piece + LANES :])
            ]
        outer_out = block_columns(outer_turned, unturned, shard)
        second_pre = hidden_rows + (outer_out + wide(small(layer, 3)))
        result, second_unit, second_inverse = norm_forward(second_pre, second_gain_row, second_shift_row)
        stashed.append(
            (
                everyone,
                packed,
                log_all,
                mixed_pair,
                first_unit,
                first_inverse,
                hidden_pair,
                active,
                slope,
                second_unit,
                second_inverse,
                joint,
                out_weights,
                places,
                weights,
                first_gain_row,
                second_gain_row,
            )
        )
        activation = low(result)
        outputs.append(activation)

    gradient = wide(cotangent[0])
    small_grads = [None] * LAYERS
    for layer in reversed(range(LAYERS)):
        (
            everyone,
            packed,
            log_all,
            mixed_pair,
            first_unit,
            first_inverse,
            hidden_pair,
            active,
            slope,
            second_unit,
            second_inverse,
            joint,
            out_weights,
            places,
            weights,
            first_gain_row,
            second_gain_row,
        ) = stashed[layer]
        grad_second, grad_second_gain, grad_second_shift = norm_backward(
            gradient, second_unit, second_inverse, second_gain_row
        )
        grad_outer = low(grad_second)
        grad_outer_bias = jnp.sum(wide(grad_outer), axis=0)
        grad_turned = block_columns(grad_outer, turned, shard)
        grad_pair = jnp.concatenate([grad_turned, swap(grad_turned, CORE)], axis=0)
        hidden_near, hidden_far, grad_inner, grad_inner_bias = feed_backward(grad_pair, slope, weights, layer)
        grad_first, first_rows, branch_spread, grad_sent = attention_output_back(
            hidden_near,
            swap(hidden_far, CORE),
            grad_second,
            first_unit,
            first_inverse,
            first_gain_row[None],
            out_weights,
            places,
        )
        grad_first_gain, grad_first_shift, grad_out_bias = first_rows[0], first_rows[1], first_rows[2]
        grad_mixed = exchange(grad_sent).reshape(8 * rows, LANES)
        branch_half = 4 * LANES
        branch_pair = jnp.concatenate(
            [branch_spread[:, :branch_half], swap(branch_spread[:, branch_half:], CORE)], axis=0
        )
        summed = weight_gradients(
            hidden_pair, grad_pair, mixed_pair, grad_inner, active, branch_pair, plane_rows, layer == 0, grad_sent
        )
        (grad_mixed,) = gate([grad_mixed], summed[0])
        grad_query, grad_key, grad_value = attention_backward(packed, labels, grad_mixed, log_all, block_order)
        first_points = ()
        if layer == 0:
            first_keep, first_send, second_keep, second_send = summed
            first_came = swap(first_send, ALONG_X)
            second_came = swap(second_send, ALONG_Y)
            first_came, second_came = gate([first_came, second_came], grad_query)
            first_next = low(wide(first_keep[1]) + wide(first_came[1]))
            second_next = low(wide(second_keep[1]) + wide(second_came[1]))
            first_points = (first_next, second_next)
        near_part, far_part, grad_packed, joint_bias_grad = token_gradients(
            (grad_query, grad_key, grad_value), joint, chip_order[0], first_points
        )
        joint_bias_grad = joint_bias_grad[0]
        if layer == 0:
            first_last = swap(first_next, ALONG_Y)
            second_last = swap(second_next, ALONG_X)
            first_sum = wide(first_keep[0]) + wide(first_came[0]) + wide(first_last)
            second_sum = wide(second_keep[0]) + wide(second_came[0]) + wide(second_last)
            first_points = (first_last, second_last)
            (plane_second,) = gate([plane_second], grad_mixed)
            sum_second = lax.psum_scatter(plane_second, "wsh", scatter_dimension=0, tiled=True)
            sum_first, sum_second, sum_joint = gate([sum_first, sum_second, sum_joint], near_part, first_last, second_last)
            everything = lax.all_gather(
                jnp.concatenate([sum_first[:, :piece], sum_second, sum_first[:, piece:], sum_joint], axis=1),
                "ctx",
                axis=0,
            )
        far_came = swap(far_part, CORE)
        gradient = grad_first + collect_tokens(near_part, far_came, *first_points)
        grad_joint = low(mm(everyone, grad_packed, TN))

        placed_query, placed_value = [
            lax.dynamic_update_slice(jnp.zeros((width,), jnp.float32), part, (here * LANES,))
            for part in (joint_bias_grad[:LANES], joint_bias_grad[2 * LANES :])
        ]
        placed_inner = jnp.zeros((hidden,), jnp.float32)
        for j in range(4):
            placed_inner = lax.dynamic_update_slice(
                placed_inner, grad_inner_bias[0, j * piece : (j + 1) * piece], (inner_order[layer][j] * piece,)
            )
        small_grads[layer] = jnp.concatenate(
            [
                row.reshape(planes, -1)
                for row in (
                    placed_query,
                    placed_value,
                    grad_out_bias,
                    grad_outer_bias,
                    grad_first_gain,
                    grad_first_shift,
                    grad_second_gain,
                    grad_second_shift,
                    placed_inner,
                )
            ],
            axis=1,
        )
        if layer == 0:
            small_sent = jnp.concatenate(small_grads, axis=1)
            small_plane = jnp.sum(lax.all_to_all(small_sent, "wsh", 0, 0, tiled=True), axis=0)
            small_spread = jnp.broadcast_to(small_plane, (8, small_plane.shape[0]))
            small_mine = jnp.sum(exchange(small_spread), axis=0).reshape(LAYERS, -1)

        if layer == 0:
            joint_rows = [
                lax.dynamic_slice_in_dim(grad_joint, turned[r] * shard, shard, 0) for r in range(planes)
            ]
            sent = (first_sum[shard:], second_sum[:shard], second_sum[shard:])
            came = [
                turn(jnp.concatenate([low(sent[r - 1]), joint_rows[r]], axis=1), planes - r)
                for r in range(1, planes)
            ]
            came = gate(came, gradient, small_mine)
            last_total = jnp.concatenate([first_sum[:shard], wide(joint_rows[0])], axis=1)
            for part in came:
                last_total = last_total + wide(part)
            last_total = low(last_total)
            (everything,) = gate([everything], last_total)
            *placed, placed_token = place_pieces(everything, everything, relative, 1, None)
        else:
            plane_first, plane_second = [
                lax.psum_scatter(
                    part.reshape(4 * width, -1),
                    "ctx",
                    scatter_dimension=0,
                    axis_index_groups=plane_groups(),
                    tiled=True,
                )
                for part in (summed[0], *gate([summed[1]], gradient))
            ]
            (plane_first,) = gate([plane_first], far_came)
            sum_first = lax.psum_scatter(plane_first, "wsh", scatter_dimension=0, tiled=True)
            sum_joint = lax.psum_scatter(grad_joint, "wsh", scatter_dimension=0, tiled=True)


    near, far = plane_pieces(last_total, placed_token)
    near_first = here ^ (2 * four)
    *placed, _ = place_pieces(near, far, jnp.concatenate([near_first, near_first ^ 1]), 0, placed)
    small_outs = [small_mine[:, i * shard : (i + 1) * shard] for i in range(8)]
    return (
        outputs[0][None],
        outputs[1][None],
        low(gradient)[None],
        *placed,
        small_outs[0],
        small_outs[1],
        small_outs[2],
        small_mine[:, 8 * shard :],
        small_outs[3],
        small_outs[4],
        small_outs[5],
        small_outs[6],
        small_outs[7],
    )


def choose_body(mesh):
    if mesh.shape["ctx"] == 8 and HEADS // 8 == 2:
        return head_split_body
    return window_body


def solution(mesh):
    in_specs = (
        P("wsh", "ctx", None),
        P("wsh", "ctx", None),
        P("wsh", None),
        P("wsh", None),
        P(None, "wsh", None),
        P(None, "wsh", None),
        P(None, "wsh", None),
        P(None, "wsh", None),
        P(None, "wsh", None),
        P(None, None, "wsh"),
        P(None, "wsh"),
        P(None, "wsh"),
        P(None, "wsh"),
        P(None, "wsh"),
        P(None, "wsh"),
        P(None, "wsh"),
        P(None, "wsh"),
        P(None, "wsh"),
        P(None, "wsh"),
    )
    out_specs = (
        P("wsh", "ctx", None),
        P("wsh", "ctx", None),
        P("wsh", "ctx", None),
        P(None, "wsh", None),
        P(None, "wsh", None),
        P(None, "wsh", None),
        P(None, "wsh", None),
        P(None, "wsh", None),
        P(None, None, "wsh"),
        P(None, "wsh"),
        P(None, "wsh"),
        P(None, "wsh"),
        P(None, "wsh"),
        P(None, "wsh"),
        P(None, "wsh"),
        P(None, "wsh"),
        P(None, "wsh"),
        P(None, "wsh"),
    )
    return jax.shard_map(choose_body(mesh), mesh=mesh, in_specs=in_specs, out_specs=out_specs, check_vma=False)
```

```python
import functools

import jax
import jax.numpy as jnp
from jax import lax
from jax.experimental import pallas as pl
from jax.experimental.pallas import tpu as pltpu
from jax.sharding import PartitionSpec as P

HEADS = 16
HDIM = 64
LAYERS = 2
DOC_CAP = 2000


epsilon = 1e-05
neg_fill = -1e30
head_pair = 2


def from_behind(block, axis, distance):
    devices = range(lax.axis_size(axis))
    route = [(i - distance, i) for i in devices if i - distance in devices]
    return lax.ppermute(block, axis, route)


def normalize(values_in, gain_row, shift_row):
    centre = values_in - jnp.mean(values_in, axis=-1, keepdims=True)
    spread = jnp.mean(centre * centre, axis=-1, keepdims=True)
    return centre * lax.rsqrt(spread + epsilon) * gain_row + shift_row


def exact_gelu(values_in):
    return jax.nn.gelu(values_in, approximate=False)


def product(form, left, right):
    return jnp.einsum(form, left, right, preferred_element_type=jnp.float32)


def doc_labels(positions, starts, lengths):
    inside = (positions[:, None] >= starts[None, :]) & (
        positions[:, None] < (starts + lengths)[None, :]
    )
    labels = jnp.arange(1, starts.shape[0] + 1, dtype=jnp.int32)
    return jnp.sum(jnp.where(inside, labels[None, :], 0), axis=1)


def extend_rows(rows_in, dim, reach, mover):
    pieces = []
    for offset in range(-reach, reach + 1):
        if offset == 0:
            pieces.append(rows_in)
        else:
            pieces.append(mover(rows_in, -offset))
    return jnp.concatenate(pieces, axis=dim)


def move_keys_fwd(rows_in, steps):
    return from_behind(rows_in, "ctx", steps)


def move_keys_back(rows_in, steps):
    return from_behind(rows_in, "ctx", steps)


def fetch_forward(params, layer_index):
    shards = [piece[layer_index].astype(jnp.bfloat16) for piece in params]
    return (
        lax.all_gather(shards[0], "wsh", axis=0, tiled=True),
        lax.all_gather(shards[1], "wsh", axis=0, tiled=True),
        lax.all_gather(shards[2], "wsh", axis=0, tiled=True),
        lax.all_gather(shards[3], "wsh", axis=0, tiled=True),
        lax.all_gather(shards[4], "wsh", axis=0, tiled=True),
        lax.all_gather(shards[5], "wsh", axis=1, tiled=True),
        lax.all_gather(shards[6], "wsh", axis=0, tiled=True),
        lax.all_gather(shards[7], "wsh", axis=0, tiled=True),
        lax.all_gather(shards[8], "wsh", axis=0, tiled=True),
        lax.all_gather(shards[9], "wsh", axis=0, tiled=True),
        lax.all_gather(shards[10], "wsh", axis=0, tiled=True),
        lax.all_gather(shards[11], "wsh", axis=0, tiled=True),
        lax.all_gather(shards[12], "wsh", axis=0, tiled=True),
        lax.all_gather(shards[13], "wsh", axis=0, tiled=True),
        lax.all_gather(shards[14], "wsh", axis=0, tiled=True),
    )


def fetch_backward(params, layer_index):
    shards = [piece[layer_index].astype(jnp.bfloat16) for piece in params]
    return (
        lax.all_gather(shards[0], "wsh", axis=0, tiled=True),
        lax.all_gather(shards[1], "wsh", axis=0, tiled=True),
        lax.all_gather(shards[2], "wsh", axis=0, tiled=True),
        lax.all_gather(shards[3], "wsh", axis=0, tiled=True),
        lax.all_gather(shards[4], "wsh", axis=0, tiled=True),
        lax.all_gather(shards[5], "wsh", axis=1, tiled=True),
        lax.all_gather(shards[6], "wsh", axis=0, tiled=True),
        lax.all_gather(shards[7], "wsh", axis=0, tiled=True),
        lax.all_gather(shards[8], "wsh", axis=0, tiled=True),
        lax.all_gather(shards[9], "wsh", axis=0, tiled=True),
        lax.all_gather(shards[10], "wsh", axis=0, tiled=True),
        lax.all_gather(shards[11], "wsh", axis=0, tiled=True),
        lax.all_gather(shards[12], "wsh", axis=0, tiled=True),
        lax.all_gather(shards[13], "wsh", axis=0, tiled=True),
        lax.all_gather(shards[14], "wsh", axis=0, tiled=True),
    )


def reduce_grads(local_grads):
    shares = (
        lax.psum_scatter(
            local_grads[0].astype(jnp.bfloat16), "wsh", scatter_dimension=0, tiled=True
        ).astype(jnp.float32),
        lax.psum_scatter(
            local_grads[1].astype(jnp.bfloat16), "wsh", scatter_dimension=0, tiled=True
        ).astype(jnp.float32),
        lax.psum_scatter(
            local_grads[2].astype(jnp.bfloat16), "wsh", scatter_dimension=0, tiled=True
        ).astype(jnp.float32),
        lax.psum_scatter(
            local_grads[3].astype(jnp.bfloat16), "wsh", scatter_dimension=0, tiled=True
        ).astype(jnp.float32),
        lax.psum_scatter(
            local_grads[4].astype(jnp.bfloat16), "wsh", scatter_dimension=0, tiled=True
        ).astype(jnp.float32),
        lax.psum_scatter(
            local_grads[5].astype(jnp.bfloat16), "wsh", scatter_dimension=1, tiled=True
        ).astype(jnp.float32),
        lax.psum_scatter(
            local_grads[6].astype(jnp.bfloat16), "wsh", scatter_dimension=0, tiled=True
        ).astype(jnp.float32),
        lax.psum_scatter(
            local_grads[7].astype(jnp.bfloat16), "wsh", scatter_dimension=0, tiled=True
        ).astype(jnp.float32),
        lax.psum_scatter(
            local_grads[8].astype(jnp.bfloat16), "wsh", scatter_dimension=0, tiled=True
        ).astype(jnp.float32),
        lax.psum_scatter(
            local_grads[9].astype(jnp.bfloat16), "wsh", scatter_dimension=0, tiled=True
        ).astype(jnp.float32),
        lax.psum_scatter(
            local_grads[10].astype(jnp.bfloat16), "wsh", scatter_dimension=0, tiled=True
        ).astype(jnp.float32),
        lax.psum_scatter(
            local_grads[11].astype(jnp.bfloat16), "wsh", scatter_dimension=0, tiled=True
        ).astype(jnp.float32),
        lax.psum_scatter(
            local_grads[12].astype(jnp.bfloat16), "wsh", scatter_dimension=0, tiled=True
        ).astype(jnp.float32),
        lax.psum_scatter(
            local_grads[13].astype(jnp.bfloat16), "wsh", scatter_dimension=0, tiled=True
        ).astype(jnp.float32),
        lax.psum_scatter(
            local_grads[14].astype(jnp.bfloat16), "wsh", scatter_dimension=0, tiled=True
        ).astype(jnp.float32),
    )
    return (
        lax.psum(shares[0].astype(jnp.bfloat16), "ctx").astype(jnp.float32),
        lax.psum(shares[1].astype(jnp.bfloat16), "ctx").astype(jnp.float32),
        lax.psum(shares[2].astype(jnp.bfloat16), "ctx").astype(jnp.float32),
        lax.psum(shares[3].astype(jnp.bfloat16), "ctx").astype(jnp.float32),
        lax.psum(shares[4].astype(jnp.bfloat16), "ctx").astype(jnp.float32),
        lax.psum(shares[5].astype(jnp.bfloat16), "ctx").astype(jnp.float32),
        lax.psum(shares[6].astype(jnp.bfloat16), "ctx").astype(jnp.float32),
        lax.psum(shares[7].astype(jnp.bfloat16), "ctx").astype(jnp.float32),
        lax.psum(shares[8].astype(jnp.bfloat16), "ctx").astype(jnp.float32),
        lax.psum(shares[9].astype(jnp.bfloat16), "ctx").astype(jnp.float32),
        lax.psum(shares[10].astype(jnp.bfloat16), "ctx").astype(jnp.float32),
        lax.psum(shares[11].astype(jnp.bfloat16), "ctx").astype(jnp.float32),
        lax.psum(shares[12].astype(jnp.bfloat16), "ctx").astype(jnp.float32),
        lax.psum(shares[13].astype(jnp.bfloat16), "ctx").astype(jnp.float32),
        lax.psum(shares[14].astype(jnp.bfloat16), "ctx").astype(jnp.float32),
    )


def attend(queries, key_ext, value_ext, allowed, score_scale):
    rows_local = queries.shape[0]
    rows_keys = key_ext.shape[0]
    groups = HEADS // head_pair
    span = head_pair * HDIM
    query_groups = queries.reshape(rows_local, groups, span)
    key_groups = key_ext.reshape(rows_keys, groups, span)
    value_groups = value_ext.reshape(rows_keys, groups, span)

    def one_group(group_index, carry):
        mixed_all, log_all = carry
        query_part = lax.dynamic_index_in_dim(query_groups, group_index, 1, keepdims=False).reshape(
            rows_local, head_pair, HDIM
        )
        key_part = lax.dynamic_index_in_dim(key_groups, group_index, 1, keepdims=False).reshape(
            rows_keys, head_pair, HDIM
        )
        value_part = lax.dynamic_index_in_dim(value_groups, group_index, 1, keepdims=False).reshape(
            rows_keys, head_pair, HDIM
        )
        raw_scores = product("qhd,khd->hqk", query_part, key_part)
        scores = jnp.where(allowed[None], raw_scores * score_scale, neg_fill)
        row_peak = jnp.max(scores, axis=2, keepdims=True)
        exponent = jnp.exp(scores - row_peak)
        row_total = jnp.sum(exponent, axis=2, keepdims=True)
        probability = (exponent / row_total).astype(jnp.bfloat16)
        mixed_part = product("hqk,khd->qhd", probability, value_part)
        mixed_all = lax.dynamic_update_index_in_dim(
            mixed_all, mixed_part.reshape(rows_local, span), group_index, 1
        )
        log_all = lax.dynamic_update_index_in_dim(
            log_all, (row_peak + jnp.log(row_total))[:, :, 0], group_index, 0
        )
        return (mixed_all, log_all)

    start_carry = (
        jnp.zeros((rows_local, groups, span), jnp.float32),
        jnp.zeros((groups, head_pair, rows_local), jnp.float32),
    )
    mixed_all, log_all = lax.fori_loop(0, groups, one_group, start_carry)
    return (mixed_all.reshape(rows_local, groups * span), log_all)


def attend_back(queries, key_ext, value_ext, grad_mixed, log_all, allowed, score_scale):
    rows_local = queries.shape[0]
    rows_keys = key_ext.shape[0]
    groups = HEADS // head_pair
    span = head_pair * HDIM
    query_groups = queries.reshape(rows_local, groups, span)
    key_groups = key_ext.reshape(rows_keys, groups, span)
    value_groups = value_ext.reshape(rows_keys, groups, span)
    grad_groups = grad_mixed.reshape(rows_local, groups, span)

    def one_group(group_index, carry):
        query_part = lax.dynamic_index_in_dim(query_groups, group_index, 1, keepdims=False).reshape(
            rows_local, head_pair, HDIM
        )
        key_part = lax.dynamic_index_in_dim(key_groups, group_index, 1, keepdims=False).reshape(
            rows_keys, head_pair, HDIM
        )
        value_part = lax.dynamic_index_in_dim(value_groups, group_index, 1, keepdims=False).reshape(
            rows_keys, head_pair, HDIM
        )
        grad_part = lax.dynamic_index_in_dim(grad_groups, group_index, 1, keepdims=False).reshape(
            rows_local, head_pair, HDIM
        )
        log_part = lax.dynamic_index_in_dim(log_all, group_index, 0, keepdims=False)
        raw_scores = product("qhd,khd->hqk", query_part, key_part)
        scores = jnp.where(allowed[None], raw_scores * score_scale, neg_fill)
        probability = jnp.exp(scores - log_part[:, :, None])
        grad_prob = product("qhd,khd->hqk", grad_part, value_part)
        row_delta = jnp.sum(probability * grad_prob, axis=2, keepdims=True)
        grad_scores = (probability * (grad_prob - row_delta) * score_scale).astype(jnp.bfloat16)
        query_term = product("hqk,khd->qhd", grad_scores, key_part)
        grad_query = lax.dynamic_update_index_in_dim(
            carry[0], query_term.reshape(rows_local, span), group_index, 1
        )
        delta_all = lax.dynamic_update_index_in_dim(carry[1], row_delta[:, :, 0], group_index, 0)
        key_term = product("hqk,qhd->khd", grad_scores, query_part)
        value_term = product("hqk,qhd->khd", probability.astype(jnp.bfloat16), grad_part)
        grad_key = lax.dynamic_update_index_in_dim(
            carry[2], key_term.reshape(rows_keys, span), group_index, 1
        )
        grad_value = lax.dynamic_update_index_in_dim(
            carry[3], value_term.reshape(rows_keys, span), group_index, 1
        )
        return (grad_query, delta_all, grad_key, grad_value)

    start_carry = (
        jnp.zeros((rows_local, groups, span), jnp.float32),
        jnp.zeros((groups, head_pair, rows_local), jnp.float32),
    )
    start_carry = start_carry + (
        jnp.zeros((rows_keys, groups, span), jnp.float32),
        jnp.zeros((rows_keys, groups, span), jnp.float32),
    )
    finals = lax.fori_loop(0, groups, one_group, start_carry)
    grad_query = finals[0].reshape(rows_local, groups * span)
    return (
        grad_query,
        finals[2].reshape(rows_keys, groups * span),
        finals[3].reshape(rows_keys, groups * span),
    )


def layer_forward(activation, gathered, allowed, halo_rows, score_scale):
    (
        query_weight,
        key_weight,
        value_weight,
        out_weight,
        inner_weight,
        outer_weight,
        query_bias,
        value_bias,
        out_bias,
        inner_bias,
        outer_bias,
        first_gain,
        first_shift,
        second_gain,
        second_shift,
    ) = gathered
    rows_local = activation.shape[0]
    queries = (product("td,de->te", activation, query_weight) + query_bias).astype(jnp.bfloat16)
    key_rows = product("td,de->te", activation, key_weight).astype(jnp.bfloat16)
    value_rows = (product("td,de->te", activation, value_weight) + value_bias).astype(jnp.bfloat16)
    stacked = jnp.stack([key_rows, value_rows])
    extended = extend_rows(stacked, 1, halo_rows // rows_local, move_keys_fwd)
    mixed_heads, log_all = attend(queries, extended[0], extended[1], allowed, score_scale)
    mixed_low = mixed_heads.astype(jnp.bfloat16)
    first_pre = activation.astype(jnp.float32) + (
        product("td,de->te", mixed_low, out_weight) + out_bias
    )
    hidden = normalize(first_pre, first_gain.astype(jnp.float32), first_shift.astype(jnp.float32))
    hidden_low = hidden.astype(jnp.bfloat16)
    inner_pre = product("td,df->tf", hidden_low, inner_weight) + inner_bias
    active_low = exact_gelu(inner_pre).astype(jnp.bfloat16)
    second_pre = hidden + (product("tf,fd->td", active_low, outer_weight) + outer_bias)
    result_rows = normalize(
        second_pre, second_gain.astype(jnp.float32), second_shift.astype(jnp.float32)
    )
    saved = (
        activation,
        queries,
        extended,
        log_all,
        mixed_low,
        first_pre,
        hidden_low,
        inner_pre,
        active_low,
        second_pre,
    )
    return (saved, result_rows)


def return_rows(grad_ext, halo_rows, rows_local):
    reach = halo_rows // rows_local
    total = grad_ext[:, halo_rows : halo_rows + rows_local]
    for offset in range(-reach, reach + 1):
        if offset != 0:
            begin = halo_rows + offset * rows_local
            block_rows = grad_ext[:, begin : begin + rows_local]
            total = total + from_behind(block_rows.astype(jnp.bfloat16), "ctx", offset).astype(
                block_rows.dtype
            )
    return total


def layer_backward(gradient, saved, weights, allowed, halo_rows, score_scale):
    (
        query_weight,
        key_weight,
        value_weight,
        out_weight,
        inner_weight,
        outer_weight,
        query_bias,
        value_bias,
        out_bias,
        inner_bias,
        outer_bias,
        first_gain,
        first_shift,
        second_gain,
        second_shift,
    ) = weights
    (
        activation,
        queries,
        extended,
        log_all,
        mixed_low,
        first_pre,
        hidden_low,
        inner_pre,
        active_low,
        second_pre,
    ) = saved
    rows_local = activation.shape[0]
    reach = halo_rows // rows_local
    _, second_pull = jax.vjp(
        normalize, second_pre, second_gain.astype(jnp.float32), second_shift.astype(jnp.float32)
    )
    grad_second, grad_second_gain, grad_second_shift = second_pull(gradient)
    grad_outer = grad_second.astype(jnp.bfloat16)
    grad_outer_weight = product("tf,td->fd", active_low, grad_outer)
    grad_outer_bias = jnp.sum(grad_outer.astype(jnp.float32), axis=0)
    grad_active = product("td,fd->tf", grad_outer, outer_weight)
    _, gelu_pull = jax.vjp(exact_gelu, inner_pre)
    (grad_inner,) = gelu_pull(grad_active)
    grad_inner_low = grad_inner.astype(jnp.bfloat16)
    grad_inner_weight = product("td,tf->df", hidden_low, grad_inner_low)
    grad_inner_bias = jnp.sum(grad_inner_low.astype(jnp.float32), axis=0)
    grad_hidden = grad_second + product("tf,df->td", grad_inner_low, inner_weight)
    _, first_pull = jax.vjp(
        normalize, first_pre, first_gain.astype(jnp.float32), first_shift.astype(jnp.float32)
    )
    grad_first, grad_first_gain, grad_first_shift = first_pull(grad_hidden)
    grad_branch = grad_first.astype(jnp.bfloat16)
    grad_out_weight = product("te,td->ed", mixed_low, grad_branch)
    grad_out_bias = jnp.sum(grad_branch.astype(jnp.float32), axis=0)
    grad_mixed = product("td,ed->te", grad_branch, out_weight).astype(jnp.bfloat16)
    own_rows = extended[:, halo_rows : halo_rows + rows_local]
    key_ext = extend_rows(own_rows, 1, reach, move_keys_back)
    query_sum, key_win, value_win = attend_back(
        queries, key_ext[0], key_ext[1], grad_mixed, log_all, allowed, score_scale
    )
    owned = return_rows(jnp.stack([key_win, value_win]), halo_rows, rows_local)
    key_sum = owned[0]
    value_sum = owned[1]
    grad_query = query_sum.astype(jnp.bfloat16)
    grad_key = key_sum.astype(jnp.bfloat16)
    grad_value = value_sum.astype(jnp.bfloat16)
    grad_query_weight = product("te,td->ed", activation, grad_query)
    grad_key_weight = product("te,td->ed", activation, grad_key)
    grad_value_weight = product("te,td->ed", activation, grad_value)
    grad_query_bias = jnp.sum(grad_query.astype(jnp.float32), axis=0)
    grad_value_bias = jnp.sum(grad_value.astype(jnp.float32), axis=0)
    grad_activation = (
        grad_first
        + product("td,ed->te", grad_query, query_weight)
        + product("td,ed->te", grad_key, key_weight)
        + product("td,ed->te", grad_value, value_weight)
    )
    local_grads = (
        grad_query_weight,
        grad_key_weight,
        grad_value_weight,
        grad_out_weight,
        grad_inner_weight,
        grad_outer_weight,
        grad_query_bias,
        grad_value_bias,
        grad_out_bias,
        grad_inner_bias,
        grad_outer_bias,
        grad_first_gain,
        grad_first_shift,
        grad_second_gain,
        grad_second_shift,
    )
    return (grad_activation, local_grads)


def window_body(
    tokens,
    cotangent,
    doc_starts,
    doc_lengths,
    query_weight,
    key_weight,
    value_weight,
    out_weight,
    inner_weight,
    outer_weight,
    query_bias,
    value_bias,
    out_bias,
    inner_bias,
    outer_bias,
    first_gain,
    first_shift,
    second_gain,
    second_shift,
):
    params = (
        query_weight,
        key_weight,
        value_weight,
        out_weight,
        inner_weight,
        outer_weight,
        query_bias,
        value_bias,
        out_bias,
        inner_bias,
        outer_bias,
        first_gain,
        first_shift,
        second_gain,
        second_shift,
    )
    rows_local = tokens.shape[1]
    ctx_count = lax.axis_size("ctx")
    reach = min(-(-(DOC_CAP - 1) // rows_local), ctx_count - 1)
    halo_rows = reach * rows_local
    window = rows_local + 2 * halo_rows
    row_start = lax.axis_index("ctx") * rows_local
    local_positions = row_start + jnp.arange(rows_local, dtype=jnp.int32)
    window_positions = row_start - halo_rows + jnp.arange(window, dtype=jnp.int32)
    local_labels = doc_labels(local_positions, doc_starts[0], doc_lengths[0])
    window_labels = doc_labels(window_positions, doc_starts[0], doc_lengths[0])
    allowed = (local_labels[:, None] == window_labels[None, :]) & (local_labels[:, None] > 0)
    score_scale = HDIM ** (-0.5)
    activation = tokens[0]
    stashed = []
    outputs = []
    for layer_index in range(LAYERS):
        gathered = fetch_forward(params, layer_index)
        saved, result_rows = layer_forward(activation, gathered, allowed, halo_rows, score_scale)
        stashed.append((saved, gathered))
        outputs.append(result_rows)
        activation = result_rows.astype(jnp.bfloat16)
    gradient = cotangent[0].astype(jnp.float32)
    reduced = [None] * LAYERS
    for layer_index in reversed(range(LAYERS)):
        saved, gathered = stashed[layer_index]
        weights_now = fetch_backward(params, layer_index)
        gradient, local_grads = layer_backward(
            gradient, saved, weights_now, allowed, halo_rows, score_scale
        )
        reduced[layer_index] = reduce_grads(local_grads)
    stacked_grads = [
        jnp.stack([reduced[layer_index][member] for layer_index in range(LAYERS)])
        for member in range(15)
    ]
    heads_out = [
        outputs[0].astype(jnp.bfloat16)[None],
        outputs[LAYERS - 1].astype(jnp.bfloat16)[None],
        gradient.astype(jnp.bfloat16)[None],
    ]
    return tuple(heads_out + stacked_grads)


NN = (((1,), (0,)), ((), ()))
NT = (((1,), (1,)), ((), ()))
TN = (((0,), (0,)), ((), ()))
LANES = 128
QUERY_BLOCK = 256
CORE, ALONG_X, ALONG_Y = 1, 2, 4
SMALL_COST = pl.CostEstimate(flops=1000, bytes_accessed=1000, transcendentals=0)


def lasting(microseconds):
    return pl.CostEstimate(
        flops=int(microseconds * 1.15e9), bytes_accessed=int(microseconds * 3.6e6), transcendentals=0
    )


def mm(left, right, dims=NN):
    return lax.dot_general(left, right, dims, preferred_element_type=jnp.float32)


def swap(block, mask):
    devices = range(lax.axis_size("ctx"))
    return lax.ppermute(block, "ctx", [(i, i ^ mask) for i in devices])


def turn(block, distance):
    count = lax.axis_size("wsh")
    return lax.ppermute(block, "wsh", [(i, (i + distance) % count) for i in range(count)])


def low(values_in):
    return values_in.astype(jnp.bfloat16)


def wide(values_in):
    return values_in.astype(jnp.float32)


def mask_features(label_col):
    rows = label_col.shape[0]
    lane = lax.broadcasted_iota(jnp.int32, (rows, LANES), 1)
    hit = lax.rem(lane, HDIM) == jnp.broadcast_to(label_col, (rows, LANES))
    return (
        jnp.where(hit, neg_fill, 0.0).astype(jnp.bfloat16),
        jnp.where(hit, 0.0, 1.0).astype(jnp.bfloat16),
    )


def fill_key_scratch(key_rows, label_col, key_mask):
    lane = lax.broadcasted_iota(jnp.int32, key_rows.shape, 1)
    _, key_features = mask_features(label_col)
    key_mask[0] = jnp.where(lane < HDIM, key_rows, key_features)
    key_mask[1] = jnp.where(lane < HDIM, key_features, key_rows)


def attention_forward_kernel(
    order_ref, query_ref, key_ref, value_ref, label_ref, query_label_ref, mixed_ref, log_ref, key_mask, value_t
):
    @pl.when(pl.program_id(0) == 0)
    def _():
        fill_key_scratch(key_ref[...], label_ref[...], key_mask)
        value_t[...] = value_ref[...].T

    scaled = low(wide(query_ref[...]) * HDIM ** (-0.5))
    lane = lax.broadcasted_iota(jnp.int32, scaled.shape, 1)
    features, _ = mask_features(query_label_ref[...])
    parts = []
    for head in range(2):
        mine = (lane < HDIM) if head == 0 else (lane >= HDIM)
        scores = mm(key_mask[head], jnp.where(mine, scaled, features), NT)
        peak = jnp.max(scores, axis=0, keepdims=True)
        exponent = jnp.exp(scores - peak)
        total = jnp.sum(exponent, axis=0, keepdims=True)
        mixed = mm(value_t[pl.ds(HDIM * head, HDIM), :], low(exponent))
        parts.append(mixed / total)
        log_ref[pl.ds(head, 1), :] = peak + jnp.log(total)
    mixed_ref[...] = low(jnp.concatenate(parts, axis=0).T)


def attention_forward(packed, labels, order):
    rows = packed.shape[0]
    mine = pl.BlockSpec((QUERY_BLOCK, LANES), lambda i, order_ref: (i, 0))
    return pl.pallas_call(
        attention_forward_kernel,
        grid_spec=pltpu.PrefetchScalarGridSpec(
            num_scalar_prefetch=1,
            grid=(rows // QUERY_BLOCK,),
            in_specs=[
                mine,
                pl.BlockSpec((rows, LANES), lambda i, order_ref: (0, 1)),
                pl.BlockSpec((rows, LANES), lambda i, order_ref: (0, 2)),
                pl.BlockSpec((rows, 1), lambda i, order_ref: (0, 0)),
                pl.BlockSpec((QUERY_BLOCK, 1), lambda i, order_ref: (i, 0)),
            ],
            out_specs=[
                pl.BlockSpec((QUERY_BLOCK, LANES), lambda i, order_ref: (order_ref[i], 0)),
                pl.BlockSpec((2, QUERY_BLOCK), lambda i, order_ref: (0, i)),
            ],
            scratch_shapes=[
                pltpu.VMEM((2, rows, LANES), jnp.bfloat16),
                pltpu.VMEM((LANES, rows), jnp.bfloat16),
            ],
        ),
        out_shape=[
            jax.ShapeDtypeStruct((rows, LANES), jnp.bfloat16),
            jax.ShapeDtypeStruct((2, rows), jnp.float32),
        ],
        cost_estimate=lasting(25),
        name="attention_forward",
    )(order, packed, packed, packed, labels, labels)


def attention_backward_kernel(
    order_ref,
    query_ref,
    key_ref,
    value_ref,
    label_ref,
    query_label_ref,
    grad_ref,
    log_ref,
    out_query_ref,
    out_key_ref,
    out_value_ref,
    key_mask,
    key_t,
    key_sum,
    value_sum,
):
    step = pl.program_id(0)

    @pl.when(step == 0)
    def _():
        fill_key_scratch(key_ref[...], label_ref[...], key_mask)
        key_t[...] = key_ref[...].T
        key_sum[...] = jnp.zeros_like(key_sum)
        value_sum[...] = jnp.zeros_like(value_sum)

    scaled = low(wide(query_ref[...]) * HDIM ** (-0.5))
    grad = grad_ref[...]
    value_rows = value_ref[...]
    lane = lax.broadcasted_iota(jnp.int32, scaled.shape, 1)
    features, _ = mask_features(query_label_ref[...])
    zero = jnp.zeros(scaled.shape, jnp.bfloat16)
    parts = []
    for head in range(2):
        mine = (lane < HDIM) if head == 0 else (lane >= HDIM)
        query_own = jnp.where(mine, scaled, zero)
        grad_own = jnp.where(mine, grad, zero)
        scores = mm(key_mask[head], jnp.where(mine, scaled, features), NT)
        probability = jnp.exp(scores - log_ref[pl.ds(head, 1), :])
        grad_prob = mm(value_rows, grad_own, NT)
        delta = jnp.sum(probability * grad_prob, axis=0, keepdims=True)
        grad_scores = low(probability * (grad_prob - delta))
        key_sum[...] += mm(grad_scores, query_own)
        value_sum[...] += mm(low(probability), grad_own)
        parts.append(mm(key_t[pl.ds(HDIM * head, HDIM), :], grad_scores) * HDIM ** (-0.5))
    out_query_ref[...] = low(jnp.concatenate(parts, axis=0).T)

    @pl.when(step == pl.num_programs(0) - 1)
    def _():
        out_key_ref[...] = low(key_sum[...])
        out_value_ref[...] = low(value_sum[...])


def attention_backward(packed, labels, grad, log_all, order):
    rows = packed.shape[0]
    mine = pl.BlockSpec((QUERY_BLOCK, LANES), lambda i, order_ref: (i, 0))
    whole = pl.BlockSpec((rows, LANES), lambda i, order_ref: (0, 0))
    return pl.pallas_call(
        attention_backward_kernel,
        grid_spec=pltpu.PrefetchScalarGridSpec(
            num_scalar_prefetch=1,
            grid=(rows // QUERY_BLOCK,),
            in_specs=[
                mine,
                pl.BlockSpec((rows, LANES), lambda i, order_ref: (0, 1)),
                pl.BlockSpec((rows, LANES), lambda i, order_ref: (0, 2)),
                pl.BlockSpec((rows, 1), lambda i, order_ref: (0, 0)),
                pl.BlockSpec((QUERY_BLOCK, 1), lambda i, order_ref: (i, 0)),
                pl.BlockSpec((QUERY_BLOCK, LANES), lambda i, order_ref: (order_ref[i], 0)),
                pl.BlockSpec((2, QUERY_BLOCK), lambda i, order_ref: (0, i)),
            ],
            out_specs=[mine, whole, whole],
            scratch_shapes=[
                pltpu.VMEM((2, rows, LANES), jnp.bfloat16),
                pltpu.VMEM((LANES, rows), jnp.bfloat16),
                pltpu.VMEM((rows, LANES), jnp.float32),
                pltpu.VMEM((rows, LANES), jnp.float32),
            ],
        ),
        out_shape=[jax.ShapeDtypeStruct((rows, LANES), jnp.bfloat16)] * 3,
        cost_estimate=lasting(33),
        name="attention_backward",
    )(order, packed, packed, packed, labels, labels, grad, log_all)


def own_pieces(inner_weight, outer_weight, out_weight, joint_weights, small_params, here, first_block):
    layers, shard, hidden = inner_weight.shape
    piece = hidden // 8
    width = 3 * LANES

    def kernel(place_ref, inner_ref, outer_ref, out_ref, query_ref, key_ref, value_ref, *refs):
        small_refs, (first_ref, second_ref, joint_ref) = refs[:-3], refs[-3:]
        first_ref[0, :, :piece] = low(inner_ref[0])
        first_ref[0, :, piece:] = low(out_ref[0])
        second_ref[0] = low(outer_ref[0]).T
        for at, ref in enumerate((query_ref, key_ref, value_ref)):
            joint_ref[0, :shard, at * LANES : (at + 1) * LANES] = low(ref[0])
        rows = [jnp.concatenate([ref[...] for ref in small_refs[:8]], axis=0)]
        rows += [small_refs[8][:, q * shard : (q + 1) * shard] for q in range(4)]
        rows += [jnp.zeros((8, shard), jnp.float32)]
        packed = low(jnp.concatenate(rows, axis=0))
        joint_ref[0, shard:] = jnp.concatenate([packed, jnp.zeros((32, width - shard), jnp.bfloat16)], axis=1)

    column = pl.BlockSpec((1, shard, LANES), lambda layer, place_ref: (layer, 0, place_ref[0]))
    return pl.pallas_call(
        kernel,
        grid_spec=pltpu.PrefetchScalarGridSpec(
            num_scalar_prefetch=1,
            grid=(layers,),
            in_specs=[
                pl.BlockSpec((1, shard, piece), lambda layer, place_ref: (layer, 0, place_ref[1])),
                pl.BlockSpec((1, piece, shard), lambda layer, place_ref: (layer, place_ref[1], 0)),
                column,
                column,
                column,
                column,
            ]
            + [pl.BlockSpec(param.shape, lambda layer, place_ref: (0, 0)) for param in small_params],
            out_specs=[
                pl.BlockSpec((1, shard, piece + LANES), lambda layer, place_ref: (layer, 0, 0)),
                pl.BlockSpec((1, shard, piece), lambda layer, place_ref: (layer, 0, 0)),
                pl.BlockSpec((1, shard + 32, width), lambda layer, place_ref: (layer, 0, 0)),
            ],
        ),
        out_shape=[
            jax.ShapeDtypeStruct((layers, shard, piece + LANES), jnp.bfloat16),
            jax.ShapeDtypeStruct((layers, shard, piece), jnp.bfloat16),
            jax.ShapeDtypeStruct((layers, shard + 32, width), jnp.bfloat16),
        ],
        cost_estimate=lasting(4),
        name="own_pieces",
    )(
        jnp.stack([here, first_block]).astype(jnp.int32),
        inner_weight,
        outer_weight,
        out_weight,
        *joint_weights,
        *small_params,
    )


def own_blocks(inner_weight, outer_weight, out_weight, inner_order, out_order, after):
    layers, shard, hidden = inner_weight.shape
    piece = hidden // 8

    def kernel(inner_order_ref, out_order_ref, *refs):
        ins, (inner_out, outer_out, out_out) = refs[:16], refs[-3:]
        for j in range(4):
            inner_out[0, j] = low(ins[j][0])
            outer_out[0, j] = low(ins[4 + j][0]).T
        for j in range(8):
            out_out[0, :, j * LANES : (j + 1) * LANES] = low(ins[8 + j][0])

    def inner_at(j):
        return pl.BlockSpec((1, shard, piece), lambda layer, inner_ref, out_ref: (layer, 0, inner_ref[layer * 4 + j]))

    def outer_at(j):
        return pl.BlockSpec((1, piece, shard), lambda layer, inner_ref, out_ref: (layer, inner_ref[layer * 4 + j], 0))

    def out_at(j):
        return pl.BlockSpec((1, shard, LANES), lambda layer, inner_ref, out_ref: (layer, 0, out_ref[layer * 8 + j]))

    block = pl.BlockSpec((1, 4, shard, piece), lambda layer, *_: (layer, 0, 0, 0))
    return pl.pallas_call(
        kernel,
        grid_spec=pltpu.PrefetchScalarGridSpec(
            num_scalar_prefetch=2,
            grid=(layers,),
            in_specs=[inner_at(j) for j in range(4)]
            + [outer_at(j) for j in range(4)]
            + [out_at(j) for j in range(8)]
            + [pl.BlockSpec(memory_space=pl.ANY)],
            out_specs=[block, block, pl.BlockSpec((1, shard, 8 * LANES), lambda layer, *_: (layer, 0, 0))],
        ),
        out_shape=[
            jax.ShapeDtypeStruct((layers, 4, shard, piece), jnp.bfloat16),
            jax.ShapeDtypeStruct((layers, 4, shard, piece), jnp.bfloat16),
            jax.ShapeDtypeStruct((layers, shard, 8 * LANES), jnp.bfloat16),
        ],
        cost_estimate=lasting(7),
        name="own_blocks",
    )(inner_order, out_order, *[inner_weight] * 4, *[outer_weight] * 4, *[out_weight] * 8, after)


def place_pieces(pieces, order, layer, previous):
    count, shard, columns = pieces.shape
    piece = (columns - 4 * LANES) // 2
    width = 8 * LANES

    def column(index, order_ref):
        return (layer, 0, order_ref[index])

    def inner_place(index, order_ref):
        return (order_ref[index] % 2) * 4 + order_ref[index] // 2

    square = jax.ShapeDtypeStruct((LAYERS, shard, width), jnp.float32)
    outs = [square] * 4 + [
        jax.ShapeDtypeStruct((LAYERS, shard, 8 * piece), jnp.float32),
        jax.ShapeDtypeStruct((LAYERS, 8 * piece, shard), jnp.float32),
        jax.ShapeDtypeStruct((8, LANES), jnp.float32),
    ]
    specs = [pl.BlockSpec((1, shard, LANES), column)] * 4 + [
        pl.BlockSpec((1, shard, piece), lambda i, order_ref: (layer, 0, inner_place(i, order_ref))),
        pl.BlockSpec((1, piece, shard), lambda i, order_ref: (layer, inner_place(i, order_ref), 0)),
        pl.BlockSpec((8, LANES), lambda i, order_ref: (0, 0)),
    ]

    def kernel(order_ref, source, *refs):
        query_out, key_out, value_out, out_out, inner_out, outer_out, token_out = refs[-7:]
        token_out[...] = jnp.zeros_like(token_out)
        inner_out[0] = wide(source[0, :, :piece])
        outer_out[0] = wide(source[0, :, piece : 2 * piece].T)
        for at, ref in enumerate((out_out, query_out, key_out, value_out)):
            begin = 2 * piece + at * LANES
            ref[0] = wide(source[0, :, begin : begin + LANES])

    held = [] if previous is None else list(previous)
    return pl.pallas_call(
        kernel,
        grid_spec=pltpu.PrefetchScalarGridSpec(
            num_scalar_prefetch=1,
            grid=(count,),
            in_specs=[pl.BlockSpec((1, shard, columns), lambda i, order_ref: (i, 0, 0))]
            + [pl.BlockSpec(memory_space=pl.ANY)] * len(held),
            out_specs=specs,
        ),
        out_shape=outs,
        input_output_aliases={2 + i: i for i in range(len(held))},
        cost_estimate=lasting(count * 5 // 4),
        name="place_pieces",
    )(order, pieces, *held)


def half_erfc(values_in):
    scaled = values_in * (2.0**-0.5)
    part = 1.0 / (1.0 + 0.5 * scaled)
    series = 0.17087277
    for coefficient in (
        -0.82215223,
        1.48851587,
        -1.13520398,
        0.27886807,
        -0.18628806,
        0.09678418,
        0.37409196,
        1.00002368,
        -1.26551223,
    ):
        series = coefficient + part * series
    return 0.5 * part * jnp.exp(series - scaled * scaled)


def load_weights(step, own_inner, own_outer, inner_refs, outer_refs, inner_now, outer_now):
    shard = own_inner.shape[2]
    inner_now[:shard] = own_inner[0, 0]
    outer_now[:shard] = own_outer[0, 0]
    if len(inner_refs) == 1:
        inner_now[shard:] = inner_refs[0][0]
        outer_now[shard:] = outer_refs[0][0]
        return
    chunks = len(inner_refs) // 4
    rows = inner_refs[0].shape[0]
    for j in range(4):

        @pl.when(step == j)
        def _(j=j):
            for chunk in range(chunks):
                begin = shard + chunk * rows
                inner_now[begin : begin + rows] = inner_refs[j * chunks + chunk][...]
                outer_now[begin : begin + rows] = outer_refs[j * chunks + chunk][...]


def weight_operands(weights, layer):
    own_inner, own_outer, inner_parts, outer_parts = weights
    shard, piece = own_inner.shape[2:]
    own = pl.BlockSpec((1, 1, shard, piece), lambda i: (layer, i, 0, 0))
    if len(inner_parts) == 1:
        rest = inner_parts[0].shape[1]
        part = pl.BlockSpec((1, rest, piece), lambda i: (i, 0, 0))
        return ([own_inner, own_outer, *inner_parts, *outer_parts], [own, own, part, part], 1)
    rows = inner_parts[0].shape[0]
    fixed = pl.BlockSpec((rows, piece), lambda i: (0, 0), pipeline_mode=pl.Buffered(1))
    return (
        [own_inner, own_outer, *inner_parts, *outer_parts],
        [own, own] + [fixed] * (2 * len(inner_parts)),
        len(inner_parts),
    )


def accumulate(step, total, part):
    @pl.when(step == 0)
    def _():
        total[...] = part

    @pl.when(step > 0)
    def _():
        total[...] += part


def finish_pair(step, total, near_ref, far_ref):
    rows = near_ref.shape[0]

    @pl.when(step == pl.num_programs(0) - 1)
    def _():
        near_ref[...] = total[:rows]
        far_ref[...] = low(total[rows:])


def feed_forward_kernel(count, hidden_ref, bias_ref, own_inner, own_outer, *refs):
    inner_refs, outer_refs = refs[:count], refs[count : 2 * count]
    near_ref, far_ref, active_ref, slope_ref, total, inner_now, outer_now = refs[2 * count :]
    step = pl.program_id(0)
    load_weights(step, own_inner, own_outer, inner_refs, outer_refs, inner_now, outer_now)
    pre = mm(hidden_ref[...], inner_now[...]) + bias_ref[...]
    tail = half_erfc(jnp.abs(pre))
    below = jnp.where(pre < 0.0, tail, 1.0 - tail)
    active = low(pre * below)
    active_ref[...] = active
    slope_ref[...] = low(below + pre * (jnp.exp(-0.5 * pre * pre) * 0.3989422804014327))
    accumulate(step, total, mm(active, outer_now[...], NT))
    finish_pair(step, total, near_ref, far_ref)


def feed_forward(hidden_pair, bias_row, weights, layer):
    rows, width = hidden_pair.shape
    hidden = bias_row.shape[1]
    block = hidden // 4
    arrays, specs, count = weight_operands(weights, layer)
    column = pl.BlockSpec((rows, block), lambda i: (0, i))
    half = pl.BlockSpec((rows // 2, width), lambda i: (0, 0))
    return pl.pallas_call(
        functools.partial(feed_forward_kernel, count),
        grid=(4,),
        in_specs=[
            pl.BlockSpec((rows, width), lambda i: (0, 0)),
            pl.BlockSpec((1, block), lambda i: (0, i)),
            *specs,
        ],
        out_specs=[half, half, column, column],
        out_shape=[
            jax.ShapeDtypeStruct((rows // 2, width), jnp.float32),
            jax.ShapeDtypeStruct((rows // 2, width), jnp.bfloat16),
            jax.ShapeDtypeStruct((rows, hidden), jnp.bfloat16),
            jax.ShapeDtypeStruct((rows, hidden), jnp.bfloat16),
        ],
        scratch_shapes=[
            pltpu.VMEM((rows, width), jnp.float32),
            pltpu.VMEM((width, block), jnp.bfloat16),
            pltpu.VMEM((width, block), jnp.bfloat16),
        ],
        cost_estimate=lasting(16),
        name="feed_forward",
    )(hidden_pair, bias_row, *arrays)


def feed_backward_kernel(count, grad_ref, slope_ref, own_inner, own_outer, *refs):
    inner_refs, outer_refs = refs[:count], refs[count : 2 * count]
    near_ref, far_ref, inner_grad_ref, bias_ref, total, inner_now, outer_now = refs[2 * count :]
    step = pl.program_id(0)
    load_weights(step, own_inner, own_outer, inner_refs, outer_refs, inner_now, outer_now)
    inner_grad = low(mm(grad_ref[...], outer_now[...]) * wide(slope_ref[...]))
    inner_grad_ref[...] = inner_grad
    bias_ref[...] = jnp.sum(wide(inner_grad), axis=0, keepdims=True)
    accumulate(step, total, mm(inner_grad, inner_now[...], NT))
    finish_pair(step, total, near_ref, far_ref)


def feed_backward(grad_pair, slope, weights, layer):
    rows, width = grad_pair.shape
    hidden = slope.shape[1]
    block = hidden // 4
    arrays, specs, count = weight_operands(weights, layer)
    column = pl.BlockSpec((rows, block), lambda i: (0, i))
    half = pl.BlockSpec((rows // 2, width), lambda i: (0, 0))
    return pl.pallas_call(
        functools.partial(feed_backward_kernel, count),
        grid=(4,),
        in_specs=[pl.BlockSpec((rows, width), lambda i: (0, 0)), column, *specs],
        out_specs=[half, half, column, pl.BlockSpec((1, block), lambda i: (0, i))],
        out_shape=[
            jax.ShapeDtypeStruct((rows // 2, width), jnp.float32),
            jax.ShapeDtypeStruct((rows // 2, width), jnp.bfloat16),
            jax.ShapeDtypeStruct((rows, hidden), jnp.bfloat16),
            jax.ShapeDtypeStruct((1, hidden), jnp.float32),
        ],
        scratch_shapes=[
            pltpu.VMEM((rows, width), jnp.float32),
            pltpu.VMEM((width, block), jnp.bfloat16),
            pltpu.VMEM((width, block), jnp.bfloat16),
        ],
        cost_estimate=lasting(11),
        name="feed_backward",
    )(grad_pair, slope, *arrays)


def weight_gradient_kernel(
    split,
    rows_ref,
    hidden_ref,
    grad_ref,
    mixed_ref,
    inner_grad_ref,
    active_ref,
    branch_ref,
    after_ref,
    *refs,
):
    outs, (hidden_t, grad_t, mixed_t) = refs[:-3], refs[-3:]
    step = pl.program_id(0)
    piece = active_ref.shape[1]

    @pl.when(step == 0)
    def _():
        hidden_t[...] = hidden_ref[...].T
        grad_t[...] = grad_ref[...].T
        mixed_t[...] = mixed_ref[...].T

    def write(store):
        store(0, piece, low(mm(hidden_t[...], inner_grad_ref[...])))
        store(piece, 2 * piece, low(mm(grad_t[...], active_ref[...])))
        store(2 * piece, 2 * piece + LANES, low(mm(mixed_t[...], branch_ref[...])))

    if not split:
        first_out, second_out = outs

        def store(begin, end, value):
            shard = value.shape[0] // 4
            ref = second_out if begin == piece else first_out
            column = {0: 0, piece: 0, 2 * piece: piece}[begin]
            for r in range(4):
                place = pl.multiple_of(rows_ref[r] * shard, shard)
                ref[0, pl.ds(place, shard), column : column + end - begin] = value[r * shard : (r + 1) * shard]

        write(store)
        return
    first_keep, first_send, second_keep, second_send = outs
    for j in range(4):

        @pl.when(step == j)
        def _(j=j):
            first = (first_send if j % 2 else first_keep, j // 2)
            second = (second_send if j // 2 else second_keep, j % 2)

            def store(begin, end, value):
                half = value.shape[0] // 2
                first[0][first[1], :, begin:end] = value[:half]
                second[0][second[1], :, begin:end] = value[half:]

            write(store)


def weight_gradients(hidden_pair, grad_pair, mixed_pair, inner_grad, active, branch_pair, plane_rows, split, after):
    rows, width = hidden_pair.shape
    hidden = active.shape[1]
    piece = hidden // 4
    total = 2 * piece + LANES
    whole = pl.BlockSpec((rows, width), lambda i, rows_ref: (0, 0))
    column = pl.BlockSpec((rows, piece), lambda i, rows_ref: (0, i))
    if split:
        shape = (2, width // 2, total)
        out_specs = [pl.BlockSpec(shape, lambda i, rows_ref: (0, 0, 0), pipeline_mode=pl.Buffered(1))] * 4
        out_shape = [jax.ShapeDtypeStruct(shape, jnp.bfloat16)] * 4
    else:
        out_specs = [
            pl.BlockSpec((1, width, columns), lambda i, rows_ref: (i, 0, 0)) for columns in (piece + LANES, piece)
        ]
        out_shape = [jax.ShapeDtypeStruct((4, width, columns), jnp.bfloat16) for columns in (piece + LANES, piece)]
    return pl.pallas_call(
        functools.partial(weight_gradient_kernel, split),
        grid_spec=pltpu.PrefetchScalarGridSpec(
            num_scalar_prefetch=1,
            grid=(4,),
            in_specs=[
                whole,
                whole,
                whole,
                column,
                column,
                pl.BlockSpec((rows, LANES), lambda i, rows_ref: (0, i)),
                pl.BlockSpec(memory_space=pl.ANY),
            ],
            out_specs=out_specs,
            scratch_shapes=[pltpu.VMEM((width, rows), jnp.bfloat16)] * 3,
        ),
        out_shape=out_shape,
        cost_estimate=lasting(13),
        name="weight_gradients",
    )(plane_rows, hidden_pair, grad_pair, mixed_pair, inner_grad, active, branch_pair, after)


def block_columns(values_in, order, width):
    return jnp.concatenate(
        [lax.dynamic_slice_in_dim(values_in, block * width, width, 1) for block in order], axis=1
    )


def norm_forward(values_in, gain_row, shift_row):
    centre = values_in - jnp.mean(values_in, axis=-1, keepdims=True)
    spread = jnp.mean(centre * centre, axis=-1, keepdims=True)
    inverse = lax.rsqrt(spread + epsilon)
    unit = centre * inverse
    return (unit * gain_row + shift_row, unit, inverse)


def norm_backward(grad, unit, inverse, gain_row):
    grad_unit = grad * gain_row
    back = inverse * (
        grad_unit
        - jnp.mean(grad_unit, axis=-1, keepdims=True)
        - unit * jnp.mean(grad_unit * unit, axis=-1, keepdims=True)
    )
    return (back, jnp.sum(grad * unit, axis=0), jnp.sum(grad, axis=0))


def attention_output_kernel(
    place_ref,
    heads_ref,
    own_ref,
    near_ref,
    far_ref,
    activation_ref,
    bias_ref,
    gain_ref,
    shift_ref,
    mixed_ref,
    unit_ref,
    inverse_ref,
    hidden_ref,
    turned_ref,
    held,
    held_low,
):
    shard = own_ref.shape[0]
    half = near_ref.shape[1]
    for p in range(8):
        mixed_ref[:, p * LANES : (p + 1) * LANES] = heads_ref[place_ref[p]]
    own, rest = mixed_ref[:, :shard], mixed_ref[:, shard:]
    held[:, :half] = mm(own, own_ref[:, :half]) + mm(rest, near_ref[...])
    held[:, half:] = mm(own, own_ref[:, half:]) + mm(rest, far_ref[...])
    attended = jnp.concatenate(
        [held[:, pl.ds(pl.multiple_of(place_ref[8 + b] * LANES, LANES), LANES)] for b in range(8)], axis=1
    )
    first_pre = wide(activation_ref[...]) + (attended + bias_ref[...])
    hidden, unit, inverse = norm_forward(first_pre, gain_ref[...], shift_ref[...])
    unit_ref[...] = unit
    inverse_ref[...] = inverse
    hidden_ref[...] = hidden
    held_low[...] = low(hidden)
    for r in range(4):
        turned_ref[:, r * shard : (r + 1) * shard] = held_low[
            :, pl.ds(pl.multiple_of(place_ref[16 + r] * shard, shard), shard)
        ]


def attention_output(heads, out_weights, activation, bias_row, gain_row, shift_row, places):
    rows, width = activation.shape
    wide_rows = jax.ShapeDtypeStruct((rows, width), jnp.float32)
    low_rows = jax.ShapeDtypeStruct((rows, width), jnp.bfloat16)
    return pl.pallas_call(
        attention_output_kernel,
        grid_spec=pltpu.PrefetchScalarGridSpec(
            num_scalar_prefetch=1,
            grid=(1,),
            in_specs=[
                pl.BlockSpec(array.shape, lambda i, place_ref, rank=array.ndim: (0,) * rank)
                for array in (heads, *out_weights, activation, bias_row, gain_row, shift_row)
            ],
            out_specs=[
                pl.BlockSpec((rows, width), lambda i, place_ref: (0, 0)),
                pl.BlockSpec((rows, width), lambda i, place_ref: (0, 0)),
                pl.BlockSpec((rows, 1), lambda i, place_ref: (0, 0)),
                pl.BlockSpec((rows, width), lambda i, place_ref: (0, 0)),
                pl.BlockSpec((rows, width), lambda i, place_ref: (0, 0)),
            ],
            scratch_shapes=[pltpu.VMEM((rows, width), jnp.float32), pltpu.VMEM((rows, width), jnp.bfloat16)],
        ),
        out_shape=[low_rows, wide_rows, jax.ShapeDtypeStruct((rows, 1), jnp.float32), wide_rows, low_rows],
        cost_estimate=lasting(5),
        name="attention_output",
    )(places, heads, *out_weights, activation, bias_row, gain_row, shift_row)


def attention_output_back_kernel(
    place_ref,
    near_back_ref,
    came_ref,
    grad_ref,
    unit_ref,
    inverse_ref,
    gain_ref,
    own_ref,
    near_ref,
    far_ref,
    first_ref,
    rows_ref,
    spread_ref,
    sent_ref,
    held,
    held_low,
):
    shard = own_ref.shape[0]
    half = near_ref.shape[1]
    held[...] = near_back_ref[...] + wide(came_ref[...])
    back = jnp.concatenate(
        [held[:, pl.ds(pl.multiple_of(place_ref[16 + r] * shard, shard), shard)] for r in range(4)], axis=1
    )
    grad_first, gain_row, shift_row = norm_backward(
        grad_ref[...] + back, unit_ref[...], inverse_ref[...], gain_ref[...]
    )
    first_ref[...] = grad_first
    branch = low(grad_first)
    rows_ref[0:1] = gain_row[None]
    rows_ref[1:2] = shift_row[None]
    rows_ref[2:3] = jnp.sum(wide(branch), axis=0, keepdims=True)
    held_low[...] = branch
    for p in range(8):
        spread_ref[:, p * LANES : (p + 1) * LANES] = held_low[
            :, pl.ds(pl.multiple_of(place_ref[24 + p] * LANES, LANES), LANES)
        ]
    spread = spread_ref[...]
    held_low[:, :shard] = low(mm(spread, own_ref[...], NT))
    held_low[:, shard:] = low(mm(spread[:, :half], near_ref[...], NT) + mm(spread[:, half:], far_ref[...], NT))
    for head in range(8):
        begin = place_ref[16 + head // 2] * shard + (head % 2) * LANES
        sent_ref[head] = held_low[:, pl.ds(pl.multiple_of(begin, LANES), LANES)]


def attention_output_back(near_back, came, grad_second, unit, inverse, gain_row, out_weights, places):
    rows, width = grad_second.shape
    operands = (near_back, came, grad_second, unit, inverse, gain_row, *out_weights)
    whole = pl.BlockSpec((rows, width), lambda i, place_ref: (0, 0))
    return pl.pallas_call(
        attention_output_back_kernel,
        grid_spec=pltpu.PrefetchScalarGridSpec(
            num_scalar_prefetch=1,
            grid=(1,),
            in_specs=[pl.BlockSpec(array.shape, lambda i, place_ref: (0, 0)) for array in operands],
            out_specs=[
                whole,
                pl.BlockSpec((3, width), lambda i, place_ref: (0, 0)),
                whole,
                pl.BlockSpec((8, rows, LANES), lambda i, place_ref: (0, 0, 0)),
            ],
            scratch_shapes=[pltpu.VMEM((rows, width), jnp.float32), pltpu.VMEM((rows, width), jnp.bfloat16)],
        ),
        out_shape=[
            jax.ShapeDtypeStruct((rows, width), jnp.float32),
            jax.ShapeDtypeStruct((3, width), jnp.float32),
            jax.ShapeDtypeStruct((rows, width), jnp.bfloat16),
            jax.ShapeDtypeStruct((8, rows, LANES), jnp.bfloat16),
        ],
        cost_estimate=lasting(6),
        name="attention_output_back",
    )(places, *operands)


def token_gradient_kernel(
    place_ref, query_ref, key_ref, value_ref, joint_ref, *refs
):
    near_ref, far_ref, packed_ref, bias_ref = refs[-4:]
    step = pl.program_id(0)
    packed = jnp.concatenate([query_ref[...], key_ref[...], value_ref[...]], axis=1)
    packed_ref[...] = packed
    accumulate(step, bias_ref, jnp.sum(wide(packed), axis=0, keepdims=True))
    part = mm(packed, joint_ref[...], NT)

    @pl.when(step < 4)
    def _():
        near_ref[0] = part

    @pl.when(step >= 4)
    def _():
        far_ref[0] = low(part)


def token_gradients(grads, joint, chips):
    tokens = grads[0].shape[0]
    rows = tokens // 8
    width, columns = joint.shape
    block = pl.BlockSpec((rows, LANES), lambda i, place_ref: (i, 0))
    return pl.pallas_call(
        token_gradient_kernel,
        grid_spec=pltpu.PrefetchScalarGridSpec(
            num_scalar_prefetch=1,
            grid=(8,),
            in_specs=[block, block, block, pl.BlockSpec((width, columns), lambda i, place_ref: (0, 0))],
            out_specs=[
                pl.BlockSpec((1, rows, width), lambda i, place_ref: (place_ref[jnp.minimum(i, 3)], 0, 0)),
                pl.BlockSpec((1, rows, width), lambda i, place_ref: (place_ref[jnp.maximum(i - 4, 0)], 0, 0)),
                pl.BlockSpec((rows, columns), lambda i, place_ref: (i, 0)),
                pl.BlockSpec((1, columns), lambda i, place_ref: (0, 0)),
            ],
        ),
        out_shape=[
            jax.ShapeDtypeStruct((4, rows, width), jnp.float32),
            jax.ShapeDtypeStruct((4, rows, width), jnp.bfloat16),
            jax.ShapeDtypeStruct((tokens, columns), jnp.bfloat16),
            jax.ShapeDtypeStruct((1, columns), jnp.float32),
        ],
        cost_estimate=lasting(10),
        name="token_gradients",
    )(chips, *grads, joint)


def plane_sum_kernel(first_keep, first_came, first_last, second_keep, second_came, second_last, *outs):
    shard = outs[0].shape[0]
    first = wide(first_keep[0]) + wide(first_came[0]) + wide(first_last[...])
    second = wide(second_keep[0]) + wide(second_came[0]) + wide(second_last[...])
    outs[0][...] = first[:shard]
    outs[1][...] = low(first[shard:])
    outs[2][...] = low(second[:shard])
    outs[3][...] = low(second[shard:])


def plane_sum(first, second):
    columns = first[0].shape[2]
    shard = first[0].shape[1] // 2
    block = pl.BlockSpec((1, 2 * shard, columns), lambda i: (0, 0, 0))
    last = pl.BlockSpec((2 * shard, columns), lambda i: (0, 0))
    return pl.pallas_call(
        plane_sum_kernel,
        grid=(1,),
        in_specs=[block, block, last] * 2,
        out_specs=[pl.BlockSpec((shard, columns), lambda i: (0, 0))] * 4,
        out_shape=[jax.ShapeDtypeStruct((shard, columns), jnp.float32)]
        + [jax.ShapeDtypeStruct((shard, columns), jnp.bfloat16)] * 3,
        cost_estimate=lasting(3),
        name="plane_sum",
    )(*first, *second)


def final_sum_kernel(*refs):
    left_ref, right_ref = refs[-2:]
    half = left_ref.shape[1]
    whole = jnp.concatenate(
        [
            low(wide(refs[at][...]) + wide(refs[at + 1][...]) + wide(refs[at + 2][...]) + wide(refs[at + 3][...]))
            for at in (0, 4)
        ],
        axis=1,
    )
    left_ref[...] = whole[:, :half]
    right_ref[...] = whole[:, half:]


def final_sum(plain, joint):
    shard = plain[0].shape[0]
    half = (plain[0].shape[1] + joint[0].shape[1]) // 2
    operands = (*plain, *joint)
    return pl.pallas_call(
        final_sum_kernel,
        grid=(1,),
        in_specs=[pl.BlockSpec(array.shape, lambda i: (0, 0)) for array in operands],
        out_specs=[pl.BlockSpec((shard, half), lambda i: (0, 0))] * 2,
        out_shape=[jax.ShapeDtypeStruct((shard, half), jnp.bfloat16)] * 2,
        cost_estimate=lasting(3),
        name="final_sum",
    )(*operands)


def small_rows_kernel(place_ref, joint_ref, first_ref, outer_ref, gain_ref, shift_ref, inner_ref, out_ref):
    shard = out_ref.shape[1] // 4
    out_ref[...] = jnp.zeros_like(out_ref)
    at = pl.ds(pl.multiple_of(place_ref[0] * LANES, LANES), LANES)
    out_ref[0:1, at] = joint_ref[:, :LANES]
    out_ref[1:2, at] = joint_ref[:, 2 * LANES :]
    out_ref[2:3] = first_ref[2:3]
    out_ref[3:4] = outer_ref[...]
    out_ref[4:6] = first_ref[0:2]
    out_ref[6:7] = gain_ref[...]
    out_ref[7:8] = shift_ref[...]
    count = inner_ref.shape[1] // shard // 4
    for j in range(4):
        block = place_ref[1 + j]
        columns = pl.ds(pl.multiple_of((block // 2) * shard, shard), shard)
        for part in range(count):
            begin = (j * count + part) * shard
            row = 8 + (block % 2) * count + part
            out_ref[pl.ds(row, 1), columns] = inner_ref[:, begin : begin + shard]


def small_rows(places, joint, first, outer, gain, shift, inner):
    width = first.shape[1]
    operands = (joint, first, outer[None], gain[None], shift[None], inner)
    return pl.pallas_call(
        small_rows_kernel,
        grid_spec=pltpu.PrefetchScalarGridSpec(
            num_scalar_prefetch=1,
            grid=(1,),
            in_specs=[pl.BlockSpec(array.shape, lambda i, place_ref: (0, 0)) for array in operands],
            out_specs=pl.BlockSpec((16, width), lambda i, place_ref: (0, 0)),
        ),
        out_shape=jax.ShapeDtypeStruct((16, width), jnp.float32),
        cost_estimate=lasting(2),
        name="small_rows",
    )(places, *operands)


def gate(values_in, *points):
    anywhere = pl.BlockSpec(memory_space=pl.ANY)
    return pl.pallas_call(
        lambda *refs: None,
        in_specs=[anywhere] * (len(values_in) + len(points)),
        out_specs=[anywhere] * len(values_in),
        out_shape=[jax.ShapeDtypeStruct(value.shape, value.dtype) for value in values_in],
        input_output_aliases={i: i for i in range(len(values_in))},
        cost_estimate=SMALL_COST,
        name="gate",
    )(*values_in, *points)


def spread_tokens(rows_in):
    half = rows_in.shape[1] // 2
    left, right = rows_in[:, :half], rows_in[:, half:]
    left_pair = jnp.stack([left, swap(left, ALONG_X)])
    right_pair = jnp.stack([right, swap(right, ALONG_Y)])
    left_far = swap(left_pair, ALONG_Y)
    right_far = swap(right_pair, ALONG_X)
    left_all = jnp.concatenate([left_pair, left_far])
    right_all = jnp.stack([right_pair[0], right_far[0], right_pair[1], right_far[1]])
    near = jnp.concatenate([left_all, right_all], axis=2).reshape(4 * rows_in.shape[0], rows_in.shape[1])
    return (near, swap(near, CORE))


def plane_groups():
    count = lax.axis_size("ctx")
    return [list(range(0, count, 2)), list(range(1, count, 2))]


def collect_tokens(sent, points, late_points):
    if points:
        (sent,) = gate([sent], *points)
    came = lax.all_to_all(sent, "ctx", 0, 0, axis_index_groups=plane_groups(), tiled=True)
    if late_points:
        (came,) = gate([came], *late_points)
    return jnp.sum(wide(came), axis=0)


def plane_pieces(left, right, *points):
    left_pair = jnp.stack([left, swap(left, ALONG_X)])
    right_pair = jnp.stack([right, swap(right, ALONG_Y)])
    left_far, right_far = gate([swap(left_pair, ALONG_Y), swap(right_pair, ALONG_X)], *points)
    left_all = jnp.concatenate([left_pair, left_far])
    right_all = jnp.stack([right_pair[0], right_far[0], right_pair[1], right_far[1]])
    near = jnp.concatenate([left_all, right_all], axis=2)
    return (near, swap(near, CORE))


def exchange(blocks):
    return lax.all_to_all(blocks, "ctx", 0, 0, tiled=True)


def head_split_body(
    tokens,
    cotangent,
    doc_starts,
    doc_lengths,
    query_weight,
    key_weight,
    value_weight,
    out_weight,
    inner_weight,
    outer_weight,
    query_bias,
    value_bias,
    out_bias,
    inner_bias,
    outer_bias,
    first_gain,
    first_shift,
    second_gain,
    second_shift,
):
    rows = tokens.shape[1]
    width = tokens.shape[2]
    here = lax.axis_index("ctx")
    plane = lax.axis_index("wsh")
    planes = lax.axis_size("wsh")
    shard = width // planes
    hidden = inner_weight.shape[2]
    piece = hidden // 8
    core = here % 2
    chip = here // 2
    relative = jnp.arange(8, dtype=jnp.int32)
    spread = jnp.array((0, 2, 4, 6, 1, 3, 5, 7), jnp.int32)
    turned = [(plane - r) % planes for r in range(planes)]
    unturned = turned
    positions = ((here ^ spread)[:, None] * rows + jnp.arange(rows, dtype=jnp.int32)).reshape(-1)
    labels = doc_labels(positions, doc_starts[0], doc_lengths[0])[:, None]

    four = jnp.arange(4, dtype=jnp.int32)
    chip_order = [chip ^ four, four]
    inner_order = [core * 4 + order for order in chip_order]
    out_order = [jnp.concatenate([2 * order + core, 2 * order + 1 - core]) for order in chip_order]
    block_order = here ^ spread
    plane_rows = jnp.stack(turned).astype(jnp.int32)
    first_own, second_own, joint_own = own_pieces(
        inner_weight,
        outer_weight,
        out_weight,
        (query_weight, key_weight, value_weight),
        (
            query_bias,
            value_bias,
            out_bias,
            outer_bias,
            first_gain,
            first_shift,
            second_gain,
            second_shift,
            inner_bias,
        ),
        here,
        core * 4 + chip,
    )
    joint_width = 3 * LANES

    def ordered(stack, order):
        return jnp.concatenate([lax.dynamic_index_in_dim(stack, i, 0, keepdims=False) for i in order], axis=0)

    first_joint = joint_own[0]
    joint_turned = jnp.stack([first_joint] + [turn(first_joint, r) for r in range(1, planes)])
    joint_first = ordered(joint_turned[:, :shard], unturned)
    small_all = ordered(joint_turned[:, None, shard:, :shard], unturned)

    def small(layer, index):
        return small_all[:, 2 * index + layer].reshape(width)

    inner_bias_all = small_all[:, 16:24].reshape(planes, 4, LAYERS, shard).transpose(2, 0, 1, 3).reshape(LAYERS, hidden)

    inner_near = ordered(lax.all_gather(first_own[0], "wsh", axis=0), turned[1:])
    first_tokens = spread_tokens(tokens[0])
    (outer_sent,) = gate([second_own[0]], first_tokens[0])
    outer_stack = lax.all_gather(outer_sent, "wsh", axis=0)
    middle = 3 * shard // 2

    def spread_first(near):
        left, right = near[:middle], near[middle:]
        return (left, right, swap(left, ALONG_X), swap(right, ALONG_Y))

    def spread_second(left, right, left_x, right_y):
        lefts = (left, left_x, swap(left, ALONG_Y), swap(left_x, ALONG_Y))
        rights = (right, swap(right, ALONG_X), right_y, swap(right_y, ALONG_X))
        return [part for pair in zip(lefts, rights) for part in pair]

    inner_half = spread_first(inner_near)
    layer_own = jnp.concatenate([first_own[1], second_own[1], joint_own[1, :shard]], axis=1)
    wide_piece = 2 * piece + LANES

    def layer_weights(layer):
        if layer == 0:
            near = jnp.concatenate(
                [
                    jnp.concatenate([inner_first[2 * j][:, piece:], inner_first[2 * j + 1][:, piece:]], axis=0)
                    for j in range(4)
                ],
                axis=1,
            )
            weights = (inner_own, outer_own, inner_first, outer_first)
        else:
            near = jnp.concatenate([inner_second[j, :, piece:] for j in range(4)], axis=1)
            weights = (inner_own, outer_own, [inner_second])
        return (weights, (out_own[layer], near, swap(near, CORE)))

    def out_place(layer, block):
        at = (block // 2) ^ chip if layer == 0 else block // 2
        return at + 4 * ((block % 2) ^ core)

    activation = tokens[0]
    stashed = []
    outputs = []
    for layer in range(LAYERS):
        joint = joint_first if layer == 0 else joint_second
        first_gain_row, first_shift_row = wide(small(layer, 4)), wide(small(layer, 5))
        second_gain_row, second_shift_row = wide(small(layer, 6)), wide(small(layer, 7))

        near_tokens, far_tokens = first_tokens if layer == 0 else spread_tokens(activation)
        everyone = jnp.concatenate([near_tokens, far_tokens], axis=0)
        query_bias_own = lax.dynamic_slice_in_dim(small(layer, 0), here * LANES, LANES, 0)
        value_bias_own = lax.dynamic_slice_in_dim(small(layer, 1), here * LANES, LANES, 0)
        joint_bias = wide(jnp.concatenate([query_bias_own, jnp.zeros_like(query_bias_own), value_bias_own]))
        packed = low(mm(everyone, joint) + joint_bias)
        if layer == 0:
            packed, layer_own = gate([packed, layer_own], inner_near)
            second_stack = lax.all_gather(layer_own, "wsh", axis=0)
        mixed, log_all = attention_forward(packed, labels, block_order)
        if layer == 0:
            inner_own, outer_own, out_own = own_blocks(
                inner_weight,
                outer_weight,
                out_weight,
                jnp.concatenate(inner_order),
                jnp.concatenate(out_order),
                mixed,
            )
            left_x, right_y, outer_stack = gate([*inner_half[2:], outer_stack], mixed)
            inner_first = spread_second(*inner_half[:2], left_x, right_y)
            outer_first = spread_second(*spread_first(ordered(outer_stack, turned[1:])))
        else:
            (inner_second,) = gate([inner_second], mixed)
        weights, out_weights = layer_weights(layer)
        mixed_heads = exchange(mixed.reshape(8, rows, LANES))
        places = jnp.stack(
            [2 * turned[p // 2] + p % 2 for p in range(8)]
            + [out_place(layer, b) for b in range(8)]
            + turned
            + [jnp.int32(0)] * 4
            + [out_order[layer][p] for p in range(8)]
        ).astype(jnp.int32)
        mixed_turned, first_unit, first_inverse, hidden_rows, hidden_turned = attention_output(
            mixed_heads,
            out_weights,
            activation,
            wide(small(layer, 2))[None],
            first_gain_row[None],
            first_shift_row[None],
            places,
        )
        if layer == 1:
            weights = (*weights, gate([outer_second], hidden_turned))
        mixed_pair = jnp.concatenate([mixed_turned, swap(mixed_turned, CORE)], axis=0)
        hidden_pair = jnp.concatenate([hidden_turned, swap(hidden_turned, CORE)], axis=0)
        inner_bias_own = jnp.concatenate(
            [lax.dynamic_slice_in_dim(inner_bias_all[layer], inner_order[layer][j] * piece, piece, 0) for j in range(4)]
        )
        outer_near, outer_far, active, slope = feed_forward(
            hidden_pair, wide(inner_bias_own)[None], weights, layer
        )
        outer_turned = outer_near + wide(swap(outer_far, CORE))
        if layer == 0:
            (second_stack,) = gate([second_stack], active)
            joint_second = second_stack[:, :, wide_piece:].reshape(width, joint_width)
            others_second = ordered(second_stack[:, :, :wide_piece], turned[1:])
            sent_second = (others_second[:, : piece + LANES], others_second[:, piece + LANES :])
            inner_second, outer_second = [
                lax.all_gather(part, "ctx", axis=0, axis_index_groups=plane_groups()) for part in sent_second
            ]
        outer_out = block_columns(outer_turned, unturned, shard)
        second_pre = hidden_rows + (outer_out + wide(small(layer, 3)))
        result, second_unit, second_inverse = norm_forward(second_pre, second_gain_row, second_shift_row)
        stashed.append(
            (
                everyone,
                packed,
                log_all,
                mixed_pair,
                first_unit,
                first_inverse,
                hidden_pair,
                active,
                slope,
                second_unit,
                second_inverse,
                joint,
                out_weights,
                places,
                weights,
                first_gain_row,
                second_gain_row,
            )
        )
        activation = low(result)
        outputs.append(activation)

    gradient = wide(cotangent[0])
    small_grads = [None] * LAYERS
    for layer in reversed(range(LAYERS)):
        (
            everyone,
            packed,
            log_all,
            mixed_pair,
            first_unit,
            first_inverse,
            hidden_pair,
            active,
            slope,
            second_unit,
            second_inverse,
            joint,
            out_weights,
            places,
            weights,
            first_gain_row,
            second_gain_row,
        ) = stashed[layer]
        grad_second, grad_second_gain, grad_second_shift = norm_backward(
            gradient, second_unit, second_inverse, second_gain_row
        )
        grad_outer = low(grad_second)
        grad_outer_bias = jnp.sum(wide(grad_outer), axis=0)
        grad_turned = block_columns(grad_outer, turned, shard)
        grad_pair = jnp.concatenate([grad_turned, swap(grad_turned, CORE)], axis=0)
        hidden_near, hidden_far, grad_inner, grad_inner_bias = feed_backward(grad_pair, slope, weights, layer)
        grad_first, first_rows, branch_spread, grad_sent = attention_output_back(
            hidden_near,
            swap(hidden_far, CORE),
            grad_second,
            first_unit,
            first_inverse,
            first_gain_row[None],
            out_weights,
            places,
        )
        grad_mixed = exchange(grad_sent).reshape(8 * rows, LANES)
        branch_half = 4 * LANES
        branch_pair = jnp.concatenate(
            [branch_spread[:, :branch_half], swap(branch_spread[:, branch_half:], CORE)], axis=0
        )
        summed = weight_gradients(
            hidden_pair, grad_pair, mixed_pair, grad_inner, active, branch_pair, plane_rows, layer == 0, grad_sent
        )
        if layer == 0:
            (grad_mixed,) = gate([grad_mixed], summed[0], plane_first)
        else:
            grad_mixed, first_sum = gate([grad_mixed, summed[0]])
        grad_query, grad_key, grad_value = attention_backward(packed, labels, grad_mixed, log_all, block_order)
        if layer == 0:
            first_keep, first_send, second_keep, second_send = summed
            first_came = swap(first_send, ALONG_X)
            second_came = swap(second_send, ALONG_Y)
        near_part, far_part, grad_packed, joint_bias_grad = token_gradients(
            (grad_query, grad_key, grad_value), joint, chip_order[0]
        )
        grad_joint = low(mm(everyone, grad_packed, TN))
        far_came = swap(far_part, CORE)
        tokens_sent = low(near_part + wide(far_came))
        small_grads[layer] = small_rows(
            jnp.concatenate([here[None], inner_order[layer]]).astype(jnp.int32),
            joint_bias_grad,
            first_rows,
            grad_outer_bias,
            grad_second_gain,
            grad_second_shift,
            grad_inner_bias,
        )
        if layer == 1:
            (plane_first,) = [
                lax.psum_scatter(
                    first_sum.reshape(4 * width, -1),
                    "ctx",
                    scatter_dimension=0,
                    axis_index_groups=plane_groups(),
                    tiled=True,
                )
            ]
            (plane_first,) = gate([plane_first], far_came)
            sum_first = lax.psum_scatter(plane_first, "wsh", scatter_dimension=0, tiled=True)
            gradient = grad_first + collect_tokens(tokens_sent, (), (grad_joint,))
            (second_sum,) = gate([summed[1]], gradient)
            plane_second = lax.psum_scatter(
                second_sum.reshape(4 * width, -1),
                "ctx",
                scatter_dimension=0,
                axis_index_groups=plane_groups(),
                tiled=True,
            )
            sum_joint = lax.psum_scatter(grad_joint, "wsh", scatter_dimension=0, tiled=True)
            continue
        small_sent = jnp.concatenate(small_grads, axis=0)
        small_plane = jnp.sum(
            lax.all_to_all(
                jnp.stack([small_sent[:, p * shard : (p + 1) * shard] for p in range(planes)]), "wsh", 0, 0, tiled=True
            ),
            axis=0,
        )
        small_spread = jnp.broadcast_to(small_plane, (8, *small_plane.shape))
        first_came, second_came = gate([first_came, second_came], near_part, grad_joint)
        first_next = low(wide(first_keep[1]) + wide(first_came[1]))
        second_next = low(wide(second_keep[1]) + wide(second_came[1]))
        joint_rows = [lax.dynamic_slice_in_dim(grad_joint, turned[r] * shard, shard, 0) for r in range(planes)]
        came_joint = [turn(joint_rows[r], planes - r) for r in range(1, planes)]
        first_last, second_last = gate(
            [swap(first_next, ALONG_Y), swap(second_next, ALONG_X)], small_plane, tokens_sent, *came_joint
        )
        own_total, *sent = plane_sum(
            (first_keep, first_came, first_last), (second_keep, second_came, second_last)
        )
        came = [turn(sent[r - 1], planes - r) for r in range(1, planes)]
        (plane_second,) = gate([plane_second], grad_mixed)
        sum_second = lax.psum_scatter(plane_second, "wsh", scatter_dimension=0, tiled=True)
        sum_first, sum_second, sum_joint = gate([sum_first, sum_second, sum_joint], own_total)
        everything = lax.all_gather(
            jnp.concatenate([sum_first[:, :piece], sum_second, sum_first[:, piece:], sum_joint], axis=1),
            "ctx",
            axis=0,
        )
        gradient = grad_first + collect_tokens(tokens_sent, (own_total,), ())
        came = gate(came, gradient)
        left_total, right_total = final_sum((own_total, *came), (joint_rows[0], *came_joint))
        (everything,) = gate([everything], left_total)
        *placed, placed_token = place_pieces(everything, relative, 1, None)
        (small_spread,) = gate([small_spread], left_total)
        small_mine = jnp.sum(exchange(small_spread), axis=0).reshape(LAYERS, 16, shard)

    near, far = plane_pieces(left_total, right_total, placed_token, small_mine)
    near_first = here ^ (2 * four)
    *placed, placed_token = place_pieces(near, near_first, 0, placed)
    (far,) = gate([far], placed_token)
    *placed, _ = place_pieces(far, near_first ^ 1, 0, placed)
    small_outs = [small_mine[:, i] for i in range(8)]
    return (
        outputs[0][None],
        outputs[1][None],
        low(gradient)[None],
        *placed,
        small_outs[0],
        small_outs[1],
        small_outs[2],
        small_mine[:, 8:12].reshape(LAYERS, 4 * shard),
        small_outs[3],
        small_outs[4],
        small_outs[5],
        small_outs[6],
        small_outs[7],
    )


def choose_body(mesh):
    if mesh.shape["ctx"] == 8 and HEADS // 8 == 2:
        return head_split_body
    return window_body


def solution(mesh):
    in_specs = (
        P("wsh", "ctx", None),
        P("wsh", "ctx", None),
        P("wsh", None),
        P("wsh", None),
        P(None, "wsh", None),
        P(None, "wsh", None),
        P(None, "wsh", None),
        P(None, "wsh", None),
        P(None, "wsh", None),
        P(None, None, "wsh"),
        P(None, "wsh"),
        P(None, "wsh"),
        P(None, "wsh"),
        P(None, "wsh"),
        P(None, "wsh"),
        P(None, "wsh"),
        P(None, "wsh"),
        P(None, "wsh"),
        P(None, "wsh"),
    )
    out_specs = (
        P("wsh", "ctx", None),
        P("wsh", "ctx", None),
        P("wsh", "ctx", None),
        P(None, "wsh", None),
        P(None, "wsh", None),
        P(None, "wsh", None),
        P(None, "wsh", None),
        P(None, "wsh", None),
        P(None, None, "wsh"),
        P(None, "wsh"),
        P(None, "wsh"),
        P(None, "wsh"),
        P(None, "wsh"),
        P(None, "wsh"),
        P(None, "wsh"),
        P(None, "wsh"),
        P(None, "wsh"),
        P(None, "wsh"),
    )
    return jax.shard_map(choose_body(mesh), mesh=mesh, in_specs=in_specs, out_specs=out_specs, check_vma=False)
```

```python
import functools

import jax
import jax.numpy as jnp
from jax import lax
from jax.experimental import pallas as pl
from jax.experimental.pallas import tpu as pltpu
from jax.sharding import PartitionSpec as P

HEADS = 16
HDIM = 64
LAYERS = 2
DOC_CAP = 2000


epsilon = 1e-05
neg_fill = -1e30
head_pair = 2


def from_behind(block, axis, distance):
    devices = range(lax.axis_size(axis))
    route = [(i - distance, i) for i in devices if i - distance in devices]
    return lax.ppermute(block, axis, route)


def normalize(values_in, gain_row, shift_row):
    centre = values_in - jnp.mean(values_in, axis=-1, keepdims=True)
    spread = jnp.mean(centre * centre, axis=-1, keepdims=True)
    return centre * lax.rsqrt(spread + epsilon) * gain_row + shift_row


def exact_gelu(values_in):
    return jax.nn.gelu(values_in, approximate=False)


def product(form, left, right):
    return jnp.einsum(form, left, right, preferred_element_type=jnp.float32)


def doc_labels(positions, starts, lengths):
    inside = (positions[:, None] >= starts[None, :]) & (
        positions[:, None] < (starts + lengths)[None, :]
    )
    labels = jnp.arange(1, starts.shape[0] + 1, dtype=jnp.int32)
    return jnp.sum(jnp.where(inside, labels[None, :], 0), axis=1)


def extend_rows(rows_in, dim, reach, mover):
    pieces = []
    for offset in range(-reach, reach + 1):
        if offset == 0:
            pieces.append(rows_in)
        else:
            pieces.append(mover(rows_in, -offset))
    return jnp.concatenate(pieces, axis=dim)


def move_keys_fwd(rows_in, steps):
    return from_behind(rows_in, "ctx", steps)


def move_keys_back(rows_in, steps):
    return from_behind(rows_in, "ctx", steps)


def fetch_forward(params, layer_index):
    shards = [piece[layer_index].astype(jnp.bfloat16) for piece in params]
    return (
        lax.all_gather(shards[0], "wsh", axis=0, tiled=True),
        lax.all_gather(shards[1], "wsh", axis=0, tiled=True),
        lax.all_gather(shards[2], "wsh", axis=0, tiled=True),
        lax.all_gather(shards[3], "wsh", axis=0, tiled=True),
        lax.all_gather(shards[4], "wsh", axis=0, tiled=True),
        lax.all_gather(shards[5], "wsh", axis=1, tiled=True),
        lax.all_gather(shards[6], "wsh", axis=0, tiled=True),
        lax.all_gather(shards[7], "wsh", axis=0, tiled=True),
        lax.all_gather(shards[8], "wsh", axis=0, tiled=True),
        lax.all_gather(shards[9], "wsh", axis=0, tiled=True),
        lax.all_gather(shards[10], "wsh", axis=0, tiled=True),
        lax.all_gather(shards[11], "wsh", axis=0, tiled=True),
        lax.all_gather(shards[12], "wsh", axis=0, tiled=True),
        lax.all_gather(shards[13], "wsh", axis=0, tiled=True),
        lax.all_gather(shards[14], "wsh", axis=0, tiled=True),
    )


def fetch_backward(params, layer_index):
    shards = [piece[layer_index].astype(jnp.bfloat16) for piece in params]
    return (
        lax.all_gather(shards[0], "wsh", axis=0, tiled=True),
        lax.all_gather(shards[1], "wsh", axis=0, tiled=True),
        lax.all_gather(shards[2], "wsh", axis=0, tiled=True),
        lax.all_gather(shards[3], "wsh", axis=0, tiled=True),
        lax.all_gather(shards[4], "wsh", axis=0, tiled=True),
        lax.all_gather(shards[5], "wsh", axis=1, tiled=True),
        lax.all_gather(shards[6], "wsh", axis=0, tiled=True),
        lax.all_gather(shards[7], "wsh", axis=0, tiled=True),
        lax.all_gather(shards[8], "wsh", axis=0, tiled=True),
        lax.all_gather(shards[9], "wsh", axis=0, tiled=True),
        lax.all_gather(shards[10], "wsh", axis=0, tiled=True),
        lax.all_gather(shards[11], "wsh", axis=0, tiled=True),
        lax.all_gather(shards[12], "wsh", axis=0, tiled=True),
        lax.all_gather(shards[13], "wsh", axis=0, tiled=True),
        lax.all_gather(shards[14], "wsh", axis=0, tiled=True),
    )


def reduce_grads(local_grads):
    shares = (
        lax.psum_scatter(
            local_grads[0].astype(jnp.bfloat16), "wsh", scatter_dimension=0, tiled=True
        ).astype(jnp.float32),
        lax.psum_scatter(
            local_grads[1].astype(jnp.bfloat16), "wsh", scatter_dimension=0, tiled=True
        ).astype(jnp.float32),
        lax.psum_scatter(
            local_grads[2].astype(jnp.bfloat16), "wsh", scatter_dimension=0, tiled=True
        ).astype(jnp.float32),
        lax.psum_scatter(
            local_grads[3].astype(jnp.bfloat16), "wsh", scatter_dimension=0, tiled=True
        ).astype(jnp.float32),
        lax.psum_scatter(
            local_grads[4].astype(jnp.bfloat16), "wsh", scatter_dimension=0, tiled=True
        ).astype(jnp.float32),
        lax.psum_scatter(
            local_grads[5].astype(jnp.bfloat16), "wsh", scatter_dimension=1, tiled=True
        ).astype(jnp.float32),
        lax.psum_scatter(
            local_grads[6].astype(jnp.bfloat16), "wsh", scatter_dimension=0, tiled=True
        ).astype(jnp.float32),
        lax.psum_scatter(
            local_grads[7].astype(jnp.bfloat16), "wsh", scatter_dimension=0, tiled=True
        ).astype(jnp.float32),
        lax.psum_scatter(
            local_grads[8].astype(jnp.bfloat16), "wsh", scatter_dimension=0, tiled=True
        ).astype(jnp.float32),
        lax.psum_scatter(
            local_grads[9].astype(jnp.bfloat16), "wsh", scatter_dimension=0, tiled=True
        ).astype(jnp.float32),
        lax.psum_scatter(
            local_grads[10].astype(jnp.bfloat16), "wsh", scatter_dimension=0, tiled=True
        ).astype(jnp.float32),
        lax.psum_scatter(
            local_grads[11].astype(jnp.bfloat16), "wsh", scatter_dimension=0, tiled=True
        ).astype(jnp.float32),
        lax.psum_scatter(
            local_grads[12].astype(jnp.bfloat16), "wsh", scatter_dimension=0, tiled=True
        ).astype(jnp.float32),
        lax.psum_scatter(
            local_grads[13].astype(jnp.bfloat16), "wsh", scatter_dimension=0, tiled=True
        ).astype(jnp.float32),
        lax.psum_scatter(
            local_grads[14].astype(jnp.bfloat16), "wsh", scatter_dimension=0, tiled=True
        ).astype(jnp.float32),
    )
    return (
        lax.psum(shares[0].astype(jnp.bfloat16), "ctx").astype(jnp.float32),
        lax.psum(shares[1].astype(jnp.bfloat16), "ctx").astype(jnp.float32),
        lax.psum(shares[2].astype(jnp.bfloat16), "ctx").astype(jnp.float32),
        lax.psum(shares[3].astype(jnp.bfloat16), "ctx").astype(jnp.float32),
        lax.psum(shares[4].astype(jnp.bfloat16), "ctx").astype(jnp.float32),
        lax.psum(shares[5].astype(jnp.bfloat16), "ctx").astype(jnp.float32),
        lax.psum(shares[6].astype(jnp.bfloat16), "ctx").astype(jnp.float32),
        lax.psum(shares[7].astype(jnp.bfloat16), "ctx").astype(jnp.float32),
        lax.psum(shares[8].astype(jnp.bfloat16), "ctx").astype(jnp.float32),
        lax.psum(shares[9].astype(jnp.bfloat16), "ctx").astype(jnp.float32),
        lax.psum(shares[10].astype(jnp.bfloat16), "ctx").astype(jnp.float32),
        lax.psum(shares[11].astype(jnp.bfloat16), "ctx").astype(jnp.float32),
        lax.psum(shares[12].astype(jnp.bfloat16), "ctx").astype(jnp.float32),
        lax.psum(shares[13].astype(jnp.bfloat16), "ctx").astype(jnp.float32),
        lax.psum(shares[14].astype(jnp.bfloat16), "ctx").astype(jnp.float32),
    )


def attend(queries, key_ext, value_ext, allowed, score_scale):
    rows_local = queries.shape[0]
    rows_keys = key_ext.shape[0]
    groups = HEADS // head_pair
    span = head_pair * HDIM
    query_groups = queries.reshape(rows_local, groups, span)
    key_groups = key_ext.reshape(rows_keys, groups, span)
    value_groups = value_ext.reshape(rows_keys, groups, span)

    def one_group(group_index, carry):
        mixed_all, log_all = carry
        query_part = lax.dynamic_index_in_dim(query_groups, group_index, 1, keepdims=False).reshape(
            rows_local, head_pair, HDIM
        )
        key_part = lax.dynamic_index_in_dim(key_groups, group_index, 1, keepdims=False).reshape(
            rows_keys, head_pair, HDIM
        )
        value_part = lax.dynamic_index_in_dim(value_groups, group_index, 1, keepdims=False).reshape(
            rows_keys, head_pair, HDIM
        )
        raw_scores = product("qhd,khd->hqk", query_part, key_part)
        scores = jnp.where(allowed[None], raw_scores * score_scale, neg_fill)
        row_peak = jnp.max(scores, axis=2, keepdims=True)
        exponent = jnp.exp(scores - row_peak)
        row_total = jnp.sum(exponent, axis=2, keepdims=True)
        probability = (exponent / row_total).astype(jnp.bfloat16)
        mixed_part = product("hqk,khd->qhd", probability, value_part)
        mixed_all = lax.dynamic_update_index_in_dim(
            mixed_all, mixed_part.reshape(rows_local, span), group_index, 1
        )
        log_all = lax.dynamic_update_index_in_dim(
            log_all, (row_peak + jnp.log(row_total))[:, :, 0], group_index, 0
        )
        return (mixed_all, log_all)

    start_carry = (
        jnp.zeros((rows_local, groups, span), jnp.float32),
        jnp.zeros((groups, head_pair, rows_local), jnp.float32),
    )
    mixed_all, log_all = lax.fori_loop(0, groups, one_group, start_carry)
    return (mixed_all.reshape(rows_local, groups * span), log_all)


def attend_back(queries, key_ext, value_ext, grad_mixed, log_all, allowed, score_scale):
    rows_local = queries.shape[0]
    rows_keys = key_ext.shape[0]
    groups = HEADS // head_pair
    span = head_pair * HDIM
    query_groups = queries.reshape(rows_local, groups, span)
    key_groups = key_ext.reshape(rows_keys, groups, span)
    value_groups = value_ext.reshape(rows_keys, groups, span)
    grad_groups = grad_mixed.reshape(rows_local, groups, span)

    def one_group(group_index, carry):
        query_part = lax.dynamic_index_in_dim(query_groups, group_index, 1, keepdims=False).reshape(
            rows_local, head_pair, HDIM
        )
        key_part = lax.dynamic_index_in_dim(key_groups, group_index, 1, keepdims=False).reshape(
            rows_keys, head_pair, HDIM
        )
        value_part = lax.dynamic_index_in_dim(value_groups, group_index, 1, keepdims=False).reshape(
            rows_keys, head_pair, HDIM
        )
        grad_part = lax.dynamic_index_in_dim(grad_groups, group_index, 1, keepdims=False).reshape(
            rows_local, head_pair, HDIM
        )
        log_part = lax.dynamic_index_in_dim(log_all, group_index, 0, keepdims=False)
        raw_scores = product("qhd,khd->hqk", query_part, key_part)
        scores = jnp.where(allowed[None], raw_scores * score_scale, neg_fill)
        probability = jnp.exp(scores - log_part[:, :, None])
        grad_prob = product("qhd,khd->hqk", grad_part, value_part)
        row_delta = jnp.sum(probability * grad_prob, axis=2, keepdims=True)
        grad_scores = (probability * (grad_prob - row_delta) * score_scale).astype(jnp.bfloat16)
        query_term = product("hqk,khd->qhd", grad_scores, key_part)
        grad_query = lax.dynamic_update_index_in_dim(
            carry[0], query_term.reshape(rows_local, span), group_index, 1
        )
        delta_all = lax.dynamic_update_index_in_dim(carry[1], row_delta[:, :, 0], group_index, 0)
        key_term = product("hqk,qhd->khd", grad_scores, query_part)
        value_term = product("hqk,qhd->khd", probability.astype(jnp.bfloat16), grad_part)
        grad_key = lax.dynamic_update_index_in_dim(
            carry[2], key_term.reshape(rows_keys, span), group_index, 1
        )
        grad_value = lax.dynamic_update_index_in_dim(
            carry[3], value_term.reshape(rows_keys, span), group_index, 1
        )
        return (grad_query, delta_all, grad_key, grad_value)

    start_carry = (
        jnp.zeros((rows_local, groups, span), jnp.float32),
        jnp.zeros((groups, head_pair, rows_local), jnp.float32),
    )
    start_carry = start_carry + (
        jnp.zeros((rows_keys, groups, span), jnp.float32),
        jnp.zeros((rows_keys, groups, span), jnp.float32),
    )
    finals = lax.fori_loop(0, groups, one_group, start_carry)
    grad_query = finals[0].reshape(rows_local, groups * span)
    return (
        grad_query,
        finals[2].reshape(rows_keys, groups * span),
        finals[3].reshape(rows_keys, groups * span),
    )


def layer_forward(activation, gathered, allowed, halo_rows, score_scale):
    (
        query_weight,
        key_weight,
        value_weight,
        out_weight,
        inner_weight,
        outer_weight,
        query_bias,
        value_bias,
        out_bias,
        inner_bias,
        outer_bias,
        first_gain,
        first_shift,
        second_gain,
        second_shift,
    ) = gathered
    rows_local = activation.shape[0]
    queries = (product("td,de->te", activation, query_weight) + query_bias).astype(jnp.bfloat16)
    key_rows = product("td,de->te", activation, key_weight).astype(jnp.bfloat16)
    value_rows = (product("td,de->te", activation, value_weight) + value_bias).astype(jnp.bfloat16)
    stacked = jnp.stack([key_rows, value_rows])
    extended = extend_rows(stacked, 1, halo_rows // rows_local, move_keys_fwd)
    mixed_heads, log_all = attend(queries, extended[0], extended[1], allowed, score_scale)
    mixed_low = mixed_heads.astype(jnp.bfloat16)
    first_pre = activation.astype(jnp.float32) + (
        product("td,de->te", mixed_low, out_weight) + out_bias
    )
    hidden = normalize(first_pre, first_gain.astype(jnp.float32), first_shift.astype(jnp.float32))
    hidden_low = hidden.astype(jnp.bfloat16)
    inner_pre = product("td,df->tf", hidden_low, inner_weight) + inner_bias
    active_low = exact_gelu(inner_pre).astype(jnp.bfloat16)
    second_pre = hidden + (product("tf,fd->td", active_low, outer_weight) + outer_bias)
    result_rows = normalize(
        second_pre, second_gain.astype(jnp.float32), second_shift.astype(jnp.float32)
    )
    saved = (
        activation,
        queries,
        extended,
        log_all,
        mixed_low,
        first_pre,
        hidden_low,
        inner_pre,
        active_low,
        second_pre,
    )
    return (saved, result_rows)


def return_rows(grad_ext, halo_rows, rows_local):
    reach = halo_rows // rows_local
    total = grad_ext[:, halo_rows : halo_rows + rows_local]
    for offset in range(-reach, reach + 1):
        if offset != 0:
            begin = halo_rows + offset * rows_local
            block_rows = grad_ext[:, begin : begin + rows_local]
            total = total + from_behind(block_rows.astype(jnp.bfloat16), "ctx", offset).astype(
                block_rows.dtype
            )
    return total


def layer_backward(gradient, saved, weights, allowed, halo_rows, score_scale):
    (
        query_weight,
        key_weight,
        value_weight,
        out_weight,
        inner_weight,
        outer_weight,
        query_bias,
        value_bias,
        out_bias,
        inner_bias,
        outer_bias,
        first_gain,
        first_shift,
        second_gain,
        second_shift,
    ) = weights
    (
        activation,
        queries,
        extended,
        log_all,
        mixed_low,
        first_pre,
        hidden_low,
        inner_pre,
        active_low,
        second_pre,
    ) = saved
    rows_local = activation.shape[0]
    reach = halo_rows // rows_local
    _, second_pull = jax.vjp(
        normalize, second_pre, second_gain.astype(jnp.float32), second_shift.astype(jnp.float32)
    )
    grad_second, grad_second_gain, grad_second_shift = second_pull(gradient)
    grad_outer = grad_second.astype(jnp.bfloat16)
    grad_outer_weight = product("tf,td->fd", active_low, grad_outer)
    grad_outer_bias = jnp.sum(grad_outer.astype(jnp.float32), axis=0)
    grad_active = product("td,fd->tf", grad_outer, outer_weight)
    _, gelu_pull = jax.vjp(exact_gelu, inner_pre)
    (grad_inner,) = gelu_pull(grad_active)
    grad_inner_low = grad_inner.astype(jnp.bfloat16)
    grad_inner_weight = product("td,tf->df", hidden_low, grad_inner_low)
    grad_inner_bias = jnp.sum(grad_inner_low.astype(jnp.float32), axis=0)
    grad_hidden = grad_second + product("tf,df->td", grad_inner_low, inner_weight)
    _, first_pull = jax.vjp(
        normalize, first_pre, first_gain.astype(jnp.float32), first_shift.astype(jnp.float32)
    )
    grad_first, grad_first_gain, grad_first_shift = first_pull(grad_hidden)
    grad_branch = grad_first.astype(jnp.bfloat16)
    grad_out_weight = product("te,td->ed", mixed_low, grad_branch)
    grad_out_bias = jnp.sum(grad_branch.astype(jnp.float32), axis=0)
    grad_mixed = product("td,ed->te", grad_branch, out_weight).astype(jnp.bfloat16)
    own_rows = extended[:, halo_rows : halo_rows + rows_local]
    key_ext = extend_rows(own_rows, 1, reach, move_keys_back)
    query_sum, key_win, value_win = attend_back(
        queries, key_ext[0], key_ext[1], grad_mixed, log_all, allowed, score_scale
    )
    owned = return_rows(jnp.stack([key_win, value_win]), halo_rows, rows_local)
    key_sum = owned[0]
    value_sum = owned[1]
    grad_query = query_sum.astype(jnp.bfloat16)
    grad_key = key_sum.astype(jnp.bfloat16)
    grad_value = value_sum.astype(jnp.bfloat16)
    grad_query_weight = product("te,td->ed", activation, grad_query)
    grad_key_weight = product("te,td->ed", activation, grad_key)
    grad_value_weight = product("te,td->ed", activation, grad_value)
    grad_query_bias = jnp.sum(grad_query.astype(jnp.float32), axis=0)
    grad_value_bias = jnp.sum(grad_value.astype(jnp.float32), axis=0)
    grad_activation = (
        grad_first
        + product("td,ed->te", grad_query, query_weight)
        + product("td,ed->te", grad_key, key_weight)
        + product("td,ed->te", grad_value, value_weight)
    )
    local_grads = (
        grad_query_weight,
        grad_key_weight,
        grad_value_weight,
        grad_out_weight,
        grad_inner_weight,
        grad_outer_weight,
        grad_query_bias,
        grad_value_bias,
        grad_out_bias,
        grad_inner_bias,
        grad_outer_bias,
        grad_first_gain,
        grad_first_shift,
        grad_second_gain,
        grad_second_shift,
    )
    return (grad_activation, local_grads)


def window_body(
    tokens,
    cotangent,
    doc_starts,
    doc_lengths,
    query_weight,
    key_weight,
    value_weight,
    out_weight,
    inner_weight,
    outer_weight,
    query_bias,
    value_bias,
    out_bias,
    inner_bias,
    outer_bias,
    first_gain,
    first_shift,
    second_gain,
    second_shift,
):
    params = (
        query_weight,
        key_weight,
        value_weight,
        out_weight,
        inner_weight,
        outer_weight,
        query_bias,
        value_bias,
        out_bias,
        inner_bias,
        outer_bias,
        first_gain,
        first_shift,
        second_gain,
        second_shift,
    )
    rows_local = tokens.shape[1]
    ctx_count = lax.axis_size("ctx")
    reach = min(-(-(DOC_CAP - 1) // rows_local), ctx_count - 1)
    halo_rows = reach * rows_local
    window = rows_local + 2 * halo_rows
    row_start = lax.axis_index("ctx") * rows_local
    local_positions = row_start + jnp.arange(rows_local, dtype=jnp.int32)
    window_positions = row_start - halo_rows + jnp.arange(window, dtype=jnp.int32)
    local_labels = doc_labels(local_positions, doc_starts[0], doc_lengths[0])
    window_labels = doc_labels(window_positions, doc_starts[0], doc_lengths[0])
    allowed = (local_labels[:, None] == window_labels[None, :]) & (local_labels[:, None] > 0)
    score_scale = HDIM ** (-0.5)
    activation = tokens[0]
    stashed = []
    outputs = []
    for layer_index in range(LAYERS):
        gathered = fetch_forward(params, layer_index)
        saved, result_rows = layer_forward(activation, gathered, allowed, halo_rows, score_scale)
        stashed.append((saved, gathered))
        outputs.append(result_rows)
        activation = result_rows.astype(jnp.bfloat16)
    gradient = cotangent[0].astype(jnp.float32)
    reduced = [None] * LAYERS
    for layer_index in reversed(range(LAYERS)):
        saved, gathered = stashed[layer_index]
        weights_now = fetch_backward(params, layer_index)
        gradient, local_grads = layer_backward(
            gradient, saved, weights_now, allowed, halo_rows, score_scale
        )
        reduced[layer_index] = reduce_grads(local_grads)
    stacked_grads = [
        jnp.stack([reduced[layer_index][member] for layer_index in range(LAYERS)])
        for member in range(15)
    ]
    heads_out = [
        outputs[0].astype(jnp.bfloat16)[None],
        outputs[LAYERS - 1].astype(jnp.bfloat16)[None],
        gradient.astype(jnp.bfloat16)[None],
    ]
    return tuple(heads_out + stacked_grads)


NN = (((1,), (0,)), ((), ()))
NT = (((1,), (1,)), ((), ()))
TN = (((0,), (0,)), ((), ()))
LANES = 128
QUERY_BLOCK = 1024
CORE, ALONG_X, ALONG_Y = 1, 2, 4
SMALL_COST = pl.CostEstimate(flops=1000, bytes_accessed=1000, transcendentals=0)


def lasting(microseconds):
    return pl.CostEstimate(
        flops=int(microseconds * 1.15e9), bytes_accessed=int(microseconds * 3.6e6), transcendentals=0
    )


def mm(left, right, dims=NN):
    return lax.dot_general(left, right, dims, preferred_element_type=jnp.float32)


def swap(block, mask):
    devices = range(lax.axis_size("ctx"))
    return lax.ppermute(block, "ctx", [(i, i ^ mask) for i in devices])


def turn(block, distance):
    count = lax.axis_size("wsh")
    return lax.ppermute(block, "wsh", [(i, (i + distance) % count) for i in range(count)])


def low(values_in):
    return values_in.astype(jnp.bfloat16)


def wide(values_in):
    return values_in.astype(jnp.float32)


def mask_features(label_col):
    rows = label_col.shape[0]
    lane = lax.broadcasted_iota(jnp.int32, (rows, LANES), 1)
    hit = lax.rem(lane, HDIM) == jnp.broadcast_to(label_col, (rows, LANES))
    return (
        jnp.where(hit, neg_fill, 0.0).astype(jnp.bfloat16),
        jnp.where(hit, 0.0, 1.0).astype(jnp.bfloat16),
    )


def fill_key_scratch(key_rows, label_col, key_mask):
    lane = lax.broadcasted_iota(jnp.int32, key_rows.shape, 1)
    _, key_features = mask_features(label_col)
    key_mask[0] = jnp.where(lane < HDIM, key_rows, key_features)
    key_mask[1] = jnp.where(lane < HDIM, key_features, key_rows)


def attention_forward_kernel(
    order_ref, query_ref, key_ref, value_ref, label_ref, query_label_ref, mixed_ref, log_ref, key_mask, value_t
):
    @pl.when(pl.program_id(0) == 0)
    def _():
        fill_key_scratch(key_ref[...], label_ref[...], key_mask)
        value_t[...] = value_ref[...].T

    scaled = low(wide(query_ref[...]) * HDIM ** (-0.5))
    lane = lax.broadcasted_iota(jnp.int32, scaled.shape, 1)
    features, _ = mask_features(query_label_ref[...])
    parts = []
    for head in range(2):
        mine = (lane < HDIM) if head == 0 else (lane >= HDIM)
        scores = mm(key_mask[head], jnp.where(mine, scaled, features), NT)
        peak = jnp.max(scores, axis=0, keepdims=True)
        exponent = jnp.exp(scores - peak)
        total = jnp.sum(exponent, axis=0, keepdims=True)
        mixed = mm(value_t[pl.ds(HDIM * head, HDIM), :], low(exponent))
        parts.append(mixed / total)
        log_ref[pl.ds(head, 1), :] = peak + jnp.log(total)
    mixed_all = low(jnp.concatenate(parts, axis=0).T)
    block_rows = mixed_ref.shape[1]
    count = mixed_all.shape[0] // block_rows
    for at in range(count):
        place = order_ref[pl.program_id(0) * count + at]
        mixed_ref[place] = mixed_all[at * block_rows : (at + 1) * block_rows]


def attention_forward(packed, labels, order):
    rows = packed.shape[0]
    mine = pl.BlockSpec((QUERY_BLOCK, LANES), lambda i, order_ref: (i, 0))
    return pl.pallas_call(
        attention_forward_kernel,
        grid_spec=pltpu.PrefetchScalarGridSpec(
            num_scalar_prefetch=1,
            grid=(rows // QUERY_BLOCK,),
            in_specs=[
                mine,
                pl.BlockSpec((rows, LANES), lambda i, order_ref: (0, 1)),
                pl.BlockSpec((rows, LANES), lambda i, order_ref: (0, 2)),
                pl.BlockSpec((rows, 1), lambda i, order_ref: (0, 0)),
                pl.BlockSpec((QUERY_BLOCK, 1), lambda i, order_ref: (i, 0)),
            ],
            out_specs=[
                pl.BlockSpec((8, rows // 8, LANES), lambda i, order_ref: (0, 0, 0)),
                pl.BlockSpec((2, QUERY_BLOCK), lambda i, order_ref: (0, i)),
            ],
            scratch_shapes=[
                pltpu.VMEM((2, rows, LANES), jnp.bfloat16),
                pltpu.VMEM((LANES, rows), jnp.bfloat16),
            ],
        ),
        out_shape=[
            jax.ShapeDtypeStruct((8, rows // 8, LANES), jnp.bfloat16),
            jax.ShapeDtypeStruct((2, rows), jnp.float32),
        ],
        cost_estimate=lasting(17),
        name="attention_forward",
    )(order, packed, packed, packed, labels, labels)


def attention_backward_kernel(
    order_ref,
    query_ref,
    key_ref,
    value_ref,
    label_ref,
    query_label_ref,
    grad_ref,
    log_ref,
    out_query_ref,
    out_key_ref,
    out_value_ref,
    key_mask,
    key_t,
    key_sum,
    value_sum,
):
    step = pl.program_id(0)

    @pl.when(step == 0)
    def _():
        fill_key_scratch(key_ref[...], label_ref[...], key_mask)
        key_t[...] = key_ref[...].T
        key_sum[...] = jnp.zeros_like(key_sum)
        value_sum[...] = jnp.zeros_like(value_sum)

    scaled = low(wide(query_ref[...]) * HDIM ** (-0.5))
    count = scaled.shape[0] // grad_ref.shape[1]
    grad = jnp.concatenate([grad_ref[order_ref[step * count + at]] for at in range(count)], axis=0)
    value_rows = value_ref[...]
    lane = lax.broadcasted_iota(jnp.int32, scaled.shape, 1)
    features, _ = mask_features(query_label_ref[...])
    zero = jnp.zeros(scaled.shape, jnp.bfloat16)
    parts = []
    for head in range(2):
        mine = (lane < HDIM) if head == 0 else (lane >= HDIM)
        query_own = jnp.where(mine, scaled, zero)
        grad_own = jnp.where(mine, grad, zero)
        scores = mm(key_mask[head], jnp.where(mine, scaled, features), NT)
        probability = jnp.exp(scores - log_ref[pl.ds(head, 1), :])
        grad_prob = mm(value_rows, grad_own, NT)
        delta = jnp.sum(probability * grad_prob, axis=0, keepdims=True)
        grad_scores = low(probability * (grad_prob - delta))
        key_sum[...] += mm(grad_scores, query_own)
        value_sum[...] += mm(low(probability), grad_own)
        parts.append(mm(key_t[pl.ds(HDIM * head, HDIM), :], grad_scores) * HDIM ** (-0.5))
    out_query_ref[...] = low(jnp.concatenate(parts, axis=0).T)

    @pl.when(step == pl.num_programs(0) - 1)
    def _():
        out_key_ref[...] = low(key_sum[...])
        out_value_ref[...] = low(value_sum[...])


def attention_backward(packed, labels, grad, log_all, order):
    rows = packed.shape[0]
    mine = pl.BlockSpec((QUERY_BLOCK, LANES), lambda i, order_ref: (i, 0))
    whole = pl.BlockSpec((rows, LANES), lambda i, order_ref: (0, 0))
    return pl.pallas_call(
        attention_backward_kernel,
        grid_spec=pltpu.PrefetchScalarGridSpec(
            num_scalar_prefetch=1,
            grid=(rows // QUERY_BLOCK,),
            in_specs=[
                mine,
                pl.BlockSpec((rows, LANES), lambda i, order_ref: (0, 1)),
                pl.BlockSpec((rows, LANES), lambda i, order_ref: (0, 2)),
                pl.BlockSpec((rows, 1), lambda i, order_ref: (0, 0)),
                pl.BlockSpec((QUERY_BLOCK, 1), lambda i, order_ref: (i, 0)),
                pl.BlockSpec((8, rows // 8, LANES), lambda i, order_ref: (0, 0, 0)),
                pl.BlockSpec((2, QUERY_BLOCK), lambda i, order_ref: (0, i)),
            ],
            out_specs=[mine, whole, whole],
            scratch_shapes=[
                pltpu.VMEM((2, rows, LANES), jnp.bfloat16),
                pltpu.VMEM((LANES, rows), jnp.bfloat16),
                pltpu.VMEM((rows, LANES), jnp.float32),
                pltpu.VMEM((rows, LANES), jnp.float32),
            ],
        ),
        out_shape=[jax.ShapeDtypeStruct((rows, LANES), jnp.bfloat16)] * 3,
        cost_estimate=lasting(29),
        name="attention_backward",
    )(order, packed, packed, packed, labels, labels, grad, log_all)


def own_pieces(inner_weight, outer_weight, out_weight, joint_weights, small_params, here, first_block):
    layers, shard, hidden = inner_weight.shape
    piece = hidden // 8
    width = 3 * LANES

    def kernel(place_ref, inner_ref, outer_ref, out_ref, query_ref, key_ref, value_ref, *refs):
        small_refs, (first_ref, second_ref, joint_ref) = refs[:-3], refs[-3:]
        first_ref[0, :, :piece] = low(inner_ref[0])
        first_ref[0, :, piece:] = low(out_ref[0])
        second_ref[0] = low(outer_ref[0]).T
        for at, ref in enumerate((query_ref, key_ref, value_ref)):
            joint_ref[0, :shard, at * LANES : (at + 1) * LANES] = low(ref[0])
        rows = [jnp.concatenate([ref[...] for ref in small_refs[:8]], axis=0)]
        rows += [small_refs[8][:, q * shard : (q + 1) * shard] for q in range(4)]
        rows += [jnp.zeros((8, shard), jnp.float32)]
        packed = low(jnp.concatenate(rows, axis=0))
        joint_ref[0, shard:] = jnp.concatenate([packed, jnp.zeros((32, width - shard), jnp.bfloat16)], axis=1)

    column = pl.BlockSpec((1, shard, LANES), lambda layer, place_ref: (layer, 0, place_ref[0]))
    return pl.pallas_call(
        kernel,
        grid_spec=pltpu.PrefetchScalarGridSpec(
            num_scalar_prefetch=1,
            grid=(layers,),
            in_specs=[
                pl.BlockSpec((1, shard, piece), lambda layer, place_ref: (layer, 0, place_ref[1])),
                pl.BlockSpec((1, piece, shard), lambda layer, place_ref: (layer, place_ref[1], 0)),
                column,
                column,
                column,
                column,
            ]
            + [pl.BlockSpec(param.shape, lambda layer, place_ref: (0, 0)) for param in small_params],
            out_specs=[
                pl.BlockSpec((1, shard, piece + LANES), lambda layer, place_ref: (layer, 0, 0)),
                pl.BlockSpec((1, shard, piece), lambda layer, place_ref: (layer, 0, 0)),
                pl.BlockSpec((1, shard + 32, width), lambda layer, place_ref: (layer, 0, 0)),
            ],
        ),
        out_shape=[
            jax.ShapeDtypeStruct((layers, shard, piece + LANES), jnp.bfloat16),
            jax.ShapeDtypeStruct((layers, shard, piece), jnp.bfloat16),
            jax.ShapeDtypeStruct((layers, shard + 32, width), jnp.bfloat16),
        ],
        cost_estimate=lasting(4),
        name="own_pieces",
    )(
        jnp.stack([here, first_block]).astype(jnp.int32),
        inner_weight,
        outer_weight,
        out_weight,
        *joint_weights,
        *small_params,
    )


def own_blocks(inner_weight, outer_weight, out_weight, inner_order, out_order, after):
    layers, shard, hidden = inner_weight.shape
    piece = hidden // 8

    def kernel(inner_order_ref, out_order_ref, *refs):
        ins, (inner_out, outer_out, out_out) = refs[:16], refs[-3:]
        for j in range(4):
            inner_out[0, j] = low(ins[j][0])
            outer_out[0, j] = low(ins[4 + j][0]).T
        for j in range(8):
            out_out[0, :, j * LANES : (j + 1) * LANES] = low(ins[8 + j][0])

    def inner_at(j):
        return pl.BlockSpec((1, shard, piece), lambda layer, inner_ref, out_ref: (layer, 0, inner_ref[layer * 4 + j]))

    def outer_at(j):
        return pl.BlockSpec((1, piece, shard), lambda layer, inner_ref, out_ref: (layer, inner_ref[layer * 4 + j], 0))

    def out_at(j):
        return pl.BlockSpec((1, shard, LANES), lambda layer, inner_ref, out_ref: (layer, 0, out_ref[layer * 8 + j]))

    block = pl.BlockSpec((1, 4, shard, piece), lambda layer, *_: (layer, 0, 0, 0))
    return pl.pallas_call(
        kernel,
        grid_spec=pltpu.PrefetchScalarGridSpec(
            num_scalar_prefetch=2,
            grid=(layers,),
            in_specs=[inner_at(j) for j in range(4)]
            + [outer_at(j) for j in range(4)]
            + [out_at(j) for j in range(8)]
            + [pl.BlockSpec(memory_space=pl.ANY)],
            out_specs=[block, block, pl.BlockSpec((1, shard, 8 * LANES), lambda layer, *_: (layer, 0, 0))],
        ),
        out_shape=[
            jax.ShapeDtypeStruct((layers, 4, shard, piece), jnp.bfloat16),
            jax.ShapeDtypeStruct((layers, 4, shard, piece), jnp.bfloat16),
            jax.ShapeDtypeStruct((layers, shard, 8 * LANES), jnp.bfloat16),
        ],
        cost_estimate=lasting(7),
        name="own_blocks",
    )(inner_order, out_order, *[inner_weight] * 4, *[outer_weight] * 4, *[out_weight] * 8, after)


def place_pieces(pieces, order, layer, previous):
    count, shard, columns = pieces.shape
    piece = (columns - 4 * LANES) // 2
    width = 8 * LANES

    def column(index, order_ref):
        return (layer, 0, order_ref[index])

    def inner_place(index, order_ref):
        return (order_ref[index] % 2) * 4 + order_ref[index] // 2

    square = jax.ShapeDtypeStruct((LAYERS, shard, width), jnp.float32)
    outs = [square] * 4 + [
        jax.ShapeDtypeStruct((LAYERS, shard, 8 * piece), jnp.float32),
        jax.ShapeDtypeStruct((LAYERS, 8 * piece, shard), jnp.float32),
        jax.ShapeDtypeStruct((8, LANES), jnp.float32),
    ]
    specs = [pl.BlockSpec((1, shard, LANES), column)] * 4 + [
        pl.BlockSpec((1, shard, piece), lambda i, order_ref: (layer, 0, inner_place(i, order_ref))),
        pl.BlockSpec((1, piece, shard), lambda i, order_ref: (layer, inner_place(i, order_ref), 0)),
        pl.BlockSpec((8, LANES), lambda i, order_ref: (0, 0)),
    ]

    def kernel(order_ref, source, *refs):
        query_out, key_out, value_out, out_out, inner_out, outer_out, token_out = refs[-7:]
        token_out[...] = jnp.zeros_like(token_out)
        inner_out[0] = wide(source[0, :, :piece])
        outer_out[0] = wide(source[0, :, piece : 2 * piece].T)
        for at, ref in enumerate((out_out, query_out, key_out, value_out)):
            begin = 2 * piece + at * LANES
            ref[0] = wide(source[0, :, begin : begin + LANES])

    held = [] if previous is None else list(previous)
    return pl.pallas_call(
        kernel,
        grid_spec=pltpu.PrefetchScalarGridSpec(
            num_scalar_prefetch=1,
            grid=(count,),
            in_specs=[pl.BlockSpec((1, shard, columns), lambda i, order_ref: (i, 0, 0))]
            + [pl.BlockSpec(memory_space=pl.ANY)] * len(held),
            out_specs=specs,
        ),
        out_shape=outs,
        input_output_aliases={2 + i: i for i in range(len(held))},
        cost_estimate=lasting(count * 5 // 4),
        name="place_pieces",
    )(order, pieces, *held)


def half_erfc(values_in):
    scaled = values_in * (2.0**-0.5)
    part = 1.0 / (1.0 + 0.5 * scaled)
    series = 0.17087277
    for coefficient in (
        -0.82215223,
        1.48851587,
        -1.13520398,
        0.27886807,
        -0.18628806,
        0.09678418,
        0.37409196,
        1.00002368,
        -1.26551223,
    ):
        series = coefficient + part * series
    return 0.5 * part * jnp.exp(series - scaled * scaled)


def load_weights(step, own_inner, own_outer, inner_refs, outer_refs, inner_now, outer_now):
    shard = own_inner.shape[2]
    inner_now[:shard] = own_inner[0, 0]
    outer_now[:shard] = own_outer[0, 0]
    if len(inner_refs) == 1:
        inner_now[shard:] = inner_refs[0][0]
        outer_now[shard:] = outer_refs[0][0]
        return
    chunks = len(inner_refs) // 4
    rows = inner_refs[0].shape[0]
    for j in range(4):

        @pl.when(step == j)
        def _(j=j):
            for chunk in range(chunks):
                begin = shard + chunk * rows
                inner_now[begin : begin + rows] = inner_refs[j * chunks + chunk][...]
                outer_now[begin : begin + rows] = outer_refs[j * chunks + chunk][...]


def weight_operands(weights, layer):
    own_inner, own_outer, inner_parts, outer_parts = weights
    shard, piece = own_inner.shape[2:]
    own = pl.BlockSpec((1, 1, shard, piece), lambda i: (layer, i, 0, 0))
    if len(inner_parts) == 1:
        rest = inner_parts[0].shape[1]
        parts = [pl.BlockSpec((1, rest, piece), lambda i, at=at: (i, 0, at)) for at in range(2)]
        return ([own_inner, own_outer, *inner_parts, *outer_parts], [own, own, *parts], 1)
    rows = inner_parts[0].shape[0]
    fixed = pl.BlockSpec((rows, piece), lambda i: (0, 0), pipeline_mode=pl.Buffered(1))
    return (
        [own_inner, own_outer, *inner_parts, *outer_parts],
        [own, own] + [fixed] * (2 * len(inner_parts)),
        len(inner_parts),
    )


def accumulate(step, total, part):
    @pl.when(step == 0)
    def _():
        total[...] = part

    @pl.when(step > 0)
    def _():
        total[...] += part


def finish_pair(step, total, near_ref, far_ref):
    rows = near_ref.shape[0]

    @pl.when(step == pl.num_programs(0) - 1)
    def _():
        near_ref[...] = total[:rows]
        far_ref[...] = low(total[rows:])


def feed_forward_kernel(count, hidden_ref, bias_ref, own_inner, own_outer, *refs):
    inner_refs, outer_refs = refs[:count], refs[count : 2 * count]
    near_ref, far_ref, active_ref, slope_ref, total, inner_now, outer_now = refs[2 * count :]
    step = pl.program_id(0)
    load_weights(step, own_inner, own_outer, inner_refs, outer_refs, inner_now, outer_now)
    pre = mm(hidden_ref[...], inner_now[...]) + bias_ref[...]
    tail = half_erfc(jnp.abs(pre))
    below = jnp.where(pre < 0.0, tail, 1.0 - tail)
    active = low(pre * below)
    active_ref[...] = active
    slope_ref[...] = low(below + pre * (jnp.exp(-0.5 * pre * pre) * 0.3989422804014327))
    accumulate(step, total, mm(active, outer_now[...], NT))
    finish_pair(step, total, near_ref, far_ref)


def feed_forward(hidden_pair, bias_row, weights, layer):
    rows, width = hidden_pair.shape
    hidden = bias_row.shape[1]
    block = hidden // 4
    arrays, specs, count = weight_operands(weights, layer)
    column = pl.BlockSpec((rows, block), lambda i: (0, i))
    half = pl.BlockSpec((rows // 2, width), lambda i: (0, 0))
    return pl.pallas_call(
        functools.partial(feed_forward_kernel, count),
        grid=(4,),
        in_specs=[
            pl.BlockSpec((rows, width), lambda i: (0, 0)),
            pl.BlockSpec((1, block), lambda i: (0, i)),
            *specs,
        ],
        out_specs=[half, half, column, column],
        out_shape=[
            jax.ShapeDtypeStruct((rows // 2, width), jnp.float32),
            jax.ShapeDtypeStruct((rows // 2, width), jnp.bfloat16),
            jax.ShapeDtypeStruct((rows, hidden), jnp.bfloat16),
            jax.ShapeDtypeStruct((rows, hidden), jnp.bfloat16),
        ],
        scratch_shapes=[
            pltpu.VMEM((rows, width), jnp.float32),
            pltpu.VMEM((width, block), jnp.bfloat16),
            pltpu.VMEM((width, block), jnp.bfloat16),
        ],
        cost_estimate=lasting(16),
        name="feed_forward",
    )(hidden_pair, bias_row, *arrays)


def feed_backward_kernel(count, grad_ref, slope_ref, own_inner, own_outer, *refs):
    inner_refs, outer_refs = refs[:count], refs[count : 2 * count]
    near_ref, far_ref, inner_grad_ref, bias_ref, total, inner_now, outer_now = refs[2 * count :]
    step = pl.program_id(0)
    load_weights(step, own_inner, own_outer, inner_refs, outer_refs, inner_now, outer_now)
    inner_grad = low(mm(grad_ref[...], outer_now[...]) * wide(slope_ref[...]))
    inner_grad_ref[...] = inner_grad
    bias_ref[...] = jnp.sum(wide(inner_grad), axis=0, keepdims=True)
    accumulate(step, total, mm(inner_grad, inner_now[...], NT))
    finish_pair(step, total, near_ref, far_ref)


def feed_backward(grad_pair, slope, weights, layer):
    rows, width = grad_pair.shape
    hidden = slope.shape[1]
    block = hidden // 4
    arrays, specs, count = weight_operands(weights, layer)
    column = pl.BlockSpec((rows, block), lambda i: (0, i))
    half = pl.BlockSpec((rows // 2, width), lambda i: (0, 0))
    return pl.pallas_call(
        functools.partial(feed_backward_kernel, count),
        grid=(4,),
        in_specs=[pl.BlockSpec((rows, width), lambda i: (0, 0)), column, *specs],
        out_specs=[half, half, column, pl.BlockSpec((1, block), lambda i: (0, i))],
        out_shape=[
            jax.ShapeDtypeStruct((rows // 2, width), jnp.float32),
            jax.ShapeDtypeStruct((rows // 2, width), jnp.bfloat16),
            jax.ShapeDtypeStruct((rows, hidden), jnp.bfloat16),
            jax.ShapeDtypeStruct((1, hidden), jnp.float32),
        ],
        scratch_shapes=[
            pltpu.VMEM((rows, width), jnp.float32),
            pltpu.VMEM((width, block), jnp.bfloat16),
            pltpu.VMEM((width, block), jnp.bfloat16),
        ],
        cost_estimate=lasting(11),
        name="feed_backward",
    )(grad_pair, slope, *arrays)


def weight_gradient_kernel(
    split,
    rows_ref,
    hidden_ref,
    grad_ref,
    mixed_ref,
    inner_grad_ref,
    active_ref,
    branch_ref,
    after_ref,
    *refs,
):
    outs, (hidden_t, grad_t, mixed_t) = refs[:-3], refs[-3:]
    step = pl.program_id(0)
    piece = active_ref.shape[1]

    @pl.when(step == 0)
    def _():
        hidden_t[...] = hidden_ref[...].T
        grad_t[...] = grad_ref[...].T
        mixed_t[...] = mixed_ref[...].T

    def write(store):
        store(0, piece, low(mm(hidden_t[...], inner_grad_ref[...])))
        store(piece, 2 * piece, low(mm(grad_t[...], active_ref[...])))
        store(2 * piece, 2 * piece + LANES, low(mm(mixed_t[...], branch_ref[...])))

    if not split:
        first_out, second_out = outs

        def store(begin, end, value):
            shard = value.shape[0] // 4
            ref = second_out if begin == piece else first_out
            column = {0: 0, piece: 0, 2 * piece: piece}[begin]
            for r in range(4):
                place = pl.multiple_of(rows_ref[r] * shard, shard)
                ref[0, pl.ds(place, shard), column : column + end - begin] = value[r * shard : (r + 1) * shard]

        write(store)
        return
    first_keep, first_send, second_keep, second_send = outs
    for j in range(4):

        @pl.when(step == j)
        def _(j=j):
            first = (first_send if j % 2 else first_keep, j // 2)
            second = (second_send if j // 2 else second_keep, j % 2)

            def store(begin, end, value):
                half = value.shape[0] // 2
                first[0][first[1], :, begin:end] = value[:half]
                second[0][second[1], :, begin:end] = value[half:]

            write(store)


def weight_gradients(hidden_pair, grad_pair, mixed_pair, inner_grad, active, branch_pair, plane_rows, split, after):
    rows, width = hidden_pair.shape
    hidden = active.shape[1]
    piece = hidden // 4
    total = 2 * piece + LANES
    whole = pl.BlockSpec((rows, width), lambda i, rows_ref: (0, 0))
    column = pl.BlockSpec((rows, piece), lambda i, rows_ref: (0, i))
    if split:
        shape = (2, width // 2, total)
        out_specs = [pl.BlockSpec(shape, lambda i, rows_ref: (0, 0, 0), pipeline_mode=pl.Buffered(1))] * 4
        out_shape = [jax.ShapeDtypeStruct(shape, jnp.bfloat16)] * 4
    else:
        out_specs = [
            pl.BlockSpec((1, width, columns), lambda i, rows_ref: (i, 0, 0)) for columns in (piece + LANES, piece)
        ]
        out_shape = [jax.ShapeDtypeStruct((4, width, columns), jnp.bfloat16) for columns in (piece + LANES, piece)]
    return pl.pallas_call(
        functools.partial(weight_gradient_kernel, split),
        grid_spec=pltpu.PrefetchScalarGridSpec(
            num_scalar_prefetch=1,
            grid=(4,),
            in_specs=[
                whole,
                whole,
                whole,
                column,
                column,
                pl.BlockSpec((rows, LANES), lambda i, rows_ref: (0, i)),
                pl.BlockSpec(memory_space=pl.ANY),
            ],
            out_specs=out_specs,
            scratch_shapes=[pltpu.VMEM((width, rows), jnp.bfloat16)] * 3,
        ),
        out_shape=out_shape,
        cost_estimate=lasting(13),
        name="weight_gradients",
    )(plane_rows, hidden_pair, grad_pair, mixed_pair, inner_grad, active, branch_pair, after)


def block_columns(values_in, order, width):
    return jnp.concatenate(
        [lax.dynamic_slice_in_dim(values_in, block * width, width, 1) for block in order], axis=1
    )


def norm_forward(values_in, gain_row, shift_row):
    centre = values_in - jnp.mean(values_in, axis=-1, keepdims=True)
    spread = jnp.mean(centre * centre, axis=-1, keepdims=True)
    inverse = lax.rsqrt(spread + epsilon)
    unit = centre * inverse
    return (unit * gain_row + shift_row, unit, inverse)


def norm_backward(grad, unit, inverse, gain_row):
    grad_unit = grad * gain_row
    back = inverse * (
        grad_unit
        - jnp.mean(grad_unit, axis=-1, keepdims=True)
        - unit * jnp.mean(grad_unit * unit, axis=-1, keepdims=True)
    )
    return (back, jnp.sum(grad * unit, axis=0), jnp.sum(grad, axis=0))


def attention_output_kernel(
    place_ref,
    heads_ref,
    own_ref,
    near_ref,
    far_ref,
    activation_ref,
    bias_ref,
    gain_ref,
    shift_ref,
    mixed_ref,
    unit_ref,
    inverse_ref,
    hidden_ref,
    turned_ref,
    held,
    held_low,
):
    shard = own_ref.shape[0]
    half = near_ref.shape[1]
    for p in range(8):
        mixed_ref[:, p * LANES : (p + 1) * LANES] = heads_ref[place_ref[p]]
    own, rest = mixed_ref[:, :shard], mixed_ref[:, shard:]
    held[:, :half] = mm(own, own_ref[:, :half]) + mm(rest, near_ref[...])
    held[:, half:] = mm(own, own_ref[:, half:]) + mm(rest, far_ref[...])
    attended = jnp.concatenate(
        [held[:, pl.ds(pl.multiple_of(place_ref[8 + b] * LANES, LANES), LANES)] for b in range(8)], axis=1
    )
    first_pre = wide(activation_ref[...]) + (attended + bias_ref[...])
    hidden, unit, inverse = norm_forward(first_pre, gain_ref[...], shift_ref[...])
    unit_ref[...] = unit
    inverse_ref[...] = inverse
    hidden_ref[...] = hidden
    held_low[...] = low(hidden)
    for r in range(4):
        turned_ref[:, r * shard : (r + 1) * shard] = held_low[
            :, pl.ds(pl.multiple_of(place_ref[16 + r] * shard, shard), shard)
        ]


def attention_output(heads, out_weights, activation, bias_row, gain_row, shift_row, places):
    rows, width = activation.shape
    wide_rows = jax.ShapeDtypeStruct((rows, width), jnp.float32)
    low_rows = jax.ShapeDtypeStruct((rows, width), jnp.bfloat16)
    return pl.pallas_call(
        attention_output_kernel,
        grid_spec=pltpu.PrefetchScalarGridSpec(
            num_scalar_prefetch=1,
            grid=(1,),
            in_specs=[
                pl.BlockSpec(array.shape, lambda i, place_ref, rank=array.ndim: (0,) * rank)
                for array in (heads, *out_weights, activation, bias_row, gain_row, shift_row)
            ],
            out_specs=[
                pl.BlockSpec((rows, width), lambda i, place_ref: (0, 0)),
                pl.BlockSpec((rows, width), lambda i, place_ref: (0, 0)),
                pl.BlockSpec((rows, 1), lambda i, place_ref: (0, 0)),
                pl.BlockSpec((rows, width), lambda i, place_ref: (0, 0)),
                pl.BlockSpec((rows, width), lambda i, place_ref: (0, 0)),
            ],
            scratch_shapes=[pltpu.VMEM((rows, width), jnp.float32), pltpu.VMEM((rows, width), jnp.bfloat16)],
        ),
        out_shape=[low_rows, wide_rows, jax.ShapeDtypeStruct((rows, 1), jnp.float32), wide_rows, low_rows],
        cost_estimate=lasting(5),
        name="attention_output",
    )(places, heads, *out_weights, activation, bias_row, gain_row, shift_row)


def attention_output_back_kernel(
    place_ref,
    near_back_ref,
    came_ref,
    grad_ref,
    unit_ref,
    inverse_ref,
    gain_ref,
    own_ref,
    near_ref,
    far_ref,
    first_ref,
    rows_ref,
    spread_ref,
    sent_ref,
    held,
    held_low,
):
    shard = own_ref.shape[0]
    half = near_ref.shape[1]
    held[...] = near_back_ref[...] + wide(came_ref[...])
    back = jnp.concatenate(
        [held[:, pl.ds(pl.multiple_of(place_ref[16 + r] * shard, shard), shard)] for r in range(4)], axis=1
    )
    grad_first, gain_row, shift_row = norm_backward(
        grad_ref[...] + back, unit_ref[...], inverse_ref[...], gain_ref[...]
    )
    first_ref[...] = grad_first
    branch = low(grad_first)
    rows_ref[0:1] = gain_row[None]
    rows_ref[1:2] = shift_row[None]
    rows_ref[2:3] = jnp.sum(wide(branch), axis=0, keepdims=True)
    held_low[...] = branch
    for p in range(8):
        spread_ref[:, p * LANES : (p + 1) * LANES] = held_low[
            :, pl.ds(pl.multiple_of(place_ref[24 + p] * LANES, LANES), LANES)
        ]
    spread = spread_ref[...]
    held_low[:, :shard] = low(mm(spread, own_ref[...], NT))
    held_low[:, shard:] = low(mm(spread[:, :half], near_ref[...], NT) + mm(spread[:, half:], far_ref[...], NT))
    for head in range(8):
        begin = place_ref[16 + head // 2] * shard + (head % 2) * LANES
        sent_ref[head] = held_low[:, pl.ds(pl.multiple_of(begin, LANES), LANES)]


def attention_output_back(near_back, came, grad_second, unit, inverse, gain_row, out_weights, places):
    rows, width = grad_second.shape
    operands = (near_back, came, grad_second, unit, inverse, gain_row, *out_weights)
    whole = pl.BlockSpec((rows, width), lambda i, place_ref: (0, 0))
    return pl.pallas_call(
        attention_output_back_kernel,
        grid_spec=pltpu.PrefetchScalarGridSpec(
            num_scalar_prefetch=1,
            grid=(1,),
            in_specs=[pl.BlockSpec(array.shape, lambda i, place_ref: (0, 0)) for array in operands],
            out_specs=[
                whole,
                pl.BlockSpec((3, width), lambda i, place_ref: (0, 0)),
                whole,
                pl.BlockSpec((8, rows, LANES), lambda i, place_ref: (0, 0, 0)),
            ],
            scratch_shapes=[pltpu.VMEM((rows, width), jnp.float32), pltpu.VMEM((rows, width), jnp.bfloat16)],
        ),
        out_shape=[
            jax.ShapeDtypeStruct((rows, width), jnp.float32),
            jax.ShapeDtypeStruct((3, width), jnp.float32),
            jax.ShapeDtypeStruct((rows, width), jnp.bfloat16),
            jax.ShapeDtypeStruct((8, rows, LANES), jnp.bfloat16),
        ],
        cost_estimate=lasting(6),
        name="attention_output_back",
    )(places, *operands)


def token_gradient_kernel(
    place_ref, query_ref, key_ref, value_ref, joint_ref, *refs
):
    near_ref, far_ref, packed_ref, bias_ref = refs[-4:]
    step = pl.program_id(0)
    packed = jnp.concatenate([query_ref[...], key_ref[...], value_ref[...]], axis=1)
    packed_ref[...] = packed
    accumulate(step, bias_ref, jnp.sum(wide(packed), axis=0, keepdims=True))
    part = mm(packed, joint_ref[...], NT)

    @pl.when(step < 4)
    def _():
        near_ref[0] = part

    @pl.when(step >= 4)
    def _():
        far_ref[0] = low(part)


def token_gradients(grads, joint, chips):
    tokens = grads[0].shape[0]
    rows = tokens // 8
    width, columns = joint.shape
    block = pl.BlockSpec((rows, LANES), lambda i, place_ref: (i, 0))
    return pl.pallas_call(
        token_gradient_kernel,
        grid_spec=pltpu.PrefetchScalarGridSpec(
            num_scalar_prefetch=1,
            grid=(8,),
            in_specs=[block, block, block, pl.BlockSpec((width, columns), lambda i, place_ref: (0, 0))],
            out_specs=[
                pl.BlockSpec((1, rows, width), lambda i, place_ref: (place_ref[jnp.minimum(i, 3)], 0, 0)),
                pl.BlockSpec((1, rows, width), lambda i, place_ref: (place_ref[jnp.maximum(i - 4, 0)], 0, 0)),
                pl.BlockSpec((rows, columns), lambda i, place_ref: (i, 0)),
                pl.BlockSpec((1, columns), lambda i, place_ref: (0, 0)),
            ],
        ),
        out_shape=[
            jax.ShapeDtypeStruct((4, rows, width), jnp.float32),
            jax.ShapeDtypeStruct((4, rows, width), jnp.bfloat16),
            jax.ShapeDtypeStruct((tokens, columns), jnp.bfloat16),
            jax.ShapeDtypeStruct((1, columns), jnp.float32),
        ],
        cost_estimate=lasting(10),
        name="token_gradients",
    )(chips, *grads, joint)


def plane_sum_kernel(first_keep, first_came, first_last, second_keep, second_came, second_last, *outs):
    shard = outs[0].shape[0]
    first = wide(first_keep[0]) + wide(first_came[0]) + wide(first_last[...])
    second = wide(second_keep[0]) + wide(second_came[0]) + wide(second_last[...])
    outs[0][...] = first[:shard]
    outs[1][...] = low(first[shard:])
    outs[2][...] = low(second[:shard])
    outs[3][...] = low(second[shard:])


def plane_sum(first, second):
    columns = first[0].shape[2]
    shard = first[0].shape[1] // 2
    block = pl.BlockSpec((1, 2 * shard, columns), lambda i: (0, 0, 0))
    last = pl.BlockSpec((2 * shard, columns), lambda i: (0, 0))
    return pl.pallas_call(
        plane_sum_kernel,
        grid=(1,),
        in_specs=[block, block, last] * 2,
        out_specs=[pl.BlockSpec((shard, columns), lambda i: (0, 0))] * 4,
        out_shape=[jax.ShapeDtypeStruct((shard, columns), jnp.float32)]
        + [jax.ShapeDtypeStruct((shard, columns), jnp.bfloat16)] * 3,
        cost_estimate=lasting(3),
        name="plane_sum",
    )(*first, *second)


def final_sum_kernel(*refs):
    left_ref, right_ref = refs[-2:]
    half = left_ref.shape[1]
    whole = jnp.concatenate(
        [
            low(wide(refs[at][...]) + wide(refs[at + 1][...]) + wide(refs[at + 2][...]) + wide(refs[at + 3][...]))
            for at in (0, 4)
        ],
        axis=1,
    )
    left_ref[...] = whole[:, :half]
    right_ref[...] = whole[:, half:]


def final_sum(plain, joint):
    shard = plain[0].shape[0]
    half = (plain[0].shape[1] + joint[0].shape[1]) // 2
    operands = (*plain, *joint)
    return pl.pallas_call(
        final_sum_kernel,
        grid=(1,),
        in_specs=[pl.BlockSpec(array.shape, lambda i: (0, 0)) for array in operands],
        out_specs=[pl.BlockSpec((shard, half), lambda i: (0, 0))] * 2,
        out_shape=[jax.ShapeDtypeStruct((shard, half), jnp.bfloat16)] * 2,
        cost_estimate=lasting(3),
        name="final_sum",
    )(*operands)


def small_rows_kernel(place_ref, joint_ref, first_ref, outer_ref, gain_ref, shift_ref, inner_ref, out_ref):
    shard = out_ref.shape[1] // 4
    out_ref[...] = jnp.zeros_like(out_ref)
    at = pl.ds(pl.multiple_of(place_ref[0] * LANES, LANES), LANES)
    out_ref[0:1, at] = joint_ref[:, :LANES]
    out_ref[1:2, at] = joint_ref[:, 2 * LANES :]
    out_ref[2:3] = first_ref[2:3]
    out_ref[3:4] = outer_ref[...]
    out_ref[4:6] = first_ref[0:2]
    out_ref[6:7] = gain_ref[...]
    out_ref[7:8] = shift_ref[...]
    count = inner_ref.shape[1] // shard // 4
    for j in range(4):
        block = place_ref[1 + j]
        columns = pl.ds(pl.multiple_of((block // 2) * shard, shard), shard)
        for part in range(count):
            begin = (j * count + part) * shard
            row = 8 + (block % 2) * count + part
            out_ref[pl.ds(row, 1), columns] = inner_ref[:, begin : begin + shard]


def small_rows(places, joint, first, outer, gain, shift, inner):
    width = first.shape[1]
    operands = (joint, first, outer[None], gain[None], shift[None], inner)
    return pl.pallas_call(
        small_rows_kernel,
        grid_spec=pltpu.PrefetchScalarGridSpec(
            num_scalar_prefetch=1,
            grid=(1,),
            in_specs=[pl.BlockSpec(array.shape, lambda i, place_ref: (0, 0)) for array in operands],
            out_specs=pl.BlockSpec((16, width), lambda i, place_ref: (0, 0)),
        ),
        out_shape=jax.ShapeDtypeStruct((16, width), jnp.float32),
        cost_estimate=lasting(2),
        name="small_rows",
    )(places, *operands)


def gate(values_in, *points):
    anywhere = pl.BlockSpec(memory_space=pl.ANY)
    return pl.pallas_call(
        lambda *refs: None,
        in_specs=[anywhere] * (len(values_in) + len(points)),
        out_specs=[anywhere] * len(values_in),
        out_shape=[jax.ShapeDtypeStruct(value.shape, value.dtype) for value in values_in],
        input_output_aliases={i: i for i in range(len(values_in))},
        cost_estimate=SMALL_COST,
        name="gate",
    )(*values_in, *points)


def spread_tokens(rows_in):
    half = rows_in.shape[1] // 2
    left, right = rows_in[:, :half], rows_in[:, half:]
    left_pair = jnp.stack([left, swap(left, ALONG_X)])
    right_pair = jnp.stack([right, swap(right, ALONG_Y)])
    left_far = swap(left_pair, ALONG_Y)
    right_far = swap(right_pair, ALONG_X)
    left_all = jnp.concatenate([left_pair, left_far])
    right_all = jnp.stack([right_pair[0], right_far[0], right_pair[1], right_far[1]])
    near = jnp.concatenate([left_all, right_all], axis=2).reshape(4 * rows_in.shape[0], rows_in.shape[1])
    return (near, swap(near, CORE))


def plane_groups():
    count = lax.axis_size("ctx")
    return [list(range(0, count, 2)), list(range(1, count, 2))]


def collect_tokens(sent, points, late_points):
    if points:
        (sent,) = gate([sent], *points)
    came = lax.all_to_all(sent, "ctx", 0, 0, axis_index_groups=plane_groups(), tiled=True)
    if late_points:
        (came,) = gate([came], *late_points)
    return jnp.sum(wide(came), axis=0)


def plane_pieces(left, right, *points):
    left_pair = jnp.stack([left, swap(left, ALONG_X)])
    right_pair = jnp.stack([right, swap(right, ALONG_Y)])
    left_far, right_far = gate([swap(left_pair, ALONG_Y), swap(right_pair, ALONG_X)], *points)
    left_all = jnp.concatenate([left_pair, left_far])
    right_all = jnp.stack([right_pair[0], right_far[0], right_pair[1], right_far[1]])
    near = jnp.concatenate([left_all, right_all], axis=2)
    return (near, swap(near, CORE))


def exchange(blocks):
    return lax.all_to_all(blocks, "ctx", 0, 0, tiled=True)


def head_split_body(
    tokens,
    cotangent,
    doc_starts,
    doc_lengths,
    query_weight,
    key_weight,
    value_weight,
    out_weight,
    inner_weight,
    outer_weight,
    query_bias,
    value_bias,
    out_bias,
    inner_bias,
    outer_bias,
    first_gain,
    first_shift,
    second_gain,
    second_shift,
):
    rows = tokens.shape[1]
    width = tokens.shape[2]
    here = lax.axis_index("ctx")
    plane = lax.axis_index("wsh")
    planes = lax.axis_size("wsh")
    shard = width // planes
    hidden = inner_weight.shape[2]
    piece = hidden // 8
    core = here % 2
    chip = here // 2
    relative = jnp.arange(8, dtype=jnp.int32)
    spread = jnp.array((0, 2, 4, 6, 1, 3, 5, 7), jnp.int32)
    turned = [(plane - r) % planes for r in range(planes)]
    unturned = turned
    positions = ((here ^ spread)[:, None] * rows + jnp.arange(rows, dtype=jnp.int32)).reshape(-1)
    labels = doc_labels(positions, doc_starts[0], doc_lengths[0])[:, None]

    four = jnp.arange(4, dtype=jnp.int32)
    chip_order = [chip ^ four, four]
    inner_order = [core * 4 + order for order in chip_order]
    out_order = [jnp.concatenate([2 * order + core, 2 * order + 1 - core]) for order in chip_order]
    block_order = here ^ spread
    plane_rows = jnp.stack(turned).astype(jnp.int32)
    first_own, second_own, joint_own = own_pieces(
        inner_weight,
        outer_weight,
        out_weight,
        (query_weight, key_weight, value_weight),
        (
            query_bias,
            value_bias,
            out_bias,
            outer_bias,
            first_gain,
            first_shift,
            second_gain,
            second_shift,
            inner_bias,
        ),
        here,
        core * 4 + chip,
    )
    joint_width = 3 * LANES

    def ordered(stack, order):
        return jnp.concatenate([lax.dynamic_index_in_dim(stack, i, 0, keepdims=False) for i in order], axis=0)

    first_joint = joint_own[0]
    joint_turned = jnp.stack([first_joint] + [turn(first_joint, r) for r in range(1, planes)])
    joint_first = ordered(joint_turned[:, :shard], unturned)
    small_all = ordered(joint_turned[:, None, shard:, :shard], unturned)

    def small(layer, index):
        return small_all[:, 2 * index + layer].reshape(width)

    inner_bias_all = small_all[:, 16:24].reshape(planes, 4, LAYERS, shard).transpose(2, 0, 1, 3).reshape(LAYERS, hidden)

    inner_near = ordered(lax.all_gather(first_own[0], "wsh", axis=0), turned[1:])
    first_tokens = spread_tokens(tokens[0])
    (outer_sent,) = gate([second_own[0]], first_tokens[0])
    outer_stack = lax.all_gather(outer_sent, "wsh", axis=0)
    middle = 3 * shard // 2

    def spread_first(near):
        left, right = near[:middle], near[middle:]
        return (left, right, swap(left, ALONG_X), swap(right, ALONG_Y))

    def spread_second(left, right, left_x, right_y):
        lefts = (left, left_x, swap(left, ALONG_Y), swap(left_x, ALONG_Y))
        rights = (right, swap(right, ALONG_X), right_y, swap(right_y, ALONG_X))
        return [part for pair in zip(lefts, rights) for part in pair]

    inner_half = spread_first(inner_near)
    layer_own = jnp.concatenate(
        [first_own[1, :, :piece], second_own[1], first_own[1, :, piece:], joint_own[1, :shard]], axis=1
    )
    wide_piece = 2 * piece + LANES

    def layer_weights(layer):
        if layer == 0:
            near = jnp.concatenate(
                [
                    jnp.concatenate([inner_first[2 * j][:, piece:], inner_first[2 * j + 1][:, piece:]], axis=0)
                    for j in range(4)
                ],
                axis=1,
            )
            weights = (inner_own, outer_own, inner_first, outer_first)
        else:
            near = jnp.concatenate([out_parts[j] for j in range(4)], axis=1)
            weights = (inner_own, outer_own)
        return (weights, (out_own[layer], near, swap(near, CORE)))

    def out_place(layer, block):
        at = (block // 2) ^ chip if layer == 0 else block // 2
        return at + 4 * ((block % 2) ^ core)

    activation = tokens[0]
    stashed = []
    outputs = []
    for layer in range(LAYERS):
        joint = joint_first if layer == 0 else joint_second
        first_gain_row, first_shift_row = wide(small(layer, 4)), wide(small(layer, 5))
        second_gain_row, second_shift_row = wide(small(layer, 6)), wide(small(layer, 7))

        near_tokens, far_tokens = first_tokens if layer == 0 else spread_tokens(activation)
        everyone = jnp.concatenate([near_tokens, far_tokens], axis=0)
        query_bias_own = lax.dynamic_slice_in_dim(small(layer, 0), here * LANES, LANES, 0)
        value_bias_own = lax.dynamic_slice_in_dim(small(layer, 1), here * LANES, LANES, 0)
        joint_bias = wide(jnp.concatenate([query_bias_own, jnp.zeros_like(query_bias_own), value_bias_own]))
        packed = low(mm(everyone, joint) + joint_bias)
        if layer == 0:
            packed, layer_own = gate([packed, layer_own], inner_near)
            second_stack = lax.all_gather(layer_own, "wsh", axis=0)
        mixed, log_all = attention_forward(packed, labels, block_order)
        if layer == 0:
            inner_own, outer_own, out_own = own_blocks(
                inner_weight,
                outer_weight,
                out_weight,
                jnp.concatenate(inner_order),
                jnp.concatenate(out_order),
                mixed,
            )
            left_x, right_y, outer_stack = gate([*inner_half[2:], outer_stack], mixed)
            inner_first = spread_second(*inner_half[:2], left_x, right_y)
            outer_first = spread_second(*spread_first(ordered(outer_stack, turned[1:])))
        else:
            out_parts = lax.all_to_all(
                jnp.broadcast_to(out_second, (4, *out_second.shape)),
                "ctx",
                0,
                0,
                axis_index_groups=plane_groups(),
                tiled=True,
            )
            (out_parts,) = gate([out_parts], mixed)
        weights, out_weights = layer_weights(layer)
        mixed_heads = exchange(mixed)
        places = jnp.stack(
            [2 * turned[p // 2] + p % 2 for p in range(8)]
            + [out_place(layer, b) for b in range(8)]
            + turned
            + [jnp.int32(0)] * 4
            + [out_order[layer][p] for p in range(8)]
        ).astype(jnp.int32)
        mixed_turned, first_unit, first_inverse, hidden_rows, hidden_turned = attention_output(
            mixed_heads,
            out_weights,
            activation,
            wide(small(layer, 2))[None],
            first_gain_row[None],
            first_shift_row[None],
            places,
        )
        if layer == 1:
            second_parts = gate([second_parts], hidden_turned)
            weights = (*weights, second_parts, second_parts)
        mixed_pair = jnp.concatenate([mixed_turned, swap(mixed_turned, CORE)], axis=0)
        hidden_pair = jnp.concatenate([hidden_turned, swap(hidden_turned, CORE)], axis=0)
        inner_bias_own = jnp.concatenate(
            [lax.dynamic_slice_in_dim(inner_bias_all[layer], inner_order[layer][j] * piece, piece, 0) for j in range(4)]
        )
        outer_near, outer_far, active, slope = feed_forward(
            hidden_pair, wide(inner_bias_own)[None], weights, layer
        )
        outer_turned = outer_near + wide(swap(outer_far, CORE))
        if layer == 0:
            (second_stack,) = gate([second_stack], active)
            joint_second = second_stack[:, :, wide_piece:].reshape(width, joint_width)
            others_second = ordered(second_stack[:, :, :wide_piece], turned[1:])
            sent_second = (others_second[:, : piece + LANES], others_second[:, piece + LANES :])
            second_parts = lax.all_gather(
                others_second[:, : 2 * piece], "ctx", axis=0, axis_index_groups=plane_groups()
            )
            out_second = others_second[:, 2 * piece :]
        outer_out = block_columns(outer_turned, unturned, shard)
        second_pre = hidden_rows + (outer_out + wide(small(layer, 3)))
        result, second_unit, second_inverse = norm_forward(second_pre, second_gain_row, second_shift_row)
        stashed.append(
            (
                everyone,
                packed,
                log_all,
                mixed_pair,
                first_unit,
                first_inverse,
                hidden_pair,
                active,
                slope,
                second_unit,
                second_inverse,
                joint,
                out_weights,
                places,
                weights,
                first_gain_row,
                second_gain_row,
            )
        )
        activation = low(result)
        outputs.append(activation)

    gradient = wide(cotangent[0])
    small_grads = [None] * LAYERS
    for layer in reversed(range(LAYERS)):
        (
            everyone,
            packed,
            log_all,
            mixed_pair,
            first_unit,
            first_inverse,
            hidden_pair,
            active,
            slope,
            second_unit,
            second_inverse,
            joint,
            out_weights,
            places,
            weights,
            first_gain_row,
            second_gain_row,
        ) = stashed[layer]
        grad_second, grad_second_gain, grad_second_shift = norm_backward(
            gradient, second_unit, second_inverse, second_gain_row
        )
        grad_outer = low(grad_second)
        grad_outer_bias = jnp.sum(wide(grad_outer), axis=0)
        grad_turned = block_columns(grad_outer, turned, shard)
        grad_pair = jnp.concatenate([grad_turned, swap(grad_turned, CORE)], axis=0)
        hidden_near, hidden_far, grad_inner, grad_inner_bias = feed_backward(grad_pair, slope, weights, layer)
        grad_first, first_rows, branch_spread, grad_sent = attention_output_back(
            hidden_near,
            swap(hidden_far, CORE),
            grad_second,
            first_unit,
            first_inverse,
            first_gain_row[None],
            out_weights,
            places,
        )
        grad_mixed = exchange(grad_sent)
        branch_half = 4 * LANES
        branch_pair = jnp.concatenate(
            [branch_spread[:, :branch_half], swap(branch_spread[:, branch_half:], CORE)], axis=0
        )
        summed = weight_gradients(
            hidden_pair, grad_pair, mixed_pair, grad_inner, active, branch_pair, plane_rows, layer == 0, grad_sent
        )
        if layer == 0:
            (grad_mixed,) = gate([grad_mixed], summed[0], plane_first)
        else:
            grad_mixed, first_sum = gate([grad_mixed, summed[0]])
        grad_query, grad_key, grad_value = attention_backward(packed, labels, grad_mixed, log_all, block_order)
        if layer == 0:
            first_keep, first_send, second_keep, second_send = summed
            first_came = swap(first_send, ALONG_X)
            second_came = swap(second_send, ALONG_Y)
        near_part, far_part, grad_packed, joint_bias_grad = token_gradients(
            (grad_query, grad_key, grad_value), joint, chip_order[0]
        )
        grad_joint = low(mm(everyone, grad_packed, TN))
        far_came = swap(far_part, CORE)
        tokens_sent = low(near_part + wide(far_came))
        small_grads[layer] = small_rows(
            jnp.concatenate([here[None], inner_order[layer]]).astype(jnp.int32),
            joint_bias_grad,
            first_rows,
            grad_outer_bias,
            grad_second_gain,
            grad_second_shift,
            grad_inner_bias,
        )
        if layer == 1:
            (plane_first,) = [
                lax.psum_scatter(
                    first_sum.reshape(4 * width, -1),
                    "ctx",
                    scatter_dimension=0,
                    axis_index_groups=plane_groups(),
                    tiled=True,
                )
            ]
            (plane_first,) = gate([plane_first], far_came)
            plane_rows_first = [
                lax.dynamic_slice_in_dim(plane_first, turned[r] * shard, shard, 0) for r in range(planes)
            ]
            came_first = [turn(plane_rows_first[r], planes - r) for r in range(1, planes)]
            gradient = grad_first + collect_tokens(tokens_sent, (), (grad_joint,))
            (second_sum,) = gate([summed[1]], gradient, plane_first)
            plane_second = lax.psum_scatter(
                second_sum.reshape(4 * width, -1),
                "ctx",
                scatter_dimension=0,
                axis_index_groups=plane_groups(),
                tiled=True,
            )
            sum_joint = lax.psum_scatter(grad_joint, "wsh", scatter_dimension=0, tiled=True)
            continue
        small_sent = jnp.concatenate(small_grads, axis=0)
        small_plane = jnp.sum(
            lax.all_to_all(
                jnp.stack([small_sent[:, p * shard : (p + 1) * shard] for p in range(planes)]), "wsh", 0, 0, tiled=True
            ),
            axis=0,
        )
        small_spread = jnp.broadcast_to(small_plane, (8, *small_plane.shape))
        first_came, second_came = gate([first_came, second_came], near_part, grad_joint, *came_first)
        sum_first = wide(plane_rows_first[0])
        for part in came_first:
            sum_first = sum_first + wide(part)
        sum_first = low(sum_first)
        first_next = low(wide(first_keep[1]) + wide(first_came[1]))
        second_next = low(wide(second_keep[1]) + wide(second_came[1]))
        joint_rows = [lax.dynamic_slice_in_dim(grad_joint, turned[r] * shard, shard, 0) for r in range(planes)]
        came_joint = [turn(joint_rows[r], planes - r) for r in range(1, planes)]
        first_last, second_last = gate(
            [swap(first_next, ALONG_Y), swap(second_next, ALONG_X)], small_plane, tokens_sent, *came_joint
        )
        own_total, *sent = plane_sum(
            (first_keep, first_came, first_last), (second_keep, second_came, second_last)
        )
        came = [turn(sent[r - 1], planes - r) for r in range(1, planes)]
        (plane_second,) = gate([plane_second], grad_mixed)
        sum_second = lax.psum_scatter(plane_second, "wsh", scatter_dimension=0, tiled=True)
        sum_first, sum_second, sum_joint = gate([sum_first, sum_second, sum_joint], own_total)
        everything = lax.all_gather(
            jnp.concatenate([sum_first[:, :piece], sum_second, sum_first[:, piece:], sum_joint], axis=1),
            "ctx",
            axis=0,
        )
        gradient = grad_first + collect_tokens(tokens_sent, (own_total,), ())
        came = gate(came, gradient)
        left_total, right_total = final_sum((own_total, *came), (joint_rows[0], *came_joint))
        (everything,) = gate([everything], left_total)
        *placed, placed_token = place_pieces(everything, relative, 1, None)
        (small_spread,) = gate([small_spread], left_total)
        small_mine = jnp.sum(exchange(small_spread), axis=0).reshape(LAYERS, 16, shard)

    near, far = plane_pieces(left_total, right_total, placed_token, small_mine)
    near_first = here ^ (2 * four)
    *placed, placed_token = place_pieces(near, near_first, 0, placed)
    (far,) = gate([far], placed_token)
    *placed, _ = place_pieces(far, near_first ^ 1, 0, placed)
    small_outs = [small_mine[:, i] for i in range(8)]
    return (
        outputs[0][None],
        outputs[1][None],
        low(gradient)[None],
        *placed,
        small_outs[0],
        small_outs[1],
        small_outs[2],
        small_mine[:, 8:12].reshape(LAYERS, 4 * shard),
        small_outs[3],
        small_outs[4],
        small_outs[5],
        small_outs[6],
        small_outs[7],
    )


def choose_body(mesh):
    if mesh.shape["ctx"] == 8 and HEADS // 8 == 2:
        return head_split_body
    return window_body


def solution(mesh):
    in_specs = (
        P("wsh", "ctx", None),
        P("wsh", "ctx", None),
        P("wsh", None),
        P("wsh", None),
        P(None, "wsh", None),
        P(None, "wsh", None),
        P(None, "wsh", None),
        P(None, "wsh", None),
        P(None, "wsh", None),
        P(None, None, "wsh"),
        P(None, "wsh"),
        P(None, "wsh"),
        P(None, "wsh"),
        P(None, "wsh"),
        P(None, "wsh"),
        P(None, "wsh"),
        P(None, "wsh"),
        P(None, "wsh"),
        P(None, "wsh"),
    )
    out_specs = (
        P("wsh", "ctx", None),
        P("wsh", "ctx", None),
        P("wsh", "ctx", None),
        P(None, "wsh", None),
        P(None, "wsh", None),
        P(None, "wsh", None),
        P(None, "wsh", None),
        P(None, "wsh", None),
        P(None, None, "wsh"),
        P(None, "wsh"),
        P(None, "wsh"),
        P(None, "wsh"),
        P(None, "wsh"),
        P(None, "wsh"),
        P(None, "wsh"),
        P(None, "wsh"),
        P(None, "wsh"),
        P(None, "wsh"),
    )
    return jax.shard_map(choose_body(mesh), mesh=mesh, in_specs=in_specs, out_specs=out_specs, check_vma=False)
```

```python
import functools

import jax
import jax.numpy as jnp
from jax import lax
from jax.experimental import pallas as pl
from jax.experimental.pallas import tpu as pltpu
from jax.sharding import PartitionSpec as P

HEADS = 16
HDIM = 64
LAYERS = 2
DOC_CAP = 2000


epsilon = 1e-05
neg_fill = -1e30
head_pair = 2


def from_behind(block, axis, distance):
    devices = range(lax.axis_size(axis))
    route = [(i - distance, i) for i in devices if i - distance in devices]
    return lax.ppermute(block, axis, route)


def normalize(values_in, gain_row, shift_row):
    centre = values_in - jnp.mean(values_in, axis=-1, keepdims=True)
    spread = jnp.mean(centre * centre, axis=-1, keepdims=True)
    return centre * lax.rsqrt(spread + epsilon) * gain_row + shift_row


def exact_gelu(values_in):
    return jax.nn.gelu(values_in, approximate=False)


def product(form, left, right):
    return jnp.einsum(form, left, right, preferred_element_type=jnp.float32)


def doc_labels(positions, starts, lengths):
    inside = (positions[:, None] >= starts[None, :]) & (
        positions[:, None] < (starts + lengths)[None, :]
    )
    labels = jnp.arange(1, starts.shape[0] + 1, dtype=jnp.int32)
    return jnp.sum(jnp.where(inside, labels[None, :], 0), axis=1)


def extend_rows(rows_in, dim, reach, mover):
    pieces = []
    for offset in range(-reach, reach + 1):
        if offset == 0:
            pieces.append(rows_in)
        else:
            pieces.append(mover(rows_in, -offset))
    return jnp.concatenate(pieces, axis=dim)


def move_keys_fwd(rows_in, steps):
    return from_behind(rows_in, "ctx", steps)


def move_keys_back(rows_in, steps):
    return from_behind(rows_in, "ctx", steps)


def fetch_forward(params, layer_index):
    shards = [piece[layer_index].astype(jnp.bfloat16) for piece in params]
    return (
        lax.all_gather(shards[0], "wsh", axis=0, tiled=True),
        lax.all_gather(shards[1], "wsh", axis=0, tiled=True),
        lax.all_gather(shards[2], "wsh", axis=0, tiled=True),
        lax.all_gather(shards[3], "wsh", axis=0, tiled=True),
        lax.all_gather(shards[4], "wsh", axis=0, tiled=True),
        lax.all_gather(shards[5], "wsh", axis=1, tiled=True),
        lax.all_gather(shards[6], "wsh", axis=0, tiled=True),
        lax.all_gather(shards[7], "wsh", axis=0, tiled=True),
        lax.all_gather(shards[8], "wsh", axis=0, tiled=True),
        lax.all_gather(shards[9], "wsh", axis=0, tiled=True),
        lax.all_gather(shards[10], "wsh", axis=0, tiled=True),
        lax.all_gather(shards[11], "wsh", axis=0, tiled=True),
        lax.all_gather(shards[12], "wsh", axis=0, tiled=True),
        lax.all_gather(shards[13], "wsh", axis=0, tiled=True),
        lax.all_gather(shards[14], "wsh", axis=0, tiled=True),
    )


def fetch_backward(params, layer_index):
    shards = [piece[layer_index].astype(jnp.bfloat16) for piece in params]
    return (
        lax.all_gather(shards[0], "wsh", axis=0, tiled=True),
        lax.all_gather(shards[1], "wsh", axis=0, tiled=True),
        lax.all_gather(shards[2], "wsh", axis=0, tiled=True),
        lax.all_gather(shards[3], "wsh", axis=0, tiled=True),
        lax.all_gather(shards[4], "wsh", axis=0, tiled=True),
        lax.all_gather(shards[5], "wsh", axis=1, tiled=True),
        lax.all_gather(shards[6], "wsh", axis=0, tiled=True),
        lax.all_gather(shards[7], "wsh", axis=0, tiled=True),
        lax.all_gather(shards[8], "wsh", axis=0, tiled=True),
        lax.all_gather(shards[9], "wsh", axis=0, tiled=True),
        lax.all_gather(shards[10], "wsh", axis=0, tiled=True),
        lax.all_gather(shards[11], "wsh", axis=0, tiled=True),
        lax.all_gather(shards[12], "wsh", axis=0, tiled=True),
        lax.all_gather(shards[13], "wsh", axis=0, tiled=True),
        lax.all_gather(shards[14], "wsh", axis=0, tiled=True),
    )


def reduce_grads(local_grads):
    shares = (
        lax.psum_scatter(
            local_grads[0].astype(jnp.bfloat16), "wsh", scatter_dimension=0, tiled=True
        ).astype(jnp.float32),
        lax.psum_scatter(
            local_grads[1].astype(jnp.bfloat16), "wsh", scatter_dimension=0, tiled=True
        ).astype(jnp.float32),
        lax.psum_scatter(
            local_grads[2].astype(jnp.bfloat16), "wsh", scatter_dimension=0, tiled=True
        ).astype(jnp.float32),
        lax.psum_scatter(
            local_grads[3].astype(jnp.bfloat16), "wsh", scatter_dimension=0, tiled=True
        ).astype(jnp.float32),
        lax.psum_scatter(
            local_grads[4].astype(jnp.bfloat16), "wsh", scatter_dimension=0, tiled=True
        ).astype(jnp.float32),
        lax.psum_scatter(
            local_grads[5].astype(jnp.bfloat16), "wsh", scatter_dimension=1, tiled=True
        ).astype(jnp.float32),
        lax.psum_scatter(
            local_grads[6].astype(jnp.bfloat16), "wsh", scatter_dimension=0, tiled=True
        ).astype(jnp.float32),
        lax.psum_scatter(
            local_grads[7].astype(jnp.bfloat16), "wsh", scatter_dimension=0, tiled=True
        ).astype(jnp.float32),
        lax.psum_scatter(
            local_grads[8].astype(jnp.bfloat16), "wsh", scatter_dimension=0, tiled=True
        ).astype(jnp.float32),
        lax.psum_scatter(
            local_grads[9].astype(jnp.bfloat16), "wsh", scatter_dimension=0, tiled=True
        ).astype(jnp.float32),
        lax.psum_scatter(
            local_grads[10].astype(jnp.bfloat16), "wsh", scatter_dimension=0, tiled=True
        ).astype(jnp.float32),
        lax.psum_scatter(
            local_grads[11].astype(jnp.bfloat16), "wsh", scatter_dimension=0, tiled=True
        ).astype(jnp.float32),
        lax.psum_scatter(
            local_grads[12].astype(jnp.bfloat16), "wsh", scatter_dimension=0, tiled=True
        ).astype(jnp.float32),
        lax.psum_scatter(
            local_grads[13].astype(jnp.bfloat16), "wsh", scatter_dimension=0, tiled=True
        ).astype(jnp.float32),
        lax.psum_scatter(
            local_grads[14].astype(jnp.bfloat16), "wsh", scatter_dimension=0, tiled=True
        ).astype(jnp.float32),
    )
    return (
        lax.psum(shares[0].astype(jnp.bfloat16), "ctx").astype(jnp.float32),
        lax.psum(shares[1].astype(jnp.bfloat16), "ctx").astype(jnp.float32),
        lax.psum(shares[2].astype(jnp.bfloat16), "ctx").astype(jnp.float32),
        lax.psum(shares[3].astype(jnp.bfloat16), "ctx").astype(jnp.float32),
        lax.psum(shares[4].astype(jnp.bfloat16), "ctx").astype(jnp.float32),
        lax.psum(shares[5].astype(jnp.bfloat16), "ctx").astype(jnp.float32),
        lax.psum(shares[6].astype(jnp.bfloat16), "ctx").astype(jnp.float32),
        lax.psum(shares[7].astype(jnp.bfloat16), "ctx").astype(jnp.float32),
        lax.psum(shares[8].astype(jnp.bfloat16), "ctx").astype(jnp.float32),
        lax.psum(shares[9].astype(jnp.bfloat16), "ctx").astype(jnp.float32),
        lax.psum(shares[10].astype(jnp.bfloat16), "ctx").astype(jnp.float32),
        lax.psum(shares[11].astype(jnp.bfloat16), "ctx").astype(jnp.float32),
        lax.psum(shares[12].astype(jnp.bfloat16), "ctx").astype(jnp.float32),
        lax.psum(shares[13].astype(jnp.bfloat16), "ctx").astype(jnp.float32),
        lax.psum(shares[14].astype(jnp.bfloat16), "ctx").astype(jnp.float32),
    )


def attend(queries, key_ext, value_ext, allowed, score_scale):
    rows_local = queries.shape[0]
    rows_keys = key_ext.shape[0]
    groups = HEADS // head_pair
    span = head_pair * HDIM
    query_groups = queries.reshape(rows_local, groups, span)
    key_groups = key_ext.reshape(rows_keys, groups, span)
    value_groups = value_ext.reshape(rows_keys, groups, span)

    def one_group(group_index, carry):
        mixed_all, log_all = carry
        query_part = lax.dynamic_index_in_dim(query_groups, group_index, 1, keepdims=False).reshape(
            rows_local, head_pair, HDIM
        )
        key_part = lax.dynamic_index_in_dim(key_groups, group_index, 1, keepdims=False).reshape(
            rows_keys, head_pair, HDIM
        )
        value_part = lax.dynamic_index_in_dim(value_groups, group_index, 1, keepdims=False).reshape(
            rows_keys, head_pair, HDIM
        )
        raw_scores = product("qhd,khd->hqk", query_part, key_part)
        scores = jnp.where(allowed[None], raw_scores * score_scale, neg_fill)
        row_peak = jnp.max(scores, axis=2, keepdims=True)
        exponent = jnp.exp(scores - row_peak)
        row_total = jnp.sum(exponent, axis=2, keepdims=True)
        probability = (exponent / row_total).astype(jnp.bfloat16)
        mixed_part = product("hqk,khd->qhd", probability, value_part)
        mixed_all = lax.dynamic_update_index_in_dim(
            mixed_all, mixed_part.reshape(rows_local, span), group_index, 1
        )
        log_all = lax.dynamic_update_index_in_dim(
            log_all, (row_peak + jnp.log(row_total))[:, :, 0], group_index, 0
        )
        return (mixed_all, log_all)

    start_carry = (
        jnp.zeros((rows_local, groups, span), jnp.float32),
        jnp.zeros((groups, head_pair, rows_local), jnp.float32),
    )
    mixed_all, log_all = lax.fori_loop(0, groups, one_group, start_carry)
    return (mixed_all.reshape(rows_local, groups * span), log_all)


def attend_back(queries, key_ext, value_ext, grad_mixed, log_all, allowed, score_scale):
    rows_local = queries.shape[0]
    rows_keys = key_ext.shape[0]
    groups = HEADS // head_pair
    span = head_pair * HDIM
    query_groups = queries.reshape(rows_local, groups, span)
    key_groups = key_ext.reshape(rows_keys, groups, span)
    value_groups = value_ext.reshape(rows_keys, groups, span)
    grad_groups = grad_mixed.reshape(rows_local, groups, span)

    def one_group(group_index, carry):
        query_part = lax.dynamic_index_in_dim(query_groups, group_index, 1, keepdims=False).reshape(
            rows_local, head_pair, HDIM
        )
        key_part = lax.dynamic_index_in_dim(key_groups, group_index, 1, keepdims=False).reshape(
            rows_keys, head_pair, HDIM
        )
        value_part = lax.dynamic_index_in_dim(value_groups, group_index, 1, keepdims=False).reshape(
            rows_keys, head_pair, HDIM
        )
        grad_part = lax.dynamic_index_in_dim(grad_groups, group_index, 1, keepdims=False).reshape(
            rows_local, head_pair, HDIM
        )
        log_part = lax.dynamic_index_in_dim(log_all, group_index, 0, keepdims=False)
        raw_scores = product("qhd,khd->hqk", query_part, key_part)
        scores = jnp.where(allowed[None], raw_scores * score_scale, neg_fill)
        probability = jnp.exp(scores - log_part[:, :, None])
        grad_prob = product("qhd,khd->hqk", grad_part, value_part)
        row_delta = jnp.sum(probability * grad_prob, axis=2, keepdims=True)
        grad_scores = (probability * (grad_prob - row_delta) * score_scale).astype(jnp.bfloat16)
        query_term = product("hqk,khd->qhd", grad_scores, key_part)
        grad_query = lax.dynamic_update_index_in_dim(
            carry[0], query_term.reshape(rows_local, span), group_index, 1
        )
        delta_all = lax.dynamic_update_index_in_dim(carry[1], row_delta[:, :, 0], group_index, 0)
        key_term = product("hqk,qhd->khd", grad_scores, query_part)
        value_term = product("hqk,qhd->khd", probability.astype(jnp.bfloat16), grad_part)
        grad_key = lax.dynamic_update_index_in_dim(
            carry[2], key_term.reshape(rows_keys, span), group_index, 1
        )
        grad_value = lax.dynamic_update_index_in_dim(
            carry[3], value_term.reshape(rows_keys, span), group_index, 1
        )
        return (grad_query, delta_all, grad_key, grad_value)

    start_carry = (
        jnp.zeros((rows_local, groups, span), jnp.float32),
        jnp.zeros((groups, head_pair, rows_local), jnp.float32),
    )
    start_carry = start_carry + (
        jnp.zeros((rows_keys, groups, span), jnp.float32),
        jnp.zeros((rows_keys, groups, span), jnp.float32),
    )
    finals = lax.fori_loop(0, groups, one_group, start_carry)
    grad_query = finals[0].reshape(rows_local, groups * span)
    return (
        grad_query,
        finals[2].reshape(rows_keys, groups * span),
        finals[3].reshape(rows_keys, groups * span),
    )


def layer_forward(activation, gathered, allowed, halo_rows, score_scale):
    (
        query_weight,
        key_weight,
        value_weight,
        out_weight,
        inner_weight,
        outer_weight,
        query_bias,
        value_bias,
        out_bias,
        inner_bias,
        outer_bias,
        first_gain,
        first_shift,
        second_gain,
        second_shift,
    ) = gathered
    rows_local = activation.shape[0]
    queries = (product("td,de->te", activation, query_weight) + query_bias).astype(jnp.bfloat16)
    key_rows = product("td,de->te", activation, key_weight).astype(jnp.bfloat16)
    value_rows = (product("td,de->te", activation, value_weight) + value_bias).astype(jnp.bfloat16)
    stacked = jnp.stack([key_rows, value_rows])
    extended = extend_rows(stacked, 1, halo_rows // rows_local, move_keys_fwd)
    mixed_heads, log_all = attend(queries, extended[0], extended[1], allowed, score_scale)
    mixed_low = mixed_heads.astype(jnp.bfloat16)
    first_pre = activation.astype(jnp.float32) + (
        product("td,de->te", mixed_low, out_weight) + out_bias
    )
    hidden = normalize(first_pre, first_gain.astype(jnp.float32), first_shift.astype(jnp.float32))
    hidden_low = hidden.astype(jnp.bfloat16)
    inner_pre = product("td,df->tf", hidden_low, inner_weight) + inner_bias
    active_low = exact_gelu(inner_pre).astype(jnp.bfloat16)
    second_pre = hidden + (product("tf,fd->td", active_low, outer_weight) + outer_bias)
    result_rows = normalize(
        second_pre, second_gain.astype(jnp.float32), second_shift.astype(jnp.float32)
    )
    saved = (
        activation,
        queries,
        extended,
        log_all,
        mixed_low,
        first_pre,
        hidden_low,
        inner_pre,
        active_low,
        second_pre,
    )
    return (saved, result_rows)


def return_rows(grad_ext, halo_rows, rows_local):
    reach = halo_rows // rows_local
    total = grad_ext[:, halo_rows : halo_rows + rows_local]
    for offset in range(-reach, reach + 1):
        if offset != 0:
            begin = halo_rows + offset * rows_local
            block_rows = grad_ext[:, begin : begin + rows_local]
            total = total + from_behind(block_rows.astype(jnp.bfloat16), "ctx", offset).astype(
                block_rows.dtype
            )
    return total


def layer_backward(gradient, saved, weights, allowed, halo_rows, score_scale):
    (
        query_weight,
        key_weight,
        value_weight,
        out_weight,
        inner_weight,
        outer_weight,
        query_bias,
        value_bias,
        out_bias,
        inner_bias,
        outer_bias,
        first_gain,
        first_shift,
        second_gain,
        second_shift,
    ) = weights
    (
        activation,
        queries,
        extended,
        log_all,
        mixed_low,
        first_pre,
        hidden_low,
        inner_pre,
        active_low,
        second_pre,
    ) = saved
    rows_local = activation.shape[0]
    reach = halo_rows // rows_local
    _, second_pull = jax.vjp(
        normalize, second_pre, second_gain.astype(jnp.float32), second_shift.astype(jnp.float32)
    )
    grad_second, grad_second_gain, grad_second_shift = second_pull(gradient)
    grad_outer = grad_second.astype(jnp.bfloat16)
    grad_outer_weight = product("tf,td->fd", active_low, grad_outer)
    grad_outer_bias = jnp.sum(grad_outer.astype(jnp.float32), axis=0)
    grad_active = product("td,fd->tf", grad_outer, outer_weight)
    _, gelu_pull = jax.vjp(exact_gelu, inner_pre)
    (grad_inner,) = gelu_pull(grad_active)
    grad_inner_low = grad_inner.astype(jnp.bfloat16)
    grad_inner_weight = product("td,tf->df", hidden_low, grad_inner_low)
    grad_inner_bias = jnp.sum(grad_inner_low.astype(jnp.float32), axis=0)
    grad_hidden = grad_second + product("tf,df->td", grad_inner_low, inner_weight)
    _, first_pull = jax.vjp(
        normalize, first_pre, first_gain.astype(jnp.float32), first_shift.astype(jnp.float32)
    )
    grad_first, grad_first_gain, grad_first_shift = first_pull(grad_hidden)
    grad_branch = grad_first.astype(jnp.bfloat16)
    grad_out_weight = product("te,td->ed", mixed_low, grad_branch)
    grad_out_bias = jnp.sum(grad_branch.astype(jnp.float32), axis=0)
    grad_mixed = product("td,ed->te", grad_branch, out_weight).astype(jnp.bfloat16)
    own_rows = extended[:, halo_rows : halo_rows + rows_local]
    key_ext = extend_rows(own_rows, 1, reach, move_keys_back)
    query_sum, key_win, value_win = attend_back(
        queries, key_ext[0], key_ext[1], grad_mixed, log_all, allowed, score_scale
    )
    owned = return_rows(jnp.stack([key_win, value_win]), halo_rows, rows_local)
    key_sum = owned[0]
    value_sum = owned[1]
    grad_query = query_sum.astype(jnp.bfloat16)
    grad_key = key_sum.astype(jnp.bfloat16)
    grad_value = value_sum.astype(jnp.bfloat16)
    grad_query_weight = product("te,td->ed", activation, grad_query)
    grad_key_weight = product("te,td->ed", activation, grad_key)
    grad_value_weight = product("te,td->ed", activation, grad_value)
    grad_query_bias = jnp.sum(grad_query.astype(jnp.float32), axis=0)
    grad_value_bias = jnp.sum(grad_value.astype(jnp.float32), axis=0)
    grad_activation = (
        grad_first
        + product("td,ed->te", grad_query, query_weight)
        + product("td,ed->te", grad_key, key_weight)
        + product("td,ed->te", grad_value, value_weight)
    )
    local_grads = (
        grad_query_weight,
        grad_key_weight,
        grad_value_weight,
        grad_out_weight,
        grad_inner_weight,
        grad_outer_weight,
        grad_query_bias,
        grad_value_bias,
        grad_out_bias,
        grad_inner_bias,
        grad_outer_bias,
        grad_first_gain,
        grad_first_shift,
        grad_second_gain,
        grad_second_shift,
    )
    return (grad_activation, local_grads)


def window_body(
    tokens,
    cotangent,
    doc_starts,
    doc_lengths,
    query_weight,
    key_weight,
    value_weight,
    out_weight,
    inner_weight,
    outer_weight,
    query_bias,
    value_bias,
    out_bias,
    inner_bias,
    outer_bias,
    first_gain,
    first_shift,
    second_gain,
    second_shift,
):
    params = (
        query_weight,
        key_weight,
        value_weight,
        out_weight,
        inner_weight,
        outer_weight,
        query_bias,
        value_bias,
        out_bias,
        inner_bias,
        outer_bias,
        first_gain,
        first_shift,
        second_gain,
        second_shift,
    )
    rows_local = tokens.shape[1]
    ctx_count = lax.axis_size("ctx")
    reach = min(-(-(DOC_CAP - 1) // rows_local), ctx_count - 1)
    halo_rows = reach * rows_local
    window = rows_local + 2 * halo_rows
    row_start = lax.axis_index("ctx") * rows_local
    local_positions = row_start + jnp.arange(rows_local, dtype=jnp.int32)
    window_positions = row_start - halo_rows + jnp.arange(window, dtype=jnp.int32)
    local_labels = doc_labels(local_positions, doc_starts[0], doc_lengths[0])
    window_labels = doc_labels(window_positions, doc_starts[0], doc_lengths[0])
    allowed = (local_labels[:, None] == window_labels[None, :]) & (local_labels[:, None] > 0)
    score_scale = HDIM ** (-0.5)
    activation = tokens[0]
    stashed = []
    outputs = []
    for layer_index in range(LAYERS):
        gathered = fetch_forward(params, layer_index)
        saved, result_rows = layer_forward(activation, gathered, allowed, halo_rows, score_scale)
        stashed.append((saved, gathered))
        outputs.append(result_rows)
        activation = result_rows.astype(jnp.bfloat16)
    gradient = cotangent[0].astype(jnp.float32)
    reduced = [None] * LAYERS
    for layer_index in reversed(range(LAYERS)):
        saved, gathered = stashed[layer_index]
        weights_now = fetch_backward(params, layer_index)
        gradient, local_grads = layer_backward(
            gradient, saved, weights_now, allowed, halo_rows, score_scale
        )
        reduced[layer_index] = reduce_grads(local_grads)
    stacked_grads = [
        jnp.stack([reduced[layer_index][member] for layer_index in range(LAYERS)])
        for member in range(15)
    ]
    heads_out = [
        outputs[0].astype(jnp.bfloat16)[None],
        outputs[LAYERS - 1].astype(jnp.bfloat16)[None],
        gradient.astype(jnp.bfloat16)[None],
    ]
    return tuple(heads_out + stacked_grads)


NN = (((1,), (0,)), ((), ()))
NT = (((1,), (1,)), ((), ()))
TN = (((0,), (0,)), ((), ()))
LANES = 128
QUERY_BLOCK = 1024
CORE, ALONG_X, ALONG_Y = 1, 2, 4
SMALL_COST = pl.CostEstimate(flops=1000, bytes_accessed=1000, transcendentals=0)


def lasting(microseconds):
    return pl.CostEstimate(
        flops=int(microseconds * 1.15e9), bytes_accessed=int(microseconds * 3.6e6), transcendentals=0
    )


def mm(left, right, dims=NN):
    return lax.dot_general(left, right, dims, preferred_element_type=jnp.float32)


def swap(block, mask):
    devices = range(lax.axis_size("ctx"))
    return lax.ppermute(block, "ctx", [(i, i ^ mask) for i in devices])


def turn(block, distance):
    count = lax.axis_size("wsh")
    return lax.ppermute(block, "wsh", [(i, (i + distance) % count) for i in range(count)])


def low(values_in):
    return values_in.astype(jnp.bfloat16)


def wide(values_in):
    return values_in.astype(jnp.float32)


def mask_features(label_col):
    rows = label_col.shape[0]
    lane = lax.broadcasted_iota(jnp.int32, (rows, LANES), 1)
    hit = lax.rem(lane, HDIM) == jnp.broadcast_to(label_col, (rows, LANES))
    return (
        jnp.where(hit, neg_fill, 0.0).astype(jnp.bfloat16),
        jnp.where(hit, 0.0, 1.0).astype(jnp.bfloat16),
    )


def fill_key_scratch(key_rows, label_col, key_mask):
    lane = lax.broadcasted_iota(jnp.int32, key_rows.shape, 1)
    _, key_features = mask_features(label_col)
    key_mask[0] = jnp.where(lane < HDIM, key_rows, key_features)
    key_mask[1] = jnp.where(lane < HDIM, key_features, key_rows)


def attention_forward_kernel(
    order_ref, query_ref, key_ref, value_ref, label_ref, query_label_ref, mixed_ref, log_ref, key_mask, value_t
):
    @pl.when(pl.program_id(0) == 0)
    def _():
        fill_key_scratch(key_ref[...], label_ref[...], key_mask)
        value_t[...] = value_ref[...].T

    scaled = low(wide(query_ref[...]) * HDIM ** (-0.5))
    lane = lax.broadcasted_iota(jnp.int32, scaled.shape, 1)
    features, _ = mask_features(query_label_ref[...])
    parts = []
    for head in range(2):
        mine = (lane < HDIM) if head == 0 else (lane >= HDIM)
        scores = mm(key_mask[head], jnp.where(mine, scaled, features), NT)
        peak = jnp.max(scores, axis=0, keepdims=True)
        exponent = jnp.exp(scores - peak)
        total = jnp.sum(exponent, axis=0, keepdims=True)
        mixed = mm(value_t[pl.ds(HDIM * head, HDIM), :], low(exponent))
        parts.append(mixed / total)
        log_ref[pl.ds(head, 1), :] = peak + jnp.log(total)
    mixed_all = low(jnp.concatenate(parts, axis=0).T)
    block_rows = mixed_ref.shape[1]
    count = mixed_all.shape[0] // block_rows
    for at in range(count):
        place = order_ref[pl.program_id(0) * count + at]
        mixed_ref[place] = mixed_all[at * block_rows : (at + 1) * block_rows]


def attention_forward(packed, labels, order):
    rows = packed.shape[0]
    mine = pl.BlockSpec((QUERY_BLOCK, LANES), lambda i, order_ref: (i, 0))
    return pl.pallas_call(
        attention_forward_kernel,
        grid_spec=pltpu.PrefetchScalarGridSpec(
            num_scalar_prefetch=1,
            grid=(rows // QUERY_BLOCK,),
            in_specs=[
                mine,
                pl.BlockSpec((rows, LANES), lambda i, order_ref: (0, 1)),
                pl.BlockSpec((rows, LANES), lambda i, order_ref: (0, 2)),
                pl.BlockSpec((rows, 1), lambda i, order_ref: (0, 0)),
                pl.BlockSpec((QUERY_BLOCK, 1), lambda i, order_ref: (i, 0)),
            ],
            out_specs=[
                pl.BlockSpec((8, rows // 8, LANES), lambda i, order_ref: (0, 0, 0)),
                pl.BlockSpec((2, QUERY_BLOCK), lambda i, order_ref: (0, i)),
            ],
            scratch_shapes=[
                pltpu.VMEM((2, rows, LANES), jnp.bfloat16),
                pltpu.VMEM((LANES, rows), jnp.bfloat16),
            ],
        ),
        out_shape=[
            jax.ShapeDtypeStruct((8, rows // 8, LANES), jnp.bfloat16),
            jax.ShapeDtypeStruct((2, rows), jnp.float32),
        ],
        cost_estimate=lasting(17),
        name="attention_forward",
    )(order, packed, packed, packed, labels, labels)


def attention_backward_kernel(
    order_ref,
    query_ref,
    key_ref,
    value_ref,
    label_ref,
    query_label_ref,
    grad_ref,
    log_ref,
    out_query_ref,
    out_key_ref,
    out_value_ref,
    key_mask,
    key_t,
    key_sum,
    value_sum,
):
    step = pl.program_id(0)

    @pl.when(step == 0)
    def _():
        fill_key_scratch(key_ref[...], label_ref[...], key_mask)
        key_t[...] = key_ref[...].T
        key_sum[...] = jnp.zeros_like(key_sum)
        value_sum[...] = jnp.zeros_like(value_sum)

    scaled = low(wide(query_ref[...]) * HDIM ** (-0.5))
    count = scaled.shape[0] // grad_ref.shape[1]
    grad = jnp.concatenate([grad_ref[order_ref[step * count + at]] for at in range(count)], axis=0)
    value_rows = value_ref[...]
    lane = lax.broadcasted_iota(jnp.int32, scaled.shape, 1)
    features, _ = mask_features(query_label_ref[...])
    zero = jnp.zeros(scaled.shape, jnp.bfloat16)
    parts = []
    for head in range(2):
        mine = (lane < HDIM) if head == 0 else (lane >= HDIM)
        query_own = jnp.where(mine, scaled, zero)
        grad_own = jnp.where(mine, grad, zero)
        scores = mm(key_mask[head], jnp.where(mine, scaled, features), NT)
        probability = jnp.exp(scores - log_ref[pl.ds(head, 1), :])
        grad_prob = mm(value_rows, grad_own, NT)
        delta = jnp.sum(probability * grad_prob, axis=0, keepdims=True)
        grad_scores = low(probability * (grad_prob - delta))
        key_sum[...] += mm(grad_scores, query_own)
        value_sum[...] += mm(low(probability), grad_own)
        parts.append(mm(key_t[pl.ds(HDIM * head, HDIM), :], grad_scores) * HDIM ** (-0.5))
    out_query_ref[...] = low(jnp.concatenate(parts, axis=0).T)

    @pl.when(step == pl.num_programs(0) - 1)
    def _():
        out_key_ref[...] = low(key_sum[...])
        out_value_ref[...] = low(value_sum[...])


def attention_backward(packed, labels, grad, log_all, order):
    rows = packed.shape[0]
    mine = pl.BlockSpec((QUERY_BLOCK, LANES), lambda i, order_ref: (i, 0))
    whole = pl.BlockSpec((rows, LANES), lambda i, order_ref: (0, 0))
    return pl.pallas_call(
        attention_backward_kernel,
        grid_spec=pltpu.PrefetchScalarGridSpec(
            num_scalar_prefetch=1,
            grid=(rows // QUERY_BLOCK,),
            in_specs=[
                mine,
                pl.BlockSpec((rows, LANES), lambda i, order_ref: (0, 1)),
                pl.BlockSpec((rows, LANES), lambda i, order_ref: (0, 2)),
                pl.BlockSpec((rows, 1), lambda i, order_ref: (0, 0)),
                pl.BlockSpec((QUERY_BLOCK, 1), lambda i, order_ref: (i, 0)),
                pl.BlockSpec((8, rows // 8, LANES), lambda i, order_ref: (0, 0, 0)),
                pl.BlockSpec((2, QUERY_BLOCK), lambda i, order_ref: (0, i)),
            ],
            out_specs=[mine, whole, whole],
            scratch_shapes=[
                pltpu.VMEM((2, rows, LANES), jnp.bfloat16),
                pltpu.VMEM((LANES, rows), jnp.bfloat16),
                pltpu.VMEM((rows, LANES), jnp.float32),
                pltpu.VMEM((rows, LANES), jnp.float32),
            ],
        ),
        out_shape=[jax.ShapeDtypeStruct((rows, LANES), jnp.bfloat16)] * 3,
        cost_estimate=lasting(29),
        name="attention_backward",
    )(order, packed, packed, packed, labels, labels, grad, log_all)


def own_pieces(inner_weight, outer_weight, out_weight, joint_weights, small_params, here, first_block):
    layers, shard, hidden = inner_weight.shape
    piece = hidden // 8
    width = 3 * LANES

    def kernel(place_ref, inner_ref, outer_ref, out_ref, query_ref, key_ref, value_ref, *refs):
        small_refs, (first_ref, second_ref, joint_ref) = refs[:-3], refs[-3:]
        first_ref[0, :, :piece] = low(inner_ref[0])
        first_ref[0, :, piece:] = low(out_ref[0])
        second_ref[0] = low(outer_ref[0]).T
        for at, ref in enumerate((query_ref, key_ref, value_ref)):
            joint_ref[0, :shard, at * LANES : (at + 1) * LANES] = low(ref[0])
        rows = [jnp.concatenate([ref[...] for ref in small_refs[:8]], axis=0)]
        rows += [small_refs[8][:, q * shard : (q + 1) * shard] for q in range(4)]
        rows += [jnp.zeros((8, shard), jnp.float32)]
        packed = low(jnp.concatenate(rows, axis=0))
        joint_ref[0, shard:] = jnp.concatenate([packed, jnp.zeros((32, width - shard), jnp.bfloat16)], axis=1)

    column = pl.BlockSpec((1, shard, LANES), lambda layer, place_ref: (layer, 0, place_ref[0]))
    return pl.pallas_call(
        kernel,
        grid_spec=pltpu.PrefetchScalarGridSpec(
            num_scalar_prefetch=1,
            grid=(layers,),
            in_specs=[
                pl.BlockSpec((1, shard, piece), lambda layer, place_ref: (layer, 0, place_ref[1])),
                pl.BlockSpec((1, piece, shard), lambda layer, place_ref: (layer, place_ref[1], 0)),
                column,
                column,
                column,
                column,
            ]
            + [pl.BlockSpec(param.shape, lambda layer, place_ref: (0, 0)) for param in small_params],
            out_specs=[
                pl.BlockSpec((1, shard, piece + LANES), lambda layer, place_ref: (layer, 0, 0)),
                pl.BlockSpec((1, shard, piece), lambda layer, place_ref: (layer, 0, 0)),
                pl.BlockSpec((1, shard + 32, width), lambda layer, place_ref: (layer, 0, 0)),
            ],
        ),
        out_shape=[
            jax.ShapeDtypeStruct((layers, shard, piece + LANES), jnp.bfloat16),
            jax.ShapeDtypeStruct((layers, shard, piece), jnp.bfloat16),
            jax.ShapeDtypeStruct((layers, shard + 32, width), jnp.bfloat16),
        ],
        cost_estimate=lasting(4),
        name="own_pieces",
    )(
        jnp.stack([here, first_block]).astype(jnp.int32),
        inner_weight,
        outer_weight,
        out_weight,
        *joint_weights,
        *small_params,
    )


def own_blocks(inner_weight, outer_weight, out_weight, inner_order, out_order, after):
    layers, shard, hidden = inner_weight.shape
    piece = hidden // 8

    def kernel(inner_order_ref, out_order_ref, *refs):
        ins, (inner_out, outer_out, out_out) = refs[:16], refs[-3:]
        for j in range(4):
            inner_out[0, j] = low(ins[j][0])
            outer_out[0, j] = low(ins[4 + j][0]).T
        for j in range(8):
            out_out[0, :, j * LANES : (j + 1) * LANES] = low(ins[8 + j][0])

    def inner_at(j):
        return pl.BlockSpec((1, shard, piece), lambda layer, inner_ref, out_ref: (layer, 0, inner_ref[layer * 4 + j]))

    def outer_at(j):
        return pl.BlockSpec((1, piece, shard), lambda layer, inner_ref, out_ref: (layer, inner_ref[layer * 4 + j], 0))

    def out_at(j):
        return pl.BlockSpec((1, shard, LANES), lambda layer, inner_ref, out_ref: (layer, 0, out_ref[layer * 8 + j]))

    block = pl.BlockSpec((1, 4, shard, piece), lambda layer, *_: (layer, 0, 0, 0))
    return pl.pallas_call(
        kernel,
        grid_spec=pltpu.PrefetchScalarGridSpec(
            num_scalar_prefetch=2,
            grid=(layers,),
            in_specs=[inner_at(j) for j in range(4)]
            + [outer_at(j) for j in range(4)]
            + [out_at(j) for j in range(8)]
            + [pl.BlockSpec(memory_space=pl.ANY)],
            out_specs=[block, block, pl.BlockSpec((1, shard, 8 * LANES), lambda layer, *_: (layer, 0, 0))],
        ),
        out_shape=[
            jax.ShapeDtypeStruct((layers, 4, shard, piece), jnp.bfloat16),
            jax.ShapeDtypeStruct((layers, 4, shard, piece), jnp.bfloat16),
            jax.ShapeDtypeStruct((layers, shard, 8 * LANES), jnp.bfloat16),
        ],
        cost_estimate=lasting(7),
        name="own_blocks",
    )(inner_order, out_order, *[inner_weight] * 4, *[outer_weight] * 4, *[out_weight] * 8, after)


def place_pieces(pieces, order, layer, previous):
    count, shard, columns = pieces.shape
    piece = (columns - 4 * LANES) // 2
    width = 8 * LANES

    def column(index, order_ref):
        return (layer, 0, order_ref[index])

    def inner_place(index, order_ref):
        return (order_ref[index] % 2) * 4 + order_ref[index] // 2

    square = jax.ShapeDtypeStruct((LAYERS, shard, width), jnp.float32)
    outs = [square] * 4 + [
        jax.ShapeDtypeStruct((LAYERS, shard, 8 * piece), jnp.float32),
        jax.ShapeDtypeStruct((LAYERS, 8 * piece, shard), jnp.float32),
        jax.ShapeDtypeStruct((8, LANES), jnp.float32),
    ]
    specs = [pl.BlockSpec((1, shard, LANES), column)] * 4 + [
        pl.BlockSpec((1, shard, piece), lambda i, order_ref: (layer, 0, inner_place(i, order_ref))),
        pl.BlockSpec((1, piece, shard), lambda i, order_ref: (layer, inner_place(i, order_ref), 0)),
        pl.BlockSpec((8, LANES), lambda i, order_ref: (0, 0)),
    ]

    def kernel(order_ref, source, *refs):
        query_out, key_out, value_out, out_out, inner_out, outer_out, token_out = refs[-7:]
        token_out[...] = jnp.zeros_like(token_out)
        inner_out[0] = wide(source[0, :, :piece])
        outer_out[0] = wide(source[0, :, piece : 2 * piece].T)
        for at, ref in enumerate((out_out, query_out, key_out, value_out)):
            begin = 2 * piece + at * LANES
            ref[0] = wide(source[0, :, begin : begin + LANES])

    held = [] if previous is None else list(previous)
    return pl.pallas_call(
        kernel,
        grid_spec=pltpu.PrefetchScalarGridSpec(
            num_scalar_prefetch=1,
            grid=(count,),
            in_specs=[pl.BlockSpec((1, shard, columns), lambda i, order_ref: (i, 0, 0))]
            + [pl.BlockSpec(memory_space=pl.ANY)] * len(held),
            out_specs=specs,
        ),
        out_shape=outs,
        input_output_aliases={2 + i: i for i in range(len(held))},
        cost_estimate=lasting(count * 5 // 4),
        name="place_pieces",
    )(order, pieces, *held)


def half_erfc(values_in):
    scaled = values_in * (2.0**-0.5)
    part = 1.0 / (1.0 + 0.5 * scaled)
    series = 0.17087277
    for coefficient in (
        -0.82215223,
        1.48851587,
        -1.13520398,
        0.27886807,
        -0.18628806,
        0.09678418,
        0.37409196,
        1.00002368,
        -1.26551223,
    ):
        series = coefficient + part * series
    return 0.5 * part * jnp.exp(series - scaled * scaled)


def load_weights(step, own_inner, own_outer, inner_refs, outer_refs, inner_now, outer_now):
    shard = own_inner.shape[2]
    inner_now[:shard] = own_inner[0, 0]
    outer_now[:shard] = own_outer[0, 0]
    if len(inner_refs) == 1:
        inner_now[shard:] = inner_refs[0][0]
        outer_now[shard:] = outer_refs[0][0]
        return
    chunks = len(inner_refs) // 4
    rows = inner_refs[0].shape[0]
    for j in range(4):

        @pl.when(step == j)
        def _(j=j):
            for chunk in range(chunks):
                begin = shard + chunk * rows
                inner_now[begin : begin + rows] = inner_refs[j * chunks + chunk][...]
                outer_now[begin : begin + rows] = outer_refs[j * chunks + chunk][...]


def weight_operands(weights, layer):
    own_inner, own_outer, inner_parts, outer_parts = weights
    shard, piece = own_inner.shape[2:]
    own = pl.BlockSpec((1, 1, shard, piece), lambda i: (layer, i, 0, 0))
    if len(inner_parts) == 1:
        rest = inner_parts[0].shape[1]
        parts = [pl.BlockSpec((1, rest, piece), lambda i, at=at: (i, 0, at)) for at in range(2)]
        return ([own_inner, own_outer, *inner_parts, *outer_parts], [own, own, *parts], 1)
    rows = inner_parts[0].shape[0]
    fixed = pl.BlockSpec((rows, piece), lambda i: (0, 0), pipeline_mode=pl.Buffered(1))
    return (
        [own_inner, own_outer, *inner_parts, *outer_parts],
        [own, own] + [fixed] * (2 * len(inner_parts)),
        len(inner_parts),
    )


def accumulate(step, total, part):
    @pl.when(step == 0)
    def _():
        total[...] = part

    @pl.when(step > 0)
    def _():
        total[...] += part


def finish_pair(step, total, near_ref, far_ref):
    rows = near_ref.shape[0]

    @pl.when(step == pl.num_programs(0) - 1)
    def _():
        near_ref[...] = total[:rows]
        far_ref[...] = low(total[rows:])


def feed_forward_kernel(count, hidden_ref, bias_ref, own_inner, own_outer, *refs):
    inner_refs, outer_refs = refs[:count], refs[count : 2 * count]
    near_ref, far_ref, active_ref, slope_ref, total, inner_now, outer_now = refs[2 * count :]
    step = pl.program_id(0)
    load_weights(step, own_inner, own_outer, inner_refs, outer_refs, inner_now, outer_now)
    pre = mm(hidden_ref[...], inner_now[...]) + bias_ref[...]
    tail = half_erfc(jnp.abs(pre))
    below = jnp.where(pre < 0.0, tail, 1.0 - tail)
    active = low(pre * below)
    active_ref[...] = active
    slope_ref[...] = low(below + pre * (jnp.exp(-0.5 * pre * pre) * 0.3989422804014327))
    accumulate(step, total, mm(active, outer_now[...], NT))
    finish_pair(step, total, near_ref, far_ref)


def feed_forward(hidden_pair, bias_row, weights, layer):
    rows, width = hidden_pair.shape
    hidden = bias_row.shape[1]
    block = hidden // 4
    arrays, specs, count = weight_operands(weights, layer)
    column = pl.BlockSpec((rows, block), lambda i: (0, i))
    half = pl.BlockSpec((rows // 2, width), lambda i: (0, 0))
    return pl.pallas_call(
        functools.partial(feed_forward_kernel, count),
        grid=(4,),
        in_specs=[
            pl.BlockSpec((rows, width), lambda i: (0, 0)),
            pl.BlockSpec((1, block), lambda i: (0, i)),
            *specs,
        ],
        out_specs=[half, half, column, column],
        out_shape=[
            jax.ShapeDtypeStruct((rows // 2, width), jnp.float32),
            jax.ShapeDtypeStruct((rows // 2, width), jnp.bfloat16),
            jax.ShapeDtypeStruct((rows, hidden), jnp.bfloat16),
            jax.ShapeDtypeStruct((rows, hidden), jnp.bfloat16),
        ],
        scratch_shapes=[
            pltpu.VMEM((rows, width), jnp.float32),
            pltpu.VMEM((width, block), jnp.bfloat16),
            pltpu.VMEM((width, block), jnp.bfloat16),
        ],
        cost_estimate=lasting(16),
        name="feed_forward",
    )(hidden_pair, bias_row, *arrays)


def feed_backward_kernel(count, grad_ref, slope_ref, own_inner, own_outer, *refs):
    inner_refs, outer_refs = refs[:count], refs[count : 2 * count]
    near_ref, far_ref, inner_grad_ref, bias_ref, total, inner_now, outer_now = refs[2 * count :]
    step = pl.program_id(0)
    load_weights(step, own_inner, own_outer, inner_refs, outer_refs, inner_now, outer_now)
    inner_grad = low(mm(grad_ref[...], outer_now[...]) * wide(slope_ref[...]))
    inner_grad_ref[...] = inner_grad
    bias_ref[...] = jnp.sum(wide(inner_grad), axis=0, keepdims=True)
    accumulate(step, total, mm(inner_grad, inner_now[...], NT))
    finish_pair(step, total, near_ref, far_ref)


def feed_backward(grad_pair, slope, weights, layer):
    rows, width = grad_pair.shape
    hidden = slope.shape[1]
    block = hidden // 4
    arrays, specs, count = weight_operands(weights, layer)
    column = pl.BlockSpec((rows, block), lambda i: (0, i))
    half = pl.BlockSpec((rows // 2, width), lambda i: (0, 0))
    return pl.pallas_call(
        functools.partial(feed_backward_kernel, count),
        grid=(4,),
        in_specs=[pl.BlockSpec((rows, width), lambda i: (0, 0)), column, *specs],
        out_specs=[half, half, column, pl.BlockSpec((1, block), lambda i: (0, i))],
        out_shape=[
            jax.ShapeDtypeStruct((rows // 2, width), jnp.float32),
            jax.ShapeDtypeStruct((rows // 2, width), jnp.bfloat16),
            jax.ShapeDtypeStruct((rows, hidden), jnp.bfloat16),
            jax.ShapeDtypeStruct((1, hidden), jnp.float32),
        ],
        scratch_shapes=[
            pltpu.VMEM((rows, width), jnp.float32),
            pltpu.VMEM((width, block), jnp.bfloat16),
            pltpu.VMEM((width, block), jnp.bfloat16),
        ],
        cost_estimate=lasting(11),
        name="feed_backward",
    )(grad_pair, slope, *arrays)


def weight_gradient_kernel(
    split,
    rows_ref,
    hidden_ref,
    grad_ref,
    mixed_ref,
    inner_grad_ref,
    active_ref,
    branch_ref,
    after_ref,
    *refs,
):
    outs, (hidden_t, grad_t, mixed_t) = refs[:-3], refs[-3:]
    step = pl.program_id(0)
    piece = active_ref.shape[1]

    @pl.when(step == 0)
    def _():
        hidden_t[...] = hidden_ref[...].T
        grad_t[...] = grad_ref[...].T
        mixed_t[...] = mixed_ref[...].T

    def write(store):
        store(0, piece, low(mm(hidden_t[...], inner_grad_ref[...])))
        store(piece, 2 * piece, low(mm(grad_t[...], active_ref[...])))
        store(2 * piece, 2 * piece + LANES, low(mm(mixed_t[...], branch_ref[...])))

    if not split:
        first_out, second_out = outs

        def store(begin, end, value):
            shard = value.shape[0] // 4
            ref = second_out if begin == piece else first_out
            column = {0: 0, piece: 0, 2 * piece: piece}[begin]
            for r in range(4):
                place = pl.multiple_of(rows_ref[r] * shard, shard)
                ref[0, pl.ds(place, shard), column : column + end - begin] = value[r * shard : (r + 1) * shard]

        write(store)
        return
    first_keep, first_send, second_keep, second_send = outs
    for j in range(4):

        @pl.when(step == j)
        def _(j=j):
            first = (first_send if j % 2 else first_keep, j // 2)
            second = (second_send if j // 2 else second_keep, j % 2)

            def store(begin, end, value):
                half = value.shape[0] // 2
                first[0][first[1], :, begin:end] = value[:half]
                second[0][second[1], :, begin:end] = value[half:]

            write(store)


def weight_gradients(hidden_pair, grad_pair, mixed_pair, inner_grad, active, branch_pair, plane_rows, split, after):
    rows, width = hidden_pair.shape
    hidden = active.shape[1]
    piece = hidden // 4
    total = 2 * piece + LANES
    whole = pl.BlockSpec((rows, width), lambda i, rows_ref: (0, 0))
    column = pl.BlockSpec((rows, piece), lambda i, rows_ref: (0, i))
    if split:
        shape = (2, width // 2, total)
        out_specs = [pl.BlockSpec(shape, lambda i, rows_ref: (0, 0, 0), pipeline_mode=pl.Buffered(1))] * 4
        out_shape = [jax.ShapeDtypeStruct(shape, jnp.bfloat16)] * 4
    else:
        out_specs = [
            pl.BlockSpec((1, width, columns), lambda i, rows_ref: (i, 0, 0)) for columns in (piece + LANES, piece)
        ]
        out_shape = [jax.ShapeDtypeStruct((4, width, columns), jnp.bfloat16) for columns in (piece + LANES, piece)]
    return pl.pallas_call(
        functools.partial(weight_gradient_kernel, split),
        grid_spec=pltpu.PrefetchScalarGridSpec(
            num_scalar_prefetch=1,
            grid=(4,),
            in_specs=[
                whole,
                whole,
                whole,
                column,
                column,
                pl.BlockSpec((rows, LANES), lambda i, rows_ref: (0, i)),
                pl.BlockSpec(memory_space=pl.ANY),
            ],
            out_specs=out_specs,
            scratch_shapes=[pltpu.VMEM((width, rows), jnp.bfloat16)] * 3,
        ),
        out_shape=out_shape,
        cost_estimate=lasting(13),
        name="weight_gradients",
    )(plane_rows, hidden_pair, grad_pair, mixed_pair, inner_grad, active, branch_pair, after)


def block_columns(values_in, order, width):
    return jnp.concatenate(
        [lax.dynamic_slice_in_dim(values_in, block * width, width, 1) for block in order], axis=1
    )


def norm_forward(values_in, gain_row, shift_row):
    centre = values_in - jnp.mean(values_in, axis=-1, keepdims=True)
    spread = jnp.mean(centre * centre, axis=-1, keepdims=True)
    inverse = lax.rsqrt(spread + epsilon)
    unit = centre * inverse
    return (unit * gain_row + shift_row, unit, inverse)


def norm_backward(grad, unit, inverse, gain_row):
    grad_unit = grad * gain_row
    back = inverse * (
        grad_unit
        - jnp.mean(grad_unit, axis=-1, keepdims=True)
        - unit * jnp.mean(grad_unit * unit, axis=-1, keepdims=True)
    )
    return (back, jnp.sum(grad * unit, axis=0), jnp.sum(grad, axis=0))


def attention_output_kernel(
    place_ref,
    heads_ref,
    own_ref,
    near_ref,
    far_ref,
    activation_ref,
    bias_ref,
    gain_ref,
    shift_ref,
    mixed_ref,
    unit_ref,
    inverse_ref,
    hidden_ref,
    turned_ref,
    held,
    held_low,
):
    shard = own_ref.shape[0]
    half = near_ref.shape[1]
    for p in range(8):
        mixed_ref[:, p * LANES : (p + 1) * LANES] = heads_ref[place_ref[p]]
    own, rest = mixed_ref[:, :shard], mixed_ref[:, shard:]
    held[:, :half] = mm(own, own_ref[:, :half]) + mm(rest, near_ref[...])
    held[:, half:] = mm(own, own_ref[:, half:]) + mm(rest, far_ref[...])
    attended = jnp.concatenate(
        [held[:, pl.ds(pl.multiple_of(place_ref[8 + b] * LANES, LANES), LANES)] for b in range(8)], axis=1
    )
    first_pre = wide(activation_ref[...]) + (attended + bias_ref[...])
    hidden, unit, inverse = norm_forward(first_pre, gain_ref[...], shift_ref[...])
    unit_ref[...] = unit
    inverse_ref[...] = inverse
    hidden_ref[...] = hidden
    held_low[...] = low(hidden)
    for r in range(4):
        turned_ref[:, r * shard : (r + 1) * shard] = held_low[
            :, pl.ds(pl.multiple_of(place_ref[16 + r] * shard, shard), shard)
        ]


def attention_output(heads, out_weights, activation, bias_row, gain_row, shift_row, places):
    rows, width = activation.shape
    wide_rows = jax.ShapeDtypeStruct((rows, width), jnp.float32)
    low_rows = jax.ShapeDtypeStruct((rows, width), jnp.bfloat16)
    return pl.pallas_call(
        attention_output_kernel,
        grid_spec=pltpu.PrefetchScalarGridSpec(
            num_scalar_prefetch=1,
            grid=(1,),
            in_specs=[
                pl.BlockSpec(array.shape, lambda i, place_ref, rank=array.ndim: (0,) * rank)
                for array in (heads, *out_weights, activation, bias_row, gain_row, shift_row)
            ],
            out_specs=[
                pl.BlockSpec((rows, width), lambda i, place_ref: (0, 0)),
                pl.BlockSpec((rows, width), lambda i, place_ref: (0, 0)),
                pl.BlockSpec((rows, 1), lambda i, place_ref: (0, 0)),
                pl.BlockSpec((rows, width), lambda i, place_ref: (0, 0)),
                pl.BlockSpec((rows, width), lambda i, place_ref: (0, 0)),
            ],
            scratch_shapes=[pltpu.VMEM((rows, width), jnp.float32), pltpu.VMEM((rows, width), jnp.bfloat16)],
        ),
        out_shape=[low_rows, wide_rows, jax.ShapeDtypeStruct((rows, 1), jnp.float32), wide_rows, low_rows],
        cost_estimate=lasting(5),
        name="attention_output",
    )(places, heads, *out_weights, activation, bias_row, gain_row, shift_row)


def attention_output_back_kernel(
    place_ref,
    near_back_ref,
    came_ref,
    grad_ref,
    unit_ref,
    inverse_ref,
    gain_ref,
    own_ref,
    near_ref,
    far_ref,
    first_ref,
    rows_ref,
    spread_ref,
    sent_ref,
    held,
    held_low,
):
    shard = own_ref.shape[0]
    half = near_ref.shape[1]
    held[...] = near_back_ref[...] + wide(came_ref[...])
    back = jnp.concatenate(
        [held[:, pl.ds(pl.multiple_of(place_ref[16 + r] * shard, shard), shard)] for r in range(4)], axis=1
    )
    grad_first, gain_row, shift_row = norm_backward(
        grad_ref[...] + back, unit_ref[...], inverse_ref[...], gain_ref[...]
    )
    first_ref[...] = grad_first
    branch = low(grad_first)
    rows_ref[0:1] = gain_row[None]
    rows_ref[1:2] = shift_row[None]
    rows_ref[2:3] = jnp.sum(wide(branch), axis=0, keepdims=True)
    held_low[...] = branch
    for p in range(8):
        spread_ref[:, p * LANES : (p + 1) * LANES] = held_low[
            :, pl.ds(pl.multiple_of(place_ref[24 + p] * LANES, LANES), LANES)
        ]
    spread = spread_ref[...]
    held_low[:, :shard] = low(mm(spread, own_ref[...], NT))
    held_low[:, shard:] = low(mm(spread[:, :half], near_ref[...], NT) + mm(spread[:, half:], far_ref[...], NT))
    for head in range(8):
        begin = place_ref[16 + head // 2] * shard + (head % 2) * LANES
        sent_ref[head] = held_low[:, pl.ds(pl.multiple_of(begin, LANES), LANES)]


def attention_output_back(near_back, came, grad_second, unit, inverse, gain_row, out_weights, places):
    rows, width = grad_second.shape
    operands = (near_back, came, grad_second, unit, inverse, gain_row, *out_weights)
    whole = pl.BlockSpec((rows, width), lambda i, place_ref: (0, 0))
    return pl.pallas_call(
        attention_output_back_kernel,
        grid_spec=pltpu.PrefetchScalarGridSpec(
            num_scalar_prefetch=1,
            grid=(1,),
            in_specs=[pl.BlockSpec(array.shape, lambda i, place_ref: (0, 0)) for array in operands],
            out_specs=[
                whole,
                pl.BlockSpec((3, width), lambda i, place_ref: (0, 0)),
                whole,
                pl.BlockSpec((8, rows, LANES), lambda i, place_ref: (0, 0, 0)),
            ],
            scratch_shapes=[pltpu.VMEM((rows, width), jnp.float32), pltpu.VMEM((rows, width), jnp.bfloat16)],
        ),
        out_shape=[
            jax.ShapeDtypeStruct((rows, width), jnp.float32),
            jax.ShapeDtypeStruct((3, width), jnp.float32),
            jax.ShapeDtypeStruct((rows, width), jnp.bfloat16),
            jax.ShapeDtypeStruct((8, rows, LANES), jnp.bfloat16),
        ],
        cost_estimate=lasting(6),
        name="attention_output_back",
    )(places, *operands)


def token_gradient_kernel(
    place_ref, query_ref, key_ref, value_ref, joint_ref, *refs
):
    near_ref, far_ref, packed_ref, bias_ref = refs[-4:]
    step = pl.program_id(0)
    packed = jnp.concatenate([query_ref[...], key_ref[...], value_ref[...]], axis=1)
    packed_ref[...] = packed
    accumulate(step, bias_ref, jnp.sum(wide(packed), axis=0, keepdims=True))
    part = mm(packed, joint_ref[...], NT)

    @pl.when(step < 4)
    def _():
        near_ref[0] = part

    @pl.when(step >= 4)
    def _():
        far_ref[0] = low(part)


def token_gradients(grads, joint, chips):
    tokens = grads[0].shape[0]
    rows = tokens // 8
    width, columns = joint.shape
    block = pl.BlockSpec((rows, LANES), lambda i, place_ref: (i, 0))
    return pl.pallas_call(
        token_gradient_kernel,
        grid_spec=pltpu.PrefetchScalarGridSpec(
            num_scalar_prefetch=1,
            grid=(8,),
            in_specs=[block, block, block, pl.BlockSpec((width, columns), lambda i, place_ref: (0, 0))],
            out_specs=[
                pl.BlockSpec((1, rows, width), lambda i, place_ref: (place_ref[jnp.minimum(i, 3)], 0, 0)),
                pl.BlockSpec((1, rows, width), lambda i, place_ref: (place_ref[jnp.maximum(i - 4, 0)], 0, 0)),
                pl.BlockSpec((rows, columns), lambda i, place_ref: (i, 0)),
                pl.BlockSpec((1, columns), lambda i, place_ref: (0, 0)),
            ],
        ),
        out_shape=[
            jax.ShapeDtypeStruct((4, rows, width), jnp.float32),
            jax.ShapeDtypeStruct((4, rows, width), jnp.bfloat16),
            jax.ShapeDtypeStruct((tokens, columns), jnp.bfloat16),
            jax.ShapeDtypeStruct((1, columns), jnp.float32),
        ],
        cost_estimate=lasting(10),
        name="token_gradients",
    )(chips, *grads, joint)


def plane_sum_kernel(first_keep, first_came, first_last, second_keep, second_came, second_last, *outs):
    shard = outs[0].shape[0]
    first = wide(first_keep[0]) + wide(first_came[0]) + wide(first_last[...])
    second = wide(second_keep[0]) + wide(second_came[0]) + wide(second_last[...])
    outs[0][...] = first[:shard]
    outs[1][...] = low(first[shard:])
    outs[2][...] = low(second[:shard])
    outs[3][...] = low(second[shard:])


def plane_sum(first, second):
    columns = first[0].shape[2]
    shard = first[0].shape[1] // 2
    block = pl.BlockSpec((1, 2 * shard, columns), lambda i: (0, 0, 0))
    last = pl.BlockSpec((2 * shard, columns), lambda i: (0, 0))
    return pl.pallas_call(
        plane_sum_kernel,
        grid=(1,),
        in_specs=[block, block, last] * 2,
        out_specs=[pl.BlockSpec((shard, columns), lambda i: (0, 0))] * 4,
        out_shape=[jax.ShapeDtypeStruct((shard, columns), jnp.float32)]
        + [jax.ShapeDtypeStruct((shard, columns), jnp.bfloat16)] * 3,
        cost_estimate=lasting(3),
        name="plane_sum",
    )(*first, *second)


def final_sum_kernel(*refs):
    left_ref, right_ref = refs[-2:]
    half = left_ref.shape[1]
    whole = jnp.concatenate(
        [
            low(wide(refs[at][...]) + wide(refs[at + 1][...]) + wide(refs[at + 2][...]) + wide(refs[at + 3][...]))
            for at in (0, 4)
        ],
        axis=1,
    )
    left_ref[...] = whole[:, :half]
    right_ref[...] = whole[:, half:]


def final_sum(plain, joint):
    shard = plain[0].shape[0]
    half = (plain[0].shape[1] + joint[0].shape[1]) // 2
    operands = (*plain, *joint)
    return pl.pallas_call(
        final_sum_kernel,
        grid=(1,),
        in_specs=[pl.BlockSpec(array.shape, lambda i: (0, 0)) for array in operands],
        out_specs=[pl.BlockSpec((shard, half), lambda i: (0, 0))] * 2,
        out_shape=[jax.ShapeDtypeStruct((shard, half), jnp.bfloat16)] * 2,
        cost_estimate=lasting(3),
        name="final_sum",
    )(*operands)


def small_rows_kernel(place_ref, joint_ref, first_ref, outer_ref, gain_ref, shift_ref, inner_ref, out_ref):
    shard = out_ref.shape[1] // 4
    out_ref[...] = jnp.zeros_like(out_ref)
    at = pl.ds(pl.multiple_of(place_ref[0] * LANES, LANES), LANES)
    out_ref[0:1, at] = joint_ref[:, :LANES]
    out_ref[1:2, at] = joint_ref[:, 2 * LANES :]
    out_ref[2:3] = first_ref[2:3]
    out_ref[3:4] = outer_ref[...]
    out_ref[4:6] = first_ref[0:2]
    out_ref[6:7] = gain_ref[...]
    out_ref[7:8] = shift_ref[...]
    count = inner_ref.shape[1] // shard // 4
    for j in range(4):
        block = place_ref[1 + j]
        columns = pl.ds(pl.multiple_of((block // 2) * shard, shard), shard)
        for part in range(count):
            begin = (j * count + part) * shard
            row = 8 + (block % 2) * count + part
            out_ref[pl.ds(row, 1), columns] = inner_ref[:, begin : begin + shard]


def small_rows(places, joint, first, outer, gain, shift, inner):
    width = first.shape[1]
    operands = (joint, first, outer[None], gain[None], shift[None], inner)
    return pl.pallas_call(
        small_rows_kernel,
        grid_spec=pltpu.PrefetchScalarGridSpec(
            num_scalar_prefetch=1,
            grid=(1,),
            in_specs=[pl.BlockSpec(array.shape, lambda i, place_ref: (0, 0)) for array in operands],
            out_specs=pl.BlockSpec((16, width), lambda i, place_ref: (0, 0)),
        ),
        out_shape=jax.ShapeDtypeStruct((16, width), jnp.float32),
        cost_estimate=lasting(2),
        name="small_rows",
    )(places, *operands)


def gate(values_in, *points):
    anywhere = pl.BlockSpec(memory_space=pl.ANY)
    return pl.pallas_call(
        lambda *refs: None,
        in_specs=[anywhere] * (len(values_in) + len(points)),
        out_specs=[anywhere] * len(values_in),
        out_shape=[jax.ShapeDtypeStruct(value.shape, value.dtype) for value in values_in],
        input_output_aliases={i: i for i in range(len(values_in))},
        cost_estimate=SMALL_COST,
        name="gate",
    )(*values_in, *points)


def spread_tokens(rows_in):
    half = rows_in.shape[1] // 2
    left, right = rows_in[:, :half], rows_in[:, half:]
    left_pair = jnp.stack([left, swap(left, ALONG_X)])
    right_pair = jnp.stack([right, swap(right, ALONG_Y)])
    left_far = swap(left_pair, ALONG_Y)
    right_far = swap(right_pair, ALONG_X)
    left_all = jnp.concatenate([left_pair, left_far])
    right_all = jnp.stack([right_pair[0], right_far[0], right_pair[1], right_far[1]])
    near = jnp.concatenate([left_all, right_all], axis=2).reshape(4 * rows_in.shape[0], rows_in.shape[1])
    return (near, swap(near, CORE))


def plane_groups():
    count = lax.axis_size("ctx")
    return [list(range(0, count, 2)), list(range(1, count, 2))]


def collect_tokens(sent, points, late_points):
    if points:
        (sent,) = gate([sent], *points)
    came = lax.all_to_all(sent, "ctx", 0, 0, axis_index_groups=plane_groups(), tiled=True)
    if late_points:
        (came,) = gate([came], *late_points)
    return jnp.sum(wide(came), axis=0)


def plane_pieces(left, right, *points):
    left_pair = jnp.stack([left, swap(left, ALONG_X)])
    right_pair = jnp.stack([right, swap(right, ALONG_Y)])
    left_far, right_far = gate([swap(left_pair, ALONG_Y), swap(right_pair, ALONG_X)], *points)
    left_all = jnp.concatenate([left_pair, left_far])
    right_all = jnp.stack([right_pair[0], right_far[0], right_pair[1], right_far[1]])
    near = jnp.concatenate([left_all, right_all], axis=2)
    return (near, swap(near, CORE))


def exchange(blocks):
    return lax.all_to_all(blocks, "ctx", 0, 0, tiled=True)


def head_split_body(
    tokens,
    cotangent,
    doc_starts,
    doc_lengths,
    query_weight,
    key_weight,
    value_weight,
    out_weight,
    inner_weight,
    outer_weight,
    query_bias,
    value_bias,
    out_bias,
    inner_bias,
    outer_bias,
    first_gain,
    first_shift,
    second_gain,
    second_shift,
):
    rows = tokens.shape[1]
    width = tokens.shape[2]
    here = lax.axis_index("ctx")
    plane = lax.axis_index("wsh")
    planes = lax.axis_size("wsh")
    shard = width // planes
    hidden = inner_weight.shape[2]
    piece = hidden // 8
    core = here % 2
    chip = here // 2
    relative = jnp.arange(8, dtype=jnp.int32)
    spread = jnp.array((0, 2, 4, 6, 1, 3, 5, 7), jnp.int32)
    turned = [(plane - r) % planes for r in range(planes)]
    unturned = turned
    positions = ((here ^ spread)[:, None] * rows + jnp.arange(rows, dtype=jnp.int32)).reshape(-1)
    labels = doc_labels(positions, doc_starts[0], doc_lengths[0])[:, None]

    four = jnp.arange(4, dtype=jnp.int32)
    chip_order = [chip ^ four, four]
    inner_order = [core * 4 + order for order in chip_order]
    out_order = [jnp.concatenate([2 * order + core, 2 * order + 1 - core]) for order in chip_order]
    block_order = here ^ spread
    plane_rows = jnp.stack(turned).astype(jnp.int32)
    first_own, second_own, joint_own = own_pieces(
        inner_weight,
        outer_weight,
        out_weight,
        (query_weight, key_weight, value_weight),
        (
            query_bias,
            value_bias,
            out_bias,
            outer_bias,
            first_gain,
            first_shift,
            second_gain,
            second_shift,
            inner_bias,
        ),
        here,
        core * 4 + chip,
    )
    joint_width = 3 * LANES

    def ordered(stack, order):
        return jnp.concatenate([lax.dynamic_index_in_dim(stack, i, 0, keepdims=False) for i in order], axis=0)

    first_joint = joint_own[0]
    joint_turned = jnp.stack([first_joint] + [turn(first_joint, r) for r in range(1, planes)])
    joint_first = ordered(joint_turned[:, :shard], unturned)
    small_all = ordered(joint_turned[:, None, shard:, :shard], unturned)

    def small(layer, index):
        return small_all[:, 2 * index + layer].reshape(width)

    inner_bias_all = small_all[:, 16:24].reshape(planes, 4, LAYERS, shard).transpose(2, 0, 1, 3).reshape(LAYERS, hidden)

    inner_near = ordered(lax.all_gather(first_own[0], "wsh", axis=0), turned[1:])
    first_tokens = spread_tokens(tokens[0])
    (outer_sent,) = gate([second_own[0]], first_tokens[0])
    outer_stack = lax.all_gather(outer_sent, "wsh", axis=0)
    middle = 3 * shard // 2

    def spread_first(near):
        left, right = near[:middle], near[middle:]
        return (left, right, swap(left, ALONG_X), swap(right, ALONG_Y))

    def spread_second(left, right, left_x, right_y):
        lefts = (left, left_x, swap(left, ALONG_Y), swap(left_x, ALONG_Y))
        rights = (right, swap(right, ALONG_X), right_y, swap(right_y, ALONG_X))
        return [part for pair in zip(lefts, rights) for part in pair]

    inner_half = spread_first(inner_near)
    layer_own = jnp.concatenate(
        [first_own[1, :, :piece], second_own[1], first_own[1, :, piece:], joint_own[1, :shard]], axis=1
    )
    wide_piece = 2 * piece + LANES

    def layer_weights(layer):
        if layer == 0:
            near = jnp.concatenate(
                [
                    jnp.concatenate([inner_first[2 * j][:, piece:], inner_first[2 * j + 1][:, piece:]], axis=0)
                    for j in range(4)
                ],
                axis=1,
            )
            weights = (inner_own, outer_own, inner_first, outer_first)
        else:
            near = jnp.concatenate([out_parts[j] for j in range(4)], axis=1)
            weights = (inner_own, outer_own)
        return (weights, (out_own[layer], near, swap(near, CORE)))

    def out_place(layer, block):
        at = (block // 2) ^ chip if layer == 0 else block // 2
        return at + 4 * ((block % 2) ^ core)

    activation = tokens[0]
    stashed = []
    outputs = []
    for layer in range(LAYERS):
        joint = joint_first if layer == 0 else joint_second
        first_gain_row, first_shift_row = wide(small(layer, 4)), wide(small(layer, 5))
        second_gain_row, second_shift_row = wide(small(layer, 6)), wide(small(layer, 7))

        near_tokens, far_tokens = first_tokens if layer == 0 else spread_tokens(activation)
        everyone = jnp.concatenate([near_tokens, far_tokens], axis=0)
        query_bias_own = lax.dynamic_slice_in_dim(small(layer, 0), here * LANES, LANES, 0)
        value_bias_own = lax.dynamic_slice_in_dim(small(layer, 1), here * LANES, LANES, 0)
        joint_bias = wide(jnp.concatenate([query_bias_own, jnp.zeros_like(query_bias_own), value_bias_own]))
        packed = low(mm(everyone, joint) + joint_bias)
        if layer == 0:
            packed, layer_own = gate([packed, layer_own], inner_near)
            second_stack = lax.all_gather(layer_own, "wsh", axis=0)
        mixed, log_all = attention_forward(packed, labels, block_order)
        if layer == 0:
            inner_own, outer_own, out_own = own_blocks(
                inner_weight,
                outer_weight,
                out_weight,
                jnp.concatenate(inner_order),
                jnp.concatenate(out_order),
                mixed,
            )
            left_x, right_y, outer_stack = gate([*inner_half[2:], outer_stack], mixed)
            inner_first = spread_second(*inner_half[:2], left_x, right_y)
            outer_first = spread_second(*spread_first(ordered(outer_stack, turned[1:])))
        else:
            out_parts = lax.all_to_all(
                jnp.broadcast_to(out_second, (4, *out_second.shape)),
                "ctx",
                0,
                0,
                axis_index_groups=plane_groups(),
                tiled=True,
            )
            (out_parts,) = gate([out_parts], mixed)
        weights, out_weights = layer_weights(layer)
        mixed_heads = exchange(mixed)
        places = jnp.stack(
            [2 * turned[p // 2] + p % 2 for p in range(8)]
            + [out_place(layer, b) for b in range(8)]
            + turned
            + [jnp.int32(0)] * 4
            + [out_order[layer][p] for p in range(8)]
        ).astype(jnp.int32)
        mixed_turned, first_unit, first_inverse, hidden_rows, hidden_turned = attention_output(
            mixed_heads,
            out_weights,
            activation,
            wide(small(layer, 2))[None],
            first_gain_row[None],
            first_shift_row[None],
            places,
        )
        if layer == 1:
            second_parts = gate([second_parts], hidden_turned)
            weights = (*weights, second_parts, second_parts)
        mixed_pair = jnp.concatenate([mixed_turned, swap(mixed_turned, CORE)], axis=0)
        hidden_pair = jnp.concatenate([hidden_turned, swap(hidden_turned, CORE)], axis=0)
        inner_bias_own = jnp.concatenate(
            [lax.dynamic_slice_in_dim(inner_bias_all[layer], inner_order[layer][j] * piece, piece, 0) for j in range(4)]
        )
        outer_near, outer_far, active, slope = feed_forward(
            hidden_pair, wide(inner_bias_own)[None], weights, layer
        )
        outer_turned = outer_near + wide(swap(outer_far, CORE))
        if layer == 0:
            (second_stack,) = gate([second_stack], active)
            joint_second = second_stack[:, :, wide_piece:].reshape(width, joint_width)
            others_second = ordered(second_stack[:, :, :wide_piece], turned[1:])
            sent_second = (others_second[:, : piece + LANES], others_second[:, piece + LANES :])
            second_parts = lax.all_gather(
                others_second[:, : 2 * piece], "ctx", axis=0, axis_index_groups=plane_groups()
            )
            out_second = others_second[:, 2 * piece :]
        outer_out = block_columns(outer_turned, unturned, shard)
        second_pre = hidden_rows + (outer_out + wide(small(layer, 3)))
        result, second_unit, second_inverse = norm_forward(second_pre, second_gain_row, second_shift_row)
        stashed.append(
            (
                everyone,
                packed,
                log_all,
                mixed_pair,
                first_unit,
                first_inverse,
                hidden_pair,
                active,
                slope,
                second_unit,
                second_inverse,
                joint,
                out_weights,
                places,
                weights,
                first_gain_row,
                second_gain_row,
            )
        )
        activation = low(result)
        outputs.append(activation)

    gradient = wide(cotangent[0])
    small_grads = [None] * LAYERS
    for layer in reversed(range(LAYERS)):
        (
            everyone,
            packed,
            log_all,
            mixed_pair,
            first_unit,
            first_inverse,
            hidden_pair,
            active,
            slope,
            second_unit,
            second_inverse,
            joint,
            out_weights,
            places,
            weights,
            first_gain_row,
            second_gain_row,
        ) = stashed[layer]
        grad_second, grad_second_gain, grad_second_shift = norm_backward(
            gradient, second_unit, second_inverse, second_gain_row
        )
        grad_outer = low(grad_second)
        grad_outer_bias = jnp.sum(wide(grad_outer), axis=0)
        grad_turned = block_columns(grad_outer, turned, shard)
        grad_pair = jnp.concatenate([grad_turned, swap(grad_turned, CORE)], axis=0)
        hidden_near, hidden_far, grad_inner, grad_inner_bias = feed_backward(grad_pair, slope, weights, layer)
        grad_first, first_rows, branch_spread, grad_sent = attention_output_back(
            hidden_near,
            swap(hidden_far, CORE),
            grad_second,
            first_unit,
            first_inverse,
            first_gain_row[None],
            out_weights,
            places,
        )
        grad_mixed = exchange(grad_sent)
        branch_half = 4 * LANES
        branch_pair = jnp.concatenate(
            [branch_spread[:, :branch_half], swap(branch_spread[:, branch_half:], CORE)], axis=0
        )
        summed = weight_gradients(
            hidden_pair, grad_pair, mixed_pair, grad_inner, active, branch_pair, plane_rows, layer == 0, grad_sent
        )
        if layer == 0:
            (grad_mixed,) = gate([grad_mixed], summed[0], plane_first)
        else:
            grad_mixed, first_sum = gate([grad_mixed, summed[0]])
        grad_query, grad_key, grad_value = attention_backward(packed, labels, grad_mixed, log_all, block_order)
        if layer == 0:
            first_keep, first_send, second_keep, second_send = summed
            first_came = swap(first_send, ALONG_X)
            second_came = swap(second_send, ALONG_Y)
        near_part, far_part, grad_packed, joint_bias_grad = token_gradients(
            (grad_query, grad_key, grad_value), joint, chip_order[0]
        )
        grad_joint = low(mm(everyone, grad_packed, TN))
        far_came = swap(far_part, CORE)
        tokens_sent = low(near_part + wide(far_came))
        small_grads[layer] = small_rows(
            jnp.concatenate([here[None], inner_order[layer]]).astype(jnp.int32),
            joint_bias_grad,
            first_rows,
            grad_outer_bias,
            grad_second_gain,
            grad_second_shift,
            grad_inner_bias,
        )
        if layer == 1:
            (plane_first,) = [
                lax.psum_scatter(
                    first_sum.reshape(4 * width, -1),
                    "ctx",
                    scatter_dimension=0,
                    axis_index_groups=plane_groups(),
                    tiled=True,
                )
            ]
            (plane_first,) = gate([plane_first], far_came)
            plane_rows_first = [
                lax.dynamic_slice_in_dim(plane_first, turned[r] * shard, shard, 0) for r in range(planes)
            ]
            came_first = [turn(plane_rows_first[r], planes - r) for r in range(1, planes)]
            gradient = grad_first + collect_tokens(tokens_sent, (), (grad_joint,))
            (second_sum,) = gate([summed[1]], gradient, plane_first)
            plane_second = lax.psum_scatter(
                second_sum.reshape(4 * width, -1),
                "ctx",
                scatter_dimension=0,
                axis_index_groups=plane_groups(),
                tiled=True,
            )
            sum_joint = lax.psum_scatter(grad_joint, "wsh", scatter_dimension=0, tiled=True)
            continue
        small_sent = jnp.concatenate(small_grads, axis=0)
        small_plane = jnp.sum(
            lax.all_to_all(
                jnp.stack([small_sent[:, p * shard : (p + 1) * shard] for p in range(planes)]), "wsh", 0, 0, tiled=True
            ),
            axis=0,
        )
        small_spread = jnp.broadcast_to(small_plane, (8, *small_plane.shape))
        first_came, second_came = gate([first_came, second_came], near_part, grad_joint, *came_first)
        sum_first = wide(plane_rows_first[0])
        for part in came_first:
            sum_first = sum_first + wide(part)
        sum_first = low(sum_first)
        first_next = low(wide(first_keep[1]) + wide(first_came[1]))
        second_next = low(wide(second_keep[1]) + wide(second_came[1]))
        joint_rows = [lax.dynamic_slice_in_dim(grad_joint, turned[r] * shard, shard, 0) for r in range(planes)]
        came_joint = [turn(joint_rows[r], planes - r) for r in range(1, planes)]
        first_last, second_last = gate(
            [swap(first_next, ALONG_Y), swap(second_next, ALONG_X)], small_plane, tokens_sent, *came_joint
        )
        own_total, *sent = plane_sum(
            (first_keep, first_came, first_last), (second_keep, second_came, second_last)
        )
        came = [turn(sent[r - 1], planes - r) for r in range(1, planes)]
        (plane_second,) = gate([plane_second], grad_mixed)
        sum_second = lax.psum_scatter(plane_second, "wsh", scatter_dimension=0, tiled=True)
        sum_first, sum_second, sum_joint = gate([sum_first, sum_second, sum_joint], own_total, tokens_sent)
        everything = lax.all_gather(
            jnp.concatenate([sum_first[:, :piece], sum_second, sum_first[:, piece:], sum_joint], axis=1),
            "ctx",
            axis=0,
        )
        gradient = grad_first + collect_tokens(tokens_sent, (own_total,), ())
        (small_spread,) = gate([small_spread], gradient)
        small_mine = jnp.sum(exchange(small_spread), axis=0).reshape(LAYERS, 16, shard)
        came = gate(came, small_mine)
        left_total, right_total = final_sum((own_total, *came), (joint_rows[0], *came_joint))
        (everything,) = gate([everything], left_total)
        *placed, placed_token = place_pieces(everything, relative, 1, None)
    near, far = plane_pieces(left_total, right_total, placed_token, small_mine)
    near_first = here ^ (2 * four)
    *placed, placed_token = place_pieces(near, near_first, 0, placed)
    (far,) = gate([far], placed_token)
    *placed, _ = place_pieces(far, near_first ^ 1, 0, placed)
    small_outs = [small_mine[:, i] for i in range(8)]
    return (
        outputs[0][None],
        outputs[1][None],
        low(gradient)[None],
        *placed,
        small_outs[0],
        small_outs[1],
        small_outs[2],
        small_mine[:, 8:12].reshape(LAYERS, 4 * shard),
        small_outs[3],
        small_outs[4],
        small_outs[5],
        small_outs[6],
        small_outs[7],
    )


def choose_body(mesh):
    if mesh.shape["ctx"] == 8 and HEADS // 8 == 2:
        return head_split_body
    return window_body


def solution(mesh):
    in_specs = (
        P("wsh", "ctx", None),
        P("wsh", "ctx", None),
        P("wsh", None),
        P("wsh", None),
        P(None, "wsh", None),
        P(None, "wsh", None),
        P(None, "wsh", None),
        P(None, "wsh", None),
        P(None, "wsh", None),
        P(None, None, "wsh"),
        P(None, "wsh"),
        P(None, "wsh"),
        P(None, "wsh"),
        P(None, "wsh"),
        P(None, "wsh"),
        P(None, "wsh"),
        P(None, "wsh"),
        P(None, "wsh"),
        P(None, "wsh"),
    )
    out_specs = (
        P("wsh", "ctx", None),
        P("wsh", "ctx", None),
        P("wsh", "ctx", None),
        P(None, "wsh", None),
        P(None, "wsh", None),
        P(None, "wsh", None),
        P(None, "wsh", None),
        P(None, "wsh", None),
        P(None, None, "wsh"),
        P(None, "wsh"),
        P(None, "wsh"),
        P(None, "wsh"),
        P(None, "wsh"),
        P(None, "wsh"),
        P(None, "wsh"),
        P(None, "wsh"),
        P(None, "wsh"),
        P(None, "wsh"),
    )
    return jax.shard_map(choose_body(mesh), mesh=mesh, in_specs=in_specs, out_specs=out_specs, check_vma=False)
```

```python
import functools

import jax
import jax.numpy as jnp
from jax import lax
from jax.experimental import pallas as pl
from jax.experimental.pallas import tpu as pltpu
from jax.sharding import PartitionSpec as P

HEADS = 16
HDIM = 64
LAYERS = 2
DOC_CAP = 2000


epsilon = 1e-05
neg_fill = -1e30
head_pair = 2


def from_behind(block, axis, distance):
    devices = range(lax.axis_size(axis))
    route = [(i - distance, i) for i in devices if i - distance in devices]
    return lax.ppermute(block, axis, route)


def normalize(values_in, gain_row, shift_row):
    centre = values_in - jnp.mean(values_in, axis=-1, keepdims=True)
    spread = jnp.mean(centre * centre, axis=-1, keepdims=True)
    return centre * lax.rsqrt(spread + epsilon) * gain_row + shift_row


def exact_gelu(values_in):
    return jax.nn.gelu(values_in, approximate=False)


def product(form, left, right):
    return jnp.einsum(form, left, right, preferred_element_type=jnp.float32)


def doc_labels(positions, starts, lengths):
    inside = (positions[:, None] >= starts[None, :]) & (
        positions[:, None] < (starts + lengths)[None, :]
    )
    labels = jnp.arange(1, starts.shape[0] + 1, dtype=jnp.int32)
    return jnp.sum(jnp.where(inside, labels[None, :], 0), axis=1)


def extend_rows(rows_in, dim, reach, mover):
    pieces = []
    for offset in range(-reach, reach + 1):
        if offset == 0:
            pieces.append(rows_in)
        else:
            pieces.append(mover(rows_in, -offset))
    return jnp.concatenate(pieces, axis=dim)


def move_keys_fwd(rows_in, steps):
    return from_behind(rows_in, "ctx", steps)


def move_keys_back(rows_in, steps):
    return from_behind(rows_in, "ctx", steps)


def fetch_forward(params, layer_index):
    shards = [piece[layer_index].astype(jnp.bfloat16) for piece in params]
    return (
        lax.all_gather(shards[0], "wsh", axis=0, tiled=True),
        lax.all_gather(shards[1], "wsh", axis=0, tiled=True),
        lax.all_gather(shards[2], "wsh", axis=0, tiled=True),
        lax.all_gather(shards[3], "wsh", axis=0, tiled=True),
        lax.all_gather(shards[4], "wsh", axis=0, tiled=True),
        lax.all_gather(shards[5], "wsh", axis=1, tiled=True),
        lax.all_gather(shards[6], "wsh", axis=0, tiled=True),
        lax.all_gather(shards[7], "wsh", axis=0, tiled=True),
        lax.all_gather(shards[8], "wsh", axis=0, tiled=True),
        lax.all_gather(shards[9], "wsh", axis=0, tiled=True),
        lax.all_gather(shards[10], "wsh", axis=0, tiled=True),
        lax.all_gather(shards[11], "wsh", axis=0, tiled=True),
        lax.all_gather(shards[12], "wsh", axis=0, tiled=True),
        lax.all_gather(shards[13], "wsh", axis=0, tiled=True),
        lax.all_gather(shards[14], "wsh", axis=0, tiled=True),
    )


def fetch_backward(params, layer_index):
    shards = [piece[layer_index].astype(jnp.bfloat16) for piece in params]
    return (
        lax.all_gather(shards[0], "wsh", axis=0, tiled=True),
        lax.all_gather(shards[1], "wsh", axis=0, tiled=True),
        lax.all_gather(shards[2], "wsh", axis=0, tiled=True),
        lax.all_gather(shards[3], "wsh", axis=0, tiled=True),
        lax.all_gather(shards[4], "wsh", axis=0, tiled=True),
        lax.all_gather(shards[5], "wsh", axis=1, tiled=True),
        lax.all_gather(shards[6], "wsh", axis=0, tiled=True),
        lax.all_gather(shards[7], "wsh", axis=0, tiled=True),
        lax.all_gather(shards[8], "wsh", axis=0, tiled=True),
        lax.all_gather(shards[9], "wsh", axis=0, tiled=True),
        lax.all_gather(shards[10], "wsh", axis=0, tiled=True),
        lax.all_gather(shards[11], "wsh", axis=0, tiled=True),
        lax.all_gather(shards[12], "wsh", axis=0, tiled=True),
        lax.all_gather(shards[13], "wsh", axis=0, tiled=True),
        lax.all_gather(shards[14], "wsh", axis=0, tiled=True),
    )


def reduce_grads(local_grads):
    shares = (
        lax.psum_scatter(
            local_grads[0].astype(jnp.bfloat16), "wsh", scatter_dimension=0, tiled=True
        ).astype(jnp.float32),
        lax.psum_scatter(
            local_grads[1].astype(jnp.bfloat16), "wsh", scatter_dimension=0, tiled=True
        ).astype(jnp.float32),
        lax.psum_scatter(
            local_grads[2].astype(jnp.bfloat16), "wsh", scatter_dimension=0, tiled=True
        ).astype(jnp.float32),
        lax.psum_scatter(
            local_grads[3].astype(jnp.bfloat16), "wsh", scatter_dimension=0, tiled=True
        ).astype(jnp.float32),
        lax.psum_scatter(
            local_grads[4].astype(jnp.bfloat16), "wsh", scatter_dimension=0, tiled=True
        ).astype(jnp.float32),
        lax.psum_scatter(
            local_grads[5].astype(jnp.bfloat16), "wsh", scatter_dimension=1, tiled=True
        ).astype(jnp.float32),
        lax.psum_scatter(
            local_grads[6].astype(jnp.bfloat16), "wsh", scatter_dimension=0, tiled=True
        ).astype(jnp.float32),
        lax.psum_scatter(
            local_grads[7].astype(jnp.bfloat16), "wsh", scatter_dimension=0, tiled=True
        ).astype(jnp.float32),
        lax.psum_scatter(
            local_grads[8].astype(jnp.bfloat16), "wsh", scatter_dimension=0, tiled=True
        ).astype(jnp.float32),
        lax.psum_scatter(
            local_grads[9].astype(jnp.bfloat16), "wsh", scatter_dimension=0, tiled=True
        ).astype(jnp.float32),
        lax.psum_scatter(
            local_grads[10].astype(jnp.bfloat16), "wsh", scatter_dimension=0, tiled=True
        ).astype(jnp.float32),
        lax.psum_scatter(
            local_grads[11].astype(jnp.bfloat16), "wsh", scatter_dimension=0, tiled=True
        ).astype(jnp.float32),
        lax.psum_scatter(
            local_grads[12].astype(jnp.bfloat16), "wsh", scatter_dimension=0, tiled=True
        ).astype(jnp.float32),
        lax.psum_scatter(
            local_grads[13].astype(jnp.bfloat16), "wsh", scatter_dimension=0, tiled=True
        ).astype(jnp.float32),
        lax.psum_scatter(
            local_grads[14].astype(jnp.bfloat16), "wsh", scatter_dimension=0, tiled=True
        ).astype(jnp.float32),
    )
    return (
        lax.psum(shares[0].astype(jnp.bfloat16), "ctx").astype(jnp.float32),
        lax.psum(shares[1].astype(jnp.bfloat16), "ctx").astype(jnp.float32),
        lax.psum(shares[2].astype(jnp.bfloat16), "ctx").astype(jnp.float32),
        lax.psum(shares[3].astype(jnp.bfloat16), "ctx").astype(jnp.float32),
        lax.psum(shares[4].astype(jnp.bfloat16), "ctx").astype(jnp.float32),
        lax.psum(shares[5].astype(jnp.bfloat16), "ctx").astype(jnp.float32),
        lax.psum(shares[6].astype(jnp.bfloat16), "ctx").astype(jnp.float32),
        lax.psum(shares[7].astype(jnp.bfloat16), "ctx").astype(jnp.float32),
        lax.psum(shares[8].astype(jnp.bfloat16), "ctx").astype(jnp.float32),
        lax.psum(shares[9].astype(jnp.bfloat16), "ctx").astype(jnp.float32),
        lax.psum(shares[10].astype(jnp.bfloat16), "ctx").astype(jnp.float32),
        lax.psum(shares[11].astype(jnp.bfloat16), "ctx").astype(jnp.float32),
        lax.psum(shares[12].astype(jnp.bfloat16), "ctx").astype(jnp.float32),
        lax.psum(shares[13].astype(jnp.bfloat16), "ctx").astype(jnp.float32),
        lax.psum(shares[14].astype(jnp.bfloat16), "ctx").astype(jnp.float32),
    )


def attend(queries, key_ext, value_ext, allowed, score_scale):
    rows_local = queries.shape[0]
    rows_keys = key_ext.shape[0]
    groups = HEADS // head_pair
    span = head_pair * HDIM
    query_groups = queries.reshape(rows_local, groups, span)
    key_groups = key_ext.reshape(rows_keys, groups, span)
    value_groups = value_ext.reshape(rows_keys, groups, span)

    def one_group(group_index, carry):
        mixed_all, log_all = carry
        query_part = lax.dynamic_index_in_dim(query_groups, group_index, 1, keepdims=False).reshape(
            rows_local, head_pair, HDIM
        )
        key_part = lax.dynamic_index_in_dim(key_groups, group_index, 1, keepdims=False).reshape(
            rows_keys, head_pair, HDIM
        )
        value_part = lax.dynamic_index_in_dim(value_groups, group_index, 1, keepdims=False).reshape(
            rows_keys, head_pair, HDIM
        )
        raw_scores = product("qhd,khd->hqk", query_part, key_part)
        scores = jnp.where(allowed[None], raw_scores * score_scale, neg_fill)
        row_peak = jnp.max(scores, axis=2, keepdims=True)
        exponent = jnp.exp(scores - row_peak)
        row_total = jnp.sum(exponent, axis=2, keepdims=True)
        probability = (exponent / row_total).astype(jnp.bfloat16)
        mixed_part = product("hqk,khd->qhd", probability, value_part)
        mixed_all = lax.dynamic_update_index_in_dim(
            mixed_all, mixed_part.reshape(rows_local, span), group_index, 1
        )
        log_all = lax.dynamic_update_index_in_dim(
            log_all, (row_peak + jnp.log(row_total))[:, :, 0], group_index, 0
        )
        return (mixed_all, log_all)

    start_carry = (
        jnp.zeros((rows_local, groups, span), jnp.float32),
        jnp.zeros((groups, head_pair, rows_local), jnp.float32),
    )
    mixed_all, log_all = lax.fori_loop(0, groups, one_group, start_carry)
    return (mixed_all.reshape(rows_local, groups * span), log_all)


def attend_back(queries, key_ext, value_ext, grad_mixed, log_all, allowed, score_scale):
    rows_local = queries.shape[0]
    rows_keys = key_ext.shape[0]
    groups = HEADS // head_pair
    span = head_pair * HDIM
    query_groups = queries.reshape(rows_local, groups, span)
    key_groups = key_ext.reshape(rows_keys, groups, span)
    value_groups = value_ext.reshape(rows_keys, groups, span)
    grad_groups = grad_mixed.reshape(rows_local, groups, span)

    def one_group(group_index, carry):
        query_part = lax.dynamic_index_in_dim(query_groups, group_index, 1, keepdims=False).reshape(
            rows_local, head_pair, HDIM
        )
        key_part = lax.dynamic_index_in_dim(key_groups, group_index, 1, keepdims=False).reshape(
            rows_keys, head_pair, HDIM
        )
        value_part = lax.dynamic_index_in_dim(value_groups, group_index, 1, keepdims=False).reshape(
            rows_keys, head_pair, HDIM
        )
        grad_part = lax.dynamic_index_in_dim(grad_groups, group_index, 1, keepdims=False).reshape(
            rows_local, head_pair, HDIM
        )
        log_part = lax.dynamic_index_in_dim(log_all, group_index, 0, keepdims=False)
        raw_scores = product("qhd,khd->hqk", query_part, key_part)
        scores = jnp.where(allowed[None], raw_scores * score_scale, neg_fill)
        probability = jnp.exp(scores - log_part[:, :, None])
        grad_prob = product("qhd,khd->hqk", grad_part, value_part)
        row_delta = jnp.sum(probability * grad_prob, axis=2, keepdims=True)
        grad_scores = (probability * (grad_prob - row_delta) * score_scale).astype(jnp.bfloat16)
        query_term = product("hqk,khd->qhd", grad_scores, key_part)
        grad_query = lax.dynamic_update_index_in_dim(
            carry[0], query_term.reshape(rows_local, span), group_index, 1
        )
        delta_all = lax.dynamic_update_index_in_dim(carry[1], row_delta[:, :, 0], group_index, 0)
        key_term = product("hqk,qhd->khd", grad_scores, query_part)
        value_term = product("hqk,qhd->khd", probability.astype(jnp.bfloat16), grad_part)
        grad_key = lax.dynamic_update_index_in_dim(
            carry[2], key_term.reshape(rows_keys, span), group_index, 1
        )
        grad_value = lax.dynamic_update_index_in_dim(
            carry[3], value_term.reshape(rows_keys, span), group_index, 1
        )
        return (grad_query, delta_all, grad_key, grad_value)

    start_carry = (
        jnp.zeros((rows_local, groups, span), jnp.float32),
        jnp.zeros((groups, head_pair, rows_local), jnp.float32),
    )
    start_carry = start_carry + (
        jnp.zeros((rows_keys, groups, span), jnp.float32),
        jnp.zeros((rows_keys, groups, span), jnp.float32),
    )
    finals = lax.fori_loop(0, groups, one_group, start_carry)
    grad_query = finals[0].reshape(rows_local, groups * span)
    return (
        grad_query,
        finals[2].reshape(rows_keys, groups * span),
        finals[3].reshape(rows_keys, groups * span),
    )


def layer_forward(activation, gathered, allowed, halo_rows, score_scale):
    (
        query_weight,
        key_weight,
        value_weight,
        out_weight,
        inner_weight,
        outer_weight,
        query_bias,
        value_bias,
        out_bias,
        inner_bias,
        outer_bias,
        first_gain,
        first_shift,
        second_gain,
        second_shift,
    ) = gathered
    rows_local = activation.shape[0]
    queries = (product("td,de->te", activation, query_weight) + query_bias).astype(jnp.bfloat16)
    key_rows = product("td,de->te", activation, key_weight).astype(jnp.bfloat16)
    value_rows = (product("td,de->te", activation, value_weight) + value_bias).astype(jnp.bfloat16)
    stacked = jnp.stack([key_rows, value_rows])
    extended = extend_rows(stacked, 1, halo_rows // rows_local, move_keys_fwd)
    mixed_heads, log_all = attend(queries, extended[0], extended[1], allowed, score_scale)
    mixed_low = mixed_heads.astype(jnp.bfloat16)
    first_pre = activation.astype(jnp.float32) + (
        product("td,de->te", mixed_low, out_weight) + out_bias
    )
    hidden = normalize(first_pre, first_gain.astype(jnp.float32), first_shift.astype(jnp.float32))
    hidden_low = hidden.astype(jnp.bfloat16)
    inner_pre = product("td,df->tf", hidden_low, inner_weight) + inner_bias
    active_low = exact_gelu(inner_pre).astype(jnp.bfloat16)
    second_pre = hidden + (product("tf,fd->td", active_low, outer_weight) + outer_bias)
    result_rows = normalize(
        second_pre, second_gain.astype(jnp.float32), second_shift.astype(jnp.float32)
    )
    saved = (
        activation,
        queries,
        extended,
        log_all,
        mixed_low,
        first_pre,
        hidden_low,
        inner_pre,
        active_low,
        second_pre,
    )
    return (saved, result_rows)


def return_rows(grad_ext, halo_rows, rows_local):
    reach = halo_rows // rows_local
    total = grad_ext[:, halo_rows : halo_rows + rows_local]
    for offset in range(-reach, reach + 1):
        if offset != 0:
            begin = halo_rows + offset * rows_local
            block_rows = grad_ext[:, begin : begin + rows_local]
            total = total + from_behind(block_rows.astype(jnp.bfloat16), "ctx", offset).astype(
                block_rows.dtype
            )
    return total


def layer_backward(gradient, saved, weights, allowed, halo_rows, score_scale):
    (
        query_weight,
        key_weight,
        value_weight,
        out_weight,
        inner_weight,
        outer_weight,
        query_bias,
        value_bias,
        out_bias,
        inner_bias,
        outer_bias,
        first_gain,
        first_shift,
        second_gain,
        second_shift,
    ) = weights
    (
        activation,
        queries,
        extended,
        log_all,
        mixed_low,
        first_pre,
        hidden_low,
        inner_pre,
        active_low,
        second_pre,
    ) = saved
    rows_local = activation.shape[0]
    reach = halo_rows // rows_local
    _, second_pull = jax.vjp(
        normalize, second_pre, second_gain.astype(jnp.float32), second_shift.astype(jnp.float32)
    )
    grad_second, grad_second_gain, grad_second_shift = second_pull(gradient)
    grad_outer = grad_second.astype(jnp.bfloat16)
    grad_outer_weight = product("tf,td->fd", active_low, grad_outer)
    grad_outer_bias = jnp.sum(grad_outer.astype(jnp.float32), axis=0)
    grad_active = product("td,fd->tf", grad_outer, outer_weight)
    _, gelu_pull = jax.vjp(exact_gelu, inner_pre)
    (grad_inner,) = gelu_pull(grad_active)
    grad_inner_low = grad_inner.astype(jnp.bfloat16)
    grad_inner_weight = product("td,tf->df", hidden_low, grad_inner_low)
    grad_inner_bias = jnp.sum(grad_inner_low.astype(jnp.float32), axis=0)
    grad_hidden = grad_second + product("tf,df->td", grad_inner_low, inner_weight)
    _, first_pull = jax.vjp(
        normalize, first_pre, first_gain.astype(jnp.float32), first_shift.astype(jnp.float32)
    )
    grad_first, grad_first_gain, grad_first_shift = first_pull(grad_hidden)
    grad_branch = grad_first.astype(jnp.bfloat16)
    grad_out_weight = product("te,td->ed", mixed_low, grad_branch)
    grad_out_bias = jnp.sum(grad_branch.astype(jnp.float32), axis=0)
    grad_mixed = product("td,ed->te", grad_branch, out_weight).astype(jnp.bfloat16)
    own_rows = extended[:, halo_rows : halo_rows + rows_local]
    key_ext = extend_rows(own_rows, 1, reach, move_keys_back)
    query_sum, key_win, value_win = attend_back(
        queries, key_ext[0], key_ext[1], grad_mixed, log_all, allowed, score_scale
    )
    owned = return_rows(jnp.stack([key_win, value_win]), halo_rows, rows_local)
    key_sum = owned[0]
    value_sum = owned[1]
    grad_query = query_sum.astype(jnp.bfloat16)
    grad_key = key_sum.astype(jnp.bfloat16)
    grad_value = value_sum.astype(jnp.bfloat16)
    grad_query_weight = product("te,td->ed", activation, grad_query)
    grad_key_weight = product("te,td->ed", activation, grad_key)
    grad_value_weight = product("te,td->ed", activation, grad_value)
    grad_query_bias = jnp.sum(grad_query.astype(jnp.float32), axis=0)
    grad_value_bias = jnp.sum(grad_value.astype(jnp.float32), axis=0)
    grad_activation = (
        grad_first
        + product("td,ed->te", grad_query, query_weight)
        + product("td,ed->te", grad_key, key_weight)
        + product("td,ed->te", grad_value, value_weight)
    )
    local_grads = (
        grad_query_weight,
        grad_key_weight,
        grad_value_weight,
        grad_out_weight,
        grad_inner_weight,
        grad_outer_weight,
        grad_query_bias,
        grad_value_bias,
        grad_out_bias,
        grad_inner_bias,
        grad_outer_bias,
        grad_first_gain,
        grad_first_shift,
        grad_second_gain,
        grad_second_shift,
    )
    return (grad_activation, local_grads)


def window_body(
    tokens,
    cotangent,
    doc_starts,
    doc_lengths,
    query_weight,
    key_weight,
    value_weight,
    out_weight,
    inner_weight,
    outer_weight,
    query_bias,
    value_bias,
    out_bias,
    inner_bias,
    outer_bias,
    first_gain,
    first_shift,
    second_gain,
    second_shift,
):
    params = (
        query_weight,
        key_weight,
        value_weight,
        out_weight,
        inner_weight,
        outer_weight,
        query_bias,
        value_bias,
        out_bias,
        inner_bias,
        outer_bias,
        first_gain,
        first_shift,
        second_gain,
        second_shift,
    )
    rows_local = tokens.shape[1]
    ctx_count = lax.axis_size("ctx")
    reach = min(-(-(DOC_CAP - 1) // rows_local), ctx_count - 1)
    halo_rows = reach * rows_local
    window = rows_local + 2 * halo_rows
    row_start = lax.axis_index("ctx") * rows_local
    local_positions = row_start + jnp.arange(rows_local, dtype=jnp.int32)
    window_positions = row_start - halo_rows + jnp.arange(window, dtype=jnp.int32)
    local_labels = doc_labels(local_positions, doc_starts[0], doc_lengths[0])
    window_labels = doc_labels(window_positions, doc_starts[0], doc_lengths[0])
    allowed = (local_labels[:, None] == window_labels[None, :]) & (local_labels[:, None] > 0)
    score_scale = HDIM ** (-0.5)
    activation = tokens[0]
    stashed = []
    outputs = []
    for layer_index in range(LAYERS):
        gathered = fetch_forward(params, layer_index)
        saved, result_rows = layer_forward(activation, gathered, allowed, halo_rows, score_scale)
        stashed.append((saved, gathered))
        outputs.append(result_rows)
        activation = result_rows.astype(jnp.bfloat16)
    gradient = cotangent[0].astype(jnp.float32)
    reduced = [None] * LAYERS
    for layer_index in reversed(range(LAYERS)):
        saved, gathered = stashed[layer_index]
        weights_now = fetch_backward(params, layer_index)
        gradient, local_grads = layer_backward(
            gradient, saved, weights_now, allowed, halo_rows, score_scale
        )
        reduced[layer_index] = reduce_grads(local_grads)
    stacked_grads = [
        jnp.stack([reduced[layer_index][member] for layer_index in range(LAYERS)])
        for member in range(15)
    ]
    heads_out = [
        outputs[0].astype(jnp.bfloat16)[None],
        outputs[LAYERS - 1].astype(jnp.bfloat16)[None],
        gradient.astype(jnp.bfloat16)[None],
    ]
    return tuple(heads_out + stacked_grads)


NN = (((1,), (0,)), ((), ()))
NT = (((1,), (1,)), ((), ()))
TN = (((0,), (0,)), ((), ()))
LANES = 128
QUERY_BLOCK = 1024
CORE, ALONG_X, ALONG_Y = 1, 2, 4
SMALL_COST = pl.CostEstimate(flops=1000, bytes_accessed=1000, transcendentals=0)


def lasting(microseconds):
    return pl.CostEstimate(
        flops=int(microseconds * 1.15e9), bytes_accessed=int(microseconds * 3.6e6), transcendentals=0
    )


def mm(left, right, dims=NN):
    return lax.dot_general(left, right, dims, preferred_element_type=jnp.float32)


def swap(block, mask):
    devices = range(lax.axis_size("ctx"))
    return lax.ppermute(block, "ctx", [(i, i ^ mask) for i in devices])


def turn(block, distance):
    count = lax.axis_size("wsh")
    return lax.ppermute(block, "wsh", [(i, (i + distance) % count) for i in range(count)])


def low(values_in):
    return values_in.astype(jnp.bfloat16)


def wide(values_in):
    return values_in.astype(jnp.float32)


def mask_features(label_col):
    rows = label_col.shape[0]
    lane = lax.broadcasted_iota(jnp.int32, (rows, LANES), 1)
    hit = lax.rem(lane, HDIM) == jnp.broadcast_to(label_col, (rows, LANES))
    return (
        jnp.where(hit, neg_fill, 0.0).astype(jnp.bfloat16),
        jnp.where(hit, 0.0, 1.0).astype(jnp.bfloat16),
    )


def fill_key_scratch(key_rows, label_col, key_mask):
    lane = lax.broadcasted_iota(jnp.int32, key_rows.shape, 1)
    _, key_features = mask_features(label_col)
    key_mask[0] = jnp.where(lane < HDIM, key_rows, key_features)
    key_mask[1] = jnp.where(lane < HDIM, key_features, key_rows)


def attention_forward_kernel(
    order_ref, query_ref, key_ref, value_ref, label_ref, query_label_ref, mixed_ref, log_ref, key_mask, value_t
):
    @pl.when(pl.program_id(0) == 0)
    def _():
        fill_key_scratch(key_ref[...], label_ref[...], key_mask)
        value_t[...] = value_ref[...].T

    scaled = low(wide(query_ref[...]) * HDIM ** (-0.5))
    lane = lax.broadcasted_iota(jnp.int32, scaled.shape, 1)
    features, _ = mask_features(query_label_ref[...])
    parts = []
    for head in range(2):
        mine = (lane < HDIM) if head == 0 else (lane >= HDIM)
        scores = mm(key_mask[head], jnp.where(mine, scaled, features), NT)
        peak = jnp.max(scores, axis=0, keepdims=True)
        exponent = jnp.exp(scores - peak)
        total = jnp.sum(exponent, axis=0, keepdims=True)
        mixed = mm(value_t[pl.ds(HDIM * head, HDIM), :], low(exponent))
        parts.append(mixed / total)
        log_ref[pl.ds(head, 1), :] = peak + jnp.log(total)
    mixed_all = low(jnp.concatenate(parts, axis=0).T)
    block_rows = mixed_ref.shape[1]
    count = mixed_all.shape[0] // block_rows
    for at in range(count):
        place = order_ref[pl.program_id(0) * count + at]
        mixed_ref[place] = mixed_all[at * block_rows : (at + 1) * block_rows]


def attention_forward(packed, labels, order):
    rows = packed.shape[0]
    mine = pl.BlockSpec((QUERY_BLOCK, LANES), lambda i, order_ref: (i, 0))
    return pl.pallas_call(
        attention_forward_kernel,
        grid_spec=pltpu.PrefetchScalarGridSpec(
            num_scalar_prefetch=1,
            grid=(rows // QUERY_BLOCK,),
            in_specs=[
                mine,
                pl.BlockSpec((rows, LANES), lambda i, order_ref: (0, 1)),
                pl.BlockSpec((rows, LANES), lambda i, order_ref: (0, 2)),
                pl.BlockSpec((rows, 1), lambda i, order_ref: (0, 0)),
                pl.BlockSpec((QUERY_BLOCK, 1), lambda i, order_ref: (i, 0)),
            ],
            out_specs=[
                pl.BlockSpec((8, rows // 8, LANES), lambda i, order_ref: (0, 0, 0)),
                pl.BlockSpec((2, QUERY_BLOCK), lambda i, order_ref: (0, i)),
            ],
            scratch_shapes=[
                pltpu.VMEM((2, rows, LANES), jnp.bfloat16),
                pltpu.VMEM((LANES, rows), jnp.bfloat16),
            ],
        ),
        out_shape=[
            jax.ShapeDtypeStruct((8, rows // 8, LANES), jnp.bfloat16),
            jax.ShapeDtypeStruct((2, rows), jnp.float32),
        ],
        cost_estimate=lasting(17),
        name="attention_forward",
    )(order, packed, packed, packed, labels, labels)


def attention_backward_kernel(
    order_ref,
    query_ref,
    key_ref,
    value_ref,
    label_ref,
    query_label_ref,
    grad_ref,
    log_ref,
    out_query_ref,
    out_key_ref,
    out_value_ref,
    key_mask,
    key_t,
    key_sum,
    value_sum,
):
    step = pl.program_id(0)

    @pl.when(step == 0)
    def _():
        fill_key_scratch(key_ref[...], label_ref[...], key_mask)
        key_t[...] = key_ref[...].T
        key_sum[...] = jnp.zeros_like(key_sum)
        value_sum[...] = jnp.zeros_like(value_sum)

    scaled = low(wide(query_ref[...]) * HDIM ** (-0.5))
    count = scaled.shape[0] // grad_ref.shape[1]
    grad = jnp.concatenate([grad_ref[order_ref[step * count + at]] for at in range(count)], axis=0)
    value_rows = value_ref[...]
    lane = lax.broadcasted_iota(jnp.int32, scaled.shape, 1)
    features, _ = mask_features(query_label_ref[...])
    zero = jnp.zeros(scaled.shape, jnp.bfloat16)
    parts = []
    for head in range(2):
        mine = (lane < HDIM) if head == 0 else (lane >= HDIM)
        query_own = jnp.where(mine, scaled, zero)
        grad_own = jnp.where(mine, grad, zero)
        scores = mm(key_mask[head], jnp.where(mine, scaled, features), NT)
        probability = jnp.exp(scores - log_ref[pl.ds(head, 1), :])
        grad_prob = mm(value_rows, grad_own, NT)
        delta = jnp.sum(probability * grad_prob, axis=0, keepdims=True)
        grad_scores = low(probability * (grad_prob - delta))
        key_sum[...] += mm(grad_scores, query_own)
        value_sum[...] += mm(low(probability), grad_own)
        parts.append(mm(key_t[pl.ds(HDIM * head, HDIM), :], grad_scores) * HDIM ** (-0.5))
    out_query_ref[...] = low(jnp.concatenate(parts, axis=0).T)

    @pl.when(step == pl.num_programs(0) - 1)
    def _():
        out_key_ref[...] = low(key_sum[...])
        out_value_ref[...] = low(value_sum[...])


def attention_backward(packed, labels, grad, log_all, order):
    rows = packed.shape[0]
    mine = pl.BlockSpec((QUERY_BLOCK, LANES), lambda i, order_ref: (i, 0))
    whole = pl.BlockSpec((rows, LANES), lambda i, order_ref: (0, 0))
    return pl.pallas_call(
        attention_backward_kernel,
        grid_spec=pltpu.PrefetchScalarGridSpec(
            num_scalar_prefetch=1,
            grid=(rows // QUERY_BLOCK,),
            in_specs=[
                mine,
                pl.BlockSpec((rows, LANES), lambda i, order_ref: (0, 1)),
                pl.BlockSpec((rows, LANES), lambda i, order_ref: (0, 2)),
                pl.BlockSpec((rows, 1), lambda i, order_ref: (0, 0)),
                pl.BlockSpec((QUERY_BLOCK, 1), lambda i, order_ref: (i, 0)),
                pl.BlockSpec((8, rows // 8, LANES), lambda i, order_ref: (0, 0, 0)),
                pl.BlockSpec((2, QUERY_BLOCK), lambda i, order_ref: (0, i)),
            ],
            out_specs=[mine, whole, whole],
            scratch_shapes=[
                pltpu.VMEM((2, rows, LANES), jnp.bfloat16),
                pltpu.VMEM((LANES, rows), jnp.bfloat16),
                pltpu.VMEM((rows, LANES), jnp.float32),
                pltpu.VMEM((rows, LANES), jnp.float32),
            ],
        ),
        out_shape=[jax.ShapeDtypeStruct((rows, LANES), jnp.bfloat16)] * 3,
        cost_estimate=lasting(29),
        name="attention_backward",
    )(order, packed, packed, packed, labels, labels, grad, log_all)


def own_pieces(inner_weight, outer_weight, out_weight, joint_weights, small_params, here, first_block):
    layers, shard, hidden = inner_weight.shape
    piece = hidden // 8
    width = 3 * LANES

    def kernel(place_ref, inner_ref, outer_ref, out_ref, query_ref, key_ref, value_ref, *refs):
        small_refs, (first_ref, second_ref, joint_ref) = refs[:-3], refs[-3:]
        first_ref[0, :, :piece] = low(inner_ref[0])
        first_ref[0, :, piece:] = low(out_ref[0])
        second_ref[0] = low(outer_ref[0]).T
        for at, ref in enumerate((query_ref, key_ref, value_ref)):
            joint_ref[0, :shard, at * LANES : (at + 1) * LANES] = low(ref[0])
        rows = [jnp.concatenate([ref[...] for ref in small_refs[:8]], axis=0)]
        rows += [small_refs[8][:, q * shard : (q + 1) * shard] for q in range(4)]
        rows += [jnp.zeros((8, shard), jnp.float32)]
        packed = low(jnp.concatenate(rows, axis=0))
        joint_ref[0, shard:] = jnp.concatenate([packed, jnp.zeros((32, width - shard), jnp.bfloat16)], axis=1)

    column = pl.BlockSpec((1, shard, LANES), lambda layer, place_ref: (layer, 0, place_ref[0]))
    return pl.pallas_call(
        kernel,
        grid_spec=pltpu.PrefetchScalarGridSpec(
            num_scalar_prefetch=1,
            grid=(layers,),
            in_specs=[
                pl.BlockSpec((1, shard, piece), lambda layer, place_ref: (layer, 0, place_ref[1])),
                pl.BlockSpec((1, piece, shard), lambda layer, place_ref: (layer, place_ref[1], 0)),
                column,
                column,
                column,
                column,
            ]
            + [pl.BlockSpec(param.shape, lambda layer, place_ref: (0, 0)) for param in small_params],
            out_specs=[
                pl.BlockSpec((1, shard, piece + LANES), lambda layer, place_ref: (layer, 0, 0)),
                pl.BlockSpec((1, shard, piece), lambda layer, place_ref: (layer, 0, 0)),
                pl.BlockSpec((1, shard + 32, width), lambda layer, place_ref: (layer, 0, 0)),
            ],
        ),
        out_shape=[
            jax.ShapeDtypeStruct((layers, shard, piece + LANES), jnp.bfloat16),
            jax.ShapeDtypeStruct((layers, shard, piece), jnp.bfloat16),
            jax.ShapeDtypeStruct((layers, shard + 32, width), jnp.bfloat16),
        ],
        cost_estimate=lasting(4),
        name="own_pieces",
    )(
        jnp.stack([here, first_block]).astype(jnp.int32),
        inner_weight,
        outer_weight,
        out_weight,
        *joint_weights,
        *small_params,
    )


def own_blocks(inner_weight, outer_weight, inner_order, after):
    layers, shard, hidden = inner_weight.shape
    piece = hidden // 8

    def kernel(inner_order_ref, *refs):
        ins, (inner_out, outer_out) = refs[:8], refs[-2:]
        for j in range(4):
            inner_out[0, j] = low(ins[j][0])
            outer_out[0, j] = low(ins[4 + j][0]).T

    def inner_at(j):
        return pl.BlockSpec((1, shard, piece), lambda layer, inner_ref: (layer, 0, inner_ref[layer * 4 + j]))

    def outer_at(j):
        return pl.BlockSpec((1, piece, shard), lambda layer, inner_ref: (layer, inner_ref[layer * 4 + j], 0))

    block = pl.BlockSpec((1, 4, shard, piece), lambda layer, *_: (layer, 0, 0, 0))
    return pl.pallas_call(
        kernel,
        grid_spec=pltpu.PrefetchScalarGridSpec(
            num_scalar_prefetch=1,
            grid=(layers,),
            in_specs=[inner_at(j) for j in range(4)]
            + [outer_at(j) for j in range(4)]
            + [pl.BlockSpec(memory_space=pl.ANY)],
            out_specs=[block, block],
        ),
        out_shape=[jax.ShapeDtypeStruct((layers, 4, shard, piece), jnp.bfloat16)] * 2,
        cost_estimate=lasting(6),
        name="own_blocks",
    )(inner_order, *[inner_weight] * 4, *[outer_weight] * 4, after)


def own_out_blocks(out_weight, out_order):
    layers, shard, width = out_weight.shape

    def kernel_layers(out_order_ref, *refs):
        for layer in range(layers):
            for j in range(8):
                refs[8 * layers + layer][:, j * LANES : (j + 1) * LANES] = low(refs[8 * layer + j][0])

    def at_layer(layer, j):
        return pl.BlockSpec((1, shard, LANES), lambda i, out_ref: (layer, 0, out_ref[8 * layer + j]))

    return pl.pallas_call(
        kernel_layers,
        grid_spec=pltpu.PrefetchScalarGridSpec(
            num_scalar_prefetch=1,
            grid=(1,),
            in_specs=[at_layer(layer, j) for layer in range(layers) for j in range(8)],
            out_specs=[pl.BlockSpec((shard, width), lambda i, out_ref: (0, 0))] * layers,
        ),
        out_shape=[jax.ShapeDtypeStruct((shard, width), jnp.bfloat16)] * layers,
        cost_estimate=lasting(2),
        name="own_out_blocks",
    )(out_order, *[out_weight] * (8 * layers))


def place_pieces(pieces, order, layer, previous):
    count, shard, columns = pieces.shape
    piece = (columns - 4 * LANES) // 2
    width = 8 * LANES

    def column(index, order_ref):
        return (layer, 0, order_ref[index])

    def inner_place(index, order_ref):
        return (order_ref[index] % 2) * 4 + order_ref[index] // 2

    square = jax.ShapeDtypeStruct((LAYERS, shard, width), jnp.float32)
    outs = [square] * 4 + [
        jax.ShapeDtypeStruct((LAYERS, shard, 8 * piece), jnp.float32),
        jax.ShapeDtypeStruct((LAYERS, 8 * piece, shard), jnp.float32),
        jax.ShapeDtypeStruct((8, LANES), jnp.float32),
    ]
    specs = [pl.BlockSpec((1, shard, LANES), column)] * 4 + [
        pl.BlockSpec((1, shard, piece), lambda i, order_ref: (layer, 0, inner_place(i, order_ref))),
        pl.BlockSpec((1, piece, shard), lambda i, order_ref: (layer, inner_place(i, order_ref), 0)),
        pl.BlockSpec((8, LANES), lambda i, order_ref: (0, 0)),
    ]

    def kernel(order_ref, source, *refs):
        query_out, key_out, value_out, out_out, inner_out, outer_out, token_out = refs[-7:]
        token_out[...] = jnp.zeros_like(token_out)
        inner_out[0] = wide(source[0, :, :piece])
        outer_out[0] = wide(source[0, :, piece : 2 * piece].T)
        for at, ref in enumerate((out_out, query_out, key_out, value_out)):
            begin = 2 * piece + at * LANES
            ref[0] = wide(source[0, :, begin : begin + LANES])

    held = [] if previous is None else list(previous)
    return pl.pallas_call(
        kernel,
        grid_spec=pltpu.PrefetchScalarGridSpec(
            num_scalar_prefetch=1,
            grid=(count,),
            in_specs=[pl.BlockSpec((1, shard, columns), lambda i, order_ref: (i, 0, 0))]
            + [pl.BlockSpec(memory_space=pl.ANY)] * len(held),
            out_specs=specs,
        ),
        out_shape=outs,
        input_output_aliases={2 + i: i for i in range(len(held))},
        cost_estimate=lasting(count * 5 // 4),
        name="place_pieces",
    )(order, pieces, *held)


def half_erfc(values_in):
    scaled = values_in * (2.0**-0.5)
    part = 1.0 / (1.0 + 0.5 * scaled)
    series = 0.17087277
    for coefficient in (
        -0.82215223,
        1.48851587,
        -1.13520398,
        0.27886807,
        -0.18628806,
        0.09678418,
        0.37409196,
        1.00002368,
        -1.26551223,
    ):
        series = coefficient + part * series
    return 0.5 * part * jnp.exp(series - scaled * scaled)


def load_weights(step, own_inner, own_outer, inner_refs, outer_refs, inner_now, outer_now):
    shard = own_inner.shape[2]
    inner_now[:shard] = own_inner[0, 0]
    outer_now[:shard] = own_outer[0, 0]
    if len(inner_refs) == 1:
        inner_now[shard:] = inner_refs[0][0]
        outer_now[shard:] = outer_refs[0][0]
        return
    chunks = len(inner_refs) // 4
    rows = inner_refs[0].shape[0]
    for j in range(4):

        @pl.when(step == j)
        def _(j=j):
            for chunk in range(chunks):
                begin = shard + chunk * rows
                inner_now[begin : begin + rows] = inner_refs[j * chunks + chunk][...]
                outer_now[begin : begin + rows] = outer_refs[j * chunks + chunk][...]


def weight_operands(weights, layer):
    own_inner, own_outer, inner_parts, outer_parts = weights
    shard, piece = own_inner.shape[2:]
    own = pl.BlockSpec((1, 1, shard, piece), lambda i: (layer, i, 0, 0))
    if len(inner_parts) == 1:
        rest = inner_parts[0].shape[1]
        parts = [pl.BlockSpec((1, rest, piece), lambda i, at=at: (i, 0, at)) for at in range(2)]
        return ([own_inner, own_outer, *inner_parts, *outer_parts], [own, own, *parts], 1)
    rows = inner_parts[0].shape[0]
    fixed = pl.BlockSpec((rows, piece), lambda i: (0, 0), pipeline_mode=pl.Buffered(1))
    return (
        [own_inner, own_outer, *inner_parts, *outer_parts],
        [own, own] + [fixed] * (2 * len(inner_parts)),
        len(inner_parts),
    )


def accumulate(step, total, part):
    @pl.when(step == 0)
    def _():
        total[...] = part

    @pl.when(step > 0)
    def _():
        total[...] += part


def finish_pair(step, total, near_ref, far_ref):
    rows = near_ref.shape[0]

    @pl.when(step == pl.num_programs(0) - 1)
    def _():
        near_ref[...] = total[:rows]
        far_ref[...] = low(total[rows:])


def feed_forward_kernel(count, hidden_ref, bias_ref, own_inner, own_outer, *refs):
    inner_refs, outer_refs = refs[:count], refs[count : 2 * count]
    near_ref, far_ref, active_ref, slope_ref, total, inner_now, outer_now = refs[2 * count :]
    step = pl.program_id(0)
    load_weights(step, own_inner, own_outer, inner_refs, outer_refs, inner_now, outer_now)
    pre = mm(hidden_ref[...], inner_now[...]) + bias_ref[...]
    tail = half_erfc(jnp.abs(pre))
    below = jnp.where(pre < 0.0, tail, 1.0 - tail)
    active = low(pre * below)
    active_ref[...] = active
    slope_ref[...] = low(below + pre * (jnp.exp(-0.5 * pre * pre) * 0.3989422804014327))
    accumulate(step, total, mm(active, outer_now[...], NT))
    finish_pair(step, total, near_ref, far_ref)


def feed_forward(hidden_pair, bias_row, weights, layer):
    rows, width = hidden_pair.shape
    hidden = bias_row.shape[1]
    block = hidden // 4
    arrays, specs, count = weight_operands(weights, layer)
    column = pl.BlockSpec((rows, block), lambda i: (0, i))
    half = pl.BlockSpec((rows // 2, width), lambda i: (0, 0))
    return pl.pallas_call(
        functools.partial(feed_forward_kernel, count),
        grid=(4,),
        in_specs=[
            pl.BlockSpec((rows, width), lambda i: (0, 0)),
            pl.BlockSpec((1, block), lambda i: (0, i)),
            *specs,
        ],
        out_specs=[half, half, column, column],
        out_shape=[
            jax.ShapeDtypeStruct((rows // 2, width), jnp.float32),
            jax.ShapeDtypeStruct((rows // 2, width), jnp.bfloat16),
            jax.ShapeDtypeStruct((rows, hidden), jnp.bfloat16),
            jax.ShapeDtypeStruct((rows, hidden), jnp.bfloat16),
        ],
        scratch_shapes=[
            pltpu.VMEM((rows, width), jnp.float32),
            pltpu.VMEM((width, block), jnp.bfloat16),
            pltpu.VMEM((width, block), jnp.bfloat16),
        ],
        cost_estimate=lasting(16),
        name="feed_forward",
    )(hidden_pair, bias_row, *arrays)


def feed_backward_kernel(count, grad_ref, slope_ref, own_inner, own_outer, *refs):
    inner_refs, outer_refs = refs[:count], refs[count : 2 * count]
    near_ref, far_ref, inner_grad_ref, bias_ref, total, inner_now, outer_now = refs[2 * count :]
    step = pl.program_id(0)
    load_weights(step, own_inner, own_outer, inner_refs, outer_refs, inner_now, outer_now)
    inner_grad = low(mm(grad_ref[...], outer_now[...]) * wide(slope_ref[...]))
    inner_grad_ref[...] = inner_grad
    bias_ref[...] = jnp.sum(wide(inner_grad), axis=0, keepdims=True)
    accumulate(step, total, mm(inner_grad, inner_now[...], NT))
    finish_pair(step, total, near_ref, far_ref)


def feed_backward(grad_pair, slope, weights, layer):
    rows, width = grad_pair.shape
    hidden = slope.shape[1]
    block = hidden // 4
    arrays, specs, count = weight_operands(weights, layer)
    column = pl.BlockSpec((rows, block), lambda i: (0, i))
    half = pl.BlockSpec((rows // 2, width), lambda i: (0, 0))
    return pl.pallas_call(
        functools.partial(feed_backward_kernel, count),
        grid=(4,),
        in_specs=[pl.BlockSpec((rows, width), lambda i: (0, 0)), column, *specs],
        out_specs=[half, half, column, pl.BlockSpec((1, block), lambda i: (0, i))],
        out_shape=[
            jax.ShapeDtypeStruct((rows // 2, width), jnp.float32),
            jax.ShapeDtypeStruct((rows // 2, width), jnp.bfloat16),
            jax.ShapeDtypeStruct((rows, hidden), jnp.bfloat16),
            jax.ShapeDtypeStruct((1, hidden), jnp.float32),
        ],
        scratch_shapes=[
            pltpu.VMEM((rows, width), jnp.float32),
            pltpu.VMEM((width, block), jnp.bfloat16),
            pltpu.VMEM((width, block), jnp.bfloat16),
        ],
        cost_estimate=lasting(11),
        name="feed_backward",
    )(grad_pair, slope, *arrays)


def weight_gradient_kernel(
    split,
    rows_ref,
    hidden_ref,
    grad_ref,
    mixed_ref,
    inner_grad_ref,
    active_ref,
    branch_ref,
    after_ref,
    *refs,
):
    outs, (hidden_t, grad_t, mixed_t) = refs[:-3], refs[-3:]
    step = pl.program_id(0)
    piece = active_ref.shape[1]

    @pl.when(step == 0)
    def _():
        hidden_t[...] = hidden_ref[...].T
        grad_t[...] = grad_ref[...].T
        mixed_t[...] = mixed_ref[...].T

    def write(store):
        store(0, piece, low(mm(hidden_t[...], inner_grad_ref[...])))
        store(piece, 2 * piece, low(mm(grad_t[...], active_ref[...])))
        store(2 * piece, 2 * piece + LANES, low(mm(mixed_t[...], branch_ref[...])))

    if not split:
        first_out, second_out = outs

        def store(begin, end, value):
            shard = value.shape[0] // 4
            ref = second_out if begin == piece else first_out
            column = {0: 0, piece: 0, 2 * piece: piece}[begin]
            for r in range(4):
                place = pl.multiple_of(rows_ref[r] * shard, shard)
                ref[0, pl.ds(place, shard), column : column + end - begin] = value[r * shard : (r + 1) * shard]

        write(store)
        return
    first_keep, first_send, second_keep, second_send = outs
    for j in range(4):

        @pl.when(step == j)
        def _(j=j):
            first = (first_send if j % 2 else first_keep, j // 2)
            second = (second_send if j // 2 else second_keep, j % 2)

            def store(begin, end, value):
                half = value.shape[0] // 2
                first[0][first[1], :, begin:end] = value[:half]
                second[0][second[1], :, begin:end] = value[half:]

            write(store)


def weight_gradients(hidden_pair, grad_pair, mixed_pair, inner_grad, active, branch_pair, plane_rows, split, after):
    rows, width = hidden_pair.shape
    hidden = active.shape[1]
    piece = hidden // 4
    total = 2 * piece + LANES
    whole = pl.BlockSpec((rows, width), lambda i, rows_ref: (0, 0))
    column = pl.BlockSpec((rows, piece), lambda i, rows_ref: (0, i))
    if split:
        shape = (2, width // 2, total)
        out_specs = [pl.BlockSpec(shape, lambda i, rows_ref: (0, 0, 0), pipeline_mode=pl.Buffered(1))] * 4
        out_shape = [jax.ShapeDtypeStruct(shape, jnp.bfloat16)] * 4
    else:
        out_specs = [
            pl.BlockSpec((1, width, columns), lambda i, rows_ref: (i, 0, 0)) for columns in (piece + LANES, piece)
        ]
        out_shape = [jax.ShapeDtypeStruct((4, width, columns), jnp.bfloat16) for columns in (piece + LANES, piece)]
    return pl.pallas_call(
        functools.partial(weight_gradient_kernel, split),
        grid_spec=pltpu.PrefetchScalarGridSpec(
            num_scalar_prefetch=1,
            grid=(4,),
            in_specs=[
                whole,
                whole,
                whole,
                column,
                column,
                pl.BlockSpec((rows, LANES), lambda i, rows_ref: (0, i)),
                pl.BlockSpec(memory_space=pl.ANY),
            ],
            out_specs=out_specs,
            scratch_shapes=[pltpu.VMEM((width, rows), jnp.bfloat16)] * 3,
        ),
        out_shape=out_shape,
        cost_estimate=lasting(13),
        name="weight_gradients",
    )(plane_rows, hidden_pair, grad_pair, mixed_pair, inner_grad, active, branch_pair, after)


def block_columns(values_in, order, width):
    return jnp.concatenate(
        [lax.dynamic_slice_in_dim(values_in, block * width, width, 1) for block in order], axis=1
    )


def norm_forward(values_in, gain_row, shift_row):
    centre = values_in - jnp.mean(values_in, axis=-1, keepdims=True)
    spread = jnp.mean(centre * centre, axis=-1, keepdims=True)
    inverse = lax.rsqrt(spread + epsilon)
    unit = centre * inverse
    return (unit * gain_row + shift_row, unit, inverse)


def norm_backward(grad, unit, inverse, gain_row):
    grad_unit = grad * gain_row
    back = inverse * (
        grad_unit
        - jnp.mean(grad_unit, axis=-1, keepdims=True)
        - unit * jnp.mean(grad_unit * unit, axis=-1, keepdims=True)
    )
    return (back, jnp.sum(grad * unit, axis=0), jnp.sum(grad, axis=0))


def attention_output_kernel(
    place_ref,
    heads_ref,
    own_ref,
    near_ref,
    far_ref,
    activation_ref,
    bias_ref,
    gain_ref,
    shift_ref,
    mixed_ref,
    unit_ref,
    inverse_ref,
    hidden_ref,
    turned_ref,
    held,
    held_low,
):
    shard = own_ref.shape[0]
    half = near_ref.shape[1]
    for p in range(8):
        mixed_ref[:, p * LANES : (p + 1) * LANES] = heads_ref[place_ref[p]]
    own, rest = mixed_ref[:, :shard], mixed_ref[:, shard:]
    held[:, :half] = mm(own, own_ref[:, :half]) + mm(rest, near_ref[...])
    held[:, half:] = mm(own, own_ref[:, half:]) + mm(rest, far_ref[...])
    attended = jnp.concatenate(
        [held[:, pl.ds(pl.multiple_of(place_ref[8 + b] * LANES, LANES), LANES)] for b in range(8)], axis=1
    )
    first_pre = wide(activation_ref[...]) + (attended + bias_ref[...])
    hidden, unit, inverse = norm_forward(first_pre, gain_ref[...], shift_ref[...])
    unit_ref[...] = unit
    inverse_ref[...] = inverse
    hidden_ref[...] = hidden
    held_low[...] = low(hidden)
    for r in range(4):
        turned_ref[:, r * shard : (r + 1) * shard] = held_low[
            :, pl.ds(pl.multiple_of(place_ref[16 + r] * shard, shard), shard)
        ]


def attention_output(heads, out_weights, activation, bias_row, gain_row, shift_row, places):
    rows, width = activation.shape
    wide_rows = jax.ShapeDtypeStruct((rows, width), jnp.float32)
    low_rows = jax.ShapeDtypeStruct((rows, width), jnp.bfloat16)
    return pl.pallas_call(
        attention_output_kernel,
        grid_spec=pltpu.PrefetchScalarGridSpec(
            num_scalar_prefetch=1,
            grid=(1,),
            in_specs=[
                pl.BlockSpec(array.shape, lambda i, place_ref, rank=array.ndim: (0,) * rank)
                for array in (heads, *out_weights, activation, bias_row, gain_row, shift_row)
            ],
            out_specs=[
                pl.BlockSpec((rows, width), lambda i, place_ref: (0, 0)),
                pl.BlockSpec((rows, width), lambda i, place_ref: (0, 0)),
                pl.BlockSpec((rows, 1), lambda i, place_ref: (0, 0)),
                pl.BlockSpec((rows, width), lambda i, place_ref: (0, 0)),
                pl.BlockSpec((rows, width), lambda i, place_ref: (0, 0)),
            ],
            scratch_shapes=[pltpu.VMEM((rows, width), jnp.float32), pltpu.VMEM((rows, width), jnp.bfloat16)],
        ),
        out_shape=[low_rows, wide_rows, jax.ShapeDtypeStruct((rows, 1), jnp.float32), wide_rows, low_rows],
        cost_estimate=lasting(5),
        name="attention_output",
    )(places, heads, *out_weights, activation, bias_row, gain_row, shift_row)


def attention_output_back_kernel(
    place_ref,
    near_back_ref,
    came_ref,
    grad_ref,
    unit_ref,
    inverse_ref,
    gain_ref,
    own_ref,
    near_ref,
    far_ref,
    first_ref,
    rows_ref,
    spread_ref,
    sent_ref,
    held,
    held_low,
):
    shard = own_ref.shape[0]
    half = near_ref.shape[1]
    held[...] = near_back_ref[...] + wide(came_ref[...])
    back = jnp.concatenate(
        [held[:, pl.ds(pl.multiple_of(place_ref[16 + r] * shard, shard), shard)] for r in range(4)], axis=1
    )
    grad_first, gain_row, shift_row = norm_backward(
        grad_ref[...] + back, unit_ref[...], inverse_ref[...], gain_ref[...]
    )
    first_ref[...] = grad_first
    branch = low(grad_first)
    rows_ref[0:1] = gain_row[None]
    rows_ref[1:2] = shift_row[None]
    rows_ref[2:3] = jnp.sum(wide(branch), axis=0, keepdims=True)
    held_low[...] = branch
    for p in range(8):
        spread_ref[:, p * LANES : (p + 1) * LANES] = held_low[
            :, pl.ds(pl.multiple_of(place_ref[24 + p] * LANES, LANES), LANES)
        ]
    spread = spread_ref[...]
    held_low[:, :shard] = low(mm(spread, own_ref[...], NT))
    held_low[:, shard:] = low(mm(spread[:, :half], near_ref[...], NT) + mm(spread[:, half:], far_ref[...], NT))
    for head in range(8):
        begin = place_ref[16 + head // 2] * shard + (head % 2) * LANES
        sent_ref[head] = held_low[:, pl.ds(pl.multiple_of(begin, LANES), LANES)]


def attention_output_back(near_back, came, grad_second, unit, inverse, gain_row, out_weights, places):
    rows, width = grad_second.shape
    operands = (near_back, came, grad_second, unit, inverse, gain_row, *out_weights)
    whole = pl.BlockSpec((rows, width), lambda i, place_ref: (0, 0))
    return pl.pallas_call(
        attention_output_back_kernel,
        grid_spec=pltpu.PrefetchScalarGridSpec(
            num_scalar_prefetch=1,
            grid=(1,),
            in_specs=[pl.BlockSpec(array.shape, lambda i, place_ref: (0, 0)) for array in operands],
            out_specs=[
                whole,
                pl.BlockSpec((3, width), lambda i, place_ref: (0, 0)),
                whole,
                pl.BlockSpec((8, rows, LANES), lambda i, place_ref: (0, 0, 0)),
            ],
            scratch_shapes=[pltpu.VMEM((rows, width), jnp.float32), pltpu.VMEM((rows, width), jnp.bfloat16)],
        ),
        out_shape=[
            jax.ShapeDtypeStruct((rows, width), jnp.float32),
            jax.ShapeDtypeStruct((3, width), jnp.float32),
            jax.ShapeDtypeStruct((rows, width), jnp.bfloat16),
            jax.ShapeDtypeStruct((8, rows, LANES), jnp.bfloat16),
        ],
        cost_estimate=lasting(6),
        name="attention_output_back",
    )(places, *operands)


def token_gradient_kernel(
    place_ref, query_ref, key_ref, value_ref, joint_ref, *refs
):
    near_ref, far_ref, packed_ref, bias_ref = refs[-4:]
    step = pl.program_id(0)
    packed = jnp.concatenate([query_ref[...], key_ref[...], value_ref[...]], axis=1)
    packed_ref[...] = packed
    accumulate(step, bias_ref, jnp.sum(wide(packed), axis=0, keepdims=True))
    part = mm(packed, joint_ref[...], NT)

    @pl.when(step < 4)
    def _():
        near_ref[0] = part

    @pl.when(step >= 4)
    def _():
        far_ref[0] = low(part)


def token_gradients(grads, joint, chips):
    tokens = grads[0].shape[0]
    rows = tokens // 8
    width, columns = joint.shape
    block = pl.BlockSpec((rows, LANES), lambda i, place_ref: (i, 0))
    return pl.pallas_call(
        token_gradient_kernel,
        grid_spec=pltpu.PrefetchScalarGridSpec(
            num_scalar_prefetch=1,
            grid=(8,),
            in_specs=[block, block, block, pl.BlockSpec((width, columns), lambda i, place_ref: (0, 0))],
            out_specs=[
                pl.BlockSpec((1, rows, width), lambda i, place_ref: (place_ref[jnp.minimum(i, 3)], 0, 0)),
                pl.BlockSpec((1, rows, width), lambda i, place_ref: (place_ref[jnp.maximum(i - 4, 0)], 0, 0)),
                pl.BlockSpec((rows, columns), lambda i, place_ref: (i, 0)),
                pl.BlockSpec((1, columns), lambda i, place_ref: (0, 0)),
            ],
        ),
        out_shape=[
            jax.ShapeDtypeStruct((4, rows, width), jnp.float32),
            jax.ShapeDtypeStruct((4, rows, width), jnp.bfloat16),
            jax.ShapeDtypeStruct((tokens, columns), jnp.bfloat16),
            jax.ShapeDtypeStruct((1, columns), jnp.float32),
        ],
        cost_estimate=lasting(10),
        name="token_gradients",
    )(chips, *grads, joint)


def plane_sum_kernel(first_keep, first_came, first_last, second_keep, second_came, second_last, *outs):
    shard = outs[0].shape[0]
    first = wide(first_keep[0]) + wide(first_came[0]) + wide(first_last[...])
    second = wide(second_keep[0]) + wide(second_came[0]) + wide(second_last[...])
    outs[0][...] = first[:shard]
    outs[1][...] = low(first[shard:])
    outs[2][...] = low(second[:shard])
    outs[3][...] = low(second[shard:])


def plane_sum(first, second):
    columns = first[0].shape[2]
    shard = first[0].shape[1] // 2
    block = pl.BlockSpec((1, 2 * shard, columns), lambda i: (0, 0, 0))
    last = pl.BlockSpec((2 * shard, columns), lambda i: (0, 0))
    return pl.pallas_call(
        plane_sum_kernel,
        grid=(1,),
        in_specs=[block, block, last] * 2,
        out_specs=[pl.BlockSpec((shard, columns), lambda i: (0, 0))] * 4,
        out_shape=[jax.ShapeDtypeStruct((shard, columns), jnp.float32)]
        + [jax.ShapeDtypeStruct((shard, columns), jnp.bfloat16)] * 3,
        cost_estimate=lasting(3),
        name="plane_sum",
    )(*first, *second)


def final_sum_kernel(*refs):
    left_ref, right_ref = refs[-2:]
    half = left_ref.shape[1]
    whole = jnp.concatenate(
        [
            low(wide(refs[at][...]) + wide(refs[at + 1][...]) + wide(refs[at + 2][...]) + wide(refs[at + 3][...]))
            for at in (0, 4)
        ],
        axis=1,
    )
    left_ref[...] = whole[:, :half]
    right_ref[...] = whole[:, half:]


def final_sum(plain, joint):
    shard = plain[0].shape[0]
    half = (plain[0].shape[1] + joint[0].shape[1]) // 2
    operands = (*plain, *joint)
    return pl.pallas_call(
        final_sum_kernel,
        grid=(1,),
        in_specs=[pl.BlockSpec(array.shape, lambda i: (0, 0)) for array in operands],
        out_specs=[pl.BlockSpec((shard, half), lambda i: (0, 0))] * 2,
        out_shape=[jax.ShapeDtypeStruct((shard, half), jnp.bfloat16)] * 2,
        cost_estimate=lasting(3),
        name="final_sum",
    )(*operands)


def small_rows_kernel(place_ref, joint_ref, first_ref, outer_ref, gain_ref, shift_ref, inner_ref, out_ref):
    shard = out_ref.shape[1] // 4
    out_ref[...] = jnp.zeros_like(out_ref)
    at = pl.ds(pl.multiple_of(place_ref[0] * LANES, LANES), LANES)
    out_ref[0:1, at] = joint_ref[:, :LANES]
    out_ref[1:2, at] = joint_ref[:, 2 * LANES :]
    out_ref[2:3] = first_ref[2:3]
    out_ref[3:4] = outer_ref[...]
    out_ref[4:6] = first_ref[0:2]
    out_ref[6:7] = gain_ref[...]
    out_ref[7:8] = shift_ref[...]
    count = inner_ref.shape[1] // shard // 4
    for j in range(4):
        block = place_ref[1 + j]
        columns = pl.ds(pl.multiple_of((block // 2) * shard, shard), shard)
        for part in range(count):
            begin = (j * count + part) * shard
            row = 8 + (block % 2) * count + part
            out_ref[pl.ds(row, 1), columns] = inner_ref[:, begin : begin + shard]


def small_rows(places, joint, first, outer, gain, shift, inner):
    width = first.shape[1]
    operands = (joint, first, outer[None], gain[None], shift[None], inner)
    return pl.pallas_call(
        small_rows_kernel,
        grid_spec=pltpu.PrefetchScalarGridSpec(
            num_scalar_prefetch=1,
            grid=(1,),
            in_specs=[pl.BlockSpec(array.shape, lambda i, place_ref: (0, 0)) for array in operands],
            out_specs=pl.BlockSpec((16, width), lambda i, place_ref: (0, 0)),
        ),
        out_shape=jax.ShapeDtypeStruct((16, width), jnp.float32),
        cost_estimate=lasting(2),
        name="small_rows",
    )(places, *operands)


def gate(values_in, *points):
    anywhere = pl.BlockSpec(memory_space=pl.ANY)
    return pl.pallas_call(
        lambda *refs: None,
        in_specs=[anywhere] * (len(values_in) + len(points)),
        out_specs=[anywhere] * len(values_in),
        out_shape=[jax.ShapeDtypeStruct(value.shape, value.dtype) for value in values_in],
        input_output_aliases={i: i for i in range(len(values_in))},
        cost_estimate=SMALL_COST,
        name="gate",
    )(*values_in, *points)


def spread_tokens(rows_in):
    half = rows_in.shape[1] // 2
    left, right = rows_in[:, :half], rows_in[:, half:]
    left_pair = jnp.stack([left, swap(left, ALONG_X)])
    right_pair = jnp.stack([right, swap(right, ALONG_Y)])
    left_far = swap(left_pair, ALONG_Y)
    right_far = swap(right_pair, ALONG_X)
    left_all = jnp.concatenate([left_pair, left_far])
    right_all = jnp.stack([right_pair[0], right_far[0], right_pair[1], right_far[1]])
    near = jnp.concatenate([left_all, right_all], axis=2).reshape(4 * rows_in.shape[0], rows_in.shape[1])
    return (near, swap(near, CORE))


def plane_groups():
    count = lax.axis_size("ctx")
    return [list(range(0, count, 2)), list(range(1, count, 2))]


def collect_tokens(sent, points, late_points):
    if points:
        (sent,) = gate([sent], *points)
    came = lax.all_to_all(sent, "ctx", 0, 0, axis_index_groups=plane_groups(), tiled=True)
    if late_points:
        (came,) = gate([came], *late_points)
    return jnp.sum(wide(came), axis=0)


def plane_pieces(left, right, *points):
    left_pair = jnp.stack([left, swap(left, ALONG_X)])
    right_pair = jnp.stack([right, swap(right, ALONG_Y)])
    left_far, right_far = gate([swap(left_pair, ALONG_Y), swap(right_pair, ALONG_X)], *points)
    left_all = jnp.concatenate([left_pair, left_far])
    right_all = jnp.stack([right_pair[0], right_far[0], right_pair[1], right_far[1]])
    near = jnp.concatenate([left_all, right_all], axis=2)
    return (near, swap(near, CORE))


def exchange(blocks):
    return lax.all_to_all(blocks, "ctx", 0, 0, tiled=True)


def head_split_body(
    tokens,
    cotangent,
    doc_starts,
    doc_lengths,
    query_weight,
    key_weight,
    value_weight,
    out_weight,
    inner_weight,
    outer_weight,
    query_bias,
    value_bias,
    out_bias,
    inner_bias,
    outer_bias,
    first_gain,
    first_shift,
    second_gain,
    second_shift,
):
    rows = tokens.shape[1]
    width = tokens.shape[2]
    here = lax.axis_index("ctx")
    plane = lax.axis_index("wsh")
    planes = lax.axis_size("wsh")
    shard = width // planes
    hidden = inner_weight.shape[2]
    piece = hidden // 8
    core = here % 2
    chip = here // 2
    relative = jnp.arange(8, dtype=jnp.int32)
    spread = jnp.array((0, 2, 4, 6, 1, 3, 5, 7), jnp.int32)
    turned = [(plane - r) % planes for r in range(planes)]
    unturned = turned
    positions = ((here ^ spread)[:, None] * rows + jnp.arange(rows, dtype=jnp.int32)).reshape(-1)
    labels = doc_labels(positions, doc_starts[0], doc_lengths[0])[:, None]

    four = jnp.arange(4, dtype=jnp.int32)
    chip_order = [chip ^ four, four]
    inner_order = [core * 4 + order for order in chip_order]
    out_order = [jnp.concatenate([2 * order + core, 2 * order + 1 - core]) for order in chip_order]
    block_order = here ^ spread
    plane_rows = jnp.stack(turned).astype(jnp.int32)
    first_own, second_own, joint_own = own_pieces(
        inner_weight,
        outer_weight,
        out_weight,
        (query_weight, key_weight, value_weight),
        (
            query_bias,
            value_bias,
            out_bias,
            outer_bias,
            first_gain,
            first_shift,
            second_gain,
            second_shift,
            inner_bias,
        ),
        here,
        core * 4 + chip,
    )
    joint_width = 3 * LANES

    def ordered(stack, order):
        return jnp.concatenate([lax.dynamic_index_in_dim(stack, i, 0, keepdims=False) for i in order], axis=0)

    first_joint = joint_own[0]
    joint_turned = jnp.stack([first_joint] + [turn(first_joint, r) for r in range(1, planes)])
    joint_first = ordered(joint_turned[:, :shard], unturned)
    small_all = ordered(joint_turned[:, None, shard:, :shard], unturned)

    def small(layer, index):
        return small_all[:, 2 * index + layer].reshape(width)

    inner_bias_all = small_all[:, 16:24].reshape(planes, 4, LAYERS, shard).transpose(2, 0, 1, 3).reshape(LAYERS, hidden)

    inner_near = ordered(lax.all_gather(first_own[0], "wsh", axis=0), turned[1:])
    first_tokens = spread_tokens(tokens[0])
    (outer_sent,) = gate([second_own[0]], first_tokens[0])
    outer_stack = lax.all_gather(outer_sent, "wsh", axis=0)
    middle = 3 * shard // 2

    def spread_first(near):
        left, right = near[:middle], near[middle:]
        return (left, right, swap(left, ALONG_X), swap(right, ALONG_Y))

    def spread_second(left, right, left_x, right_y):
        lefts = (left, left_x, swap(left, ALONG_Y), swap(left_x, ALONG_Y))
        rights = (right, swap(right, ALONG_X), right_y, swap(right_y, ALONG_X))
        return [part for pair in zip(lefts, rights) for part in pair]

    inner_half = spread_first(inner_near)
    layer_own = jnp.concatenate(
        [first_own[1, :, :piece], second_own[1], first_own[1, :, piece:], joint_own[1, :shard]], axis=1
    )
    wide_piece = 2 * piece + LANES

    def layer_weights(layer):
        if layer == 0:
            near = jnp.concatenate(
                [
                    jnp.concatenate([inner_first[2 * j][:, piece:], inner_first[2 * j + 1][:, piece:]], axis=0)
                    for j in range(4)
                ],
                axis=1,
            )
            weights = (inner_first, outer_first)
        else:
            near = jnp.concatenate([out_parts[j] for j in range(4)], axis=1)
            weights = ()
        return (weights, (out_own[layer], near, swap(near, CORE)))

    def out_place(layer, block):
        at = (block // 2) ^ chip if layer == 0 else block // 2
        return at + 4 * ((block % 2) ^ core)

    activation = tokens[0]
    stashed = []
    outputs = []
    for layer in range(LAYERS):
        joint = joint_first if layer == 0 else joint_second
        first_gain_row, first_shift_row = wide(small(layer, 4)), wide(small(layer, 5))
        second_gain_row, second_shift_row = wide(small(layer, 6)), wide(small(layer, 7))

        near_tokens, far_tokens = first_tokens if layer == 0 else spread_tokens(activation)
        everyone = jnp.concatenate([near_tokens, far_tokens], axis=0)
        query_bias_own = lax.dynamic_slice_in_dim(small(layer, 0), here * LANES, LANES, 0)
        value_bias_own = lax.dynamic_slice_in_dim(small(layer, 1), here * LANES, LANES, 0)
        joint_bias = wide(jnp.concatenate([query_bias_own, jnp.zeros_like(query_bias_own), value_bias_own]))
        packed = low(mm(everyone, joint) + joint_bias)
        if layer == 0:
            out_own = own_out_blocks(out_weight, jnp.concatenate(out_order))
            packed, layer_own = gate([packed, layer_own], inner_near, out_own[0])
            second_stack = lax.all_gather(layer_own, "wsh", axis=0)
        mixed, log_all = attention_forward(packed, labels, block_order)
        if layer == 0:
            left_x, right_y, outer_stack = gate([*inner_half[2:], outer_stack], mixed)
            inner_first = spread_second(*inner_half[:2], left_x, right_y)
            outer_first = spread_second(*spread_first(ordered(outer_stack, turned[1:])))
        else:
            out_parts = lax.all_to_all(
                jnp.broadcast_to(out_second, (4, *out_second.shape)),
                "ctx",
                0,
                0,
                axis_index_groups=plane_groups(),
                tiled=True,
            )
            (out_parts,) = gate([out_parts], mixed)
        weights, out_weights = layer_weights(layer)
        mixed_heads = exchange(mixed)
        places = jnp.stack(
            [2 * turned[p // 2] + p % 2 for p in range(8)]
            + [out_place(layer, b) for b in range(8)]
            + turned
            + [jnp.int32(0)] * 4
            + [out_order[layer][p] for p in range(8)]
        ).astype(jnp.int32)
        mixed_turned, first_unit, first_inverse, hidden_rows, hidden_turned = attention_output(
            mixed_heads,
            out_weights,
            activation,
            wide(small(layer, 2))[None],
            first_gain_row[None],
            first_shift_row[None],
            places,
        )
        if layer == 0:
            inner_own, outer_own = own_blocks(
                inner_weight, outer_weight, jnp.concatenate(inner_order), hidden_turned
            )
        else:
            second_parts = gate([second_parts], hidden_turned)
            weights = (second_parts, second_parts)
        weights = (inner_own, outer_own, *weights)
        mixed_pair = jnp.concatenate([mixed_turned, swap(mixed_turned, CORE)], axis=0)
        hidden_pair = jnp.concatenate([hidden_turned, swap(hidden_turned, CORE)], axis=0)
        inner_bias_own = jnp.concatenate(
            [lax.dynamic_slice_in_dim(inner_bias_all[layer], inner_order[layer][j] * piece, piece, 0) for j in range(4)]
        )
        outer_near, outer_far, active, slope = feed_forward(
            hidden_pair, wide(inner_bias_own)[None], weights, layer
        )
        outer_turned = outer_near + wide(swap(outer_far, CORE))
        if layer == 0:
            (second_stack,) = gate([second_stack], active)
            joint_second = second_stack[:, :, wide_piece:].reshape(width, joint_width)
            others_second = ordered(second_stack[:, :, :wide_piece], turned[1:])
            sent_second = (others_second[:, : piece + LANES], others_second[:, piece + LANES :])
            second_parts = lax.all_gather(
                others_second[:, : 2 * piece], "ctx", axis=0, axis_index_groups=plane_groups()
            )
            out_second = others_second[:, 2 * piece :]
        outer_out = block_columns(outer_turned, unturned, shard)
        second_pre = hidden_rows + (outer_out + wide(small(layer, 3)))
        result, second_unit, second_inverse = norm_forward(second_pre, second_gain_row, second_shift_row)
        stashed.append(
            (
                everyone,
                packed,
                log_all,
                mixed_pair,
                first_unit,
                first_inverse,
                hidden_pair,
                active,
                slope,
                second_unit,
                second_inverse,
                joint,
                out_weights,
                places,
                weights,
                first_gain_row,
                second_gain_row,
            )
        )
        activation = low(result)
        outputs.append(activation)

    gradient = wide(cotangent[0])
    small_grads = [None] * LAYERS
    for layer in reversed(range(LAYERS)):
        (
            everyone,
            packed,
            log_all,
            mixed_pair,
            first_unit,
            first_inverse,
            hidden_pair,
            active,
            slope,
            second_unit,
            second_inverse,
            joint,
            out_weights,
            places,
            weights,
            first_gain_row,
            second_gain_row,
        ) = stashed[layer]
        grad_second, grad_second_gain, grad_second_shift = norm_backward(
            gradient, second_unit, second_inverse, second_gain_row
        )
        grad_outer = low(grad_second)
        grad_outer_bias = jnp.sum(wide(grad_outer), axis=0)
        grad_turned = block_columns(grad_outer, turned, shard)
        grad_pair = jnp.concatenate([grad_turned, swap(grad_turned, CORE)], axis=0)
        hidden_near, hidden_far, grad_inner, grad_inner_bias = feed_backward(grad_pair, slope, weights, layer)
        grad_first, first_rows, branch_spread, grad_sent = attention_output_back(
            hidden_near,
            swap(hidden_far, CORE),
            grad_second,
            first_unit,
            first_inverse,
            first_gain_row[None],
            out_weights,
            places,
        )
        grad_mixed = exchange(grad_sent)
        branch_half = 4 * LANES
        branch_pair = jnp.concatenate(
            [branch_spread[:, :branch_half], swap(branch_spread[:, branch_half:], CORE)], axis=0
        )
        summed = weight_gradients(
            hidden_pair, grad_pair, mixed_pair, grad_inner, active, branch_pair, plane_rows, layer == 0, grad_sent
        )
        if layer == 0:
            (grad_mixed,) = gate([grad_mixed], summed[0], plane_first)
            (plane_second,) = gate([plane_second], grad_mixed)
        else:
            grad_mixed, first_sum = gate([grad_mixed, summed[0]])
        grad_query, grad_key, grad_value = attention_backward(packed, labels, grad_mixed, log_all, block_order)
        if layer == 0:
            first_keep, first_send, second_keep, second_send = summed
            first_came = swap(first_send, ALONG_X)
            second_came = swap(second_send, ALONG_Y)
        near_part, far_part, grad_packed, joint_bias_grad = token_gradients(
            (grad_query, grad_key, grad_value), joint, chip_order[0]
        )
        grad_joint = low(mm(everyone, grad_packed, TN))
        far_came = swap(far_part, CORE)
        tokens_sent = low(near_part + wide(far_came))
        small_grads[layer] = small_rows(
            jnp.concatenate([here[None], inner_order[layer]]).astype(jnp.int32),
            joint_bias_grad,
            first_rows,
            grad_outer_bias,
            grad_second_gain,
            grad_second_shift,
            grad_inner_bias,
        )
        if layer == 1:
            (plane_first,) = [
                lax.psum_scatter(
                    first_sum.reshape(4 * width, -1),
                    "ctx",
                    scatter_dimension=0,
                    axis_index_groups=plane_groups(),
                    tiled=True,
                )
            ]
            (plane_first,) = gate([plane_first], far_came)
            plane_rows_first = [
                lax.dynamic_slice_in_dim(plane_first, turned[r] * shard, shard, 0) for r in range(planes)
            ]
            came_first = [turn(plane_rows_first[r], planes - r) for r in range(1, planes)]
            gradient = grad_first + collect_tokens(tokens_sent, (), (grad_joint,))
            (second_sum,) = gate([summed[1]], gradient, plane_first)
            plane_second = lax.psum_scatter(
                second_sum.reshape(4 * width, -1),
                "ctx",
                scatter_dimension=0,
                axis_index_groups=plane_groups(),
                tiled=True,
            )
            sum_joint = lax.psum_scatter(grad_joint, "wsh", scatter_dimension=0, tiled=True)
            continue
        small_sent = jnp.concatenate(small_grads, axis=0)
        small_plane = jnp.sum(
            lax.all_to_all(
                jnp.stack([small_sent[:, p * shard : (p + 1) * shard] for p in range(planes)]), "wsh", 0, 0, tiled=True
            ),
            axis=0,
        )
        small_spread = jnp.broadcast_to(small_plane, (8, *small_plane.shape))
        first_came, second_came = gate([first_came, second_came], near_part, grad_joint, *came_first)
        sum_first = wide(plane_rows_first[0])
        for part in came_first:
            sum_first = sum_first + wide(part)
        sum_first = low(sum_first)
        first_next = low(wide(first_keep[1]) + wide(first_came[1]))
        second_next = low(wide(second_keep[1]) + wide(second_came[1]))
        joint_rows = [lax.dynamic_slice_in_dim(grad_joint, turned[r] * shard, shard, 0) for r in range(planes)]
        came_joint = [turn(joint_rows[r], planes - r) for r in range(1, planes)]
        first_last, second_last = gate(
            [swap(first_next, ALONG_Y), swap(second_next, ALONG_X)], small_plane, tokens_sent, *came_joint
        )
        own_total, *sent = plane_sum(
            (first_keep, first_came, first_last), (second_keep, second_came, second_last)
        )
        came = [turn(sent[r - 1], planes - r) for r in range(1, planes)]
        sum_second = lax.psum_scatter(plane_second, "wsh", scatter_dimension=0, tiled=True)
        sum_first, sum_second, sum_joint = gate([sum_first, sum_second, sum_joint], own_total, tokens_sent)
        everything = lax.all_gather(
            jnp.concatenate([sum_first[:, :piece], sum_second, sum_first[:, piece:], sum_joint], axis=1),
            "ctx",
            axis=0,
        )
        gradient = grad_first + collect_tokens(tokens_sent, (own_total,), ())
        (small_spread,) = gate([small_spread], gradient)
        small_mine = jnp.sum(exchange(small_spread), axis=0).reshape(LAYERS, 16, shard)
        came = gate(came, small_mine)
        left_total, right_total = final_sum((own_total, *came), (joint_rows[0], *came_joint))
        (everything,) = gate([everything], left_total)
        *placed, placed_token = place_pieces(everything, relative, 1, None)
    near, far = plane_pieces(left_total, right_total, placed_token, small_mine)
    near_first = here ^ (2 * four)
    *placed, placed_token = place_pieces(near, near_first, 0, placed)
    (far,) = gate([far], placed_token)
    *placed, _ = place_pieces(far, near_first ^ 1, 0, placed)
    small_outs = [small_mine[:, i] for i in range(8)]
    return (
        outputs[0][None],
        outputs[1][None],
        low(gradient)[None],
        *placed,
        small_outs[0],
        small_outs[1],
        small_outs[2],
        small_mine[:, 8:12].reshape(LAYERS, 4 * shard),
        small_outs[3],
        small_outs[4],
        small_outs[5],
        small_outs[6],
        small_outs[7],
    )


def choose_body(mesh):
    if mesh.shape["ctx"] == 8 and HEADS // 8 == 2:
        return head_split_body
    return window_body


def solution(mesh):
    in_specs = (
        P("wsh", "ctx", None),
        P("wsh", "ctx", None),
        P("wsh", None),
        P("wsh", None),
        P(None, "wsh", None),
        P(None, "wsh", None),
        P(None, "wsh", None),
        P(None, "wsh", None),
        P(None, "wsh", None),
        P(None, None, "wsh"),
        P(None, "wsh"),
        P(None, "wsh"),
        P(None, "wsh"),
        P(None, "wsh"),
        P(None, "wsh"),
        P(None, "wsh"),
        P(None, "wsh"),
        P(None, "wsh"),
        P(None, "wsh"),
    )
    out_specs = (
        P("wsh", "ctx", None),
        P("wsh", "ctx", None),
        P("wsh", "ctx", None),
        P(None, "wsh", None),
        P(None, "wsh", None),
        P(None, "wsh", None),
        P(None, "wsh", None),
        P(None, "wsh", None),
        P(None, None, "wsh"),
        P(None, "wsh"),
        P(None, "wsh"),
        P(None, "wsh"),
        P(None, "wsh"),
        P(None, "wsh"),
        P(None, "wsh"),
        P(None, "wsh"),
        P(None, "wsh"),
        P(None, "wsh"),
    )
    return jax.shard_map(choose_body(mesh), mesh=mesh, in_specs=in_specs, out_specs=out_specs, check_vma=False)
```
